32 devices in a mesh: heads: 4 (over y, x), fsdp: 8 (over z, core).
Axes of the slice: x: 2, y: 2, z: 4, core: 2. Of those that a mesh axis runs over, the one named last changes fastest.
Arguments:
- inputs: bfloat16 [8, 3072, 1280], P('fsdp', 'heads'), may hold values from -6 to 6
- cotangent: bfloat16 [8, 3072, 1280], P('fsdp', 'heads'), may hold values from -6 to 6
- lengths: int32 [8, 3], P('fsdp'), may hold values from 1 to 1024, 1536 in all within a row
- adapter_ids: int32 [8, 4], P('fsdp'), may hold values from 0 to 7
- query_weight: bfloat16 [1280, 1280], P('fsdp'), may hold values from -0.15625 to 0.15625
- key_weight: bfloat16 [1280, 1280], P('fsdp'), may hold values from -0.15625 to 0.15625
- value_weight: bfloat16 [1280, 1280], P('fsdp'), may hold values from -0.15625 to 0.15625
- out_weight: bfloat16 [1280, 1280], P('fsdp'), may hold values from -1.25 to 1.25
- up_weight: bfloat16 [1280, 1280], P('fsdp'), may hold values from -0.15625 to 0.15625
- down_weight: bfloat16 [1280, 1280], P('fsdp'), may hold values from -0.15625 to 0.15625
- attn_gain: bfloat16 [1280], replicated, may hold values from 0.099609375 to 1.8984375
- mlp_gain: bfloat16 [1280], replicated, may hold values from 0.099609375 to 1.8984375
- query_scale: float32 [80], replicated, may hold values from 0.5 to 2
- adapter_in: bfloat16 [4, 8, 1280, 16], replicated, may hold values from -0.15625 to 0.15625
- adapter_out: bfloat16 [4, 8, 16, 1280], replicated, may hold values from -1.5 to 1.5
Outputs:
- outputs: bfloat16 [8, 3072, 1280], P('fsdp', 'heads')
- grad_inputs: float32 [8, 3072, 1280], P('fsdp', 'heads')
- grad_adapter_in: float32 [4, 8, 1280, 16], replicated
- grad_adapter_out: float32 [4, 8, 16, 1280], replicated
The draws below stay inside these ranges and needn't reach their ends.
Inputs may be any that keep to these rules, and one draw needn't show every extreme that they name: In every group the 3 lengths sum to 1536, and the longest is 1024.
All inputs are finite; a program needn't handle non-finite values.
Results may differ from the reference program's by a relative error of at most 0.015.
The reference program's roundings to bfloat16 on the way count: a program that leaves them out, or rounds other values in their place, can miss the bound.
Values may be sent and summed in bfloat16 or wider, within the bound.
No kernel may reach another device: no remote copies, remote signals or barrier semaphores. Data moves between devices by JAX's collectives and lax.ppermute only.
A program may use at most 256 MiB of HBM per device.

```python
import math
import jax
import jax.numpy as jnp
import numpy as np
from jax import lax

D = 1280
HEADS = 16
HEAD_DIM = 80
FF = 1280
RANK = 16
ADAPTERS = 8
CONTS = 3
CONT_LEN = 512
PROMPT_LEN = 1536
CONT_MOST = 1024
GROUP_TOK = 3072
GROUPS = 8


def plant(array, key, least, high):
    longest = array.shape.index(max(array.shape))
    spots = []
    for shift in (0, 1):
        where = [jax.random.randint(jax.random.fold_in(key, axis), (), 0, length) for axis, length in enumerate(array.shape)]
        where[longest] = (where[longest] + shift) % array.shape[longest]
        spots.append(tuple(where))
    return array.at[spots[0]].set(least).at[spots[1]].set(high)


def block_levels(rng, shape, split, smallest, high):
    gain = 1.0
    for dim, shards_of in split:
        draws = jax.random.uniform(jax.random.fold_in(jax.random.fold_in(rng, 6), dim), (shards_of,), jnp.float32, smallest / len(split), high / len(split))
        gain = gain * jnp.repeat(jnp.exp(draws), shape[dim] // shards_of).reshape((-1,) + (1,) * (len(shape) - 1 - dim))
    return gain


def profile(amount, total, limit, lean):
    portions = [(1 << 20) // math.isqrt(rank ** lean) + 1 for rank in range(2, amount + 1)]
    spare, counts = total - limit - (amount - 1), [1] * (amount - 1)
    while spare > 0:
        movable = [i for i in range(amount - 1) if counts[i] < limit]
        whole, remaining = sum([portions[i] for i in movable]), spare
        for i in movable:
            addition = min(limit - counts[i], max(1, remaining * portions[i] // whole), spare)
            counts[i] = counts[i] + addition
            spare = spare - addition
    return np.array([limit] + counts)


def ragged_sizes(rng, number_of, total, bound, skew):
    if number_of == 2:
        one = jax.random.randint(rng, (), max(1, total - bound), min(bound, total - 1) + 1)
        return jnp.stack([one, total - one])
    sizes = jnp.asarray(profile(number_of, total, bound, skew), jnp.int32)
    couples = (number_of - 1) // 2
    source_of, receiver = sizes[1:1 + 2 * couples:2], sizes[2:2 + 2 * couples:2]
    room = jnp.minimum(source_of - 1, bound - receiver)
    moved = jax.random.randint(jax.random.fold_in(rng, 1), (couples,), 0, 1 << 20) % (room + 1)
    sizes = sizes.at[1:1 + 2 * couples:2].set(source_of - moved).at[2:2 + 2 * couples:2].set(receiver + moved)
    return sizes[jax.random.permutation(jax.random.fold_in(rng, 2), number_of)]


def gaussian(key, dims, deviation, most, cuts=(), held_as=jnp.bfloat16):
    level = block_levels(key, dims, cuts, -0.22, 0.18) if cuts else 1.0
    drawn = jax.random.normal(key, dims, jnp.float32) * deviation * level
    return jnp.minimum(jnp.maximum(drawn, -most), most).astype(held_as)


def setup_inputs(seed: int = 0) -> dict:
    arg_keys = jax.random.split(jax.random.key(seed), 16)
    inputs = gaussian(arg_keys[0], (GROUPS, GROUP_TOK, D), 1.0, 6.0, ((0, 8), (1, 4)))
    cotangent = gaussian(arg_keys[1], (GROUPS, GROUP_TOK, D), 1.0, 6.0, ((0, 8), (1, 4)))
    lengths = jax.vmap(lambda own: ragged_sizes(own, CONTS, CONTS * CONT_LEN, CONT_MOST, 1))(jax.random.split(arg_keys[2], GROUPS)).reshape((GROUPS, CONTS)).astype(jnp.int32)
    adapter_ids = plant(jax.random.randint(arg_keys[3], (GROUPS, CONTS + 1), 0, ADAPTERS), jax.random.fold_in(arg_keys[3], 1), 0, ADAPTERS - 1).astype(jnp.int32)
    query_weight = gaussian(arg_keys[4], (D, D), D ** -0.5, 0.15625, ((0, 8),))
    key_weight = gaussian(arg_keys[5], (D, D), D ** -0.5, 0.15625, ((0, 8),))
    value_weight = gaussian(arg_keys[6], (D, D), D ** -0.5, 0.15625, ((0, 8),))
    out_weight = gaussian(arg_keys[7], (D, D), (D // 64) ** -0.5, 1.25, ((0, 8),))
    up_weight = gaussian(arg_keys[8], (D, FF), D ** -0.5, 0.15625, ((0, 8),))
    down_weight = gaussian(arg_keys[9], (FF, D), FF ** -0.5, 0.15625, ((0, 8),))
    attn_gain = jnp.clip(1.0 + 0.18 * jax.random.normal(arg_keys[10], (D,), jnp.float32), 0.099609375, 1.8984375).astype(jnp.bfloat16)
    mlp_gain = jnp.clip(1.0 + 0.18 * jax.random.normal(arg_keys[11], (D,), jnp.float32), 0.099609375, 1.8984375).astype(jnp.bfloat16)
    query_scale = jnp.clip(jnp.exp(jax.random.uniform(arg_keys[12], (HEAD_DIM,), jnp.float32, math.log(0.5), math.log(2.0))), 0.5, 2.0)
    adapter_in = gaussian(arg_keys[13], (4, ADAPTERS, D, RANK), D ** -0.5, 0.15625)
    adapter_out = gaussian(arg_keys[14], (4, ADAPTERS, RANK, D), RANK ** -0.5, 1.5)
    return {"inputs": inputs, "cotangent": cotangent, "lengths": lengths, "adapter_ids": adapter_ids, "query_weight": query_weight, "key_weight": key_weight, "value_weight": value_weight, "out_weight": out_weight, "up_weight": up_weight, "down_weight": down_weight, "attn_gain": attn_gain, "mlp_gain": mlp_gain, "query_scale": query_scale, "adapter_in": adapter_in, "adapter_out": adapter_out}


PRECISE = lax.Precision.HIGHEST
EPSILON = 1e-06

@jax.custom_vjp
def low(v):
    return lax.optimization_barrier(v.astype(jnp.bfloat16)).astype(jnp.float32)

@jax.custom_vjp
def low_back(v):
    return v

def low_keep(v):
    return (low(v), None)

def low_pass(kept, grad):
    return (grad,)

def back_keep(v):
    return (v, None)

def back_low(kept, grad):
    return (low(grad),)
low.defvjp(low_keep, low_pass)
low_back.defvjp(back_keep, back_low)

def matmul(left, right):
    return jnp.dot(left, right, precision=PRECISE)

def normalize(values, gain_vec):
    return values * lax.rsqrt(lax.optimization_barrier(jnp.mean(values * values, axis=-1, keepdims=True)) + EPSILON) * gain_vec

def segment_of(length_row):
    places = jnp.arange(GROUP_TOK, dtype=jnp.int32)
    bounds = jnp.cumsum(length_row).astype(jnp.int32)
    passed = lax.optimization_barrier(jnp.sum((places[:, None] - PROMPT_LEN >= bounds[None, :]).astype(jnp.int32), axis=1))
    return jnp.where(places < PROMPT_LEN, 0, 1 + passed).astype(jnp.int32)

def picker(segments, id_row):
    member = (segments[:, None] == jnp.arange(CONTS + 1, dtype=jnp.int32)[None, :]).astype(jnp.int32)
    token_ids = lax.optimization_barrier(jnp.sum(member * id_row[None, :], axis=1))
    columns = jnp.arange(ADAPTERS * RANK, dtype=jnp.int32) // RANK
    return (token_ids[:, None] == columns[None, :]).astype(jnp.float32)

def adapter(normed, down_all, up_all, chosen):
    flat_down = jnp.transpose(down_all, (1, 0, 2)).reshape(down_all.shape[1], ADAPTERS * RANK)
    inner_low = low(low_back(matmul(normed, flat_down) * chosen))
    return matmul(inner_low, up_all.reshape(ADAPTERS * RANK, up_all.shape[2]))

def attention(queries, key_rows, value_rows, segments):
    block_count = GROUP_TOK // CONT_LEN
    query_blocks = queries.reshape(block_count, CONT_LEN, HEADS, HEAD_DIM)
    key_heads = key_rows.reshape(GROUP_TOK, HEADS, HEAD_DIM)
    value_heads = value_rows.reshape(GROUP_TOK, HEADS, HEAD_DIM)
    places = jnp.arange(GROUP_TOK, dtype=jnp.int32)
    prompt_col = segments == 0

    def one_block(pieces):
        query_block, row_places, row_segments = pieces
        scores = low_back(jnp.einsum('qhd,khd->hqk', query_block, key_heads, precision=PRECISE))
        allowed = (places[None, :] <= row_places[:, None]) & (prompt_col[None, :] | (segments[None, :] == row_segments[:, None]))
        probability = jax.nn.softmax(jnp.where(allowed[None], scores, -1e+30), axis=-1)
        mixture = jnp.einsum('hqk,khd->qhd', low(probability), value_heads, precision=PRECISE)
        return mixture.reshape(CONT_LEN, HEADS * HEAD_DIM)
    outputs = lax.map(jax.checkpoint(one_block), (query_blocks, places.reshape(block_count, CONT_LEN), segments.reshape(block_count, CONT_LEN)))
    return outputs.reshape(GROUP_TOK, HEADS * HEAD_DIM)

def layer(inputs_f, down_all, up_all, frozen, segments, chosen):
    w_query, w_key, w_value, w_out, w_up, w_down, gain_attn, gain_mlp, scale_row = frozen
    normed = low(normalize(inputs_f, gain_attn))
    query_pre = low_back(matmul(normed, w_query) + adapter(normed, down_all[0], up_all[0], chosen))
    queries = low(low_back(query_pre * scale_row))
    key_rows = low(low_back(matmul(normed, w_key)))
    value_rows = low(low_back(matmul(normed, w_value) + adapter(normed, down_all[1], up_all[1], chosen)))
    mixed = low(low_back(attention(queries, key_rows, value_rows, segments)))
    middle = inputs_f + low_back(matmul(mixed, w_out))
    normed_mlp = low(normalize(middle, gain_mlp))
    before = low_back(matmul(normed_mlp, w_up) + adapter(normed_mlp, down_all[2], up_all[2], chosen))
    hidden = low(before * jax.nn.sigmoid(before))
    after = low_back(matmul(hidden, w_down) + adapter(hidden, down_all[3], up_all[3], chosen))
    return middle + after

def reference(inputs, cotangent, lengths, adapter_ids, query_weight, key_weight, value_weight, out_weight, up_weight, down_weight, attn_gain, mlp_gain, query_scale, adapter_in, adapter_out):
    scale_row = jnp.tile(query_scale.astype(jnp.float32), HEADS) * HEAD_DIM ** (-0.5)
    frozen = (query_weight.astype(jnp.float32), key_weight.astype(jnp.float32), value_weight.astype(jnp.float32), out_weight.astype(jnp.float32), up_weight.astype(jnp.float32), down_weight.astype(jnp.float32), attn_gain.astype(jnp.float32), mlp_gain.astype(jnp.float32), scale_row)
    down_all = adapter_in.astype(jnp.float32)
    up_all = adapter_out.astype(jnp.float32)

    def per_group(carry, pieces):
        inputs_g, cot_g, length_row, id_row = pieces
        segments = segment_of(length_row)
        chosen = picker(segments, id_row)

        def forward(inputs_f, down_part, up_part):
            return layer(inputs_f, down_part, up_part, frozen, segments, chosen)
        result, pullback = jax.vjp(forward, inputs_g.astype(jnp.float32), down_all, up_all)
        grad_in_g, grad_down, grad_up = pullback(cot_g.astype(jnp.float32))
        return ((carry[0] + grad_down, carry[1] + grad_up), (result.astype(jnp.bfloat16), grad_in_g))
    start_carry = (jnp.zeros_like(down_all), jnp.zeros_like(up_all))
    (grad_down, grad_up), (outputs, grad_inputs) = lax.scan(per_group, start_carry, (inputs, cotangent, lengths, adapter_ids))
    return (outputs, grad_inputs, grad_down, grad_up)
```

```python
import jax
import jax.numpy as jnp
from jax import lax
from jax.experimental import pallas as pl
from jax.experimental.pallas import tpu as pltpu
from jax.sharding import PartitionSpec as P

D = 1280
HEADS = 16
HD = 80
RANK = 16
ADAPTERS = 8
AR = ADAPTERS * RANK
TOK = 3072
PROMPT = 1536
ROWS = 768
PARTS = TOK // ROWS
LH = HEADS // PARTS
EPSILON = 1e-06
B = 256
f32, bf16 = jnp.float32, jnp.bfloat16


def nt(a, b):
    return lax.dot_general(a, b, (((1,), (1,)), ((), ())), preferred_element_type=f32)


def tn(a, b):
    return lax.dot_general(a, b, (((0,), (0,)), ((), ())), preferred_element_type=f32)


def qkv_kernel(bounds, ids, x_ref, gain_ref, w_ref, down_ref, up_ref, scale_ref, out_ref, wt, ut):
    @pl.when(pl.program_id(0) == 0)
    def _():
        wt[...] = w_ref[...].T
        ut[...] = up_ref[...].T

    x = x_ref[...].astype(f32)
    q = lax.rsqrt(jnp.mean(x * x, axis=1, keepdims=True) + EPSILON)
    normed = (x * q * gain_ref[...]).astype(bf16)
    pos = pl.program_id(0) * B + lax.broadcasted_iota(jnp.int32, (B, 1), 0)
    token = jnp.where(
        pos < PROMPT, ids[0], jnp.where(pos < bounds[0], ids[1], jnp.where(pos < bounds[1], ids[2], ids[3]))
    )
    lane = lax.broadcasted_iota(jnp.int32, (B, 2 * AR), 1)
    chosen = (lane % AR) // RANK == token
    inner = jnp.where(chosen, nn(normed, down_ref[...]), 0.0).astype(bf16)
    out = nt(wt[...], normed) + nt(ut[...], inner)
    out_ref[...] = (out * scale_ref[...]).astype(bf16)


def qkv_project(bounds, ids, x, gain, w, down, up, scale):
    width = w.shape[1]
    return pl.pallas_call(
        qkv_kernel,
        out_shape=jax.ShapeDtypeStruct((width, TOK), bf16),
        grid_spec=pltpu.PrefetchScalarGridSpec(
            num_scalar_prefetch=2,
            grid=(TOK // B,),
            in_specs=[
                pl.BlockSpec((B, D), lambda i, *_: (i, 0)),
                pl.BlockSpec((1, D), lambda i, *_: (0, 0)),
                pl.BlockSpec((D, width), lambda i, *_: (0, 0)),
                pl.BlockSpec((D, 2 * AR), lambda i, *_: (0, 0)),
                pl.BlockSpec((2 * AR, width), lambda i, *_: (0, 0)),
                pl.BlockSpec((width, 1), lambda i, *_: (0, 0)),
            ],
            out_specs=pl.BlockSpec((width, B), lambda i, *_: (0, i)),
            scratch_shapes=[pltpu.VMEM((width, D), bf16), pltpu.VMEM((width, 2 * AR), bf16)],
        ),
        compiler_params=pltpu.CompilerParams(dimension_semantics=("arbitrary",), vmem_limit_bytes=60 << 20),
        cost_estimate=pl.CostEstimate(flops=2 * TOK * D * width, bytes_accessed=TOK * D * 2, transcendentals=0),
        name="qkv_project",
    )(bounds, ids, x, gain, w, down, up, scale)


NEG = -1e30

def nn(a, b):
    return lax.dot_general(a, b, (((1,), (0,)), ((), ())), preferred_element_type=f32)

def start_row(qpos, b1, b2):
    return jnp.where(qpos < PROMPT, 0, jnp.where(qpos < b1, PROMPT, jnp.where(qpos < b2, b1, b2)))

def first_block(i, b1, b2):
    q0 = i * B
    return jnp.where(q0 < b1, PROMPT, jnp.where(q0 < b2, b1, b2)) // B


HPB = 4
FW = 512
def fwd_kernel(bounds, qkv_ref, o_ref, lse_ref, kp, qt, vt):
    b1, b2 = bounds[0], bounds[1]
    zpad = jnp.zeros((128 - HD, 128), bf16)
    for h in range(HPB):
        r = h * 3 * HD
        qt[h, 0:HD, :] = qkv_ref[r:r + HD, :]
        qt[h, HD:128, :] = jnp.zeros((128 - HD, TOK), bf16)
        vt[h, 0:HD, :] = qkv_ref[r + 2 * HD:r + 3 * HD, :]
        vt[h, HD:96, :] = (lax.broadcasted_iota(jnp.int32, (16, TOK), 0) == 0).astype(bf16)
        for t in range(TOK // 128):
            kt = qkv_ref[r + HD:r + 2 * HD, t * 128:(t + 1) * 128]
            kp[h, t * 128:(t + 1) * 128, :] = jnp.concatenate([kt, zpad], axis=0).T

    def qblock(i, _):
        q0 = pl.multiple_of(i * B, B)
        qpos = q0 + lax.broadcasted_iota(jnp.int32, (1, B), 1)
        srow = start_row(qpos, b1, b2)

        def step(k0, width, masked, carry):
            ks = pl.ds(k0, width)
            ss = [nn(kp[h, ks, :], qt[h, :, pl.ds(q0, B)]) for h in range(HPB)]
            if masked:
                kpos = k0 + lax.broadcasted_iota(jnp.int32, (width, B), 0)
                ok = (kpos >= srow) & (kpos <= qpos)
                ss = [jnp.where(ok, s, NEG) for s in ss]
            out = []
            for h in range(HPB):
                m, acc = carry[h]
                m_new = jnp.maximum(m, jnp.max(ss[h], axis=0, keepdims=True))
                p = jnp.exp(ss[h] - m_new).astype(bf16)
                a = jnp.exp(m - m_new)
                out.append((m_new, acc * a + nn(vt[h, :, ks], p)))
            return tuple(out)

        full = jnp.minimum(i * B // FW, PROMPT // FW)
        lo = jnp.where(i < PROMPT // B, (FW // B) * (i * B // FW), first_block(i, b1, b2))
        carry = tuple((jnp.full((1, B), NEG, f32), jnp.zeros((96, B), f32)) for _ in range(HPB))
        carry = lax.fori_loop(0, full, lambda j, c: step(pl.multiple_of(j * FW, FW), FW, False, c), carry)
        carry = lax.fori_loop(lo, i + 1, lambda j, c: step(pl.multiple_of(j * B, B), B, True, c), carry)
        for h in range(HPB):
            m, acc = carry[h]
            l = acc[HD:HD + 1, :]
            o_ref[i // 3, h * HD:(h + 1) * HD, pl.ds(pl.multiple_of((i % 3) * B, B), B)] = (acc[0:HD, :] / l).astype(bf16)
            lse_ref[h, :, pl.ds(q0, B)] = m + jnp.log(l)
        return 0
    lax.fori_loop(0, TOK // B, qblock, 0)

def attn_fwd(bounds, qkvt):
    nh = qkvt.shape[0] // (3 * HD)
    return pl.pallas_call(
        fwd_kernel,
        out_shape=(jax.ShapeDtypeStruct((4, nh * HD, 768), bf16), jax.ShapeDtypeStruct((nh, 1, TOK), f32)),
        grid_spec=pltpu.PrefetchScalarGridSpec(
            num_scalar_prefetch=1, grid=(nh // HPB,),
            in_specs=[pl.BlockSpec((HPB * 3 * HD, TOK), lambda h, b: (h, 0))],
            out_specs=[pl.BlockSpec((4, HPB * HD, 768), lambda h, b: (0, h, 0)), pl.BlockSpec((HPB, 1, TOK), lambda h, b: (h, 0, 0))],
            scratch_shapes=[pltpu.VMEM((HPB, TOK, 128), bf16), pltpu.VMEM((HPB, 128, TOK), bf16), pltpu.VMEM((HPB, 96, TOK), bf16)]),
        compiler_params=pltpu.CompilerParams(dimension_semantics=("arbitrary",), vmem_limit_bytes=60 << 20),
        name="attn_fwd",
    )(bounds, qkvt)

def parts3(x):
    hi = x.astype(bf16)
    r = x - hi.astype(f32)
    mid = r.astype(bf16)
    lo = (r - mid.astype(f32)).astype(bf16)
    return hi, mid, lo

def bwd_kernel(bounds, scale_ref, qkv_ref, do_ref, o_ref, lse_ref, out_ref, kp, vp, qt, dot_, qr, dor, dk, dv, dqt):
    b1, b2 = bounds[0], bounds[1]
    row16 = lax.broadcasted_iota(jnp.int32, (16, 128), 0)
    ones3 = (row16 < 3).astype(bf16)
    z32 = jnp.zeros((32, 128), bf16)
    for t in range(TOK // 128):
        sl = slice(t * 128, (t + 1) * 128)
        c, off = t // 6, (t % 6) * 128
        q = qkv_ref[0:HD, sl]; k = qkv_ref[HD:2 * HD, sl]; v = qkv_ref[2 * HD:3 * HD, sl]
        do = do_ref[c, :, off:off + 128]; o = o_ref[c, :, off:off + 128]
        delta = jnp.sum(do.astype(f32) * o.astype(f32), axis=0, keepdims=True)
        def tail(x):
            h, m, l = parts3(-x)
            return (jnp.where(row16 == 0, h.astype(f32), jnp.where(row16 == 1, m.astype(f32), jnp.where(row16 == 2, l.astype(f32), 0.0)))).astype(bf16)
        qa = jnp.concatenate([q, tail(lse_ref[0, :, sl]), z32], axis=0)
        da = jnp.concatenate([do, tail(delta), z32], axis=0)
        qt[:, sl] = qa; dot_[:, sl] = da
        qr[sl, :] = qa.T; dor[sl, :] = da.T
        kp[sl, :] = jnp.concatenate([k, ones3, z32], axis=0).T
        vp[sl, :] = jnp.concatenate([v, ones3, z32], axis=0).T
    dk[...] = jnp.zeros_like(dk); dv[...] = jnp.zeros_like(dv); dqt[...] = jnp.zeros_like(dqt)

    def block(k0, q0, kw, qw, masked):
        ks, qs = pl.ds(k0, kw), pl.ds(q0, qw)
        p = jnp.exp(nn(kp[ks, :], qt[:, qs]))
        if masked:
            qpos = q0 + lax.broadcasted_iota(jnp.int32, (1, qw), 1)
            srow = start_row(qpos, b1, b2)
            kpos = k0 + lax.broadcasted_iota(jnp.int32, (kw, qw), 0)
            p = jnp.where((kpos >= srow) & (kpos <= qpos), p, 0.0)
        ds = (p * nn(vp[ks, :], dot_[:, qs])).astype(bf16)
        dv[ks, :] += nn(p.astype(bf16), dor[qs, :])
        dk[ks, :] += nn(ds, qr[qs, :])
        dqt[:, qs] += nn(qkv_ref[HD:2 * HD, ks], ds)

    F = 512
    def full(n, _):
        block(pl.multiple_of((n % 3) * F, F), pl.multiple_of(PROMPT + (n // 3) * F, F), F, F, False)
        return 0
    lax.fori_loop(0, 9, full, 0)
    def tri(n, _):
        qb = jnp.where(n == 0, 1, 2); kb = jnp.where(n == 2, 1, 0)
        block(pl.multiple_of(kb * F, F), pl.multiple_of(qb * F, F), F, F, False)
        return 0
    lax.fori_loop(0, 3, tri, 0)
    def outer(i, _):
        lo = jnp.where(i < PROMPT // B, 2 * (i // 2), first_block(i, b1, b2))
        def inner(j, _):
            block(pl.multiple_of(j * B, B), pl.multiple_of(i * B, B), B, B, True)
            return 0
        return lax.fori_loop(lo, i + 1, inner, 0)
    lax.fori_loop(0, TOK // B, outer, 0)

    scale = scale_ref[...]
    for t in range(TOK // 128):
        sl = slice(t * 128, (t + 1) * 128)
        c, off = t // 6, (t % 6) * 128
        dq = dqt[:, sl].astype(bf16).astype(f32) * scale
        out_ref[c, 0:HD, off:off + 128] = dq.astype(bf16)
        out_ref[c, HD:2 * HD, off:off + 128] = dk[sl, :].T[0:HD, :].astype(bf16)
        out_ref[c, 2 * HD:3 * HD, off:off + 128] = dv[sl, :].T[0:HD, :].astype(bf16)

def attn_bwd(bounds, scale, qkvt, dot_, ot, lse):
    nh = qkvt.shape[0] // (3 * HD)
    return pl.pallas_call(
        bwd_kernel,
        out_shape=jax.ShapeDtypeStruct((4, nh * 3 * HD, 768), bf16),
        grid_spec=pltpu.PrefetchScalarGridSpec(
            num_scalar_prefetch=1, grid=(nh,),
            in_specs=[pl.BlockSpec((HD, 1), lambda h, b: (0, 0)),
                      pl.BlockSpec((3 * HD, TOK), lambda h, b: (h, 0)),
                      pl.BlockSpec((4, HD, 768), lambda h, b: (0, h, 0)),
                      pl.BlockSpec((4, HD, 768), lambda h, b: (0, h, 0)),
                      pl.BlockSpec((1, 1, TOK), lambda h, b: (h, 0, 0))],
            out_specs=pl.BlockSpec((4, 3 * HD, 768), lambda h, b: (0, h, 0)),
            scratch_shapes=[pltpu.VMEM((TOK, 128), bf16), pltpu.VMEM((TOK, 128), bf16), pltpu.VMEM((128, TOK), bf16), pltpu.VMEM((128, TOK), bf16),
                            pltpu.VMEM((TOK, 128), bf16), pltpu.VMEM((TOK, 128), bf16),
                            pltpu.VMEM((TOK, 128), f32), pltpu.VMEM((TOK, 128), f32), pltpu.VMEM((HD, TOK), f32)]),
        compiler_params=pltpu.CompilerParams(dimension_semantics=("arbitrary",), vmem_limit_bytes=60 << 20),
        name="attn_bwd",
    )(bounds, scale, qkvt, dot_, ot, lse)


def normalize(values, gain_vec):
    scaling = lax.rsqrt(jnp.mean(values * values, axis=-1, keepdims=True) + EPSILON)
    return (values * scaling * gain_vec, scaling)


def normalize_back(values, scaling, gain_vec, upstream):
    weighted = gain_vec * upstream
    return scaling * weighted - values * scaling**3 * jnp.mean(values * weighted, axis=-1, keepdims=True)


def by_head(query, key, value):
    rows, width = query.shape
    split = (rows, width // HD, 1, HD)
    stacked = jnp.concatenate([query.reshape(split), key.reshape(split), value.reshape(split)], axis=2)
    return stacked.reshape(rows, 3 * width)


def exchange(value):
    return lax.all_to_all(value, "heads", split_axis=0, concat_axis=0, tiled=True)


def body(
    inputs,
    cotangent,
    lengths,
    adapter_ids,
    query_weight,
    key_weight,
    value_weight,
    out_weight,
    up_weight,
    down_weight,
    attn_gain,
    mlp_gain,
    query_scale,
    adapter_in,
    adapter_out,
):
    part = lax.axis_index("heads")
    offset = part * ROWS
    ends = PROMPT + jnp.cumsum(lengths[0])
    bounds = ends[:2].astype(jnp.int32)
    ids = adapter_ids[0]
    places = offset + jnp.arange(ROWS, dtype=jnp.int32)
    token = jnp.where(
        places < PROMPT,
        ids[0],
        jnp.where(places < bounds[0], ids[1], jnp.where(places < bounds[1], ids[2], ids[3])),
    )
    chosen = (token[:, None] == (jnp.arange(AR, dtype=jnp.int32) // RANK)[None, :]).astype(f32)
    chosen2 = jnp.concatenate([chosen, chosen], axis=1)
    flat_down = jnp.transpose(adapter_in, (0, 2, 1, 3)).reshape(4, D, AR)
    flat_up = adapter_out.reshape(4, AR, D)
    gain_attn = attn_gain.astype(f32)
    gain_mlp = mlp_gain.astype(f32)
    width = LH * HD

    def mine(weight):
        return lax.dynamic_slice_in_dim(weight, part * width, width, axis=1)

    weights_mine = by_head(mine(query_weight), mine(key_weight), mine(value_weight))
    weights_mine = lax.all_gather(weights_mine, "fsdp", axis=0, tiled=True)
    rows_all = lax.all_gather(inputs[0], "heads", axis=0, tiled=True)
    w_out = lax.all_gather(out_weight, "fsdp", axis=0, tiled=True)
    w_up = lax.all_gather(up_weight, "fsdp", axis=0, tiled=True)
    w_down = lax.all_gather(down_weight, "fsdp", axis=0, tiled=True)
    weights_all = lax.all_gather(by_head(query_weight, key_weight, value_weight), "fsdp", axis=0, tiled=True)

    down_pair = jnp.concatenate([flat_down[0], flat_down[1]], axis=1)
    zero = jnp.zeros((AR, D), bf16)
    up_pair = jnp.concatenate(
        [by_head(flat_up[0], zero, zero), by_head(zero, zero, flat_up[1])], axis=0
    )
    up_mine = lax.dynamic_slice_in_dim(up_pair, part * 3 * width, 3 * width, axis=1)
    scale_row = query_scale * HD ** (-0.5)
    scale_mine = jnp.tile(jnp.concatenate([scale_row, jnp.ones((2 * HD,), f32)]), LH)[:, None]

    qkvt = qkv_project(
        bounds, ids, rows_all, gain_attn[None, :], weights_mine, down_pair, up_mine, scale_mine
    )
    mixture, logsum = attn_fwd(bounds, qkvt)
    mixed = exchange(mixture).reshape(D, ROWS)

    rows_in = inputs[0].astype(f32)
    normed, scaling_attn = normalize(rows_in, gain_attn)
    normed_low = normed.astype(bf16)
    inner_pair = (nn(normed_low, down_pair) * chosen2).astype(bf16)

    middle = rows_in + tn(mixed, w_out)
    normed_mlp, scaling_mlp = normalize(middle, gain_mlp)
    normed_mlp_low = normed_mlp.astype(bf16)
    inner_up = (nn(normed_mlp_low, flat_down[2]) * chosen).astype(bf16)
    before = nn(normed_mlp_low, w_up) + nn(inner_up, flat_up[2])
    gate = jax.nn.sigmoid(before)
    hidden_low = (before * gate).astype(bf16)
    inner_down = (nn(hidden_low, flat_down[3]) * chosen).astype(bf16)
    outputs = (middle + (nn(hidden_low, w_down) + nn(inner_down, flat_up[3]))).astype(bf16)

    upstream = cotangent[0].astype(f32)
    grad_after = cotangent[0]
    spread_down = (nt(grad_after, flat_up[3]) * chosen).astype(bf16)
    grad_hidden = nt(grad_after, w_down) + nt(spread_down, flat_down[3])
    grad_before = (grad_hidden * gate * (1.0 + before * (1.0 - gate))).astype(bf16)
    spread_up = (nt(grad_before, flat_up[2]) * chosen).astype(bf16)
    grad_normed_mlp = nt(grad_before, w_up) + nt(spread_up, flat_down[2])
    grad_middle = upstream + normalize_back(middle, scaling_mlp, gain_mlp, grad_normed_mlp)
    grad_branch = grad_middle.astype(bf16)
    grad_mixed = nt(w_out, grad_branch).astype(bf16).reshape(PARTS, width, ROWS)
    grad_heads = exchange(grad_mixed)

    first_mlp = jnp.stack([tn(normed_mlp_low, spread_up), tn(hidden_low, spread_down)]).astype(bf16)
    second_mlp = jnp.stack([tn(inner_up, grad_before), tn(inner_down, grad_after)]).astype(bf16)
    first_mlp, second_mlp = lax.psum((first_mlp, second_mlp), ("heads", "fsdp"))

    grad_qkv = attn_bwd(bounds, scale_row[:, None], qkvt, grad_heads, mixture, logsum)
    grad_rows = exchange(grad_qkv).reshape(3 * D, ROWS)

    spread_pair = (lax.dot_general(grad_rows, up_pair, (((0,), (1,)), ((), ())), preferred_element_type=f32) * chosen2).astype(bf16)
    first_attn = tn(normed_low, spread_pair).astype(bf16)
    grad_split = grad_rows.reshape(HEADS, 3, HD, ROWS)
    second_query = lax.dot_general(inner_pair[:, :AR], grad_split[:, 0], (((0,), (2,)), ((), ())), preferred_element_type=f32)
    second_value = lax.dot_general(inner_pair[:, AR:], grad_split[:, 2], (((0,), (2,)), ((), ())), preferred_element_type=f32)
    second_attn = jnp.stack([second_query.reshape(AR, D), second_value.reshape(AR, D)]).astype(bf16)
    first_attn, second_attn = lax.psum((first_attn, second_attn), ("heads", "fsdp"))
    grad_normed = lax.dot_general(
        grad_rows, weights_all, (((0,), (1,)), ((), ())), preferred_element_type=f32
    ) + nt(spread_pair, down_pair)
    grad_inputs = grad_middle + normalize_back(rows_in, scaling_attn, gain_attn, grad_normed)

    first = jnp.stack([first_attn[:, :AR], first_attn[:, AR:], first_mlp[0], first_mlp[1]]).astype(f32)
    second = jnp.concatenate([second_attn, second_mlp]).astype(f32)
    grad_first = jnp.transpose(first.reshape(4, D, ADAPTERS, RANK), (0, 2, 1, 3))
    grad_second = second.reshape(4, ADAPTERS, RANK, D)
    return (outputs[None], grad_inputs[None], grad_first, grad_second)


def solution(mesh):
    placed = (
        P("fsdp", "heads", None),
        P("fsdp", "heads", None),
        P("fsdp", None),
        P("fsdp", None),
        P("fsdp", None),
        P("fsdp", None),
        P("fsdp", None),
        P("fsdp", None),
        P("fsdp", None),
        P("fsdp", None),
        P(),
        P(),
        P(),
        P(),
        P(),
    )
    return jax.shard_map(
        body,
        mesh=mesh,
        in_specs=placed,
        out_specs=(P("fsdp", "heads", None), P("fsdp", "heads", None), P(), P()),
        check_vma=False,
    )
```

```python
import jax
import jax.numpy as jnp
from jax import lax
from jax.experimental import pallas as pl
from jax.experimental.pallas import tpu as pltpu
from jax.sharding import PartitionSpec as P

D = 1280
HEADS = 16
HD = 80
RANK = 16
ADAPTERS = 8
AR = ADAPTERS * RANK
TOK = 3072
PROMPT = 1536
ROWS = 768
QB = 384
PARTS = TOK // ROWS
LH = HEADS // PARTS
EPSILON = 1e-06
B = 256
f32, bf16 = jnp.float32, jnp.bfloat16


def nt(a, b):
    return lax.dot_general(a, b, (((1,), (1,)), ((), ())), preferred_element_type=f32)


def tn(a, b):
    return lax.dot_general(a, b, (((0,), (0,)), ((), ())), preferred_element_type=f32)


def nn(a, b):
    return lax.dot_general(a, b, (((1,), (0,)), ((), ())), preferred_element_type=f32)

def start_row(qpos, b1, b2):
    return jnp.where(qpos < PROMPT, 0, jnp.where(qpos < b1, PROMPT, jnp.where(qpos < b2, b1, b2)))

def first_block(i, b1, b2):
    q0 = i * B
    return jnp.where(q0 < b1, PROMPT, jnp.where(q0 < b2, b1, b2)) // B


def token_adapter(pos, meta):
    return jnp.where(
        pos < PROMPT, meta[2], jnp.where(pos < meta[0], meta[3], jnp.where(pos < meta[1], meta[4], meta[5]))
    )


def qkv_kernel(meta, first, x_ref, gain_ref, wt_ref, down_ref, up_ref, scale_ref, *refs):
    out_ref, normed_ref, inner_ref = refs[-3:]
    x = x_ref[...].astype(f32)
    q = lax.rsqrt(jnp.mean(x * x, axis=1, keepdims=True) + EPSILON)
    normed = (x * q * gain_ref[...]).astype(bf16)
    normed_ref[...] = normed
    pos = (first[0] + pl.program_id(0)) * QB + lax.broadcasted_iota(jnp.int32, (QB, 1), 0)
    lane = lax.broadcasted_iota(jnp.int32, (QB, 2 * AR), 1)
    chosen = (lane % AR) // RANK == token_adapter(pos, meta)
    inner = jnp.where(chosen, nn(normed, down_ref[...]), 0.0).astype(bf16)
    inner_ref[...] = inner
    out = nt(wt_ref[...], normed) + nt(up_ref[...], inner)
    out_ref[...] = (out * scale_ref[...]).astype(bf16)


def qkv_project(meta, first, x, gain, wt, down, up, scale, done):
    width = wt.shape[0]
    whole = lambda shape: pl.BlockSpec(shape, lambda i, *_: (0, 0))
    return pl.pallas_call(
        qkv_kernel,
        out_shape=(
            jax.ShapeDtypeStruct((width, TOK), bf16),
            jax.ShapeDtypeStruct((TOK, D), bf16),
            jax.ShapeDtypeStruct((TOK, 2 * AR), bf16),
        ),
        grid_spec=pltpu.PrefetchScalarGridSpec(
            num_scalar_prefetch=2,
            grid=(x.shape[0] // QB,),
            in_specs=[
                pl.BlockSpec((QB, D), lambda i, *_: (i, 0)),
                whole((1, D)),
                whole((width, D)),
                whole((D, 2 * AR)),
                whole((width, 2 * AR)),
                whole((width, 1)),
            ]
            + [pl.BlockSpec(memory_space=pl.ANY)] * len(done),
            out_specs=[
                pl.BlockSpec((width, QB), lambda i, m, first: (0, first[0] + i)),
                pl.BlockSpec((QB, D), lambda i, m, first: (first[0] + i, 0)),
                pl.BlockSpec((QB, 2 * AR), lambda i, m, first: (first[0] + i, 0)),
            ],
        ),
        input_output_aliases={8 + i: i for i in range(len(done))},
        compiler_params=pltpu.CompilerParams(dimension_semantics=("arbitrary",), vmem_limit_bytes=60 << 20),
        cost_estimate=pl.CostEstimate(
            flops=2 * x.shape[0] * D * (width + 2 * AR), bytes_accessed=2 * x.shape[0] * D + 2 * D * width, transcendentals=0
        ),
        name="qkv_project",
    )(meta, first, x, gain, wt, down, up, scale, *done)


def adapter_kernel(meta, *refs):
    grad_refs, (normed_ref, inner_ref, up_ref, first_ref, second_ref) = refs[: LH * PARTS], refs[LH * PARTS :]

    @pl.when(pl.program_id(0) == 0)
    def _():
        first_ref[...] = jnp.zeros_like(first_ref)
        second_ref[...] = jnp.zeros_like(second_ref)

    for m in range(PARTS):

        @pl.when(pl.program_id(0) == m)
        def _(m=m):
            grads = [grad_refs[h * PARTS + m][...] for h in range(LH)]
            spread = nn(up_ref[0], grads[0])
            for h in range(1, LH):
                spread += nn(up_ref[h], grads[h])
            pos = (meta[6] ^ m) * ROWS + lax.broadcasted_iota(jnp.int32, (1, ROWS), 1)
            rank = lax.broadcasted_iota(jnp.int32, (2 * AR, ROWS), 0)
            chosen = (rank % AR) // RANK == token_adapter(pos, meta)
            spread = jnp.where(chosen, spread, 0.0).astype(bf16)
            first = nn(spread, normed_ref[...])
            for c in range(D // 128):
                first_ref[c] += first[:, c * 128 : (c + 1) * 128]
            for h in range(LH):
                second_ref[h, 0] += nn(grads[h][:HD], inner_ref[:, :AR])
                second_ref[h, 1] += nn(grads[h][2 * HD :], inner_ref[:, AR:])


def adapter_grads(meta, grads, normed, inner, up):
    return pl.pallas_call(
        adapter_kernel,
        out_shape=(jax.ShapeDtypeStruct((D // 128, 2 * AR, 128), f32), jax.ShapeDtypeStruct((LH, 2, HD, AR), f32)),
        grid_spec=pltpu.PrefetchScalarGridSpec(
            num_scalar_prefetch=1,
            grid=(PARTS,),
            in_specs=[pl.BlockSpec((3 * HD, ROWS), lambda i, m: (0, 0))] * (LH * PARTS)
            + [
                pl.BlockSpec((ROWS, D), lambda i, m: (m[6] ^ i, 0)),
                pl.BlockSpec((ROWS, 2 * AR), lambda i, m: (m[6] ^ i, 0)),
                pl.BlockSpec((LH, 2 * AR, 3 * HD), lambda i, m: (0, 0, 0)),
            ],
            out_specs=[
                pl.BlockSpec((D // 128, 2 * AR, 128), lambda i, m: (0, 0, 0)),
                pl.BlockSpec((LH, 2, HD, AR), lambda i, m: (0, 0, 0, 0)),
            ],
        ),
        compiler_params=pltpu.CompilerParams(dimension_semantics=("arbitrary",), vmem_limit_bytes=60 << 20),
        cost_estimate=pl.CostEstimate(flops=4 * TOK * D * 2 * AR, bytes_accessed=20 << 20, transcendentals=0),
        name="adapter_grads",
    )(meta, *grads, normed, inner, up)


HPB = 4
NEG = -1e30
FW = 512


def fwd_kernel(bounds, qkv_ref, o_ref, lse_ref, kp, qt, vt):
    b1, b2 = bounds[0], bounds[1]
    zpad = jnp.zeros((128 - HD, 128), bf16)
    for h in range(HPB):
        r = h * 3 * HD
        qt[h, 0:HD, :] = qkv_ref[r:r + HD, :]
        qt[h, HD:128, :] = jnp.zeros((128 - HD, TOK), bf16)
        vt[h, 0:HD, :] = qkv_ref[r + 2 * HD:r + 3 * HD, :]
        vt[h, HD:96, :] = (lax.broadcasted_iota(jnp.int32, (16, TOK), 0) == 0).astype(bf16)
        for t in range(TOK // 128):
            kt = qkv_ref[r + HD:r + 2 * HD, t * 128:(t + 1) * 128]
            kp[h, t * 128:(t + 1) * 128, :] = jnp.concatenate([kt, zpad], axis=0).T

    def qblock(i, _):
        q0 = pl.multiple_of(i * B, B)
        qpos = q0 + lax.broadcasted_iota(jnp.int32, (1, B), 1)
        srow = start_row(qpos, b1, b2)

        def step(k0, width, masked, carry):
            ks = pl.ds(k0, width)
            ss = [nn(kp[h, ks, :], qt[h, :, pl.ds(q0, B)]) for h in range(HPB)]
            if masked:
                kpos = k0 + lax.broadcasted_iota(jnp.int32, (width, B), 0)
                ok = (kpos >= srow) & (kpos <= qpos)
                ss = [jnp.where(ok, s, NEG) for s in ss]
            out = []
            for h in range(HPB):
                m, acc = carry[h]
                m_new = jnp.maximum(m, jnp.max(ss[h], axis=0, keepdims=True))
                p = jnp.exp(ss[h] - m_new).astype(bf16)
                a = jnp.exp(m - m_new)
                out.append((m_new, acc * a + nn(vt[h, :, ks], p)))
            return tuple(out)

        full = jnp.minimum(i * B // FW, PROMPT // FW)
        lo = jnp.where(i < PROMPT // B, (FW // B) * (i * B // FW), first_block(i, b1, b2))
        carry = tuple((jnp.full((1, B), NEG, f32), jnp.zeros((96, B), f32)) for _ in range(HPB))
        carry = lax.fori_loop(0, full, lambda j, c: step(pl.multiple_of(j * FW, FW), FW, False, c), carry)
        carry = lax.fori_loop(lo, i + 1, lambda j, c: step(pl.multiple_of(j * B, B), B, True, c), carry)
        for h in range(HPB):
            m, acc = carry[h]
            l = acc[HD:HD + 1, :]
            o_ref[i // 3, h * HD:(h + 1) * HD, pl.ds(pl.multiple_of((i % 3) * B, B), B)] = (acc[0:HD, :] / l).astype(bf16)
            lse_ref[h, :, pl.ds(q0, B)] = m + jnp.log(l)
        return 0
    lax.fori_loop(0, TOK // B, qblock, 0)

def attn_fwd(bounds, qkvt):
    nh = qkvt.shape[0] // (3 * HD)
    return pl.pallas_call(
        fwd_kernel,
        out_shape=(jax.ShapeDtypeStruct((4, nh * HD, 768), bf16), jax.ShapeDtypeStruct((nh, 1, TOK), f32)),
        grid_spec=pltpu.PrefetchScalarGridSpec(
            num_scalar_prefetch=1, grid=(nh // HPB,),
            in_specs=[pl.BlockSpec((HPB * 3 * HD, TOK), lambda h, b: (h, 0))],
            out_specs=[pl.BlockSpec((4, HPB * HD, 768), lambda h, b: (0, h, 0)), pl.BlockSpec((HPB, 1, TOK), lambda h, b: (h, 0, 0))],
            scratch_shapes=[pltpu.VMEM((HPB, TOK, 128), bf16), pltpu.VMEM((HPB, 128, TOK), bf16), pltpu.VMEM((HPB, 96, TOK), bf16)]),
        compiler_params=pltpu.CompilerParams(dimension_semantics=("arbitrary",), vmem_limit_bytes=60 << 20),
        cost_estimate=pl.CostEstimate(flops=40 * 10**9, bytes_accessed=10 << 20, transcendentals=0),
        name="attn_fwd",
    )(bounds, qkvt)

def parts3(x):
    hi = x.astype(bf16)
    r = x - hi.astype(f32)
    mid = r.astype(bf16)
    lo = (r - mid.astype(f32)).astype(bf16)
    return hi, mid, lo

def bwd_kernel(meta, scale_ref, qkv_ref, *refs):
    do_ref, o_ref, lse_ref = refs[:3]
    out_refs = refs[3 : 3 + PARTS]
    kp, vp, qt, dot, qr, dor, dk, dv, dqt = refs[3 + PARTS :]
    b1, b2, part = meta[0], meta[1], meta[6]
    row16 = lax.broadcasted_iota(jnp.int32, (16, 128), 0)
    ones3 = (row16 < 3).astype(bf16)
    pad = jnp.zeros((32, 128), bf16)
    scale = scale_ref[...]

    def tail(x):
        hi, mid, lo = parts3(-x)
        rest = jnp.where(row16 == 1, mid.astype(f32), jnp.where(row16 == 2, lo.astype(f32), 0.0))
        return jnp.where(row16 == 0, hi.astype(f32), rest).astype(bf16)

    for m in range(PARTS):
        chunk = part ^ m

        @pl.loop(0, 2)
        def _(step, m=m, chunk=chunk):
            for t in range(3):
                off = pl.multiple_of(step * 384 + t * 128, 128)
                sl, here = pl.ds(pl.multiple_of(chunk * ROWS + off, 128), 128), pl.ds(off, 128)
                q, k, v = qkv_ref[0:HD, sl], qkv_ref[HD : 2 * HD, sl], qkv_ref[2 * HD : 3 * HD, sl]
                do, o = do_ref[chunk, :, here], o_ref[chunk, :, here]
                delta = jnp.sum(do.astype(f32) * o.astype(f32), axis=0, keepdims=True)
                qa = jnp.concatenate([q, tail(lse_ref[0, :, sl]), pad], axis=0)
                da = jnp.concatenate([do, tail(delta), pad], axis=0)
                qt[:, sl] = qa
                dot[:, sl] = da
                qr[sl, :] = qa.T
                dor[sl, :] = da.T
                kp[sl, :] = jnp.concatenate([k, ones3, pad], axis=0).T
                vp[sl, :] = jnp.concatenate([v, ones3, pad], axis=0).T

    dk[...] = jnp.zeros_like(dk)
    dv[...] = jnp.zeros_like(dv)
    dqt[...] = jnp.zeros_like(dqt)

    def block(k0, q0, width, masked):
        k0, q0 = pl.multiple_of(k0, width), pl.multiple_of(q0, width)
        ks, qs = pl.ds(k0, width), pl.ds(q0, width)
        p = jnp.exp(nn(kp[ks, :], qt[:, qs]))
        if masked:
            qpos = q0 + lax.broadcasted_iota(jnp.int32, (1, width), 1)
            kpos = k0 + lax.broadcasted_iota(jnp.int32, (width, width), 0)
            p = jnp.where((kpos >= start_row(qpos, b1, b2)) & (kpos <= qpos), p, 0.0)
        ds = (p * nn(vp[ks, :], dot[:, qs])).astype(bf16)
        dv[ks, :] += nn(p.astype(bf16), dor[qs, :])
        dk[ks, :] += nn(ds, qr[qs, :])
        dqt[:, qs] += nn(qkv_ref[HD : 2 * HD, ks], ds)

    @pl.loop(0, 12)
    def _(n):
        qb = jnp.where(n < 9, 3 + n // 3, jnp.where(n == 9, 1, 2))
        kb = jnp.where(n < 9, n % 3, jnp.where(n == 11, 1, 0))
        block(kb * FW, qb * FW, FW, False)

    @pl.loop(0, TOK // B)
    def _(i):
        lo = jnp.where(i < PROMPT // B, 2 * (i // 2), first_block(i, b1, b2))

        @pl.loop(lo, i + 1)
        def _(j):
            block(j * B, i * B, B, True)

    for m in range(PARTS):
        chunk = part ^ m

        @pl.loop(0, 2)
        def _(step, m=m, chunk=chunk):
            for t in range(3):
                off = pl.multiple_of(step * 384 + t * 128, 128)
                sl, here = pl.ds(pl.multiple_of(chunk * ROWS + off, 128), 128), pl.ds(off, 128)
                dq = dqt[:, sl].astype(bf16).astype(f32) * scale
                out_refs[m][0:HD, here] = dq.astype(bf16)
                out_refs[m][HD : 2 * HD, here] = dk[sl, :].T[0:HD, :].astype(bf16)
                out_refs[m][2 * HD : 3 * HD, here] = dv[sl, :].T[0:HD, :].astype(bf16)


def attn_bwd(meta, scale, qkvt, grads, slot, mixture, logsum, head):
    whole = lambda rows: pl.BlockSpec((rows, ROWS), lambda i, b: (0, 0))
    return pl.pallas_call(
        bwd_kernel,
        out_shape=[jax.ShapeDtypeStruct((3 * HD, ROWS), bf16)] * PARTS,
        grid_spec=pltpu.PrefetchScalarGridSpec(
            num_scalar_prefetch=1,
            grid=(1,),
            in_specs=[
                pl.BlockSpec((HD, 1), lambda i, b: (0, 0)),
                pl.BlockSpec((3 * HD, TOK), lambda i, b: (head, 0)),
            ]
            + [
                pl.BlockSpec((PARTS, HD, ROWS), lambda i, b: (0, slot, 0)),
                pl.BlockSpec((PARTS, HD, ROWS), lambda i, b: (0, head, 0)),
                pl.BlockSpec((1, 1, TOK), lambda i, b: (head, 0, 0)),
            ],
            out_specs=[whole(3 * HD)] * PARTS,
            scratch_shapes=[pltpu.VMEM((TOK, 128), bf16)] * 2
            + [pltpu.VMEM((128, TOK), bf16)] * 2
            + [pltpu.VMEM((TOK, 128), bf16)] * 2
            + [pltpu.VMEM((TOK, 128), f32)] * 2
            + [pltpu.VMEM((HD, TOK), f32)],
        ),
        compiler_params=pltpu.CompilerParams(dimension_semantics=("arbitrary",), vmem_limit_bytes=60 << 20),
        cost_estimate=pl.CostEstimate(flops=18 * 10**9, bytes_accessed=8 << 20, transcendentals=0),
        name="attn_bwd",
    )(meta, scale, qkvt, grads, mixture, logsum)


def normalize(values, gain_vec):
    scaling = lax.rsqrt(jnp.mean(values * values, axis=-1, keepdims=True) + EPSILON)
    return (values * scaling * gain_vec, scaling)


def normalize_back(values, scaling, gain_vec, upstream):
    weighted = gain_vec * upstream
    return scaling * weighted - values * scaling**3 * jnp.mean(values * weighted, axis=-1, keepdims=True)


def by_head(query, key, value):
    rows, width = query.shape
    split = (rows, width // HD, 1, HD)
    stacked = jnp.concatenate([query.reshape(split), key.reshape(split), value.reshape(split)], axis=2)
    return stacked.reshape(rows, 3 * width)


def by_slot(query, key, value, part):
    rows = query.shape[0]
    stacked = by_head(query, key, value).reshape(rows, PARTS, LH, 3 * HD)
    pieces = [lax.dynamic_index_in_dim(stacked, part ^ m, axis=1, keepdims=False) for m in range(PARTS)]
    return jnp.stack(pieces, axis=2).reshape(rows, 3 * D)


def exchange(value):
    return lax.all_to_all(value, "heads", split_axis=0, concat_axis=0, tiled=True)


def swap(value, axis, mask):
    count = lax.axis_size(axis)
    return lax.ppermute(value, axis, [(i, i ^ mask) for i in range(count)])


def piece(value, index, count):
    rows = value.shape[-2] // count
    return lax.dynamic_slice_in_dim(value, index * rows, rows, axis=value.ndim - 2)


def sum_low(*terms):
    total = terms[0].astype(f32)
    for term in terms[1:]:
        total = total + term.astype(f32)
    return total.astype(bf16)


def far_bits():
    bits = [2]
    while bits[-1] * 2 < lax.axis_size("fsdp"):
        bits.append(bits[-1] * 2)
    return bits


def sum_far(value):
    bits = far_bits()
    for bit, twice in zip(bits[0::2], bits[1::2]):
        value = sum_low(value, *[swap(value, "fsdp", m) for m in (bit, twice, bit | twice)])
    if len(bits) % 2:
        value = sum_low(value, swap(value, "fsdp", bits[-1]))
    return value


def scatter_near(value):
    core = lax.axis_index("fsdp") & 1
    return sum_low(piece(value, core, 2), swap(piece(value, 1 - core, 2), "fsdp", 1))


def paired(value, axis, mask, high):
    other = swap(value, axis, mask)
    return jnp.where(
        high, jnp.concatenate([other, value], axis=-2), jnp.concatenate([value, other], axis=-2)
    )


def gather_near(value):
    return paired(value, "fsdp", 1, lax.axis_index("fsdp") % 2 == 1)


def scatter_heads(value):
    part = lax.axis_index("heads")
    terms = [swap(piece(value, part ^ m, PARTS), "heads", m) for m in (1, 2, 3)]
    return sum_low(piece(value, part, PARTS), *terms)


def gather_heads(value):
    part = lax.axis_index("heads")
    near, far, both = [swap(value, "heads", m) for m in (1, 2, 3)]
    odd, high = part % 2 == 1, part >= 2
    low_pair = [jnp.where(odd, near, value), jnp.where(odd, value, near)]
    high_pair = [jnp.where(odd, both, far), jnp.where(odd, far, both)]
    pieces = [jnp.where(high, b, a) for a, b in zip(low_pair, high_pair)]
    pieces += [jnp.where(high, a, b) for a, b in zip(low_pair, high_pair)]
    return jnp.concatenate(pieces, axis=-2)


def body(
    inputs,
    cotangent,
    lengths,
    adapter_ids,
    query_weight,
    key_weight,
    value_weight,
    out_weight,
    up_weight,
    down_weight,
    attn_gain,
    mlp_gain,
    query_scale,
    adapter_in,
    adapter_out,
):
    part = lax.axis_index("heads")
    rows = inputs[0]
    near = swap(rows, "heads", 1)
    far = swap(rows, "heads", 2)
    half = ROWS // 2
    both_low = swap(far[:half], "heads", 1)
    both_high = swap(near[half:], "heads", 2)

    offset = part * ROWS
    ends = PROMPT + jnp.cumsum(lengths[0])
    bounds = ends[:2].astype(jnp.int32)
    ids = adapter_ids[0]
    meta = jnp.concatenate([bounds, ids, part[None].astype(jnp.int32)])
    places = offset + jnp.arange(ROWS, dtype=jnp.int32)
    token = token_adapter(places, meta)
    chosen = (token[:, None] == (jnp.arange(AR, dtype=jnp.int32) // RANK)[None, :]).astype(f32)
    chosen2 = jnp.concatenate([chosen, chosen], axis=1)
    flat_down = jnp.transpose(adapter_in, (0, 2, 1, 3)).reshape(4, D, AR)
    flat_up = adapter_out.reshape(4, AR, D)
    gain_attn = attn_gain.astype(f32)
    gain_mlp = mlp_gain.astype(f32)
    width = LH * HD

    def mine(weight):
        return lax.dynamic_slice_in_dim(weight, part * width, width, axis=1)

    weights_mine = by_head(mine(query_weight), mine(key_weight), mine(value_weight))
    weights_mine = lax.all_gather(weights_mine, "fsdp", axis=0, tiled=True)
    w_out = lax.all_gather(out_weight, "fsdp", axis=0, tiled=True)
    w_up = lax.all_gather(up_weight, "fsdp", axis=0, tiled=True)
    w_down = lax.all_gather(down_weight, "fsdp", axis=0, tiled=True)
    weights_all = lax.all_gather(by_slot(query_weight, key_weight, value_weight, part), "fsdp", axis=0, tiled=True)

    down_pair = jnp.concatenate([flat_down[0], flat_down[1]], axis=1)
    zero = jnp.zeros((AR, D), bf16)
    up_slots = jnp.concatenate([by_slot(flat_up[0], zero, zero, part), by_slot(zero, zero, flat_up[1], part)], axis=0)
    up_mine = jnp.concatenate(
        [by_head(mine(flat_up[0]), zero[:, :width], zero[:, :width]), by_head(zero[:, :width], zero[:, :width], mine(flat_up[1]))], axis=0
    )
    up_heads = jnp.transpose(up_mine.reshape(2 * AR, LH, 3 * HD), (1, 0, 2))
    scale_row = query_scale * HD ** (-0.5)
    scale_mine = jnp.tile(jnp.concatenate([scale_row, jnp.ones((2 * HD,), f32)]), LH)[:, None]

    wt, ut = weights_mine.T, up_mine.T
    per = ROWS // QB
    done = ()
    for source, first in ((rows, part * per), (near, (part ^ 1) * per), (far, (part ^ 2) * per),
                          (both_low, (part ^ 3) * per), (both_high, (part ^ 3) * per + per // 2)):
        done = qkv_project(
            meta, first[None].astype(jnp.int32), source, gain_attn[None, :], wt, down_pair, ut, scale_mine, done
        )
    qkvt, normed_all, inner_all = done
    mixture, logsum = attn_fwd(bounds, qkvt)
    mixed = exchange(mixture).reshape(D, ROWS)

    rows_in = inputs[0].astype(f32)
    scaling_attn = lax.rsqrt(jnp.mean(rows_in * rows_in, axis=-1, keepdims=True) + EPSILON)

    middle = rows_in + tn(mixed, w_out)
    normed_mlp, scaling_mlp = normalize(middle, gain_mlp)
    normed_mlp_low = normed_mlp.astype(bf16)
    inner_up = (nn(normed_mlp_low, flat_down[2]) * chosen).astype(bf16)
    before = nn(normed_mlp_low, w_up) + nn(inner_up, flat_up[2])
    gate = jax.nn.sigmoid(before)
    hidden_low = (before * gate).astype(bf16)
    inner_down = (nn(hidden_low, flat_down[3]) * chosen).astype(bf16)
    outputs = (middle + (nn(hidden_low, w_down) + nn(inner_down, flat_up[3]))).astype(bf16)

    upstream = cotangent[0].astype(f32)
    grad_after = cotangent[0]
    spread_down = (nt(grad_after, flat_up[3]) * chosen).astype(bf16)
    grad_hidden = nt(grad_after, w_down) + nt(spread_down, flat_down[3])
    grad_before = (grad_hidden * gate * (1.0 + before * (1.0 - gate))).astype(bf16)
    spread_up = (nt(grad_before, flat_up[2]) * chosen).astype(bf16)
    grad_normed_mlp = nt(grad_before, w_up) + nt(spread_up, flat_down[2])
    grad_middle = upstream + normalize_back(middle, scaling_mlp, gain_mlp, grad_normed_mlp)
    grad_branch = grad_middle.astype(bf16)
    grad_mixed = nt(w_out, grad_branch).astype(bf16).reshape(PARTS, LH, HD, ROWS)
    grad_first_head = exchange(grad_mixed[:, 0])
    grad_rest = exchange(grad_mixed[:, 1:].reshape(PARTS, (LH - 1) * HD, ROWS))

    terms = [tn(spread_up, normed_mlp_low), tn(spread_down, hidden_low), tn(inner_up, grad_before), tn(inner_down, grad_after)]
    mlp_total = jnp.concatenate(terms).astype(bf16)
    bits = far_bits()

    def add_far(value, chosen_bits):
        for bit in chosen_bits:
            value = sum_low(value, swap(value, "fsdp", bit))
        return value

    stages = [
        lambda v: scatter_heads(scatter_near(v)),
        lambda v: add_far(v, bits[:1]),
        lambda v: add_far(v, bits[1:]),
        lambda v: paired(v, "heads", 1, part % 2 == 1),
    ]

    grads, arrived = [], []
    for h in range(LH):
        if h >= 2:
            meta, _ = lax.optimization_barrier((meta, arrived[h - 2]))
        if h >= 1:
            mlp_total = stages[h - 1](mlp_total)
            meta, _ = lax.optimization_barrier((meta, mlp_total))
        source, slot = (grad_first_head, 0) if h == 0 else (grad_rest, h - 1)
        grad = attn_bwd(meta, scale_row[:, None], qkvt, source, slot, mixture, logsum, h)
        grads += grad
        arrived.append([grad[0]] + [swap(grad[m], "heads", m) for m in (1, 2, 3)])
    mlp_total = stages[3](mlp_total)
    meta, _ = lax.optimization_barrier((meta, (mlp_total, arrived[2])))

    first_attn, second_attn = adapter_grads(meta, grads, normed_all, inner_all, up_heads)
    tiles = D // 128
    first_half = scatter_heads(scatter_near(first_attn.astype(bf16)))
    second_half = scatter_near(second_attn.astype(bf16).reshape(tiles, -1, 128))
    total = sum_far(jnp.concatenate([first_half, second_half]))
    total = gather_near(gather_heads(total))
    mlp_total = gather_near(paired(mlp_total, "heads", 2, part >= 2))
    first_total = total[:tiles]
    second_total = total[tiles:].reshape(tiles, 2, PARTS, -1, 128)
    second_total = jnp.transpose(second_total, (2, 0, 1, 3, 4))

    slot = PARTS * 3 * HD
    grad_normed, spread = 0.0, 0.0
    for h in range(LH):
        cut = slice(h * slot, (h + 1) * slot)
        both = jnp.concatenate(arrived[h])
        grad_normed = grad_normed + lax.dot_general(
            both, weights_all[:, cut], (((0,), (1,)), ((), ())), preferred_element_type=f32
        )
        spread = spread + lax.dot_general(
            both, up_slots[:, cut], (((0,), (1,)), ((), ())), preferred_element_type=f32
        )
    grad_normed = grad_normed + nt((spread * chosen2).astype(bf16), down_pair)
    grad_inputs = grad_middle + normalize_back(rows_in, scaling_attn, gain_attn, grad_normed)

    first_pair = jnp.transpose(first_total.reshape(tiles, 2, ADAPTERS, RANK, 128), (1, 2, 0, 4, 3))
    first_rest = jnp.transpose(mlp_total[: 2 * AR].reshape(2, ADAPTERS, RANK, D), (0, 1, 3, 2))
    grad_first = jnp.concatenate([first_pair.reshape(2, ADAPTERS, D, RANK), first_rest]).astype(f32)
    second_pair = jnp.transpose(second_total.reshape(PARTS, LH, 2, HD, AR), (2, 4, 0, 1, 3)).reshape(2 * AR, D)
    grad_second = jnp.concatenate([second_pair, mlp_total[2 * AR :]]).astype(f32).reshape(4, ADAPTERS, RANK, D)
    return (outputs[None], grad_inputs[None], grad_first, grad_second)


def solution(mesh):
    placed = (
        P("fsdp", "heads", None),
        P("fsdp", "heads", None),
        P("fsdp", None),
        P("fsdp", None),
        P("fsdp", None),
        P("fsdp", None),
        P("fsdp", None),
        P("fsdp", None),
        P("fsdp", None),
        P("fsdp", None),
        P(),
        P(),
        P(),
        P(),
        P(),
    )
    return jax.shard_map(
        body,
        mesh=mesh,
        in_specs=placed,
        out_specs=(P("fsdp", "heads", None), P("fsdp", "heads", None), P(), P()),
        check_vma=False,
    )
```

```python
import jax
import jax.numpy as jnp
from jax import lax
from jax.experimental import pallas as pl
from jax.experimental.pallas import tpu as pltpu
from jax.sharding import PartitionSpec as P

D = 1280
HEADS = 16
HD = 80
RANK = 16
ADAPTERS = 8
AR = ADAPTERS * RANK
TOK = 3072
PROMPT = 1536
ROWS = 768
QB = 256
PARTS = TOK // ROWS
LH = HEADS // PARTS
HALF = ROWS // 2
PH = LH // 2
PW = PH * HD
WIDTH = LH * HD
EPSILON = 1e-06
B = 256
f32, bf16 = jnp.float32, jnp.bfloat16


def nt(a, b):
    return lax.dot_general(a, b, (((1,), (1,)), ((), ())), preferred_element_type=f32)


def tn(a, b):
    return lax.dot_general(a, b, (((0,), (0,)), ((), ())), preferred_element_type=f32)


def nn(a, b):
    return lax.dot_general(a, b, (((1,), (0,)), ((), ())), preferred_element_type=f32)

def start_row(qpos, b1, b2):
    return jnp.where(qpos < PROMPT, 0, jnp.where(qpos < b1, PROMPT, jnp.where(qpos < b2, b1, b2)))

def first_block(i, b1, b2):
    q0 = i * B
    return jnp.where(q0 < b1, PROMPT, jnp.where(q0 < b2, b1, b2)) // B


def token_adapter(pos, meta):
    return jnp.where(
        pos < PROMPT, meta[2], jnp.where(pos < meta[0], meta[3], jnp.where(pos < meta[1], meta[4], meta[5]))
    )


def qkv_kernel(meta, first, low_ref, high_ref, gain_ref, wt_ref, down_ref, up_ref, scale_ref, *refs):
    out_ref, normed_ref, inner_ref, rows = refs[-4:]
    step = pl.program_id(0)

    @pl.when(step == 0)
    def _():
        rows[0:HALF, :] = low_ref[...]
        rows[HALF:ROWS, :] = high_ref[...]

    x = rows[pl.ds(pl.multiple_of(step * QB, QB), QB), :].astype(f32)
    q = lax.rsqrt(jnp.mean(x * x, axis=1, keepdims=True) + EPSILON)
    normed = (x * q * gain_ref[...]).astype(bf16)
    normed_ref[...] = normed
    pos = (first[0] + step) * QB + lax.broadcasted_iota(jnp.int32, (QB, 1), 0)
    lane = lax.broadcasted_iota(jnp.int32, (QB, 2 * AR), 1)
    chosen = (lane % AR) // RANK == token_adapter(pos, meta)
    inner = jnp.where(chosen, nn(normed, down_ref[...]), 0.0).astype(bf16)
    inner_ref[...] = inner
    out = nt(wt_ref[...], normed) + nt(up_ref[...], inner)
    out_ref[...] = (out * scale_ref[...]).astype(bf16)


def qkv_project(meta, chunk, low, high, gain, wt, down, up, scale, done):
    whole = lambda shape: pl.BlockSpec(shape, lambda i, *_: (0, 0))
    second = 1 if high is None else 0
    first = (chunk * (ROWS // QB))[None].astype(jnp.int32)
    return pl.pallas_call(
        qkv_kernel,
        out_shape=(
            jax.ShapeDtypeStruct((3 * WIDTH, TOK), bf16),
            jax.ShapeDtypeStruct((TOK, D), bf16),
            jax.ShapeDtypeStruct((TOK, 2 * AR), bf16),
        ),
        grid_spec=pltpu.PrefetchScalarGridSpec(
            num_scalar_prefetch=2,
            grid=(ROWS // QB,),
            in_specs=[
                whole((HALF, D)),
                pl.BlockSpec((HALF, D), lambda i, *_: (second, 0)),
                whole((1, D)),
                whole((3 * WIDTH, D)),
                whole((D, 2 * AR)),
                whole((3 * WIDTH, 2 * AR)),
                whole((3 * WIDTH, 1)),
            ]
            + [pl.BlockSpec(memory_space=pl.ANY)] * len(done),
            out_specs=[
                pl.BlockSpec((3 * WIDTH, QB), lambda i, m, first: (0, first[0] + i)),
                pl.BlockSpec((QB, D), lambda i, m, first: (first[0] + i, 0)),
                pl.BlockSpec((QB, 2 * AR), lambda i, m, first: (first[0] + i, 0)),
            ],
            scratch_shapes=[pltpu.VMEM((ROWS, D), bf16)],
        ),
        input_output_aliases={9 + i: i for i in range(len(done))},
        compiler_params=pltpu.CompilerParams(dimension_semantics=("arbitrary",), vmem_limit_bytes=60 << 20),
        cost_estimate=pl.CostEstimate(flops=2 * ROWS * D * (3 * WIDTH + 2 * AR), bytes_accessed=8 << 20, transcendentals=0),
        name="qkv_project",
    )(meta, first, low, low if high is None else high, gain, wt, down, up, scale, *done)


def adapter_kernel(meta, g0_ref, g1_ref, normed_ref, inner_ref, up_ref, first_ref, second_ref, facc, sacc):
    step = pl.program_id(0)

    @pl.when(step == 0)
    def _():
        facc[...] = jnp.zeros_like(facc)
        sacc[...] = jnp.zeros_like(sacc)

    grads = [g0_ref[0], g1_ref[0]]
    spread = nn(up_ref[0], grads[0]) + nn(up_ref[1], grads[1])
    pos = step * ROWS + lax.broadcasted_iota(jnp.int32, (1, ROWS), 1)
    rank = lax.broadcasted_iota(jnp.int32, (2 * AR, ROWS), 0)
    chosen = (rank % AR) // RANK == token_adapter(pos, meta)
    spread = jnp.where(chosen, spread, 0.0).astype(bf16)
    facc[...] += nn(spread, normed_ref[...])
    for p in range(2):
        sacc[p, 0] += nn(grads[p][0:PW], inner_ref[:, :AR])
        sacc[p, 1] += nn(grads[p][2 * PW :], inner_ref[:, AR:])

    @pl.when(step == PARTS - 1)
    def _():
        for c in range(D // 128):
            first_ref[c] = facc[:, c * 128 : (c + 1) * 128].astype(bf16)
        second_ref[...] = sacc[...].astype(bf16)


def adapter_grads(meta, grads, normed, inner, up):
    return pl.pallas_call(
        adapter_kernel,
        out_shape=(jax.ShapeDtypeStruct((D // 128, 2 * AR, 128), bf16), jax.ShapeDtypeStruct((2, 2, PW, AR), bf16)),
        grid_spec=pltpu.PrefetchScalarGridSpec(
            num_scalar_prefetch=1,
            grid=(PARTS,),
            in_specs=[pl.BlockSpec((1, 3 * PW, ROWS), lambda i, m: (i, 0, 0))] * 2
            + [
                pl.BlockSpec((ROWS, D), lambda i, m: (i, 0)),
                pl.BlockSpec((ROWS, 2 * AR), lambda i, m: (i, 0)),
                pl.BlockSpec((2, 2 * AR, 3 * PW), lambda i, m: (0, 0, 0)),
            ],
            out_specs=[
                pl.BlockSpec((D // 128, 2 * AR, 128), lambda i, m: (0, 0, 0)),
                pl.BlockSpec((2, 2, PW, AR), lambda i, m: (0, 0, 0, 0)),
            ],
            scratch_shapes=[pltpu.VMEM((2 * AR, D), f32), pltpu.VMEM((2, 2, PW, AR), f32)],
        ),
        compiler_params=pltpu.CompilerParams(dimension_semantics=("arbitrary",), vmem_limit_bytes=60 << 20),
        cost_estimate=pl.CostEstimate(flops=4 * TOK * D * 2 * AR, bytes_accessed=20 << 20, transcendentals=0),
        name="adapter_grads",
    )(meta, *grads, normed, inner, up)


HPB = PH
NEG = -1e30
FW = 512


def fwd_kernel(bounds, q_ref, k_ref, v_ref, o_ref, lse_ref, kp, qt, vt):
    b1, b2 = bounds[0], bounds[1]
    zpad = jnp.zeros((128 - HD, 128), bf16)
    for h in range(HPB):
        own = slice(h * HD, (h + 1) * HD)
        qt[h, 0:HD, :] = q_ref[own, :]
        qt[h, HD:128, :] = jnp.zeros((128 - HD, TOK), bf16)
        vt[h, 0:HD, :] = v_ref[own, :]
        vt[h, HD:96, :] = (lax.broadcasted_iota(jnp.int32, (16, TOK), 0) == 0).astype(bf16)
        for t in range(TOK // 128):
            kt = k_ref[own, t * 128:(t + 1) * 128]
            kp[h, t * 128:(t + 1) * 128, :] = jnp.concatenate([kt, zpad], axis=0).T

    def qblock(i, _):
        q0 = pl.multiple_of(i * B, B)
        qpos = q0 + lax.broadcasted_iota(jnp.int32, (1, B), 1)
        srow = start_row(qpos, b1, b2)

        def step(k0, width, masked, carry):
            ks = pl.ds(k0, width)
            ss = [nn(kp[h, ks, :], qt[h, :, pl.ds(q0, B)]) for h in range(HPB)]
            if masked:
                kpos = k0 + lax.broadcasted_iota(jnp.int32, (width, B), 0)
                ok = (kpos >= srow) & (kpos <= qpos)
                ss = [jnp.where(ok, s, NEG) for s in ss]
            out = []
            for h in range(HPB):
                m, acc = carry[h]
                m_new = jnp.maximum(m, jnp.max(ss[h], axis=0, keepdims=True))
                p = jnp.exp(ss[h] - m_new).astype(bf16)
                a = jnp.exp(m - m_new)
                out.append((m_new, acc * a + nn(vt[h, :, ks], p)))
            return tuple(out)

        full = jnp.minimum(i * B // FW, PROMPT // FW)
        lo = jnp.where(i < PROMPT // B, (FW // B) * (i * B // FW), first_block(i, b1, b2))
        carry = tuple((jnp.full((1, B), NEG, f32), jnp.zeros((96, B), f32)) for _ in range(HPB))
        carry = lax.fori_loop(0, full, lambda j, c: step(pl.multiple_of(j * FW, FW), FW, False, c), carry)
        carry = lax.fori_loop(lo, i + 1, lambda j, c: step(pl.multiple_of(j * B, B), B, True, c), carry)
        for h in range(HPB):
            m, acc = carry[h]
            l = acc[HD:HD + 1, :]
            o_ref[i // 3, h * HD:(h + 1) * HD, pl.ds(pl.multiple_of((i % 3) * B, B), B)] = (acc[0:HD, :] / l).astype(bf16)
            lse_ref[h, :, pl.ds(q0, B)] = m + jnp.log(l)
        return 0
    lax.fori_loop(0, TOK // B, qblock, 0)

def attn_fwd(bounds, qkvt, pair):
    rows = lambda a: pl.BlockSpec((PW, TOK), lambda i, b: (2 * a + pair, 0))
    return pl.pallas_call(
        fwd_kernel,
        out_shape=(jax.ShapeDtypeStruct((PARTS, PW, ROWS), bf16), jax.ShapeDtypeStruct((PH, 1, TOK), f32)),
        grid_spec=pltpu.PrefetchScalarGridSpec(
            num_scalar_prefetch=1,
            grid=(1,),
            in_specs=[rows(0), rows(1), rows(2)],
            out_specs=[pl.BlockSpec((PARTS, PW, ROWS), lambda i, b: (0, 0, 0)), pl.BlockSpec((PH, 1, TOK), lambda i, b: (0, 0, 0))],
            scratch_shapes=[pltpu.VMEM((HPB, TOK, 128), bf16), pltpu.VMEM((HPB, 128, TOK), bf16), pltpu.VMEM((HPB, 96, TOK), bf16)],
        ),
        compiler_params=pltpu.CompilerParams(dimension_semantics=("arbitrary",), vmem_limit_bytes=60 << 20),
        cost_estimate=pl.CostEstimate(flops=20 * 10**9, bytes_accessed=5 << 20, transcendentals=0),
        name="attn_fwd",
    )(bounds, qkvt, qkvt, qkvt)


def parts3(x):
    hi = x.astype(bf16)
    r = x - hi.astype(f32)
    mid = r.astype(bf16)
    lo = (r - mid.astype(f32)).astype(bf16)
    return hi, mid, lo

def bwd_kernel(meta, scale_ref, q_ref, k_ref, v_ref, do_ref, o_ref, lse_ref, out_ref, kp, vp, qt, dot, qr, dor, dk, dv, dqt):
    b1, b2 = meta[0], meta[1]
    row16 = lax.broadcasted_iota(jnp.int32, (16, 128), 0)
    ones3 = (row16 < 3).astype(bf16)
    pad = jnp.zeros((32, 128), bf16)
    scale = scale_ref[...]

    def tail(x):
        hi, mid, lo = parts3(-x)
        rest = jnp.where(row16 == 1, mid.astype(f32), jnp.where(row16 == 2, lo.astype(f32), 0.0))
        return jnp.where(row16 == 0, hi.astype(f32), rest).astype(bf16)

    @pl.loop(0, 2 * PARTS)
    def _(step):
        chunk = step // 2
        for t in range(3):
            off = pl.multiple_of((step % 2) * HALF + t * 128, 128)
            sl, here = pl.ds(pl.multiple_of(chunk * ROWS + off, 128), 128), pl.ds(off, 128)
            q, k, v = q_ref[:, sl], k_ref[:, sl], v_ref[:, sl]
            do, o = do_ref[chunk, :, here], o_ref[chunk, :, here]
            delta = jnp.sum(do.astype(f32) * o.astype(f32), axis=0, keepdims=True)
            qa = jnp.concatenate([q, tail(lse_ref[0, :, sl]), pad], axis=0)
            da = jnp.concatenate([do, tail(delta), pad], axis=0)
            qt[:, sl] = qa
            dot[:, sl] = da
            qr[sl, :] = qa.T
            dor[sl, :] = da.T
            kp[sl, :] = jnp.concatenate([k, ones3, pad], axis=0).T
            vp[sl, :] = jnp.concatenate([v, ones3, pad], axis=0).T

    dk[...] = jnp.zeros_like(dk)
    dv[...] = jnp.zeros_like(dv)
    dqt[...] = jnp.zeros_like(dqt)

    def block(k0, q0, width, masked):
        k0, q0 = pl.multiple_of(k0, width), pl.multiple_of(q0, width)
        ks, qs = pl.ds(k0, width), pl.ds(q0, width)
        p = jnp.exp(nn(kp[ks, :], qt[:, qs]))
        if masked:
            qpos = q0 + lax.broadcasted_iota(jnp.int32, (1, width), 1)
            kpos = k0 + lax.broadcasted_iota(jnp.int32, (width, width), 0)
            p = jnp.where((kpos >= start_row(qpos, b1, b2)) & (kpos <= qpos), p, 0.0)
        ds = (p * nn(vp[ks, :], dot[:, qs])).astype(bf16)
        dv[ks, :] += nn(p.astype(bf16), dor[qs, :])
        dk[ks, :] += nn(ds, qr[qs, :])
        dqt[:, qs] += nn(k_ref[:, ks], ds)

    @pl.loop(0, 12)
    def _(n):
        qb = jnp.where(n < 9, 3 + n // 3, jnp.where(n == 9, 1, 2))
        kb = jnp.where(n < 9, n % 3, jnp.where(n == 11, 1, 0))
        block(kb * FW, qb * FW, FW, False)

    @pl.loop(0, TOK // B)
    def _(i):
        lo = jnp.where(i < PROMPT // B, 2 * (i // 2), first_block(i, b1, b2))

        @pl.loop(lo, i + 1)
        def _(j):
            block(j * B, i * B, B, True)

    @pl.loop(0, 2 * PARTS)
    def _(step):
        chunk = step // 2
        for t in range(3):
            off = pl.multiple_of((step % 2) * HALF + t * 128, 128)
            sl, here = pl.ds(pl.multiple_of(chunk * ROWS + off, 128), 128), pl.ds(off, 128)
            dq = dqt[:, sl].astype(bf16).astype(f32) * scale
            out_ref[chunk, 0, :, here] = dq.astype(bf16)
            out_ref[chunk, 1, :, here] = dk[sl, :].T[0:HD, :].astype(bf16)
            out_ref[chunk, 2, :, here] = dv[sl, :].T[0:HD, :].astype(bf16)


def attn_bwd(meta, scale, qkvt, grad, mixture, logsum, pair):
    rows = lambda a: pl.BlockSpec((HD, TOK), lambda i, b: (LH * a + PH * pair + i, 0))
    chunks = pl.BlockSpec((PARTS, HD, ROWS), lambda i, b: (0, i, 0))
    return pl.pallas_call(
        bwd_kernel,
        out_shape=jax.ShapeDtypeStruct((PARTS, 3, PW, ROWS), bf16),
        grid_spec=pltpu.PrefetchScalarGridSpec(
            num_scalar_prefetch=1,
            grid=(PH,),
            in_specs=[
                pl.BlockSpec((HD, 1), lambda i, b: (0, 0)),
                rows(0),
                rows(1),
                rows(2),
                chunks,
                chunks,
                pl.BlockSpec((1, 1, TOK), lambda i, b: (i, 0, 0)),
            ],
            out_specs=pl.BlockSpec((PARTS, 3, HD, ROWS), lambda i, b: (0, 0, i, 0)),
            scratch_shapes=[pltpu.VMEM((TOK, 128), bf16)] * 2
            + [pltpu.VMEM((128, TOK), bf16)] * 2
            + [pltpu.VMEM((TOK, 128), bf16)] * 2
            + [pltpu.VMEM((TOK, 128), f32)] * 2
            + [pltpu.VMEM((HD, TOK), f32)],
        ),
        compiler_params=pltpu.CompilerParams(dimension_semantics=("arbitrary",), vmem_limit_bytes=60 << 20),
        cost_estimate=pl.CostEstimate(flops=36 * 10**9, bytes_accessed=16 << 20, transcendentals=0),
        name="attn_bwd",
    )(meta, scale, qkvt, qkvt, qkvt, grad, mixture, logsum)


def normalize(values, gain_vec):
    scaling = lax.rsqrt(jnp.mean(values * values, axis=-1, keepdims=True) + EPSILON)
    return (values * scaling * gain_vec, scaling)


def normalize_back(values, scaling, gain_vec, upstream):
    weighted = gain_vec * upstream
    return scaling * weighted - values * scaling**3 * jnp.mean(values * weighted, axis=-1, keepdims=True)


def by_pair(query, key, value):
    rows = query.shape[0]
    split = jnp.stack([query, key, value], axis=1).reshape(rows, 3, PARTS, 2, PW)
    return jnp.transpose(split, (0, 3, 2, 1, 4)).reshape(rows, 3 * D)


def exchange(value):
    return lax.all_to_all(value, "heads", split_axis=0, concat_axis=0, tiled=True)


def swap(value, axis, mask):
    count = lax.axis_size(axis)
    return lax.ppermute(value, axis, [(i, i ^ mask) for i in range(count)])


def piece(value, index, count):
    rows = value.shape[-2] // count
    return lax.dynamic_slice_in_dim(value, index * rows, rows, axis=value.ndim - 2)


def sum_low(*terms):
    total = terms[0].astype(f32)
    for term in terms[1:]:
        total = total + term.astype(f32)
    return total.astype(bf16)


def far_bits():
    bits = [2]
    while bits[-1] * 2 < lax.axis_size("fsdp"):
        bits.append(bits[-1] * 2)
    return bits


def sum_far(value):
    bits = far_bits()
    for bit, twice in zip(bits[0::2], bits[1::2]):
        value = sum_low(value, *[swap(value, "fsdp", m) for m in (bit, twice, bit | twice)])
    if len(bits) % 2:
        value = sum_low(value, swap(value, "fsdp", bits[-1]))
    return value


def scatter_near(value):
    core = lax.axis_index("fsdp") & 1
    return sum_low(piece(value, core, 2), swap(piece(value, 1 - core, 2), "fsdp", 1))


def paired(value, axis, mask, high):
    other = swap(value, axis, mask)
    return jnp.where(
        high, jnp.concatenate([other, value], axis=-2), jnp.concatenate([value, other], axis=-2)
    )


def gather_near(value):
    return paired(value, "fsdp", 1, lax.axis_index("fsdp") % 2 == 1)


def scatter_heads(value):
    part = lax.axis_index("heads")
    terms = [swap(piece(value, part ^ m, PARTS), "heads", m) for m in (1, 2, 3)]
    return sum_low(piece(value, part, PARTS), *terms)


def gather_heads(value):
    part = lax.axis_index("heads")
    near, far, both = [swap(value, "heads", m) for m in (1, 2, 3)]
    odd, high = part % 2 == 1, part >= 2
    low_pair = [jnp.where(odd, near, value), jnp.where(odd, value, near)]
    high_pair = [jnp.where(odd, both, far), jnp.where(odd, far, both)]
    pieces = [jnp.where(high, b, a) for a, b in zip(low_pair, high_pair)]
    pieces += [jnp.where(high, a, b) for a, b in zip(low_pair, high_pair)]
    return jnp.concatenate(pieces, axis=-2)


def body(
    inputs,
    cotangent,
    lengths,
    adapter_ids,
    query_weight,
    key_weight,
    value_weight,
    out_weight,
    up_weight,
    down_weight,
    attn_gain,
    mlp_gain,
    query_scale,
    adapter_in,
    adapter_out,
):
    part = lax.axis_index("heads")
    rows = inputs[0]
    near_high = swap(rows[HALF:], "heads", 1)
    far_low = swap(rows[:HALF], "heads", 2)
    near_low = swap(rows[:HALF], "heads", 1)
    far_high = swap(rows[HALF:], "heads", 2)
    both_low = swap(far_low, "heads", 1)
    both_high = swap(near_high, "heads", 2)

    offset = part * ROWS
    ends = PROMPT + jnp.cumsum(lengths[0])
    bounds = ends[:2].astype(jnp.int32)
    ids = adapter_ids[0]
    meta = jnp.concatenate([bounds, ids, part[None].astype(jnp.int32)])
    places = offset + jnp.arange(ROWS, dtype=jnp.int32)
    token = token_adapter(places, meta)
    chosen = (token[:, None] == (jnp.arange(AR, dtype=jnp.int32) // RANK)[None, :]).astype(f32)
    chosen2 = jnp.concatenate([chosen, chosen], axis=1)
    flat_down = jnp.transpose(adapter_in, (0, 2, 1, 3)).reshape(4, D, AR)
    flat_up = adapter_out.reshape(4, AR, D)
    gain_attn = attn_gain.astype(f32)
    gain_mlp = mlp_gain.astype(f32)

    def mine(weight):
        return lax.dynamic_slice_in_dim(weight, part * WIDTH, WIDTH, axis=1)

    weights_mine = jnp.concatenate([mine(query_weight), mine(key_weight), mine(value_weight)], axis=1)
    weights_mine = lax.all_gather(weights_mine, "fsdp", axis=0, tiled=True)
    w_out = lax.all_gather(out_weight, "fsdp", axis=0, tiled=True)
    w_up = lax.all_gather(up_weight, "fsdp", axis=0, tiled=True)
    w_down = lax.all_gather(down_weight, "fsdp", axis=0, tiled=True)
    weights_all = lax.all_gather(by_pair(query_weight, key_weight, value_weight), "fsdp", axis=0, tiled=True)

    down_pair = jnp.concatenate([flat_down[0], flat_down[1]], axis=1)
    zero = jnp.zeros((AR, D), bf16)
    up_query = jnp.concatenate([flat_up[0], zero])
    up_value = jnp.concatenate([zero, flat_up[1]])
    up_pairs = by_pair(up_query, jnp.zeros_like(up_query), up_value)
    up_mine = jnp.concatenate([mine(up_query), jnp.zeros((2 * AR, WIDTH), bf16), mine(up_value)], axis=1)
    up_heads = jnp.transpose(up_mine.reshape(2 * AR, 3, 2, PW), (2, 0, 1, 3)).reshape(2, 2 * AR, 3 * PW)
    scale_row = query_scale * HD ** (-0.5)
    scale_mine = jnp.concatenate([jnp.tile(scale_row, LH), jnp.ones((2 * WIDTH,), f32)])[:, None]

    wt, ut = weights_mine.T, up_mine.T
    done = ()
    for m, low, high in ((0, rows, None), (1, near_low, near_high), (2, far_low, far_high), (3, both_low, both_high)):
        done = qkv_project(meta, part ^ m, low, high, gain_attn[None, :], wt, down_pair, ut, scale_mine, done)
    qkvt, normed_all, inner_all = done
    out_pairs = w_out.reshape(PARTS, 2, PW, D)
    pair_weight = [out_pairs[:, p].reshape(PARTS * PW, D) for p in range(2)]
    forward = [attn_fwd(bounds, qkvt, 0)]
    mixed_first = exchange(forward[0][0])
    forward.append(attn_fwd(bounds, qkvt, 1))
    mixed_second = exchange(forward[1][0])

    rows_in = inputs[0].astype(f32)
    scaling_attn = lax.rsqrt(jnp.mean(rows_in * rows_in, axis=-1, keepdims=True) + EPSILON)

    middle = rows_in + tn(mixed_first.reshape(PARTS * PW, ROWS), pair_weight[0])
    middle = middle + tn(mixed_second.reshape(PARTS * PW, ROWS), pair_weight[1])
    normed_mlp, scaling_mlp = normalize(middle, gain_mlp)
    normed_mlp_low = normed_mlp.astype(bf16)
    inner_up = (nn(normed_mlp_low, flat_down[2]) * chosen).astype(bf16)
    before = nn(normed_mlp_low, w_up) + nn(inner_up, flat_up[2])
    gate = jax.nn.sigmoid(before)
    hidden_low = (before * gate).astype(bf16)
    inner_down = (nn(hidden_low, flat_down[3]) * chosen).astype(bf16)
    outputs = (middle + (nn(hidden_low, w_down) + nn(inner_down, flat_up[3]))).astype(bf16)

    upstream = cotangent[0].astype(f32)
    grad_after = cotangent[0]
    spread_down = (nt(grad_after, flat_up[3]) * chosen).astype(bf16)
    grad_hidden = nt(grad_after, w_down) + nt(spread_down, flat_down[3])
    grad_before = (grad_hidden * gate * (1.0 + before * (1.0 - gate))).astype(bf16)
    spread_up = (nt(grad_before, flat_up[2]) * chosen).astype(bf16)
    grad_normed_mlp = nt(grad_before, w_up) + nt(spread_up, flat_down[2])
    grad_middle = upstream + normalize_back(middle, scaling_mlp, gain_mlp, grad_normed_mlp)
    grad_branch = grad_middle.astype(bf16)
    grad_heads = [exchange(nt(w, grad_branch).astype(bf16).reshape(PARTS, PW, ROWS)) for w in pair_weight]

    terms = [tn(spread_up, normed_mlp_low), tn(spread_down, hidden_low), tn(inner_up, grad_before), tn(inner_down, grad_after)]
    mlp_total = scatter_near(jnp.concatenate(terms).astype(bf16))
    mlp_total, grad_heads[0] = lax.optimization_barrier((mlp_total, grad_heads[0]))
    mlp_total = scatter_heads(mlp_total)
    grad_first_pair = attn_bwd(meta, scale_row[:, None], qkvt, grad_heads[0], forward[0][0], forward[0][1], 0)
    arrived = [exchange(grad_first_pair.reshape(PARTS, 3 * PW, ROWS))]
    mlp_total, grad_heads[1] = lax.optimization_barrier((mlp_total, grad_heads[1]))
    mlp_total = sum_far(mlp_total)
    grad_second_pair = attn_bwd(meta, scale_row[:, None], qkvt, grad_heads[1], forward[1][0], forward[1][1], 1)
    arrived.append(exchange(grad_second_pair.reshape(PARTS, 3 * PW, ROWS)))

    grads = [g.reshape(PARTS, 3 * PW, ROWS) for g in (grad_first_pair, grad_second_pair)]
    meta, arrived[0] = lax.optimization_barrier((meta, arrived[0]))
    first_attn, second_attn = adapter_grads(meta, grads, normed_all, inner_all, up_heads)

    slot = PARTS * 3 * PW

    def back(p):
        both, cut = arrived[p].reshape(slot, ROWS), slice(p * slot, (p + 1) * slot)
        contract = (((0,), (1,)), ((), ()))
        return (
            lax.dot_general(both, weights_all[:, cut], contract, preferred_element_type=f32),
            lax.dot_general(both, up_pairs[:, cut], contract, preferred_element_type=f32),
        )

    tiles = D // 128
    mlp_total = gather_heads(mlp_total)
    near_first = scatter_near(first_attn)
    near_second = scatter_near(second_attn.reshape(tiles, -1, 128))
    grad_normed, spread = back(0)
    near_first, grad_normed = lax.optimization_barrier((near_first, grad_normed))
    total = sum_far(jnp.concatenate([scatter_heads(near_first), near_second]))
    grad_second_part, spread_second = back(1)
    total, grad_second_part = lax.optimization_barrier((total, grad_second_part))
    total = gather_near(gather_heads(total))
    mlp_total = gather_near(mlp_total)
    grad_normed, spread = grad_normed + grad_second_part, spread + spread_second
    first_total = total[:tiles]
    second_total = total[tiles:].reshape(tiles, 2, PARTS, -1, 128)
    second_total = jnp.transpose(second_total, (2, 0, 1, 3, 4))
    grad_normed = grad_normed + nt((spread * chosen2).astype(bf16), down_pair)
    grad_inputs = grad_middle + normalize_back(rows_in, scaling_attn, gain_attn, grad_normed)

    first_pair = jnp.transpose(first_total.reshape(tiles, 2, ADAPTERS, RANK, 128), (1, 2, 0, 4, 3))
    first_rest = jnp.transpose(mlp_total[: 2 * AR].reshape(2, ADAPTERS, RANK, D), (0, 1, 3, 2))
    grad_first = jnp.concatenate([first_pair.reshape(2, ADAPTERS, D, RANK), first_rest]).astype(f32)
    second_pair = jnp.transpose(second_total.reshape(PARTS, 2, 2, PW, AR), (2, 4, 0, 1, 3)).reshape(2 * AR, D)
    grad_second = jnp.concatenate([second_pair, mlp_total[2 * AR :]]).astype(f32).reshape(4, ADAPTERS, RANK, D)
    return (outputs[None], grad_inputs[None], grad_first, grad_second)


def solution(mesh):
    placed = (
        P("fsdp", "heads", None),
        P("fsdp", "heads", None),
        P("fsdp", None),
        P("fsdp", None),
        P("fsdp", None),
        P("fsdp", None),
        P("fsdp", None),
        P("fsdp", None),
        P("fsdp", None),
        P("fsdp", None),
        P(),
        P(),
        P(),
        P(),
        P(),
    )
    return jax.shard_map(
        body,
        mesh=mesh,
        in_specs=placed,
        out_specs=(P("fsdp", "heads", None), P("fsdp", "heads", None), P(), P()),
        check_vma=False,
    )
```

```python
import jax
import jax.numpy as jnp
from jax import lax
from jax.experimental import pallas as pl
from jax.experimental.pallas import tpu as pltpu
from jax.sharding import PartitionSpec as P

D = 1280
HEADS = 16
HD = 80
RANK = 16
ADAPTERS = 8
AR = ADAPTERS * RANK
TOK = 3072
PROMPT = 1536
ROWS = 768
QB = 256
PARTS = TOK // ROWS
LH = HEADS // PARTS
HALF = ROWS // 2
PH = LH // 2
PW = PH * HD
WIDTH = LH * HD
EPSILON = 1e-06
B = 256
f32, bf16 = jnp.float32, jnp.bfloat16


def nt(a, b):
    return lax.dot_general(a, b, (((1,), (1,)), ((), ())), preferred_element_type=f32)


def tn(a, b):
    return lax.dot_general(a, b, (((0,), (0,)), ((), ())), preferred_element_type=f32)


def nn(a, b):
    return lax.dot_general(a, b, (((1,), (0,)), ((), ())), preferred_element_type=f32)

def start_row(qpos, b1, b2):
    return jnp.where(qpos < PROMPT, 0, jnp.where(qpos < b1, PROMPT, jnp.where(qpos < b2, b1, b2)))

def first_block(i, b1, b2):
    q0 = i * B
    return jnp.where(q0 < b1, PROMPT, jnp.where(q0 < b2, b1, b2)) // B


def token_adapter(pos, meta):
    return jnp.where(
        pos < PROMPT, meta[2], jnp.where(pos < meta[0], meta[3], jnp.where(pos < meta[1], meta[4], meta[5]))
    )


def qkv_kernel(meta, first, low_ref, high_ref, gain_ref, wt_ref, down_ref, up_ref, scale_ref, *refs):
    out_ref, normed_ref, inner_ref, rows = refs[-4:]
    step = pl.program_id(0)

    @pl.when(step == 0)
    def _():
        rows[0:HALF, :] = low_ref[...]
        rows[HALF:ROWS, :] = high_ref[...]

    x = rows[pl.ds(pl.multiple_of(step * QB, QB), QB), :].astype(f32)
    q = lax.rsqrt(jnp.mean(x * x, axis=1, keepdims=True) + EPSILON)
    normed = (x * q * gain_ref[...]).astype(bf16)
    normed_ref[...] = normed
    pos = (first[0] + step) * QB + lax.broadcasted_iota(jnp.int32, (QB, 1), 0)
    lane = lax.broadcasted_iota(jnp.int32, (QB, 2 * AR), 1)
    chosen = (lane % AR) // RANK == token_adapter(pos, meta)
    inner = jnp.where(chosen, nn(normed, down_ref[...]), 0.0).astype(bf16)
    inner_ref[...] = inner
    out = nt(wt_ref[...], normed) + nt(up_ref[...], inner)
    out_ref[...] = (out * scale_ref[...]).astype(bf16)


def qkv_project(meta, chunk, low, high, gain, wt, down, up, scale, done):
    whole = lambda shape: pl.BlockSpec(shape, lambda i, *_: (0, 0))
    second = 1 if high is None else 0
    first = (chunk * (ROWS // QB))[None].astype(jnp.int32)
    return pl.pallas_call(
        qkv_kernel,
        out_shape=(
            jax.ShapeDtypeStruct((3 * WIDTH, TOK), bf16),
            jax.ShapeDtypeStruct((TOK, D), bf16),
            jax.ShapeDtypeStruct((TOK, 2 * AR), bf16),
        ),
        grid_spec=pltpu.PrefetchScalarGridSpec(
            num_scalar_prefetch=2,
            grid=(ROWS // QB,),
            in_specs=[
                whole((HALF, D)),
                pl.BlockSpec((HALF, D), lambda i, *_: (second, 0)),
                whole((1, D)),
                whole((3 * WIDTH, D)),
                whole((D, 2 * AR)),
                whole((3 * WIDTH, 2 * AR)),
                whole((3 * WIDTH, 1)),
            ]
            + [pl.BlockSpec(memory_space=pl.ANY)] * len(done),
            out_specs=[
                pl.BlockSpec((3 * WIDTH, QB), lambda i, m, first: (0, first[0] + i)),
                pl.BlockSpec((QB, D), lambda i, m, first: (first[0] + i, 0)),
                pl.BlockSpec((QB, 2 * AR), lambda i, m, first: (first[0] + i, 0)),
            ],
            scratch_shapes=[pltpu.VMEM((ROWS, D), bf16)],
        ),
        input_output_aliases={9 + i: i for i in range(len(done))},
        compiler_params=pltpu.CompilerParams(dimension_semantics=("arbitrary",), vmem_limit_bytes=60 << 20),
        cost_estimate=pl.CostEstimate(flops=2 * ROWS * D * (3 * WIDTH + 2 * AR), bytes_accessed=8 << 20, transcendentals=0),
        name="qkv_project",
    )(meta, first, low, low if high is None else high, gain, wt, down, up, scale, *done)


def adapter_kernel(meta, g0_ref, g1_ref, normed_ref, inner_ref, up_ref, first_ref, second_ref, facc, sacc):
    step = pl.program_id(0)

    @pl.when(step == 0)
    def _():
        facc[...] = jnp.zeros_like(facc)
        sacc[...] = jnp.zeros_like(sacc)

    grads = [g0_ref[0], g1_ref[0]]
    spread = nn(up_ref[0], grads[0]) + nn(up_ref[1], grads[1])
    pos = step * ROWS + lax.broadcasted_iota(jnp.int32, (1, ROWS), 1)
    rank = lax.broadcasted_iota(jnp.int32, (2 * AR, ROWS), 0)
    chosen = (rank % AR) // RANK == token_adapter(pos, meta)
    spread = jnp.where(chosen, spread, 0.0).astype(bf16)
    facc[...] += nn(spread, normed_ref[...])
    for p in range(2):
        sacc[p, 0] += nn(grads[p][0:PW], inner_ref[:, :AR])
        sacc[p, 1] += nn(grads[p][2 * PW :], inner_ref[:, AR:])

    @pl.when(step == PARTS - 1)
    def _():
        for c in range(D // 128):
            first_ref[c] = facc[:, c * 128 : (c + 1) * 128].astype(bf16)
        second_ref[...] = sacc[...].astype(bf16)


def adapter_grads(meta, grads, normed, inner, up):
    return pl.pallas_call(
        adapter_kernel,
        out_shape=(jax.ShapeDtypeStruct((D // 128, 2 * AR, 128), bf16), jax.ShapeDtypeStruct((2, 2, PW, AR), bf16)),
        grid_spec=pltpu.PrefetchScalarGridSpec(
            num_scalar_prefetch=1,
            grid=(PARTS,),
            in_specs=[pl.BlockSpec((1, 3 * PW, ROWS), lambda i, m: (i, 0, 0))] * 2
            + [
                pl.BlockSpec((ROWS, D), lambda i, m: (i, 0)),
                pl.BlockSpec((ROWS, 2 * AR), lambda i, m: (i, 0)),
                pl.BlockSpec((2, 2 * AR, 3 * PW), lambda i, m: (0, 0, 0)),
            ],
            out_specs=[
                pl.BlockSpec((D // 128, 2 * AR, 128), lambda i, m: (0, 0, 0)),
                pl.BlockSpec((2, 2, PW, AR), lambda i, m: (0, 0, 0, 0)),
            ],
            scratch_shapes=[pltpu.VMEM((2 * AR, D), f32), pltpu.VMEM((2, 2, PW, AR), f32)],
        ),
        compiler_params=pltpu.CompilerParams(dimension_semantics=("arbitrary",), vmem_limit_bytes=60 << 20),
        cost_estimate=pl.CostEstimate(flops=4 * TOK * D * 2 * AR, bytes_accessed=20 << 20, transcendentals=0),
        name="adapter_grads",
    )(meta, *grads, normed, inner, up)


HPB = LH
BLOCKS = ROWS // B
NEG = -1e30
FW = 512


def fwd_kernel(bounds, q_ref, k_ref, v_ref, o_ref, lse_ref, kp, qt, vt):
    b1, b2 = bounds[0], bounds[1]
    zpad = jnp.zeros((128 - HD, 128), bf16)
    for h in range(HPB):
        own = slice(h * HD, (h + 1) * HD)
        qt[h, 0:HD, :] = q_ref[own, :]
        qt[h, HD:128, :] = jnp.zeros((128 - HD, TOK), bf16)
        vt[h, 0:HD, :] = v_ref[own, :]
        vt[h, HD:96, :] = (lax.broadcasted_iota(jnp.int32, (16, TOK), 0) == 0).astype(bf16)
        for t in range(TOK // 128):
            kt = k_ref[own, t * 128:(t + 1) * 128]
            kp[h, t * 128:(t + 1) * 128, :] = jnp.concatenate([kt, zpad], axis=0).T

    subs = o_ref.shape[2] // B
    base = 0 if subs > 1 else BLOCKS - 1

    def qblock(n, _):
        chunk, sub = n // subs, n % subs
        i = chunk * BLOCKS + base + sub
        q0 = pl.multiple_of(i * B, B)
        here = pl.ds(pl.multiple_of(sub * B, B), B)
        qpos = q0 + lax.broadcasted_iota(jnp.int32, (1, B), 1)
        srow = start_row(qpos, b1, b2)

        def step(k0, width, masked, carry):
            ks = pl.ds(k0, width)
            ss = [nn(kp[h, ks, :], qt[h, :, pl.ds(q0, B)]) for h in range(HPB)]
            if masked:
                kpos = k0 + lax.broadcasted_iota(jnp.int32, (width, B), 0)
                ok = (kpos >= srow) & (kpos <= qpos)
                ss = [jnp.where(ok, s, NEG) for s in ss]
            out = []
            for h in range(HPB):
                m, acc = carry[h]
                m_new = jnp.maximum(m, jnp.max(ss[h], axis=0, keepdims=True))
                p = jnp.exp(ss[h] - m_new).astype(bf16)
                a = jnp.exp(m - m_new)
                out.append((m_new, acc * a + nn(vt[h, :, ks], p)))
            return tuple(out)

        full = jnp.minimum(i * B // FW, PROMPT // FW)
        lo = jnp.where(i < PROMPT // B, (FW // B) * (i * B // FW), first_block(i, b1, b2))
        carry = tuple((jnp.full((1, B), NEG, f32), jnp.zeros((96, B), f32)) for _ in range(HPB))
        carry = lax.fori_loop(0, full, lambda j, c: step(pl.multiple_of(j * FW, FW), FW, False, c), carry)
        carry = lax.fori_loop(lo, i + 1, lambda j, c: step(pl.multiple_of(j * B, B), B, True, c), carry)
        for h in range(HPB):
            m, acc = carry[h]
            l = acc[HD:HD + 1, :]
            o_ref[chunk, h * HD:(h + 1) * HD, here] = (acc[0:HD, :] / l).astype(bf16)
            lse_ref[h, chunk, :, here] = m + jnp.log(l)
        return 0
    lax.fori_loop(0, PARTS * subs, qblock, 0)

def attn_fwd(bounds, qkvt, subs):
    rows = lambda a: pl.BlockSpec((WIDTH, TOK), lambda i, b: (a, 0))
    width = subs * B
    return pl.pallas_call(
        fwd_kernel,
        out_shape=(jax.ShapeDtypeStruct((PARTS, WIDTH, width), bf16), jax.ShapeDtypeStruct((LH, PARTS, 1, width), f32)),
        grid_spec=pltpu.PrefetchScalarGridSpec(
            num_scalar_prefetch=1,
            grid=(1,),
            in_specs=[rows(0), rows(1), rows(2)],
            out_specs=[
                pl.BlockSpec((PARTS, WIDTH, width), lambda i, b: (0, 0, 0)),
                pl.BlockSpec((LH, PARTS, 1, width), lambda i, b: (0, 0, 0, 0)),
            ],
            scratch_shapes=[pltpu.VMEM((HPB, TOK, 128), bf16), pltpu.VMEM((HPB, 128, TOK), bf16), pltpu.VMEM((HPB, 96, TOK), bf16)],
        ),
        compiler_params=pltpu.CompilerParams(dimension_semantics=("arbitrary",), vmem_limit_bytes=60 << 20),
        cost_estimate=pl.CostEstimate(flops=subs * 13 * 10**9, bytes_accessed=5 << 20, transcendentals=0),
        name="attn_fwd",
    )(bounds, qkvt, qkvt, qkvt)


def parts3(x):
    hi = x.astype(bf16)
    r = x - hi.astype(f32)
    mid = r.astype(bf16)
    lo = (r - mid.astype(f32)).astype(bf16)
    return hi, mid, lo

def bwd_kernel(meta, scale_ref, q_ref, k_ref, v_ref, do_ref, o_ref, lse_ref, out_ref, kp, vp, qt, dot, qr, dor, dk, dv, dqt):
    b1, b2 = meta[0], meta[1]
    row16 = lax.broadcasted_iota(jnp.int32, (16, 128), 0)
    ones3 = (row16 < 3).astype(bf16)
    pad = jnp.zeros((32, 128), bf16)
    scale = scale_ref[...]

    def tail(x):
        hi, mid, lo = parts3(-x)
        rest = jnp.where(row16 == 1, mid.astype(f32), jnp.where(row16 == 2, lo.astype(f32), 0.0))
        return jnp.where(row16 == 0, hi.astype(f32), rest).astype(bf16)

    @pl.loop(0, 2 * PARTS)
    def _(step):
        chunk = step // 2
        for t in range(3):
            off = pl.multiple_of((step % 2) * HALF + t * 128, 128)
            sl, here = pl.ds(pl.multiple_of(chunk * ROWS + off, 128), 128), pl.ds(off, 128)
            q, k, v = q_ref[:, sl], k_ref[:, sl], v_ref[:, sl]
            do, o = do_ref[chunk, :, here], o_ref[chunk, :, here]
            delta = jnp.sum(do.astype(f32) * o.astype(f32), axis=0, keepdims=True)
            qa = jnp.concatenate([q, tail(lse_ref[0, chunk, :, here]), pad], axis=0)
            da = jnp.concatenate([do, tail(delta), pad], axis=0)
            qt[:, sl] = qa
            dot[:, sl] = da
            qr[sl, :] = qa.T
            dor[sl, :] = da.T
            kp[sl, :] = jnp.concatenate([k, ones3, pad], axis=0).T
            vp[sl, :] = jnp.concatenate([v, ones3, pad], axis=0).T

    dk[...] = jnp.zeros_like(dk)
    dv[...] = jnp.zeros_like(dv)
    dqt[...] = jnp.zeros_like(dqt)

    def block(k0, q0, width, masked):
        k0, q0 = pl.multiple_of(k0, width), pl.multiple_of(q0, width)
        ks, qs = pl.ds(k0, width), pl.ds(q0, width)
        p = jnp.exp(nn(kp[ks, :], qt[:, qs]))
        if masked:
            qpos = q0 + lax.broadcasted_iota(jnp.int32, (1, width), 1)
            kpos = k0 + lax.broadcasted_iota(jnp.int32, (width, width), 0)
            p = jnp.where((kpos >= start_row(qpos, b1, b2)) & (kpos <= qpos), p, 0.0)
        ds = (p * nn(vp[ks, :], dot[:, qs])).astype(bf16)
        dv[ks, :] += nn(p.astype(bf16), dor[qs, :])
        dk[ks, :] += nn(ds, qr[qs, :])
        dqt[:, qs] += nn(k_ref[:, ks], ds)

    @pl.loop(0, 12)
    def _(n):
        qb = jnp.where(n < 9, 3 + n // 3, jnp.where(n == 9, 1, 2))
        kb = jnp.where(n < 9, n % 3, jnp.where(n == 11, 1, 0))
        block(kb * FW, qb * FW, FW, False)

    @pl.loop(0, TOK // B)
    def _(i):
        lo = jnp.where(i < PROMPT // B, 2 * (i // 2), first_block(i, b1, b2))

        @pl.loop(lo, i + 1)
        def _(j):
            block(j * B, i * B, B, True)

    @pl.loop(0, 2 * PARTS)
    def _(step):
        chunk = step // 2
        for t in range(3):
            off = pl.multiple_of((step % 2) * HALF + t * 128, 128)
            sl, here = pl.ds(pl.multiple_of(chunk * ROWS + off, 128), 128), pl.ds(off, 128)
            dq = dqt[:, sl].astype(bf16).astype(f32) * scale
            out_ref[chunk, 0, :, here] = dq.astype(bf16)
            out_ref[chunk, 1, :, here] = dk[sl, :].T[0:HD, :].astype(bf16)
            out_ref[chunk, 2, :, here] = dv[sl, :].T[0:HD, :].astype(bf16)


def attn_bwd(meta, scale, qkvt, grad, mixture, logsum, pair):
    rows = lambda a: pl.BlockSpec((HD, TOK), lambda i, b: (LH * a + PH * pair + i, 0))
    return pl.pallas_call(
        bwd_kernel,
        out_shape=jax.ShapeDtypeStruct((PARTS, 3, PW, ROWS), bf16),
        grid_spec=pltpu.PrefetchScalarGridSpec(
            num_scalar_prefetch=1,
            grid=(PH,),
            in_specs=[
                pl.BlockSpec((HD, 1), lambda i, b: (0, 0)),
                rows(0),
                rows(1),
                rows(2),
                pl.BlockSpec((PARTS, HD, ROWS), lambda i, b: (0, i, 0)),
                pl.BlockSpec((PARTS, HD, ROWS), lambda i, b: (0, PH * pair + i, 0)),
                pl.BlockSpec((1, PARTS, 1, ROWS), lambda i, b: (PH * pair + i, 0, 0, 0)),
            ],
            out_specs=pl.BlockSpec((PARTS, 3, HD, ROWS), lambda i, b: (0, 0, i, 0)),
            scratch_shapes=[pltpu.VMEM((TOK, 128), bf16)] * 2
            + [pltpu.VMEM((128, TOK), bf16)] * 2
            + [pltpu.VMEM((TOK, 128), bf16)] * 2
            + [pltpu.VMEM((TOK, 128), f32)] * 2
            + [pltpu.VMEM((HD, TOK), f32)],
        ),
        compiler_params=pltpu.CompilerParams(dimension_semantics=("arbitrary",), vmem_limit_bytes=60 << 20),
        cost_estimate=pl.CostEstimate(flops=36 * 10**9, bytes_accessed=16 << 20, transcendentals=0),
        name="attn_bwd",
    )(meta, scale, qkvt, qkvt, qkvt, grad, mixture, logsum)


def normalize(values, gain_vec):
    scaling = lax.rsqrt(jnp.mean(values * values, axis=-1, keepdims=True) + EPSILON)
    return (values * scaling * gain_vec, scaling)


def normalize_back(values, scaling, gain_vec, upstream):
    weighted = gain_vec * upstream
    return scaling * weighted - values * scaling**3 * jnp.mean(values * weighted, axis=-1, keepdims=True)


def by_pair(query, key, value):
    rows = query.shape[0]
    split = jnp.stack([query, key, value], axis=1).reshape(rows, 3, PARTS, 2, PW)
    return jnp.transpose(split, (0, 3, 2, 1, 4)).reshape(rows, 3 * D)


def exchange(value):
    return lax.all_to_all(value, "heads", split_axis=0, concat_axis=0, tiled=True)


def swap(value, axis, mask):
    count = lax.axis_size(axis)
    return lax.ppermute(value, axis, [(i, i ^ mask) for i in range(count)])


def piece(value, index, count):
    rows = value.shape[-2] // count
    return lax.dynamic_slice_in_dim(value, index * rows, rows, axis=value.ndim - 2)


def sum_low(*terms):
    total = terms[0].astype(f32)
    for term in terms[1:]:
        total = total + term.astype(f32)
    return total.astype(bf16)


def far_bits():
    bits = [2]
    while bits[-1] * 2 < lax.axis_size("fsdp"):
        bits.append(bits[-1] * 2)
    return bits


def sum_far(value):
    bits = far_bits()
    for bit, twice in zip(bits[0::2], bits[1::2]):
        value = sum_low(value, *[swap(value, "fsdp", m) for m in (bit, twice, bit | twice)])
    if len(bits) % 2:
        value = sum_low(value, swap(value, "fsdp", bits[-1]))
    return value


def scatter_near(value):
    core = lax.axis_index("fsdp") & 1
    return sum_low(piece(value, core, 2), swap(piece(value, 1 - core, 2), "fsdp", 1))


def paired(value, axis, mask, high):
    other = swap(value, axis, mask)
    return jnp.where(
        high, jnp.concatenate([other, value], axis=-2), jnp.concatenate([value, other], axis=-2)
    )


def gather_near(value):
    return paired(value, "fsdp", 1, lax.axis_index("fsdp") % 2 == 1)


def scatter_heads(value):
    part = lax.axis_index("heads")
    terms = [swap(piece(value, part ^ m, PARTS), "heads", m) for m in (1, 2, 3)]
    return sum_low(piece(value, part, PARTS), *terms)


def gather_heads(value):
    part = lax.axis_index("heads")
    near, far, both = [swap(value, "heads", m) for m in (1, 2, 3)]
    odd, high = part % 2 == 1, part >= 2
    low_pair = [jnp.where(odd, near, value), jnp.where(odd, value, near)]
    high_pair = [jnp.where(odd, both, far), jnp.where(odd, far, both)]
    pieces = [jnp.where(high, b, a) for a, b in zip(low_pair, high_pair)]
    pieces += [jnp.where(high, a, b) for a, b in zip(low_pair, high_pair)]
    return jnp.concatenate(pieces, axis=-2)


def body(
    inputs,
    cotangent,
    lengths,
    adapter_ids,
    query_weight,
    key_weight,
    value_weight,
    out_weight,
    up_weight,
    down_weight,
    attn_gain,
    mlp_gain,
    query_scale,
    adapter_in,
    adapter_out,
):
    part = lax.axis_index("heads")
    rows = inputs[0]
    low, high = rows[:HALF], rows[HALF:]
    near_high = swap(high, "heads", 1)
    far_low = swap(low, "heads", 2)
    offset = part * ROWS
    ends = PROMPT + jnp.cumsum(lengths[0])
    bounds = ends[:2].astype(jnp.int32)
    ids = adapter_ids[0]
    meta = jnp.concatenate([bounds, ids, part[None].astype(jnp.int32)])
    places = offset + jnp.arange(ROWS, dtype=jnp.int32)
    token = token_adapter(places, meta)
    chosen = (token[:, None] == (jnp.arange(AR, dtype=jnp.int32) // RANK)[None, :]).astype(f32)
    chosen2 = jnp.concatenate([chosen, chosen], axis=1)
    flat_down = jnp.transpose(adapter_in, (0, 2, 1, 3)).reshape(4, D, AR)
    flat_up = adapter_out.reshape(4, AR, D)
    gain_attn = attn_gain.astype(f32)
    gain_mlp = mlp_gain.astype(f32)

    def mine(weight):
        return lax.dynamic_slice_in_dim(weight, part * WIDTH, WIDTH, axis=1)

    weights_mine = jnp.concatenate([mine(query_weight), mine(key_weight), mine(value_weight)], axis=1)
    weights_mine = lax.all_gather(weights_mine, "fsdp", axis=0, tiled=True)
    w_out = lax.all_gather(out_weight, "fsdp", axis=0, tiled=True)
    w_up = lax.all_gather(up_weight, "fsdp", axis=0, tiled=True)
    w_down = lax.all_gather(down_weight, "fsdp", axis=0, tiled=True)
    weights_all = lax.all_gather(by_pair(query_weight, key_weight, value_weight), "fsdp", axis=0, tiled=True)

    down_pair = jnp.concatenate([flat_down[0], flat_down[1]], axis=1)
    zero = jnp.zeros((AR, D), bf16)
    up_query = jnp.concatenate([flat_up[0], zero])
    up_value = jnp.concatenate([zero, flat_up[1]])
    up_pairs = by_pair(up_query, jnp.zeros_like(up_query), up_value)
    up_mine = jnp.concatenate([mine(up_query), jnp.zeros((2 * AR, WIDTH), bf16), mine(up_value)], axis=1)
    up_heads = jnp.transpose(up_mine.reshape(2 * AR, 3, 2, PW), (2, 0, 1, 3)).reshape(2, 2 * AR, 3 * PW)
    low_late, high_late, up_heads, up_mine = lax.optimization_barrier((low, high, up_heads, up_mine))
    near_low = swap(low_late, "heads", 1)
    far_high = swap(high_late, "heads", 2)
    both_low = swap(far_low, "heads", 1)
    both_high = swap(near_high, "heads", 2)
    scale_row = query_scale * HD ** (-0.5)
    scale_mine = jnp.concatenate([jnp.tile(scale_row, LH), jnp.ones((2 * WIDTH,), f32)])[:, None]

    wt, ut = weights_mine.T, up_mine.T
    done = ()
    for m, low, high in ((0, rows, None), (1, near_low, near_high), (2, far_low, far_high), (3, both_low, both_high)):
        done = qkv_project(meta, part ^ m, low, high, gain_attn[None, :], wt, down_pair, ut, scale_mine, done)
    qkvt, normed_all, inner_all = done
    out_pairs = w_out.reshape(PARTS, 2, PW, D)
    pair_weight = [out_pairs[:, p].reshape(PARTS * PW, D) for p in range(2)]
    head_mix, head_log = attn_fwd(bounds, qkvt, 2)
    mixed_head = exchange(head_mix)
    later, head_log = lax.optimization_barrier((bounds, head_log))
    tail_mix, tail_log = attn_fwd(later, qkvt, 1)
    tail_sent, mixed_head = lax.optimization_barrier((tail_mix, mixed_head))
    mixed_tail = exchange(tail_sent)
    mixture = jnp.concatenate([head_mix, tail_mix], axis=2)
    logsum = jnp.concatenate([head_log, tail_log], axis=3)

    rows_in = inputs[0].astype(f32)
    scaling_attn = lax.rsqrt(jnp.mean(rows_in * rows_in, axis=-1, keepdims=True) + EPSILON)

    branch = [tn(m.reshape(D, m.shape[2]), w_out) for m in (mixed_head, mixed_tail)]
    middle = rows_in + jnp.concatenate(branch)
    normed_mlp, scaling_mlp = normalize(middle, gain_mlp)
    normed_mlp_low = normed_mlp.astype(bf16)
    inner_up = (nn(normed_mlp_low, flat_down[2]) * chosen).astype(bf16)
    before = nn(normed_mlp_low, w_up) + nn(inner_up, flat_up[2])
    gate = jax.nn.sigmoid(before)
    hidden_low = (before * gate).astype(bf16)
    inner_down = (nn(hidden_low, flat_down[3]) * chosen).astype(bf16)
    outputs = (middle + (nn(hidden_low, w_down) + nn(inner_down, flat_up[3]))).astype(bf16)

    upstream = cotangent[0].astype(f32)
    grad_after = cotangent[0]
    spread_down = (nt(grad_after, flat_up[3]) * chosen).astype(bf16)
    grad_hidden = nt(grad_after, w_down) + nt(spread_down, flat_down[3])
    grad_before = (grad_hidden * gate * (1.0 + before * (1.0 - gate))).astype(bf16)
    spread_up = (nt(grad_before, flat_up[2]) * chosen).astype(bf16)
    grad_normed_mlp = nt(grad_before, w_up) + nt(spread_up, flat_down[2])
    grad_middle = upstream + normalize_back(middle, scaling_mlp, gain_mlp, grad_normed_mlp)
    grad_branch = grad_middle.astype(bf16)
    grad_heads = [exchange(nt(w, grad_branch).astype(bf16).reshape(PARTS, PW, ROWS)) for w in pair_weight]

    terms = [tn(spread_up, normed_mlp_low), tn(spread_down, hidden_low), tn(inner_up, grad_before), tn(inner_down, grad_after)]
    mlp_total = scatter_near(jnp.concatenate(terms).astype(bf16))
    mlp_total, grad_heads[0] = lax.optimization_barrier((mlp_total, grad_heads[0]))
    mlp_total = scatter_heads(mlp_total)
    grad_first_pair = attn_bwd(meta, scale_row[:, None], qkvt, grad_heads[0], mixture, logsum, 0)
    mlp_total, grad_first_pair = lax.optimization_barrier((mlp_total, grad_first_pair))
    arrived = [exchange(grad_first_pair.reshape(PARTS, 3 * PW, ROWS))]
    mlp_total = sum_far(mlp_total)
    meta, _ = lax.optimization_barrier((meta, grad_first_pair))
    grad_second_pair = attn_bwd(meta, scale_row[:, None], qkvt, grad_heads[1], mixture, logsum, 1)
    mlp_total, grad_second_pair = lax.optimization_barrier((mlp_total, grad_second_pair))
    arrived.append(exchange(grad_second_pair.reshape(PARTS, 3 * PW, ROWS)))

    grads = [g.reshape(PARTS, 3 * PW, ROWS) for g in (grad_first_pair, grad_second_pair)]
    meta, arrived[0] = lax.optimization_barrier((meta, arrived[0]))
    first_attn, second_attn = adapter_grads(meta, grads, normed_all, inner_all, up_heads)

    slot = PARTS * 3 * PW

    def back(p):
        both, cut = arrived[p].reshape(slot, ROWS), slice(p * slot, (p + 1) * slot)
        contract = (((0,), (1,)), ((), ()))
        return (
            lax.dot_general(both, weights_all[:, cut], contract, preferred_element_type=f32),
            lax.dot_general(both, up_pairs[:, cut], contract, preferred_element_type=f32),
        )

    tiles = D // 128
    mlp_total, first_attn = lax.optimization_barrier((mlp_total, first_attn))
    mlp_total = gather_heads(mlp_total)
    near_first = scatter_near(first_attn)
    near_second = scatter_near(second_attn.reshape(tiles, -1, 128))
    grad_normed, spread = back(0)
    near_first, grad_normed = lax.optimization_barrier((near_first, grad_normed))
    total = sum_far(jnp.concatenate([scatter_heads(near_first), near_second]))
    grad_second_part, spread_second = back(1)
    total, grad_second_part = lax.optimization_barrier((total, grad_second_part))
    total = gather_near(gather_heads(total))
    mlp_total = gather_near(mlp_total)
    grad_normed, spread = grad_normed + grad_second_part, spread + spread_second
    first_total = total[:tiles]
    second_total = total[tiles:].reshape(tiles, 2, PARTS, -1, 128)
    second_total = jnp.transpose(second_total, (2, 0, 1, 3, 4))
    grad_normed = grad_normed + nt((spread * chosen2).astype(bf16), down_pair)
    grad_inputs = grad_middle + normalize_back(rows_in, scaling_attn, gain_attn, grad_normed)

    first_pair = jnp.transpose(first_total.reshape(tiles, 2, ADAPTERS, RANK, 128), (1, 2, 0, 4, 3))
    first_rest = jnp.transpose(mlp_total[: 2 * AR].reshape(2, ADAPTERS, RANK, D), (0, 1, 3, 2))
    grad_first = jnp.concatenate([first_pair.reshape(2, ADAPTERS, D, RANK), first_rest]).astype(f32)
    second_pair = jnp.transpose(second_total.reshape(PARTS, 2, 2, PW, AR), (2, 4, 0, 1, 3)).reshape(2 * AR, D)
    grad_second = jnp.concatenate([second_pair, mlp_total[2 * AR :]]).astype(f32).reshape(4, ADAPTERS, RANK, D)
    return (outputs[None], grad_inputs[None], grad_first, grad_second)


def solution(mesh):
    placed = (
        P("fsdp", "heads", None),
        P("fsdp", "heads", None),
        P("fsdp", None),
        P("fsdp", None),
        P("fsdp", None),
        P("fsdp", None),
        P("fsdp", None),
        P("fsdp", None),
        P("fsdp", None),
        P("fsdp", None),
        P(),
        P(),
        P(),
        P(),
        P(),
    )
    return jax.shard_map(
        body,
        mesh=mesh,
        in_specs=placed,
        out_specs=(P("fsdp", "heads", None), P("fsdp", "heads", None), P(), P()),
        check_vma=False,
    )
```

```python
import jax
import jax.numpy as jnp
from jax import lax
from jax.experimental import pallas as pl
from jax.experimental.pallas import tpu as pltpu
from jax.sharding import PartitionSpec as P

D = 1280
HEADS = 16
HD = 80
RANK = 16
ADAPTERS = 8
AR = ADAPTERS * RANK
TOK = 3072
PROMPT = 1536
ROWS = 768
QB = 256
PARTS = TOK // ROWS
LH = HEADS // PARTS
HALF = ROWS // 2
PH = LH // 2
PW = PH * HD
WIDTH = LH * HD
SR = WIDTH * 128 // D
EPSILON = 1e-06
B = 256
f32, bf16 = jnp.float32, jnp.bfloat16


def nt(a, b):
    return lax.dot_general(a, b, (((1,), (1,)), ((), ())), preferred_element_type=f32)


def tn(a, b):
    return lax.dot_general(a, b, (((0,), (0,)), ((), ())), preferred_element_type=f32)


def nn(a, b):
    return lax.dot_general(a, b, (((1,), (0,)), ((), ())), preferred_element_type=f32)

def start_row(qpos, b1, b2):
    return jnp.where(qpos < PROMPT, 0, jnp.where(qpos < b1, PROMPT, jnp.where(qpos < b2, b1, b2)))

def first_block(i, b1, b2):
    q0 = i * B
    return jnp.where(q0 < b1, PROMPT, jnp.where(q0 < b2, b1, b2)) // B


def token_adapter(pos, meta):
    return jnp.where(
        pos < PROMPT, meta[2], jnp.where(pos < meta[0], meta[3], jnp.where(pos < meta[1], meta[4], meta[5]))
    )


def qkv_kernel(meta, first, low_ref, high_ref, gain_ref, wt_ref, down_ref, up_ref, scale_ref, *refs):
    out_ref, normed_ref, inner_ref, rows = refs[-4:]
    step = pl.program_id(0)

    @pl.when(step == 0)
    def _():
        rows[0:HALF, :] = low_ref[...]
        rows[HALF:ROWS, :] = high_ref[...]

    x = rows[pl.ds(pl.multiple_of(step * QB, QB), QB), :].astype(f32)
    q = lax.rsqrt(jnp.mean(x * x, axis=1, keepdims=True) + EPSILON)
    normed = (x * q * gain_ref[...]).astype(bf16)
    normed_ref[...] = normed
    pos = (first[0] + step) * QB + lax.broadcasted_iota(jnp.int32, (QB, 1), 0)
    lane = lax.broadcasted_iota(jnp.int32, (QB, 2 * AR), 1)
    chosen = (lane % AR) // RANK == token_adapter(pos, meta)
    inner = jnp.where(chosen, nn(normed, down_ref[...]), 0.0).astype(bf16)
    inner_ref[...] = inner
    out = nt(wt_ref[0:WIDTH, :], normed) + nt(up_ref[0], inner[:, :AR])
    out_ref[0:WIDTH, :] = (out * scale_ref[...]).astype(bf16)
    out_ref[WIDTH : 2 * WIDTH, :] = nt(wt_ref[WIDTH : 2 * WIDTH, :], normed).astype(bf16)
    out_ref[2 * WIDTH :, :] = (nt(wt_ref[2 * WIDTH :, :], normed) + nt(up_ref[1], inner[:, AR:])).astype(bf16)


def qkv_project(meta, chunk, low, high, gain, wt, down, up, scale, done):
    whole = lambda shape: pl.BlockSpec(shape, lambda i, *_: (0, 0))
    second = 1 if high is None else 0
    first = (chunk * (ROWS // QB))[None].astype(jnp.int32)
    return pl.pallas_call(
        qkv_kernel,
        out_shape=(
            jax.ShapeDtypeStruct((3 * WIDTH, TOK), bf16),
            jax.ShapeDtypeStruct((TOK, D), bf16),
            jax.ShapeDtypeStruct((TOK, 2 * AR), bf16),
        ),
        grid_spec=pltpu.PrefetchScalarGridSpec(
            num_scalar_prefetch=2,
            grid=(ROWS // QB,),
            in_specs=[
                whole((HALF, D)),
                pl.BlockSpec((HALF, D), lambda i, *_: (second, 0)),
                whole((1, D)),
                whole((3 * WIDTH, D)),
                whole((D, 2 * AR)),
                pl.BlockSpec((2, WIDTH, AR), lambda i, *_: (0, 0, 0)),
                whole((WIDTH, 1)),
            ]
            + [pl.BlockSpec(memory_space=pl.ANY)] * len(done),
            out_specs=[
                pl.BlockSpec((3 * WIDTH, QB), lambda i, m, first: (0, first[0] + i)),
                pl.BlockSpec((QB, D), lambda i, m, first: (first[0] + i, 0)),
                pl.BlockSpec((QB, 2 * AR), lambda i, m, first: (first[0] + i, 0)),
            ],
            scratch_shapes=[pltpu.VMEM((ROWS, D), bf16)],
        ),
        input_output_aliases={9 + i: i for i in range(len(done))},
        compiler_params=pltpu.CompilerParams(dimension_semantics=("arbitrary",), vmem_limit_bytes=60 << 20),
        cost_estimate=pl.CostEstimate(flops=2 * ROWS * D * (3 * WIDTH + 2 * AR), bytes_accessed=8 << 20, transcendentals=0),
        name="qkv_project",
    )(meta, first, low, low if high is None else high, gain, wt, down, up, scale, *done)


def adapter_kernel(meta, g0_ref, g1_ref, normed_ref, inner_ref, up_ref, keep_ref, send_ref, facc, sacc):
    step = pl.program_id(0)

    @pl.when(step == 0)
    def _():
        facc[...] = jnp.zeros_like(facc)
        sacc[...] = jnp.zeros_like(sacc)

    query = jnp.concatenate([g0_ref[0, 0], g1_ref[0, 0]], axis=0)
    value = jnp.concatenate([g0_ref[0, 2], g1_ref[0, 2]], axis=0)
    pos = step * ROWS + lax.broadcasted_iota(jnp.int32, (1, ROWS), 1)
    rank = lax.broadcasted_iota(jnp.int32, (AR, ROWS), 0)
    chosen = rank // RANK == token_adapter(pos, meta)
    for a, grad in enumerate((query, value)):
        spread = jnp.where(chosen, nn(up_ref[a], grad), 0.0).astype(bf16)
        facc[a] += nn(spread, normed_ref[...])
        sacc[a] += nn(grad, inner_ref[:, a * AR : (a + 1) * AR])

    @pl.when(step == PARTS - 1)
    def _():
        for ref, a in ((keep_ref, meta[7]), (send_ref, 1 - meta[7])):
            ref[0:AR, :] = facc[a].astype(bf16)
            for c in range(D // 128):
                ref[AR : AR + SR, c * 128 : (c + 1) * 128] = sacc[a, c * SR : (c + 1) * SR, :].astype(bf16)


def adapter_grads(meta, grads, normed, inner, up):
    return pl.pallas_call(
        adapter_kernel,
        out_shape=[jax.ShapeDtypeStruct((AR + SR, D), bf16)] * 2,
        grid_spec=pltpu.PrefetchScalarGridSpec(
            num_scalar_prefetch=1,
            grid=(PARTS,),
            in_specs=[pl.BlockSpec((1, 3, PW, ROWS), lambda i, m: (i, 0, 0, 0))] * 2
            + [
                pl.BlockSpec((ROWS, D), lambda i, m: (i, 0)),
                pl.BlockSpec((ROWS, 2 * AR), lambda i, m: (i, 0)),
                pl.BlockSpec((2, AR, WIDTH), lambda i, m: (0, 0, 0)),
            ],
            out_specs=[pl.BlockSpec((AR + SR, D), lambda i, m: (0, 0))] * 2,
            scratch_shapes=[pltpu.VMEM((2, AR, D), f32), pltpu.VMEM((2, WIDTH, AR), f32)],
        ),
        compiler_params=pltpu.CompilerParams(dimension_semantics=("arbitrary",), vmem_limit_bytes=60 << 20),
        cost_estimate=pl.CostEstimate(flops=4 * TOK * D * 2 * AR, bytes_accessed=20 << 20, transcendentals=0),
        name="adapter_grads",
    )(meta, *grads, normed, inner, up)


def back_kernel(meta, b0_ref, b1_ref, w_ref, up_ref, down_ref, rows_ref, gain_ref, middle_ref, out_ref, cols, total, spread):
    step = pl.program_id(0)
    for s in range(PARTS):
        for p, ref in enumerate((b0_ref, b1_ref)):
            r = (2 * s + p) * PW
            cols[r : r + PW, :] = ref[s, 0]

    part_sum = nn(w_ref[...], cols[...])

    @pl.when(step == 0)
    def _():
        total[...] = part_sum
        spread[0] = nn(up_ref[0], cols[...])

    @pl.when(step > 0)
    def _():
        total[...] += part_sum

    @pl.when(step == 2)
    def _():
        spread[1] = nn(up_ref[1], cols[...])
        pos = meta[6] * ROWS + lax.broadcasted_iota(jnp.int32, (1, ROWS), 1)
        rank = lax.broadcasted_iota(jnp.int32, (AR, ROWS), 0)
        chosen = rank // RANK == token_adapter(pos, meta)
        both = jnp.concatenate([jnp.where(chosen, spread[a], 0.0).astype(bf16) for a in range(2)], axis=0)
        total[...] += nn(down_ref[...], both)
        gain = gain_ref[...]
        for t in range(ROWS // 128):
            own = slice(t * 128, (t + 1) * 128)
            x = rows_ref[own, :].astype(f32)
            q = lax.rsqrt(jnp.mean(x * x, axis=1, keepdims=True) + EPSILON)
            weighted = gain * total[:, own].T
            inside = jnp.mean(x * weighted, axis=1, keepdims=True)
            out_ref[own, :] = middle_ref[own, :] + (q * weighted - x * (q * q * q * inside))


def back_inputs(meta, arrived, weights, up, down, rows, gain, grad_middle):
    whole = lambda shape: pl.BlockSpec(shape, lambda i, m: (0,) * len(shape))
    return pl.pallas_call(
        back_kernel,
        out_shape=jax.ShapeDtypeStruct((ROWS, D), f32),
        grid_spec=pltpu.PrefetchScalarGridSpec(
            num_scalar_prefetch=1,
            grid=(3,),
            in_specs=[pl.BlockSpec((PARTS, 1, PW, ROWS), lambda i, m: (0, i, 0, 0))] * 2
            + [
                pl.BlockSpec((D, D), lambda i, m: (0, i)),
                whole((2, AR, D)),
                whole((D, 2 * AR)),
                whole((ROWS, D)),
                whole((1, D)),
                whole((ROWS, D)),
            ],
            out_specs=whole((ROWS, D)),
            scratch_shapes=[pltpu.VMEM((D, ROWS), bf16), pltpu.VMEM((D, ROWS), f32), pltpu.VMEM((2, AR, ROWS), f32)],
        ),
        compiler_params=pltpu.CompilerParams(dimension_semantics=("arbitrary",), vmem_limit_bytes=60 << 20),
        cost_estimate=pl.CostEstimate(flops=6 * ROWS * D * D, bytes_accessed=24 << 20, transcendentals=0),
        name="back_inputs",
    )(meta, *arrived, weights, up, down, rows, gain, grad_middle)


HPB = LH
BLOCKS = ROWS // B
NEG = -1e30
FW = 512


def fwd_kernel(bounds, q_ref, k_ref, v_ref, o_ref, lse_ref, kp, qt, vt):
    b1, b2 = bounds[0], bounds[1]
    zpad = jnp.zeros((128 - HD, 128), bf16)
    for h in range(HPB):
        own = slice(h * HD, (h + 1) * HD)
        qt[h, 0:HD, :] = q_ref[own, :]
        qt[h, HD:128, :] = jnp.zeros((128 - HD, TOK), bf16)
        vt[h, 0:HD, :] = v_ref[own, :]
        vt[h, HD:96, :] = (lax.broadcasted_iota(jnp.int32, (16, TOK), 0) == 0).astype(bf16)
        for t in range(TOK // 128):
            kt = k_ref[own, t * 128:(t + 1) * 128]
            kp[h, t * 128:(t + 1) * 128, :] = jnp.concatenate([kt, zpad], axis=0).T

    subs = o_ref.shape[2] // B
    base = 0 if subs > 1 else BLOCKS - 1

    def qblock(n, _):
        chunk, sub = n // subs, n % subs
        i = chunk * BLOCKS + base + sub
        q0 = pl.multiple_of(i * B, B)
        here = pl.ds(pl.multiple_of(sub * B, B), B)
        qpos = q0 + lax.broadcasted_iota(jnp.int32, (1, B), 1)
        srow = start_row(qpos, b1, b2)

        def step(k0, width, masked, carry):
            ks = pl.ds(k0, width)
            ss = [nn(kp[h, ks, :], qt[h, :, pl.ds(q0, B)]) for h in range(HPB)]
            if masked:
                kpos = k0 + lax.broadcasted_iota(jnp.int32, (width, B), 0)
                ok = (kpos >= srow) & (kpos <= qpos)
                ss = [jnp.where(ok, s, NEG) for s in ss]
            out = []
            for h in range(HPB):
                m, acc = carry[h]
                m_new = jnp.maximum(m, jnp.max(ss[h], axis=0, keepdims=True))
                p = jnp.exp(ss[h] - m_new).astype(bf16)
                a = jnp.exp(m - m_new)
                out.append((m_new, acc * a + nn(vt[h, :, ks], p)))
            return tuple(out)

        full = jnp.minimum(i * B // FW, PROMPT // FW)
        lo = jnp.where(i < PROMPT // B, (FW // B) * (i * B // FW), first_block(i, b1, b2))
        carry = tuple((jnp.full((1, B), NEG, f32), jnp.zeros((96, B), f32)) for _ in range(HPB))
        carry = lax.fori_loop(0, full, lambda j, c: step(pl.multiple_of(j * FW, FW), FW, False, c), carry)
        carry = lax.fori_loop(lo, i + 1, lambda j, c: step(pl.multiple_of(j * B, B), B, True, c), carry)
        for h in range(HPB):
            m, acc = carry[h]
            l = acc[HD:HD + 1, :]
            o_ref[chunk, h * HD:(h + 1) * HD, here] = (acc[0:HD, :] / l).astype(bf16)
            lse_ref[h, chunk, :, here] = m + jnp.log(l)
        return 0
    lax.fori_loop(0, PARTS * subs, qblock, 0)

def attn_fwd(bounds, qkvt, subs):
    rows = lambda a: pl.BlockSpec((WIDTH, TOK), lambda i, b: (a, 0))
    width = subs * B
    return pl.pallas_call(
        fwd_kernel,
        out_shape=(jax.ShapeDtypeStruct((PARTS, WIDTH, width), bf16), jax.ShapeDtypeStruct((LH, PARTS, 1, width), f32)),
        grid_spec=pltpu.PrefetchScalarGridSpec(
            num_scalar_prefetch=1,
            grid=(1,),
            in_specs=[rows(0), rows(1), rows(2)],
            out_specs=[
                pl.BlockSpec((PARTS, WIDTH, width), lambda i, b: (0, 0, 0)),
                pl.BlockSpec((LH, PARTS, 1, width), lambda i, b: (0, 0, 0, 0)),
            ],
            scratch_shapes=[pltpu.VMEM((HPB, TOK, 128), bf16), pltpu.VMEM((HPB, 128, TOK), bf16), pltpu.VMEM((HPB, 96, TOK), bf16)],
        ),
        compiler_params=pltpu.CompilerParams(dimension_semantics=("arbitrary",), vmem_limit_bytes=60 << 20),
        cost_estimate=pl.CostEstimate(flops=subs * 13 * 10**9, bytes_accessed=5 << 20, transcendentals=0),
        name="attn_fwd",
    )(bounds, qkvt, qkvt, qkvt)


def parts3(x):
    hi = x.astype(bf16)
    r = x - hi.astype(f32)
    mid = r.astype(bf16)
    lo = (r - mid.astype(f32)).astype(bf16)
    return hi, mid, lo

def bwd_kernel(meta, scale_ref, q_ref, k_ref, v_ref, do_ref, o_ref, lse_ref, out_ref, kp, vp, qt, dot, qr, dor, dk, dv, dqt):
    b1, b2 = meta[0], meta[1]
    row16 = lax.broadcasted_iota(jnp.int32, (16, 128), 0)
    ones3 = (row16 < 3).astype(bf16)
    pad = jnp.zeros((32, 128), bf16)
    scale = scale_ref[...]

    def tail(x):
        hi, mid, lo = parts3(-x)
        rest = jnp.where(row16 == 1, mid.astype(f32), jnp.where(row16 == 2, lo.astype(f32), 0.0))
        return jnp.where(row16 == 0, hi.astype(f32), rest).astype(bf16)

    @pl.loop(0, 2 * PARTS)
    def _(step):
        chunk = step // 2
        for t in range(3):
            off = pl.multiple_of((step % 2) * HALF + t * 128, 128)
            sl, here = pl.ds(pl.multiple_of(chunk * ROWS + off, 128), 128), pl.ds(off, 128)
            q, k, v = q_ref[:, sl], k_ref[:, sl], v_ref[:, sl]
            do, o = do_ref[chunk, :, here], o_ref[chunk, :, here]
            delta = jnp.sum(do.astype(f32) * o.astype(f32), axis=0, keepdims=True)
            qa = jnp.concatenate([q, tail(lse_ref[0, chunk, :, here]), pad], axis=0)
            da = jnp.concatenate([do, tail(delta), pad], axis=0)
            qt[:, sl] = qa
            dot[:, sl] = da
            qr[sl, :] = qa.T
            dor[sl, :] = da.T
            kp[sl, :] = jnp.concatenate([k, ones3, pad], axis=0).T
            vp[sl, :] = jnp.concatenate([v, ones3, pad], axis=0).T

    dk[...] = jnp.zeros_like(dk)
    dv[...] = jnp.zeros_like(dv)
    dqt[...] = jnp.zeros_like(dqt)

    def block(k0, q0, width, masked):
        k0, q0 = pl.multiple_of(k0, width), pl.multiple_of(q0, width)
        ks, qs = pl.ds(k0, width), pl.ds(q0, width)
        p = jnp.exp(nn(kp[ks, :], qt[:, qs]))
        if masked:
            qpos = q0 + lax.broadcasted_iota(jnp.int32, (1, width), 1)
            kpos = k0 + lax.broadcasted_iota(jnp.int32, (width, width), 0)
            p = jnp.where((kpos >= start_row(qpos, b1, b2)) & (kpos <= qpos), p, 0.0)
        ds = (p * nn(vp[ks, :], dot[:, qs])).astype(bf16)
        dv[ks, :] += nn(p.astype(bf16), dor[qs, :])
        dk[ks, :] += nn(ds, qr[qs, :])
        dqt[:, qs] += nn(k_ref[:, ks], ds)

    @pl.loop(0, 12)
    def _(n):
        qb = jnp.where(n < 9, 3 + n // 3, jnp.where(n == 9, 1, 2))
        kb = jnp.where(n < 9, n % 3, jnp.where(n == 11, 1, 0))
        block(kb * FW, qb * FW, FW, False)

    @pl.loop(0, TOK // B)
    def _(i):
        lo = jnp.where(i < PROMPT // B, 2 * (i // 2), first_block(i, b1, b2))

        @pl.loop(lo, i + 1)
        def _(j):
            block(j * B, i * B, B, True)

    @pl.loop(0, 2 * PARTS)
    def _(step):
        chunk = step // 2
        for t in range(3):
            off = pl.multiple_of((step % 2) * HALF + t * 128, 128)
            sl, here = pl.ds(pl.multiple_of(chunk * ROWS + off, 128), 128), pl.ds(off, 128)
            dq = dqt[:, sl].astype(bf16).astype(f32) * scale
            out_ref[chunk, 0, :, here] = dq.astype(bf16)
            out_ref[chunk, 1, :, here] = dk[sl, :].T[0:HD, :].astype(bf16)
            out_ref[chunk, 2, :, here] = dv[sl, :].T[0:HD, :].astype(bf16)


def attn_bwd(meta, scale, qkvt, grad, mixture, logsum, pair):
    rows = lambda a: pl.BlockSpec((HD, TOK), lambda i, b: (LH * a + PH * pair + i, 0))
    return pl.pallas_call(
        bwd_kernel,
        out_shape=jax.ShapeDtypeStruct((PARTS, 3, PW, ROWS), bf16),
        grid_spec=pltpu.PrefetchScalarGridSpec(
            num_scalar_prefetch=1,
            grid=(PH,),
            in_specs=[
                pl.BlockSpec((HD, 1), lambda i, b: (0, 0)),
                rows(0),
                rows(1),
                rows(2),
                pl.BlockSpec((PARTS, HD, ROWS), lambda i, b: (0, i, 0)),
                pl.BlockSpec((PARTS, HD, ROWS), lambda i, b: (0, PH * pair + i, 0)),
                pl.BlockSpec((1, PARTS, 1, ROWS), lambda i, b: (PH * pair + i, 0, 0, 0)),
            ],
            out_specs=pl.BlockSpec((PARTS, 3, HD, ROWS), lambda i, b: (0, 0, i, 0)),
            scratch_shapes=[pltpu.VMEM((TOK, 128), bf16)] * 2
            + [pltpu.VMEM((128, TOK), bf16)] * 2
            + [pltpu.VMEM((TOK, 128), bf16)] * 2
            + [pltpu.VMEM((TOK, 128), f32)] * 2
            + [pltpu.VMEM((HD, TOK), f32)],
        ),
        compiler_params=pltpu.CompilerParams(dimension_semantics=("arbitrary",), vmem_limit_bytes=60 << 20),
        cost_estimate=pl.CostEstimate(flops=36 * 10**9, bytes_accessed=16 << 20, transcendentals=0),
        name="attn_bwd",
    )(meta, scale, qkvt, qkvt, qkvt, grad, mixture, logsum)


def normalize(values, gain_vec):
    scaling = lax.rsqrt(jnp.mean(values * values, axis=-1, keepdims=True) + EPSILON)
    return (values * scaling * gain_vec, scaling)


def normalize_back(values, scaling, gain_vec, upstream):
    weighted = gain_vec * upstream
    return scaling * weighted - values * scaling**3 * jnp.mean(values * weighted, axis=-1, keepdims=True)


def exchange(value):
    return lax.all_to_all(value, "heads", split_axis=0, concat_axis=0, tiled=True)


def swap(value, axis, mask):
    count = lax.axis_size(axis)
    return lax.ppermute(value, axis, [(i, i ^ mask) for i in range(count)])


def piece(value, index, count):
    rows = value.shape[-2] // count
    return lax.dynamic_slice_in_dim(value, index * rows, rows, axis=value.ndim - 2)


def sum_low(*terms):
    total = terms[0].astype(f32)
    for term in terms[1:]:
        total = total + term.astype(f32)
    return total.astype(bf16)


def far_bits():
    bits = [2]
    while bits[-1] * 2 < lax.axis_size("fsdp"):
        bits.append(bits[-1] * 2)
    return bits


def sum_far(value):
    bits = far_bits()
    for bit, twice in zip(bits[0::2], bits[1::2]):
        value = sum_low(value, *[swap(value, "fsdp", m) for m in (bit, twice, bit | twice)])
    if len(bits) % 2:
        value = sum_low(value, swap(value, "fsdp", bits[-1]))
    return value


def scatter_near(value):
    core = lax.axis_index("fsdp") & 1
    return sum_low(piece(value, core, 2), swap(piece(value, 1 - core, 2), "fsdp", 1))


def paired(value, axis, mask, high):
    other = swap(value, axis, mask)
    return jnp.where(
        high, jnp.concatenate([other, value], axis=-2), jnp.concatenate([value, other], axis=-2)
    )


def gather_near(value):
    return paired(value, "fsdp", 1, lax.axis_index("fsdp") % 2 == 1)


def scatter_heads(value):
    part = lax.axis_index("heads")
    terms = [swap(piece(value, part ^ m, PARTS), "heads", m) for m in (1, 2, 3)]
    return sum_low(piece(value, part, PARTS), *terms)


def gather_heads(value):
    part = lax.axis_index("heads")
    near, far, both = [swap(value, "heads", m) for m in (1, 2, 3)]
    odd, high = part % 2 == 1, part >= 2
    low_pair = [jnp.where(odd, near, value), jnp.where(odd, value, near)]
    high_pair = [jnp.where(odd, both, far), jnp.where(odd, far, both)]
    pieces = [jnp.where(high, b, a) for a, b in zip(low_pair, high_pair)]
    pieces += [jnp.where(high, a, b) for a, b in zip(low_pair, high_pair)]
    return jnp.concatenate(pieces, axis=-2)


def body(
    inputs,
    cotangent,
    lengths,
    adapter_ids,
    query_weight,
    key_weight,
    value_weight,
    out_weight,
    up_weight,
    down_weight,
    attn_gain,
    mlp_gain,
    query_scale,
    adapter_in,
    adapter_out,
):
    part = lax.axis_index("heads")
    rows = inputs[0]
    low, high = rows[:HALF], rows[HALF:]
    near_high = swap(high, "heads", 1)
    far_low = swap(low, "heads", 2)
    offset = part * ROWS
    ends = PROMPT + jnp.cumsum(lengths[0])
    bounds = ends[:2].astype(jnp.int32)
    ids = adapter_ids[0]
    core = lax.axis_index("fsdp") & 1
    meta = jnp.concatenate([bounds, ids, jnp.stack([part, core]).astype(jnp.int32)])
    places = offset + lax.broadcasted_iota(jnp.int32, (ROWS, AR), 0)
    lanes = lax.broadcasted_iota(jnp.int32, (ROWS, AR), 1)
    chosen = (lanes // RANK == token_adapter(places, meta)).astype(f32)
    flat_down = jnp.transpose(adapter_in, (0, 2, 1, 3)).reshape(4, D, AR)
    flat_up = adapter_out.reshape(4, AR, D)
    gain_attn = attn_gain.astype(f32)
    gain_mlp = mlp_gain.astype(f32)

    def mine(weight):
        return lax.dynamic_slice_in_dim(weight, part * WIDTH, WIDTH, axis=1)

    weights_mine = jnp.concatenate([mine(query_weight), mine(key_weight), mine(value_weight)], axis=1)
    weights_mine = lax.all_gather(weights_mine, "fsdp", axis=0, tiled=True)
    w_out = lax.all_gather(out_weight, "fsdp", axis=0, tiled=True)
    w_up = lax.all_gather(up_weight, "fsdp", axis=0, tiled=True)
    w_down = lax.all_gather(down_weight, "fsdp", axis=0, tiled=True)
    weights_all = lax.all_gather(jnp.concatenate([query_weight, key_weight, value_weight], axis=1), "fsdp", axis=0, tiled=True)

    down_pair = jnp.concatenate([flat_down[0], flat_down[1]], axis=1)
    up_mine = lax.dynamic_slice_in_dim(flat_up[:2], part * WIDTH, WIDTH, axis=2)
    low_late, high_late, down_pair = lax.optimization_barrier((low, high, down_pair))
    near_low = swap(low_late, "heads", 1)
    far_high = swap(high_late, "heads", 2)
    both_low = swap(far_low, "heads", 1)
    both_high = swap(near_high, "heads", 2)
    scale_row = query_scale * HD ** (-0.5)
    scale_mine = jnp.tile(scale_row, LH)[:, None]

    wt, ut = weights_mine.T, jnp.transpose(up_mine, (0, 2, 1))
    done = ()
    for m, low, high in ((0, rows, None), (1, near_low, near_high), (2, far_low, far_high), (3, both_low, both_high)):
        done = qkv_project(meta, part ^ m, low, high, gain_attn[None, :], wt, down_pair, ut, scale_mine, done)
    qkvt, normed_all, inner_all = done
    out_pairs = w_out.reshape(PARTS, 2, PW, D)
    pair_weight = [out_pairs[:, p].reshape(PARTS * PW, D) for p in range(2)]
    head_mix, head_log = attn_fwd(bounds, qkvt, 2)
    mixed_head = exchange(head_mix)
    later, head_log = lax.optimization_barrier((bounds, head_log))
    tail_mix, tail_log = attn_fwd(later, qkvt, 1)
    tail_sent, mixed_head = lax.optimization_barrier((tail_mix, mixed_head))
    mixed_tail = exchange(tail_sent)
    mixture = jnp.concatenate([head_mix, tail_mix], axis=2)
    logsum = jnp.concatenate([head_log, tail_log], axis=3)

    rows_in = inputs[0].astype(f32)

    branch = [tn(m.reshape(D, m.shape[2]), w_out) for m in (mixed_head, mixed_tail)]
    middle = rows_in + jnp.concatenate(branch)
    normed_mlp, scaling_mlp = normalize(middle, gain_mlp)
    normed_mlp_low = normed_mlp.astype(bf16)
    inner_up = (nn(normed_mlp_low, flat_down[2]) * chosen).astype(bf16)
    before = nn(normed_mlp_low, w_up) + nn(inner_up, flat_up[2])
    gate = jax.nn.sigmoid(before)
    hidden_low = (before * gate).astype(bf16)
    inner_down = (nn(hidden_low, flat_down[3]) * chosen).astype(bf16)

    upstream = cotangent[0].astype(f32)
    grad_after = cotangent[0]
    spread_down = (nt(grad_after, flat_up[3]) * chosen).astype(bf16)
    grad_hidden = nt(grad_after, w_down) + nt(spread_down, flat_down[3])
    grad_before = (grad_hidden * gate * (1.0 + before * (1.0 - gate))).astype(bf16)
    spread_up = (nt(grad_before, flat_up[2]) * chosen).astype(bf16)
    grad_normed_mlp = nt(grad_before, w_up) + nt(spread_up, flat_down[2])
    grad_middle = upstream + normalize_back(middle, scaling_mlp, gain_mlp, grad_normed_mlp)
    grad_branch = grad_middle.astype(bf16)
    grad_heads = [exchange(nt(w, grad_branch).astype(bf16).reshape(PARTS, PW, ROWS)) for w in pair_weight]

    terms = [tn(spread_up, normed_mlp_low), tn(spread_down, hidden_low), tn(inner_up, grad_before), tn(inner_down, grad_after)]
    mlp_total = scatter_near(jnp.concatenate(terms).astype(bf16))
    mlp_total, grad_heads[0] = lax.optimization_barrier((mlp_total, grad_heads[0]))
    mlp_total = scatter_heads(mlp_total)
    grad_first_pair = attn_bwd(meta, scale_row[:, None], qkvt, grad_heads[0], mixture, logsum, 0)
    mlp_total, grad_first_pair = lax.optimization_barrier((mlp_total, grad_first_pair))
    arrived = [exchange(grad_first_pair.reshape(PARTS, 3 * PW, ROWS))]
    mlp_total = sum_far(mlp_total)
    meta, _ = lax.optimization_barrier((meta, grad_first_pair))
    grad_second_pair = attn_bwd(meta, scale_row[:, None], qkvt, grad_heads[1], mixture, logsum, 1)
    mlp_total, grad_second_pair = lax.optimization_barrier((mlp_total, grad_second_pair))
    arrived.append(exchange(grad_second_pair.reshape(PARTS, 3 * PW, ROWS)))

    meta, arrived[0] = lax.optimization_barrier((meta, arrived[0]))
    keep, send = adapter_grads(meta, [grad_first_pair, grad_second_pair], normed_all, inner_all, up_mine)
    hidden_late, inner_late, keep = lax.optimization_barrier((hidden_low, inner_down, keep))
    outputs = (middle + (nn(hidden_late, w_down) + nn(inner_late, flat_up[3]))).astype(bf16)
    total = sum_low(keep, swap(send, "fsdp", 1))
    total = jnp.concatenate([scatter_heads(total[:AR]), total[AR:]])
    total, arrived = lax.optimization_barrier((total, arrived))
    total = sum_far(total)
    meta, total, arrived = lax.optimization_barrier((meta, total, arrived))
    total = gather_heads(jnp.concatenate([total, mlp_total]))
    arrived = [a.reshape(PARTS, 3, PW, ROWS) for a in arrived]
    grad_inputs = back_inputs(meta, arrived, weights_all, flat_up[:2], down_pair, rows, gain_attn[None, :], grad_middle)
    total, grad_inputs = lax.optimization_barrier((total, grad_inputs))
    total = gather_near(total).reshape(2, PARTS, 2 * SR + 2 * SR, D)

    first_pair = total[:, :, :SR].reshape(2, AR, D)
    second_pair = total[:, :, SR : 2 * SR].reshape(2, PARTS, SR, D // 128, AR)
    second_pair = jnp.transpose(second_pair, (0, 4, 1, 3, 2)).reshape(2, AR, D)
    mlp_pair = total[:, :, 2 * SR :].reshape(2, 2, AR, D)
    grad_first = jnp.concatenate([first_pair, mlp_pair[0]]).reshape(4, ADAPTERS, RANK, D)
    grad_first = jnp.transpose(grad_first, (0, 1, 3, 2)).astype(f32)
    grad_second = jnp.concatenate([second_pair, mlp_pair[1]]).reshape(4, ADAPTERS, RANK, D).astype(f32)
    return (outputs[None], grad_inputs[None], grad_first, grad_second)


def solution(mesh):
    placed = (
        P("fsdp", "heads", None),
        P("fsdp", "heads", None),
        P("fsdp", None),
        P("fsdp", None),
        P("fsdp", None),
        P("fsdp", None),
        P("fsdp", None),
        P("fsdp", None),
        P("fsdp", None),
        P("fsdp", None),
        P(),
        P(),
        P(),
        P(),
        P(),
    )
    return jax.shard_map(
        body,
        mesh=mesh,
        in_specs=placed,
        out_specs=(P("fsdp", "heads", None), P("fsdp", "heads", None), P(), P()),
        check_vma=False,
    )
```

```python
import jax
import jax.numpy as jnp
from jax import lax
from jax.experimental import pallas as pl
from jax.experimental.pallas import tpu as pltpu
from jax.sharding import PartitionSpec as P

D = 1280
HEADS = 16
HD = 80
RANK = 16
ADAPTERS = 8
AR = ADAPTERS * RANK
TOK = 3072
PROMPT = 1536
ROWS = 768
QB = 256
PARTS = TOK // ROWS
LH = HEADS // PARTS
HALF = ROWS // 2
PH = LH // 2
PW = PH * HD
WIDTH = LH * HD
SR = WIDTH * 128 // D
EPSILON = 1e-06
B = 256
f32, bf16 = jnp.float32, jnp.bfloat16


def nt(a, b):
    return lax.dot_general(a, b, (((1,), (1,)), ((), ())), preferred_element_type=f32)


def tn(a, b):
    return lax.dot_general(a, b, (((0,), (0,)), ((), ())), preferred_element_type=f32)


def nn(a, b):
    return lax.dot_general(a, b, (((1,), (0,)), ((), ())), preferred_element_type=f32)

def start_row(qpos, b1, b2):
    return jnp.where(qpos < PROMPT, 0, jnp.where(qpos < b1, PROMPT, jnp.where(qpos < b2, b1, b2)))

def first_block(i, b1, b2):
    q0 = i * B
    return jnp.where(q0 < b1, PROMPT, jnp.where(q0 < b2, b1, b2)) // B


def token_adapter(pos, meta):
    return jnp.where(
        pos < PROMPT, meta[2], jnp.where(pos < meta[0], meta[3], jnp.where(pos < meta[1], meta[4], meta[5]))
    )


def qkv_kernel(meta, first, low_ref, high_ref, gain_ref, wt_ref, down_ref, up_ref, scale_ref, *refs):
    out_ref, normed_ref, inner_ref, rows = refs[-4:]
    step = pl.program_id(0)

    @pl.when(step == 0)
    def _():
        rows[0:HALF, :] = low_ref[...]
        rows[HALF:ROWS, :] = high_ref[...]

    x = rows[pl.ds(pl.multiple_of(step * QB, QB), QB), :].astype(f32)
    q = lax.rsqrt(jnp.mean(x * x, axis=1, keepdims=True) + EPSILON)
    normed = (x * q * gain_ref[...]).astype(bf16)
    normed_ref[...] = normed
    pos = (first[0] + step) * QB + lax.broadcasted_iota(jnp.int32, (QB, 1), 0)
    lane = lax.broadcasted_iota(jnp.int32, (QB, 2 * AR), 1)
    chosen = (lane % AR) // RANK == token_adapter(pos, meta)
    inner = jnp.where(chosen, nn(normed, down_ref[...]), 0.0).astype(bf16)
    inner_ref[...] = inner
    out = nt(wt_ref[...], normed)
    query = out[:WIDTH] + nt(up_ref[0], inner[:, :AR])
    out_ref[0:WIDTH, :] = (query * scale_ref[...]).astype(bf16)
    out_ref[WIDTH : 2 * WIDTH, :] = out[WIDTH : 2 * WIDTH].astype(bf16)
    out_ref[2 * WIDTH :, :] = (out[2 * WIDTH :] + nt(up_ref[1], inner[:, AR:])).astype(bf16)


def qkv_project(meta, chunk, low, high, gain, wt, down, up, scale, done):
    whole = lambda shape: pl.BlockSpec(shape, lambda i, *_: (0, 0))
    second = 1 if high is None else 0
    first = (chunk * (ROWS // QB))[None].astype(jnp.int32)
    return pl.pallas_call(
        qkv_kernel,
        out_shape=(
            jax.ShapeDtypeStruct((3 * WIDTH, TOK), bf16),
            jax.ShapeDtypeStruct((TOK, D), bf16),
            jax.ShapeDtypeStruct((TOK, 2 * AR), bf16),
        ),
        grid_spec=pltpu.PrefetchScalarGridSpec(
            num_scalar_prefetch=2,
            grid=(ROWS // QB,),
            in_specs=[
                whole((HALF, D)),
                pl.BlockSpec((HALF, D), lambda i, *_: (second, 0)),
                whole((1, D)),
                whole((3 * WIDTH, D)),
                whole((D, 2 * AR)),
                pl.BlockSpec((2, WIDTH, AR), lambda i, *_: (0, 0, 0)),
                whole((WIDTH, 1)),
            ]
            + [pl.BlockSpec(memory_space=pl.ANY)] * len(done),
            out_specs=[
                pl.BlockSpec((3 * WIDTH, QB), lambda i, m, first: (0, first[0] + i)),
                pl.BlockSpec((QB, D), lambda i, m, first: (first[0] + i, 0)),
                pl.BlockSpec((QB, 2 * AR), lambda i, m, first: (first[0] + i, 0)),
            ],
            scratch_shapes=[pltpu.VMEM((ROWS, D), bf16)],
        ),
        input_output_aliases={9 + i: i for i in range(len(done))},
        compiler_params=pltpu.CompilerParams(dimension_semantics=("arbitrary",), vmem_limit_bytes=60 << 20),
        cost_estimate=pl.CostEstimate(flops=2 * ROWS * D * (3 * WIDTH + 2 * AR), bytes_accessed=8 << 20, transcendentals=0),
        name="qkv_project",
    )(meta, first, low, low if high is None else high, gain, wt, down, up, scale, *done)


def adapter_kernel(meta, g0_ref, g1_ref, normed_ref, inner_ref, up_ref, keep_ref, send_ref, facc, sacc):
    step = pl.program_id(0)

    @pl.when(step == 0)
    def _():
        facc[...] = jnp.zeros_like(facc)
        sacc[...] = jnp.zeros_like(sacc)

    query = jnp.concatenate([g0_ref[0, 0], g1_ref[0, 0]], axis=0)
    value = jnp.concatenate([g0_ref[0, 2], g1_ref[0, 2]], axis=0)
    pos = step * ROWS + lax.broadcasted_iota(jnp.int32, (1, ROWS), 1)
    rank = lax.broadcasted_iota(jnp.int32, (AR, ROWS), 0)
    chosen = rank // RANK == token_adapter(pos, meta)
    for a, grad in enumerate((query, value)):
        spread = jnp.where(chosen, nn(up_ref[a], grad), 0.0).astype(bf16)
        facc[a] += nn(spread, normed_ref[...])
        sacc[a] += nn(grad, inner_ref[:, a * AR : (a + 1) * AR])

    @pl.when(step == PARTS - 1)
    def _():
        for ref, a in ((keep_ref, meta[7]), (send_ref, 1 - meta[7])):
            ref[0:AR, :] = facc[a].astype(bf16)
            for c in range(D // 128):
                ref[AR : AR + SR, c * 128 : (c + 1) * 128] = sacc[a, c * SR : (c + 1) * SR, :].astype(bf16)


def adapter_grads(meta, grads, normed, inner, up):
    return pl.pallas_call(
        adapter_kernel,
        out_shape=[jax.ShapeDtypeStruct((AR + SR, D), bf16)] * 2,
        grid_spec=pltpu.PrefetchScalarGridSpec(
            num_scalar_prefetch=1,
            grid=(PARTS,),
            in_specs=[pl.BlockSpec((1, 3, PW, ROWS), lambda i, m: (i, 0, 0, 0))] * 2
            + [
                pl.BlockSpec((ROWS, D), lambda i, m: (i, 0)),
                pl.BlockSpec((ROWS, 2 * AR), lambda i, m: (i, 0)),
                pl.BlockSpec((2, AR, WIDTH), lambda i, m: (0, 0, 0)),
            ],
            out_specs=[pl.BlockSpec((AR + SR, D), lambda i, m: (0, 0))] * 2,
            scratch_shapes=[pltpu.VMEM((2, AR, D), f32), pltpu.VMEM((2, WIDTH, AR), f32)],
        ),
        compiler_params=pltpu.CompilerParams(dimension_semantics=("arbitrary",), vmem_limit_bytes=60 << 20),
        cost_estimate=pl.CostEstimate(flops=4 * TOK * D * 2 * AR, bytes_accessed=20 << 20, transcendentals=0),
        name="adapter_grads",
    )(meta, *grads, normed, inner, up)


def back_kernel(meta, b0_ref, b1_ref, w_ref, up_ref, down_ref, rows_ref, gain_ref, middle_ref, out_ref, cols, total, spread):
    step = pl.program_id(0)
    for s in range(PARTS):
        for p, ref in enumerate((b0_ref, b1_ref)):
            r = (2 * s + p) * PW
            cols[r : r + PW, :] = ref[s, 0]

    part_sum = nn(w_ref[...], cols[...])

    @pl.when(step == 0)
    def _():
        total[...] = part_sum
        spread[0] = nn(up_ref[0], cols[...])

    @pl.when(step > 0)
    def _():
        total[...] += part_sum

    @pl.when(step == 2)
    def _():
        spread[1] = nn(up_ref[1], cols[...])
        pos = meta[6] * ROWS + lax.broadcasted_iota(jnp.int32, (1, ROWS), 1)
        rank = lax.broadcasted_iota(jnp.int32, (AR, ROWS), 0)
        chosen = rank // RANK == token_adapter(pos, meta)
        both = jnp.concatenate([jnp.where(chosen, spread[a], 0.0).astype(bf16) for a in range(2)], axis=0)
        total[...] += nn(down_ref[...], both)
        gain = gain_ref[...]
        for t in range(ROWS // 128):
            own = slice(t * 128, (t + 1) * 128)
            x = rows_ref[own, :].astype(f32)
            q = lax.rsqrt(jnp.mean(x * x, axis=1, keepdims=True) + EPSILON)
            weighted = gain * total[:, own].T
            inside = jnp.mean(x * weighted, axis=1, keepdims=True)
            out_ref[own, :] = middle_ref[own, :] + (q * weighted - x * (q * q * q * inside))


def back_inputs(meta, arrived, weights, up, down, rows, gain, grad_middle):
    whole = lambda shape: pl.BlockSpec(shape, lambda i, m: (0,) * len(shape))
    return pl.pallas_call(
        back_kernel,
        out_shape=jax.ShapeDtypeStruct((ROWS, D), f32),
        grid_spec=pltpu.PrefetchScalarGridSpec(
            num_scalar_prefetch=1,
            grid=(3,),
            in_specs=[pl.BlockSpec((PARTS, 1, PW, ROWS), lambda i, m: (0, i, 0, 0))] * 2
            + [
                pl.BlockSpec((D, D), lambda i, m: (0, i)),
                whole((2, AR, D)),
                whole((D, 2 * AR)),
                whole((ROWS, D)),
                whole((1, D)),
                whole((ROWS, D)),
            ],
            out_specs=whole((ROWS, D)),
            scratch_shapes=[pltpu.VMEM((D, ROWS), bf16), pltpu.VMEM((D, ROWS), f32), pltpu.VMEM((2, AR, ROWS), f32)],
        ),
        compiler_params=pltpu.CompilerParams(dimension_semantics=("arbitrary",), vmem_limit_bytes=60 << 20),
        cost_estimate=pl.CostEstimate(flops=6 * ROWS * D * D, bytes_accessed=24 << 20, transcendentals=0),
        name="back_inputs",
    )(meta, *arrived, weights, up, down, rows, gain, grad_middle)


def assemble_kernel(meta, own_ref, other_ref, first_ref, second_ref, turned):
    part, core = meta[6], meta[7]
    for ref, a in ((own_ref, core), (other_ref, 1 - core)):
        for m in range(PARTS):
            where = part ^ m
            piece_rows = lambda n: pl.ds(pl.multiple_of(where * n, n), n)
            first_ref[a, piece_rows(SR), :] = ref[m, 0:SR, :].astype(f32)
            for c in range(D // 128):
                turned[pl.ds(pl.multiple_of(where * WIDTH + c * SR, SR), SR), :] = ref[m, SR : 2 * SR, c * 128 : (c + 1) * 128]
            rows = pl.ds(pl.multiple_of((where % 2) * 2 * SR, 2 * SR), 2 * SR)
            mlp = ref[m, 2 * SR :, :].astype(f32)

            @pl.when(a == 0)
            def _(mlp=mlp, rows=rows, where=where):
                first_ref[2 + where // 2, rows, :] = mlp

            @pl.when(a == 1)
            def _(mlp=mlp, rows=rows, where=where):
                second_ref[2 + where // 2, rows, :] = mlp

        for c in range(D // 128):
            second_ref[a, :, c * 128 : (c + 1) * 128] = turned[c * 128 : (c + 1) * 128, :].T.astype(f32)


def assemble(meta, own, other):
    whole = lambda shape: pl.BlockSpec(shape, lambda i, m: (0,) * len(shape))
    return pl.pallas_call(
        assemble_kernel,
        out_shape=[jax.ShapeDtypeStruct((4, AR, D), f32)] * 2,
        grid_spec=pltpu.PrefetchScalarGridSpec(
            num_scalar_prefetch=1,
            grid=(1,),
            in_specs=[whole((PARTS, 4 * SR, D))] * 2,
            out_specs=[whole((4, AR, D))] * 2,
            scratch_shapes=[pltpu.VMEM((D, AR), bf16)],
        ),
        compiler_params=pltpu.CompilerParams(dimension_semantics=("arbitrary",), vmem_limit_bytes=60 << 20),
        cost_estimate=pl.CostEstimate(flops=1 << 20, bytes_accessed=8 << 20, transcendentals=0),
        name="assemble",
    )(meta, own, other)


HPB = LH
BLOCKS = ROWS // B
NEG = -1e30
FW = 512


def fwd_kernel(bounds, q_ref, k_ref, v_ref, o_ref, lse_ref, kp, qt, vt):
    b1, b2 = bounds[0], bounds[1]
    zpad = jnp.zeros((128 - HD, 128), bf16)
    for h in range(HPB):
        own = slice(h * HD, (h + 1) * HD)
        qt[h, 0:HD, :] = q_ref[own, :]
        qt[h, HD:128, :] = jnp.zeros((128 - HD, TOK), bf16)
        vt[h, 0:HD, :] = v_ref[own, :]
        vt[h, HD:96, :] = (lax.broadcasted_iota(jnp.int32, (16, TOK), 0) == 0).astype(bf16)
        for t in range(TOK // 128):
            kt = k_ref[own, t * 128:(t + 1) * 128]
            kp[h, t * 128:(t + 1) * 128, :] = jnp.concatenate([kt, zpad], axis=0).T

    subs = o_ref.shape[2] // B
    base = 0 if subs > 1 else BLOCKS - 1

    def qblock(n, _):
        chunk, sub = n // subs, n % subs
        i = chunk * BLOCKS + base + sub
        q0 = pl.multiple_of(i * B, B)
        here = pl.ds(pl.multiple_of(sub * B, B), B)
        qpos = q0 + lax.broadcasted_iota(jnp.int32, (1, B), 1)
        srow = start_row(qpos, b1, b2)

        def step(k0, width, masked, carry):
            ks = pl.ds(k0, width)
            ss = [nn(kp[h, ks, :], qt[h, :, pl.ds(q0, B)]) for h in range(HPB)]
            if masked:
                kpos = k0 + lax.broadcasted_iota(jnp.int32, (width, B), 0)
                ok = (kpos >= srow) & (kpos <= qpos)
                ss = [jnp.where(ok, s, NEG) for s in ss]
            out = []
            for h in range(HPB):
                m, acc = carry[h]
                m_new = jnp.maximum(m, jnp.max(ss[h], axis=0, keepdims=True))
                p = jnp.exp(ss[h] - m_new).astype(bf16)
                a = jnp.exp(m - m_new)
                out.append((m_new, acc * a + nn(vt[h, :, ks], p)))
            return tuple(out)

        full = jnp.minimum(i * B // FW, PROMPT // FW)
        lo = jnp.where(i < PROMPT // B, (FW // B) * (i * B // FW), first_block(i, b1, b2))
        carry = tuple((jnp.full((1, B), NEG, f32), jnp.zeros((96, B), f32)) for _ in range(HPB))
        carry = lax.fori_loop(0, full, lambda j, c: step(pl.multiple_of(j * FW, FW), FW, False, c), carry)
        carry = lax.fori_loop(lo, i + 1, lambda j, c: step(pl.multiple_of(j * B, B), B, True, c), carry)
        for h in range(HPB):
            m, acc = carry[h]
            l = acc[HD:HD + 1, :]
            o_ref[chunk, h * HD:(h + 1) * HD, here] = (acc[0:HD, :] / l).astype(bf16)
            lse_ref[h, chunk, :, here] = m + jnp.log(l)
        return 0
    lax.fori_loop(0, PARTS * subs, qblock, 0)

def attn_fwd(bounds, qkvt, subs):
    rows = lambda a: pl.BlockSpec((WIDTH, TOK), lambda i, b: (a, 0))
    width = subs * B
    return pl.pallas_call(
        fwd_kernel,
        out_shape=(jax.ShapeDtypeStruct((PARTS, WIDTH, width), bf16), jax.ShapeDtypeStruct((LH, PARTS, 1, width), f32)),
        grid_spec=pltpu.PrefetchScalarGridSpec(
            num_scalar_prefetch=1,
            grid=(1,),
            in_specs=[rows(0), rows(1), rows(2)],
            out_specs=[
                pl.BlockSpec((PARTS, WIDTH, width), lambda i, b: (0, 0, 0)),
                pl.BlockSpec((LH, PARTS, 1, width), lambda i, b: (0, 0, 0, 0)),
            ],
            scratch_shapes=[pltpu.VMEM((HPB, TOK, 128), bf16), pltpu.VMEM((HPB, 128, TOK), bf16), pltpu.VMEM((HPB, 96, TOK), bf16)],
        ),
        compiler_params=pltpu.CompilerParams(dimension_semantics=("arbitrary",), vmem_limit_bytes=60 << 20),
        cost_estimate=pl.CostEstimate(flops=subs * 13 * 10**9, bytes_accessed=5 << 20, transcendentals=0),
        name="attn_fwd",
    )(bounds, qkvt, qkvt, qkvt)


def parts3(x):
    hi = x.astype(bf16)
    r = x - hi.astype(f32)
    mid = r.astype(bf16)
    lo = (r - mid.astype(f32)).astype(bf16)
    return hi, mid, lo

def bwd_kernel(meta, scale_ref, q_ref, k_ref, v_ref, do_ref, o_ref, lse_ref, out_ref, kp, vp, qt, dot, qr, dor, dk, dv, dqt):
    b1, b2 = meta[0], meta[1]
    row16 = lax.broadcasted_iota(jnp.int32, (16, 128), 0)
    ones3 = (row16 < 3).astype(bf16)
    pad = jnp.zeros((32, 128), bf16)
    scale = scale_ref[...]

    def tail(x):
        hi, mid, lo = parts3(-x)
        rest = jnp.where(row16 == 1, mid.astype(f32), jnp.where(row16 == 2, lo.astype(f32), 0.0))
        return jnp.where(row16 == 0, hi.astype(f32), rest).astype(bf16)

    @pl.loop(0, 2 * PARTS)
    def _(step):
        chunk = step // 2
        for t in range(3):
            off = pl.multiple_of((step % 2) * HALF + t * 128, 128)
            sl, here = pl.ds(pl.multiple_of(chunk * ROWS + off, 128), 128), pl.ds(off, 128)
            q, k, v = q_ref[:, sl], k_ref[:, sl], v_ref[:, sl]
            do, o = do_ref[chunk, :, here], o_ref[chunk, :, here]
            delta = jnp.sum(do.astype(f32) * o.astype(f32), axis=0, keepdims=True)
            qa = jnp.concatenate([q, tail(lse_ref[0, chunk, :, here]), pad], axis=0)
            da = jnp.concatenate([do, tail(delta), pad], axis=0)
            qt[:, sl] = qa
            dot[:, sl] = da
            qr[sl, :] = qa.T
            dor[sl, :] = da.T
            kp[sl, :] = jnp.concatenate([k, ones3, pad], axis=0).T
            vp[sl, :] = jnp.concatenate([v, ones3, pad], axis=0).T

    dk[...] = jnp.zeros_like(dk)
    dv[...] = jnp.zeros_like(dv)
    dqt[...] = jnp.zeros_like(dqt)

    def block(k0, q0, width, masked):
        k0, q0 = pl.multiple_of(k0, width), pl.multiple_of(q0, width)
        ks, qs = pl.ds(k0, width), pl.ds(q0, width)
        p = jnp.exp(nn(kp[ks, :], qt[:, qs]))
        if masked:
            qpos = q0 + lax.broadcasted_iota(jnp.int32, (1, width), 1)
            kpos = k0 + lax.broadcasted_iota(jnp.int32, (width, width), 0)
            p = jnp.where((kpos >= start_row(qpos, b1, b2)) & (kpos <= qpos), p, 0.0)
        ds = (p * nn(vp[ks, :], dot[:, qs])).astype(bf16)
        dv[ks, :] += nn(p.astype(bf16), dor[qs, :])
        dk[ks, :] += nn(ds, qr[qs, :])
        dqt[:, qs] += nn(k_ref[:, ks], ds)

    @pl.loop(0, 12)
    def _(n):
        qb = jnp.where(n < 9, 3 + n // 3, jnp.where(n == 9, 1, 2))
        kb = jnp.where(n < 9, n % 3, jnp.where(n == 11, 1, 0))
        block(kb * FW, qb * FW, FW, False)

    @pl.loop(0, TOK // B)
    def _(i):
        lo = jnp.where(i < PROMPT // B, 2 * (i // 2), first_block(i, b1, b2))

        @pl.loop(lo, i + 1)
        def _(j):
            block(j * B, i * B, B, True)

    @pl.loop(0, 2 * PARTS)
    def _(step):
        chunk = step // 2
        for t in range(3):
            off = pl.multiple_of((step % 2) * HALF + t * 128, 128)
            sl, here = pl.ds(pl.multiple_of(chunk * ROWS + off, 128), 128), pl.ds(off, 128)
            dq = dqt[:, sl].astype(bf16).astype(f32) * scale
            out_ref[chunk, 0, :, here] = dq.astype(bf16)
            out_ref[chunk, 1, :, here] = dk[sl, :].T[0:HD, :].astype(bf16)
            out_ref[chunk, 2, :, here] = dv[sl, :].T[0:HD, :].astype(bf16)


def attn_bwd(meta, scale, qkvt, grad, mixture, logsum, pair):
    rows = lambda a: pl.BlockSpec((HD, TOK), lambda i, b: (LH * a + PH * pair + i, 0))
    return pl.pallas_call(
        bwd_kernel,
        out_shape=jax.ShapeDtypeStruct((PARTS, 3, PW, ROWS), bf16),
        grid_spec=pltpu.PrefetchScalarGridSpec(
            num_scalar_prefetch=1,
            grid=(PH,),
            in_specs=[
                pl.BlockSpec((HD, 1), lambda i, b: (0, 0)),
                rows(0),
                rows(1),
                rows(2),
                pl.BlockSpec((PARTS, HD, ROWS), lambda i, b: (0, i, 0)),
                pl.BlockSpec((PARTS, HD, ROWS), lambda i, b: (0, PH * pair + i, 0)),
                pl.BlockSpec((1, PARTS, 1, ROWS), lambda i, b: (PH * pair + i, 0, 0, 0)),
            ],
            out_specs=pl.BlockSpec((PARTS, 3, HD, ROWS), lambda i, b: (0, 0, i, 0)),
            scratch_shapes=[pltpu.VMEM((TOK, 128), bf16)] * 2
            + [pltpu.VMEM((128, TOK), bf16)] * 2
            + [pltpu.VMEM((TOK, 128), bf16)] * 2
            + [pltpu.VMEM((TOK, 128), f32)] * 2
            + [pltpu.VMEM((HD, TOK), f32)],
        ),
        compiler_params=pltpu.CompilerParams(dimension_semantics=("arbitrary",), vmem_limit_bytes=60 << 20),
        cost_estimate=pl.CostEstimate(flops=36 * 10**9, bytes_accessed=16 << 20, transcendentals=0),
        name="attn_bwd",
    )(meta, scale, qkvt, qkvt, qkvt, grad, mixture, logsum)


def normalize(values, gain_vec):
    scaling = lax.rsqrt(jnp.mean(values * values, axis=-1, keepdims=True) + EPSILON)
    return (values * scaling * gain_vec, scaling)


def normalize_back(values, scaling, gain_vec, upstream):
    weighted = gain_vec * upstream
    return scaling * weighted - values * scaling**3 * jnp.mean(values * weighted, axis=-1, keepdims=True)


def exchange(value):
    return lax.all_to_all(value, "heads", split_axis=0, concat_axis=0, tiled=True)


def swap(value, axis, mask):
    count = lax.axis_size(axis)
    return lax.ppermute(value, axis, [(i, i ^ mask) for i in range(count)])


def piece(value, index, count):
    rows = value.shape[-2] // count
    return lax.dynamic_slice_in_dim(value, index * rows, rows, axis=value.ndim - 2)


def sum_low(*terms):
    total = terms[0].astype(f32)
    for term in terms[1:]:
        total = total + term.astype(f32)
    return total.astype(bf16)


def far_bits():
    bits = [2]
    while bits[-1] * 2 < lax.axis_size("fsdp"):
        bits.append(bits[-1] * 2)
    return bits


def sum_far(value):
    bits = far_bits()
    for bit, twice in zip(bits[0::2], bits[1::2]):
        value = sum_low(value, *[swap(value, "fsdp", m) for m in (bit, twice, bit | twice)])
    if len(bits) % 2:
        value = sum_low(value, swap(value, "fsdp", bits[-1]))
    return value


def scatter_near(value):
    core = lax.axis_index("fsdp") & 1
    return sum_low(piece(value, core, 2), swap(piece(value, 1 - core, 2), "fsdp", 1))


def scatter_heads(value):
    part = lax.axis_index("heads")
    terms = [swap(piece(value, part ^ m, PARTS), "heads", m) for m in (1, 2, 3)]
    return sum_low(piece(value, part, PARTS), *terms)


def body(
    inputs,
    cotangent,
    lengths,
    adapter_ids,
    query_weight,
    key_weight,
    value_weight,
    out_weight,
    up_weight,
    down_weight,
    attn_gain,
    mlp_gain,
    query_scale,
    adapter_in,
    adapter_out,
):
    part = lax.axis_index("heads")
    rows = inputs[0]
    low, high = rows[:HALF], rows[HALF:]
    near_high = swap(high, "heads", 1)
    far_low = swap(low, "heads", 2)
    offset = part * ROWS
    ends = PROMPT + jnp.cumsum(lengths[0])
    bounds = ends[:2].astype(jnp.int32)
    ids = adapter_ids[0]
    core = lax.axis_index("fsdp") & 1
    meta = jnp.concatenate([bounds, ids, jnp.stack([part, core]).astype(jnp.int32)])
    places = offset + lax.broadcasted_iota(jnp.int32, (ROWS, AR), 0)
    lanes = lax.broadcasted_iota(jnp.int32, (ROWS, AR), 1)
    chosen = (lanes // RANK == token_adapter(places, meta)).astype(f32)
    flat_down = jnp.transpose(adapter_in, (0, 2, 1, 3)).reshape(4, D, AR)
    flat_up = adapter_out.reshape(4, AR, D)
    gain_attn = attn_gain.astype(f32)
    gain_mlp = mlp_gain.astype(f32)

    def mine(weight):
        return lax.dynamic_slice_in_dim(weight, part * WIDTH, WIDTH, axis=1)

    weights_mine = jnp.concatenate([mine(query_weight), mine(key_weight), mine(value_weight)], axis=1)
    weights_mine = lax.all_gather(weights_mine, "fsdp", axis=0, tiled=True)
    w_out = lax.all_gather(out_weight, "fsdp", axis=0, tiled=True)
    w_up = lax.all_gather(up_weight, "fsdp", axis=0, tiled=True)
    w_down = lax.all_gather(down_weight, "fsdp", axis=0, tiled=True)
    weights_all = lax.all_gather(jnp.concatenate([query_weight, key_weight, value_weight], axis=1), "fsdp", axis=0, tiled=True)

    down_pair = jnp.concatenate([flat_down[0], flat_down[1]], axis=1)
    up_mine = lax.dynamic_slice_in_dim(flat_up[:2], part * WIDTH, WIDTH, axis=2)
    low_late, high_late, down_pair = lax.optimization_barrier((low, high, down_pair))
    near_low = swap(low_late, "heads", 1)
    far_high = swap(high_late, "heads", 2)
    both_low = swap(far_low, "heads", 1)
    both_high = swap(near_high, "heads", 2)
    scale_row = query_scale * HD ** (-0.5)
    scale_mine = jnp.tile(scale_row, LH)[:, None]

    wt, ut = weights_mine.T, jnp.transpose(up_mine, (0, 2, 1))
    done = ()
    for m, low, high in ((0, rows, None), (1, near_low, near_high), (2, far_low, far_high), (3, both_low, both_high)):
        done = qkv_project(meta, part ^ m, low, high, gain_attn[None, :], wt, down_pair, ut, scale_mine, done)
    qkvt, normed_all, inner_all = done
    out_pairs = w_out.reshape(PARTS, 2, PW, D)
    pair_weight = [out_pairs[:, p].reshape(PARTS * PW, D) for p in range(2)]
    head_mix, head_log = attn_fwd(bounds, qkvt, 2)
    mixed_head = exchange(head_mix)
    later, head_log = lax.optimization_barrier((bounds, head_log))
    tail_mix, tail_log = attn_fwd(later, qkvt, 1)
    tail_sent, mixed_head = lax.optimization_barrier((tail_mix, mixed_head))
    mixed_tail = exchange(tail_sent)
    mixture = jnp.concatenate([head_mix, tail_mix], axis=2)
    logsum = jnp.concatenate([head_log, tail_log], axis=3)

    rows_in = inputs[0].astype(f32)

    branch = [tn(m.reshape(D, m.shape[2]), w_out) for m in (mixed_head, mixed_tail)]
    middle = rows_in + jnp.concatenate(branch)
    normed_mlp, scaling_mlp = normalize(middle, gain_mlp)
    normed_mlp_low = normed_mlp.astype(bf16)
    inner_up = (nn(normed_mlp_low, flat_down[2]) * chosen).astype(bf16)
    before = nn(normed_mlp_low, w_up) + nn(inner_up, flat_up[2])
    gate = jax.nn.sigmoid(before)
    hidden_low = (before * gate).astype(bf16)
    inner_down = (nn(hidden_low, flat_down[3]) * chosen).astype(bf16)

    upstream = cotangent[0].astype(f32)
    grad_after = cotangent[0]
    spread_down = (nt(grad_after, flat_up[3]) * chosen).astype(bf16)
    grad_hidden = nt(grad_after, w_down) + nt(spread_down, flat_down[3])
    grad_before = (grad_hidden * gate * (1.0 + before * (1.0 - gate))).astype(bf16)
    spread_up = (nt(grad_before, flat_up[2]) * chosen).astype(bf16)
    grad_normed_mlp = nt(grad_before, w_up) + nt(spread_up, flat_down[2])
    grad_middle = upstream + normalize_back(middle, scaling_mlp, gain_mlp, grad_normed_mlp)
    grad_branch = grad_middle.astype(bf16)
    grad_heads = [exchange(nt(w, grad_branch).astype(bf16).reshape(PARTS, PW, ROWS)) for w in pair_weight]

    terms = [tn(spread_up, normed_mlp_low), tn(spread_down, hidden_low), tn(inner_up, grad_before), tn(inner_down, grad_after)]
    mlp_total = scatter_near(jnp.concatenate(terms).astype(bf16))
    mlp_total, grad_heads[0] = lax.optimization_barrier((mlp_total, grad_heads[0]))
    mlp_total = scatter_heads(mlp_total)
    grad_first_pair = attn_bwd(meta, scale_row[:, None], qkvt, grad_heads[0], mixture, logsum, 0)
    mlp_total, grad_first_pair = lax.optimization_barrier((mlp_total, grad_first_pair))
    arrived = [exchange(grad_first_pair.reshape(PARTS, 3 * PW, ROWS))]
    mlp_total = sum_far(mlp_total)
    meta, _ = lax.optimization_barrier((meta, grad_first_pair))
    grad_second_pair = attn_bwd(meta, scale_row[:, None], qkvt, grad_heads[1], mixture, logsum, 1)
    mlp_total, grad_second_pair = lax.optimization_barrier((mlp_total, grad_second_pair))
    arrived.append(exchange(grad_second_pair.reshape(PARTS, 3 * PW, ROWS)))

    meta, arrived[0] = lax.optimization_barrier((meta, arrived[0]))
    keep, send = adapter_grads(meta, [grad_first_pair, grad_second_pair], normed_all, inner_all, up_mine)
    hidden_late, inner_late, keep = lax.optimization_barrier((hidden_low, inner_down, keep))
    outputs = (middle + (nn(hidden_late, w_down) + nn(inner_late, flat_up[3]))).astype(bf16)
    total = sum_low(keep, swap(send, "fsdp", 1))
    total = jnp.concatenate([scatter_heads(total[:AR]), total[AR:]])
    total, arrived, outputs = lax.optimization_barrier((total, arrived, outputs))
    total = sum_far(total)
    meta, total = lax.optimization_barrier((meta, total))
    own = jnp.concatenate([total, mlp_total])
    pieces = [own] + [swap(own, "heads", m) for m in (1, 2, 3)]
    arrived = [a.reshape(PARTS, 3, PW, ROWS) for a in arrived]
    grad_inputs = back_inputs(meta, arrived, weights_all, flat_up[:2], down_pair, rows, gain_attn[None, :], grad_middle)
    pieces, grad_inputs = lax.optimization_barrier((pieces, grad_inputs))
    own = jnp.stack(pieces)
    grad_first, grad_second = assemble(meta, own, swap(own, "fsdp", 1))
    grad_first = jnp.transpose(grad_first.reshape(4, ADAPTERS, RANK, D), (0, 1, 3, 2))
    grad_second = grad_second.reshape(4, ADAPTERS, RANK, D)
    return (outputs[None], grad_inputs[None], grad_first, grad_second)


def solution(mesh):
    placed = (
        P("fsdp", "heads", None),
        P("fsdp", "heads", None),
        P("fsdp", None),
        P("fsdp", None),
        P("fsdp", None),
        P("fsdp", None),
        P("fsdp", None),
        P("fsdp", None),
        P("fsdp", None),
        P("fsdp", None),
        P(),
        P(),
        P(),
        P(),
        P(),
    )
    return jax.shard_map(
        body,
        mesh=mesh,
        in_specs=placed,
        out_specs=(P("fsdp", "heads", None), P("fsdp", "heads", None), P(), P()),
        check_vma=False,
    )
```

```python
import jax
import jax.numpy as jnp
from jax import lax
from jax.experimental import pallas as pl
from jax.experimental.pallas import tpu as pltpu
from jax.sharding import PartitionSpec as P

D = 1280
HEADS = 16
HD = 80
RANK = 16
ADAPTERS = 8
AR = ADAPTERS * RANK
TOK = 3072
PROMPT = 1536
ROWS = 768
QB = 256
PARTS = TOK // ROWS
LH = HEADS // PARTS
HALF = ROWS // 2
PH = LH // 2
PW = PH * HD
WIDTH = LH * HD
SR = WIDTH * 128 // D
EPSILON = 1e-06
B = 256
f32, bf16 = jnp.float32, jnp.bfloat16


def nt(a, b):
    return lax.dot_general(a, b, (((1,), (1,)), ((), ())), preferred_element_type=f32)


def tn(a, b):
    return lax.dot_general(a, b, (((0,), (0,)), ((), ())), preferred_element_type=f32)


def nn(a, b):
    return lax.dot_general(a, b, (((1,), (0,)), ((), ())), preferred_element_type=f32)

def start_row(qpos, b1, b2):
    return jnp.where(qpos < PROMPT, 0, jnp.where(qpos < b1, PROMPT, jnp.where(qpos < b2, b1, b2)))

def first_block(i, b1, b2):
    q0 = i * B
    return jnp.where(q0 < b1, PROMPT, jnp.where(q0 < b2, b1, b2)) // B


def token_adapter(pos, meta):
    return jnp.where(
        pos < PROMPT, meta[2], jnp.where(pos < meta[0], meta[3], jnp.where(pos < meta[1], meta[4], meta[5]))
    )


def qkv_kernel(meta, first, low_ref, high_ref, gain_ref, wt_ref, down_ref, up_ref, scale_ref, *refs):
    out_ref, normed_ref, inner_ref, rows = refs[-4:]
    step = pl.program_id(0)

    @pl.when(step == 0)
    def _():
        rows[0:HALF, :] = low_ref[...]
        rows[HALF:ROWS, :] = high_ref[...]

    x = rows[pl.ds(pl.multiple_of(step * QB, QB), QB), :].astype(f32)
    q = lax.rsqrt(jnp.mean(x * x, axis=1, keepdims=True) + EPSILON)
    normed = (x * q * gain_ref[...]).astype(bf16)
    normed_ref[...] = normed
    pos = (first[0] + step) * QB + lax.broadcasted_iota(jnp.int32, (QB, 1), 0)
    lane = lax.broadcasted_iota(jnp.int32, (QB, 2 * AR), 1)
    chosen = (lane % AR) // RANK == token_adapter(pos, meta)
    inner = jnp.where(chosen, nn(normed, down_ref[...]), 0.0).astype(bf16)
    inner_ref[...] = inner
    out = nt(wt_ref[...], normed)
    query = out[:WIDTH] + nt(up_ref[0], inner[:, :AR])
    out_ref[0:WIDTH, :] = (query * scale_ref[...]).astype(bf16)
    out_ref[WIDTH : 2 * WIDTH, :] = out[WIDTH : 2 * WIDTH].astype(bf16)
    out_ref[2 * WIDTH :, :] = (out[2 * WIDTH :] + nt(up_ref[1], inner[:, AR:])).astype(bf16)


def qkv_project(meta, chunk, low, high, gain, wt, down, up, scale, done):
    whole = lambda shape: pl.BlockSpec(shape, lambda i, *_: (0, 0))
    second = 1 if high is None else 0
    first = (chunk * (ROWS // QB))[None].astype(jnp.int32)
    return pl.pallas_call(
        qkv_kernel,
        out_shape=(
            jax.ShapeDtypeStruct((3 * WIDTH, TOK), bf16),
            jax.ShapeDtypeStruct((TOK, D), bf16),
            jax.ShapeDtypeStruct((TOK, 2 * AR), bf16),
        ),
        grid_spec=pltpu.PrefetchScalarGridSpec(
            num_scalar_prefetch=2,
            grid=(ROWS // QB,),
            in_specs=[
                whole((HALF, D)),
                pl.BlockSpec((HALF, D), lambda i, *_: (second, 0)),
                whole((1, D)),
                whole((3 * WIDTH, D)),
                whole((D, 2 * AR)),
                pl.BlockSpec((2, WIDTH, AR), lambda i, *_: (0, 0, 0)),
                whole((WIDTH, 1)),
            ]
            + [pl.BlockSpec(memory_space=pl.ANY)] * len(done),
            out_specs=[
                pl.BlockSpec((3 * WIDTH, QB), lambda i, m, first: (0, first[0] + i)),
                pl.BlockSpec((QB, D), lambda i, m, first: (first[0] + i, 0)),
                pl.BlockSpec((QB, 2 * AR), lambda i, m, first: (first[0] + i, 0)),
            ],
            scratch_shapes=[pltpu.VMEM((ROWS, D), bf16)],
        ),
        input_output_aliases={9 + i: i for i in range(len(done))},
        compiler_params=pltpu.CompilerParams(dimension_semantics=("arbitrary",), vmem_limit_bytes=60 << 20),
        cost_estimate=pl.CostEstimate(flops=2 * ROWS * D * (3 * WIDTH + 2 * AR), bytes_accessed=8 << 20, transcendentals=0),
        name="qkv_project",
    )(meta, first, low, low if high is None else high, gain, wt, down, up, scale, *done)


def adapter_kernel(meta, g0_ref, g1_ref, normed_ref, inner_ref, up_ref, keep_ref, send_ref, facc, sacc):
    step = pl.program_id(0)

    @pl.when(step == 0)
    def _():
        facc[...] = jnp.zeros_like(facc)
        sacc[...] = jnp.zeros_like(sacc)

    query = jnp.concatenate([g0_ref[0, 0], g1_ref[0, 0]], axis=0)
    value = jnp.concatenate([g0_ref[0, 2], g1_ref[0, 2]], axis=0)
    pos = step * ROWS + lax.broadcasted_iota(jnp.int32, (1, ROWS), 1)
    rank = lax.broadcasted_iota(jnp.int32, (AR, ROWS), 0)
    chosen = rank // RANK == token_adapter(pos, meta)
    for a, grad in enumerate((query, value)):
        spread = jnp.where(chosen, nn(up_ref[a], grad), 0.0).astype(bf16)
        facc[a] += nn(spread, normed_ref[...])
        sacc[a] += nn(grad, inner_ref[:, a * AR : (a + 1) * AR])

    @pl.when(step == PARTS - 1)
    def _():
        for ref, a in ((keep_ref, meta[7]), (send_ref, 1 - meta[7])):
            ref[0:AR, :] = facc[a].astype(bf16)
            for c in range(D // 128):
                ref[AR : AR + SR, c * 128 : (c + 1) * 128] = sacc[a, c * SR : (c + 1) * SR, :].astype(bf16)


def adapter_grads(meta, grads, normed, inner, up):
    return pl.pallas_call(
        adapter_kernel,
        out_shape=[jax.ShapeDtypeStruct((AR + SR, D), bf16)] * 2,
        grid_spec=pltpu.PrefetchScalarGridSpec(
            num_scalar_prefetch=1,
            grid=(PARTS,),
            in_specs=[pl.BlockSpec((1, 3, PW, ROWS), lambda i, m: (i, 0, 0, 0))] * 2
            + [
                pl.BlockSpec((ROWS, D), lambda i, m: (i, 0)),
                pl.BlockSpec((ROWS, 2 * AR), lambda i, m: (i, 0)),
                pl.BlockSpec((2, AR, WIDTH), lambda i, m: (0, 0, 0)),
            ],
            out_specs=[pl.BlockSpec((AR + SR, D), lambda i, m: (0, 0))] * 2,
            scratch_shapes=[pltpu.VMEM((2, AR, D), f32), pltpu.VMEM((2, WIDTH, AR), f32)],
        ),
        compiler_params=pltpu.CompilerParams(dimension_semantics=("arbitrary",), vmem_limit_bytes=60 << 20),
        cost_estimate=pl.CostEstimate(flops=4 * TOK * D * 2 * AR, bytes_accessed=20 << 20, transcendentals=0),
        name="adapter_grads",
    )(meta, *grads, normed, inner, up)


def back_kernel(meta, b0_ref, b1_ref, w_ref, up_ref, down_ref, rows_ref, gain_ref, middle_ref, out_ref, cols, total, spread):
    step = pl.program_id(0)
    for s in range(PARTS):
        for p, ref in enumerate((b0_ref, b1_ref)):
            r = (2 * s + p) * PW
            cols[r : r + PW, :] = ref[s, 0]

    part_sum = nn(w_ref[...], cols[...])

    @pl.when(step == 0)
    def _():
        total[...] = part_sum
        spread[0] = nn(up_ref[0], cols[...])

    @pl.when(step > 0)
    def _():
        total[...] += part_sum

    @pl.when(step == 2)
    def _():
        spread[1] = nn(up_ref[1], cols[...])
        pos = meta[6] * ROWS + lax.broadcasted_iota(jnp.int32, (1, ROWS), 1)
        rank = lax.broadcasted_iota(jnp.int32, (AR, ROWS), 0)
        chosen = rank // RANK == token_adapter(pos, meta)
        both = jnp.concatenate([jnp.where(chosen, spread[a], 0.0).astype(bf16) for a in range(2)], axis=0)
        total[...] += nn(down_ref[...], both)
        gain = gain_ref[...]
        for t in range(ROWS // 128):
            own = slice(t * 128, (t + 1) * 128)
            x = rows_ref[own, :].astype(f32)
            q = lax.rsqrt(jnp.mean(x * x, axis=1, keepdims=True) + EPSILON)
            weighted = gain * total[:, own].T
            inside = jnp.mean(x * weighted, axis=1, keepdims=True)
            out_ref[own, :] = middle_ref[own, :] + (q * weighted - x * (q * q * q * inside))


def back_inputs(meta, arrived, weights, up, down, rows, gain, grad_middle):
    whole = lambda shape: pl.BlockSpec(shape, lambda i, m: (0,) * len(shape))
    return pl.pallas_call(
        back_kernel,
        out_shape=jax.ShapeDtypeStruct((ROWS, D), f32),
        grid_spec=pltpu.PrefetchScalarGridSpec(
            num_scalar_prefetch=1,
            grid=(3,),
            in_specs=[pl.BlockSpec((PARTS, 1, PW, ROWS), lambda i, m: (0, i, 0, 0))] * 2
            + [
                pl.BlockSpec((D, D), lambda i, m: (0, i)),
                whole((2, AR, D)),
                whole((D, 2 * AR)),
                whole((ROWS, D)),
                whole((1, D)),
                whole((ROWS, D)),
            ],
            out_specs=whole((ROWS, D)),
            scratch_shapes=[pltpu.VMEM((D, ROWS), bf16), pltpu.VMEM((D, ROWS), f32), pltpu.VMEM((2, AR, ROWS), f32)],
        ),
        compiler_params=pltpu.CompilerParams(dimension_semantics=("arbitrary",), vmem_limit_bytes=60 << 20),
        cost_estimate=pl.CostEstimate(flops=6 * ROWS * D * D, bytes_accessed=24 << 20, transcendentals=0),
        name="back_inputs",
    )(meta, *arrived, weights, up, down, rows, gain, grad_middle)


def assemble_kernel(meta, own_ref, other_ref, first_ref, second_ref, turned):
    part, core = meta[6], meta[7]
    for ref, a in ((own_ref, core), (other_ref, 1 - core)):
        for m in range(PARTS):
            where = part ^ m
            piece_rows = lambda n: pl.ds(pl.multiple_of(where * n, n), n)
            first_ref[a, piece_rows(SR), :] = ref[m, 0:SR, :].astype(f32)
            for c in range(D // 128):
                turned[pl.ds(pl.multiple_of(where * WIDTH + c * SR, SR), SR), :] = ref[m, SR : 2 * SR, c * 128 : (c + 1) * 128]
            rows = pl.ds(pl.multiple_of((where % 2) * 2 * SR, 2 * SR), 2 * SR)
            mlp = ref[m, 2 * SR :, :].astype(f32)

            @pl.when(a == 0)
            def _(mlp=mlp, rows=rows, where=where):
                first_ref[2 + where // 2, rows, :] = mlp

            @pl.when(a == 1)
            def _(mlp=mlp, rows=rows, where=where):
                second_ref[2 + where // 2, rows, :] = mlp

        for c in range(D // 128):
            second_ref[a, :, c * 128 : (c + 1) * 128] = turned[c * 128 : (c + 1) * 128, :].T.astype(f32)


def assemble(meta, own, other):
    whole = lambda shape: pl.BlockSpec(shape, lambda i, m: (0,) * len(shape))
    return pl.pallas_call(
        assemble_kernel,
        out_shape=[jax.ShapeDtypeStruct((4, AR, D), f32)] * 2,
        grid_spec=pltpu.PrefetchScalarGridSpec(
            num_scalar_prefetch=1,
            grid=(1,),
            in_specs=[whole((PARTS, 4 * SR, D))] * 2,
            out_specs=[whole((4, AR, D))] * 2,
            scratch_shapes=[pltpu.VMEM((D, AR), bf16)],
        ),
        compiler_params=pltpu.CompilerParams(dimension_semantics=("arbitrary",), vmem_limit_bytes=60 << 20),
        cost_estimate=pl.CostEstimate(flops=1 << 20, bytes_accessed=8 << 20, transcendentals=0),
        name="assemble",
    )(meta, own, other)


HPB = LH
BLOCKS = ROWS // B
NEG = -1e30
FW = 512
NH = 2


def fwd_kernel(bounds, q_ref, k_ref, v_ref, o_ref, lse_ref, kp, qt, vt):
    b1, b2 = bounds[0], bounds[1]
    zpad = jnp.zeros((128 - HD, 128), bf16)
    for h in range(HPB):
        own = slice(h * HD, (h + 1) * HD)
        qt[h, 0:HD, :] = q_ref[own, :]
        qt[h, HD:128, :] = jnp.zeros((128 - HD, TOK), bf16)
        vt[h, 0:HD, :] = v_ref[own, :]
        vt[h, HD:96, :] = (lax.broadcasted_iota(jnp.int32, (16, TOK), 0) == 0).astype(bf16)
        for t in range(TOK // 128):
            kt = k_ref[own, t * 128:(t + 1) * 128]
            kp[h, t * 128:(t + 1) * 128, :] = jnp.concatenate([kt, zpad], axis=0).T

    subs = o_ref.shape[2] // B
    base = 0 if subs > 1 else BLOCKS - 1

    def qblock(n, _):
        chunk, sub = n // subs, n % subs
        i = chunk * BLOCKS + base + sub
        q0 = pl.multiple_of(i * B, B)
        here = pl.ds(pl.multiple_of(sub * B, B), B)
        qpos = q0 + lax.broadcasted_iota(jnp.int32, (1, B), 1)
        srow = start_row(qpos, b1, b2)

        def step(k0, width, masked, carry):
            ks = pl.ds(k0, width)
            ss = [nn(kp[h, ks, :], qt[h, :, pl.ds(q0, B)]) for h in range(HPB)]
            if masked:
                kpos = k0 + lax.broadcasted_iota(jnp.int32, (width, B), 0)
                ok = (kpos >= srow) & (kpos <= qpos)
                ss = [jnp.where(ok, s, NEG) for s in ss]
            out = []
            for h in range(HPB):
                m, acc = carry[h]
                m_new = jnp.maximum(m, jnp.max(ss[h], axis=0, keepdims=True))
                p = jnp.exp(ss[h] - m_new).astype(bf16)
                a = jnp.exp(m - m_new)
                out.append((m_new, acc * a + nn(vt[h, :, ks], p)))
            return tuple(out)

        full = jnp.minimum(i * B // FW, PROMPT // FW)
        lo = jnp.where(i < PROMPT // B, (FW // B) * (i * B // FW), first_block(i, b1, b2))
        carry = tuple((jnp.full((1, B), NEG, f32), jnp.zeros((96, B), f32)) for _ in range(HPB))
        carry = lax.fori_loop(0, full, lambda j, c: step(pl.multiple_of(j * FW, FW), FW, False, c), carry)
        carry = lax.fori_loop(lo, i + 1, lambda j, c: step(pl.multiple_of(j * B, B), B, True, c), carry)
        for h in range(HPB):
            m, acc = carry[h]
            l = acc[HD:HD + 1, :]
            o_ref[chunk, h * HD:(h + 1) * HD, here] = (acc[0:HD, :] / l).astype(bf16)
            lse_ref[h, chunk, :, here] = m + jnp.log(l)
        return 0
    lax.fori_loop(0, PARTS * subs, qblock, 0)

def attn_fwd(bounds, qkvt, subs):
    rows = lambda a: pl.BlockSpec((WIDTH, TOK), lambda i, b: (a, 0))
    width = subs * B
    return pl.pallas_call(
        fwd_kernel,
        out_shape=(jax.ShapeDtypeStruct((PARTS, WIDTH, width), bf16), jax.ShapeDtypeStruct((LH, PARTS, 1, width), f32)),
        grid_spec=pltpu.PrefetchScalarGridSpec(
            num_scalar_prefetch=1,
            grid=(1,),
            in_specs=[rows(0), rows(1), rows(2)],
            out_specs=[
                pl.BlockSpec((PARTS, WIDTH, width), lambda i, b: (0, 0, 0)),
                pl.BlockSpec((LH, PARTS, 1, width), lambda i, b: (0, 0, 0, 0)),
            ],
            scratch_shapes=[pltpu.VMEM((HPB, TOK, 128), bf16), pltpu.VMEM((HPB, 128, TOK), bf16), pltpu.VMEM((HPB, 96, TOK), bf16)],
        ),
        compiler_params=pltpu.CompilerParams(dimension_semantics=("arbitrary",), vmem_limit_bytes=60 << 20),
        cost_estimate=pl.CostEstimate(flops=subs * 13 * 10**9, bytes_accessed=5 << 20, transcendentals=0),
        name="attn_fwd",
    )(bounds, qkvt, qkvt, qkvt)


def parts3(x):
    hi = x.astype(bf16)
    r = x - hi.astype(f32)
    mid = r.astype(bf16)
    lo = (r - mid.astype(f32)).astype(bf16)
    return hi, mid, lo

def bwd_kernel(meta, scale_ref, q_ref, k_ref, v_ref, do_ref, o_ref, lse_ref, out_ref, kp, vp, qt, dot, dkt, dvt, dqt):
    b1, b2 = meta[0], meta[1]
    row16 = lax.broadcasted_iota(jnp.int32, (16, 128), 0)
    ones3 = (row16 < 3).astype(bf16)
    pad = jnp.zeros((32, 128), bf16)
    scale = scale_ref[...]

    def tail(x):
        hi, mid, lo = parts3(-x)
        rest = jnp.where(row16 == 1, mid.astype(f32), jnp.where(row16 == 2, lo.astype(f32), 0.0))
        return jnp.where(row16 == 0, hi.astype(f32), rest).astype(bf16)

    @pl.loop(0, 2 * PARTS)
    def _(step):
        chunk = step // 2
        for t in range(3):
            off = pl.multiple_of((step % 2) * HALF + t * 128, 128)
            sl, here = pl.ds(pl.multiple_of(chunk * ROWS + off, 128), 128), pl.ds(off, 128)
            for h in range(NH):
                own = slice(h * HD, (h + 1) * HD)
                do, o = do_ref[chunk, own, here], o_ref[chunk, own, here]
                delta = jnp.sum(do.astype(f32) * o.astype(f32), axis=0, keepdims=True)
                qt[h, :, sl] = jnp.concatenate([q_ref[own, sl], tail(lse_ref[h, chunk, :, here]), pad], axis=0)
                dot[h, :, sl] = jnp.concatenate([do, tail(delta), pad], axis=0)
                kp[h, sl, :] = jnp.concatenate([k_ref[own, sl], ones3, pad], axis=0).T
                vp[h, sl, :] = jnp.concatenate([v_ref[own, sl], ones3, pad], axis=0).T

    dkt[...] = jnp.zeros_like(dkt)
    dvt[...] = jnp.zeros_like(dvt)
    dqt[...] = jnp.zeros_like(dqt)

    def block(k0, q0, kw, qw, masked):
        k0, q0 = pl.multiple_of(k0, B), pl.multiple_of(q0, B)
        ks, qs = pl.ds(k0, kw), pl.ds(q0, qw)
        if masked:
            qpos = q0 + lax.broadcasted_iota(jnp.int32, (1, qw), 1)
            kpos = k0 + lax.broadcasted_iota(jnp.int32, (kw, qw), 0)
            ok = (kpos >= start_row(qpos, b1, b2)) & (kpos <= qpos)
        for h in range(NH):
            p = jnp.exp(nn(kp[h, ks, :], qt[h, :, qs]))
            if masked:
                p = jnp.where(ok, p, 0.0)
            ds = (p * nn(vp[h, ks, :], dot[h, :, qs])).astype(bf16)
            dvt[h, :, ks] += nt(dot[h, 0:HD, qs], p.astype(bf16))
            dkt[h, :, ks] += nt(qt[h, 0:HD, qs], ds)
            dqt[h, :, qs] += nn(k_ref[h * HD : (h + 1) * HD, ks], ds)

    @pl.loop(0, 12)
    def _(n):
        qb = jnp.where(n < 9, 3 + n // 3, jnp.where(n == 9, 1, 2))
        kb = jnp.where(n < 9, n % 3, jnp.where(n == 11, 1, 0))
        block(kb * FW, qb * FW, FW, FW, False)

    @pl.loop(0, TOK // FW)
    def _(i):
        lo = jnp.where(i < PROMPT // FW, i, first_block(i * (FW // B), b1, b2) * B // FW)

        @pl.loop(lo, i + 1)
        def _(j):
            block(j * FW, i * FW, FW, FW, True)

    @pl.loop(0, 2 * PARTS)
    def _(step):
        chunk = step // 2
        off = pl.multiple_of((step % 2) * HALF, 128)
        sl, here = pl.ds(pl.multiple_of(chunk * ROWS + off, 128), HALF), pl.ds(off, HALF)
        for h in range(NH):
            own = slice(h * HD, (h + 1) * HD)
            dq = dqt[h, :, sl].astype(bf16).astype(f32) * scale
            out_ref[chunk, 0, own, here] = dq.astype(bf16)
            out_ref[chunk, 1, own, here] = dkt[h, :, sl].astype(bf16)
            out_ref[chunk, 2, own, here] = dvt[h, :, sl].astype(bf16)


def attn_bwd(meta, scale, qkvt, grad, mixture, logsum, pair):
    steps = PH // NH
    rows = lambda a: pl.BlockSpec((NH * HD, TOK), lambda i, b: (steps * (2 * a + pair) + i, 0))
    return pl.pallas_call(
        bwd_kernel,
        out_shape=jax.ShapeDtypeStruct((PARTS, 3, PW, ROWS), bf16),
        grid_spec=pltpu.PrefetchScalarGridSpec(
            num_scalar_prefetch=1,
            grid=(steps,),
            in_specs=[
                pl.BlockSpec((HD, 1), lambda i, b: (0, 0)),
                rows(0),
                rows(1),
                rows(2),
                pl.BlockSpec((PARTS, NH * HD, ROWS), lambda i, b: (0, i, 0)),
                pl.BlockSpec((PARTS, NH * HD, ROWS), lambda i, b: (0, steps * pair + i, 0)),
                pl.BlockSpec((NH, PARTS, 1, ROWS), lambda i, b: (steps * pair + i, 0, 0, 0)),
            ],
            out_specs=pl.BlockSpec((PARTS, 3, NH * HD, ROWS), lambda i, b: (0, 0, i, 0)),
            scratch_shapes=[pltpu.VMEM((NH, TOK, 128), bf16)] * 2
            + [pltpu.VMEM((NH, 128, TOK), bf16)] * 2
            + [pltpu.VMEM((NH, HD, TOK), f32)] * 3,
        ),
        compiler_params=pltpu.CompilerParams(dimension_semantics=("arbitrary",), vmem_limit_bytes=60 << 20),
        cost_estimate=pl.CostEstimate(flops=36 * 10**9, bytes_accessed=16 << 20, transcendentals=0),
        name="attn_bwd",
    )(meta, scale, qkvt, qkvt, qkvt, grad, mixture, logsum)


def normalize(values, gain_vec):
    scaling = lax.rsqrt(jnp.mean(values * values, axis=-1, keepdims=True) + EPSILON)
    return (values * scaling * gain_vec, scaling)


def normalize_back(values, scaling, gain_vec, upstream):
    weighted = gain_vec * upstream
    return scaling * weighted - values * scaling**3 * jnp.mean(values * weighted, axis=-1, keepdims=True)


def exchange(value):
    return lax.all_to_all(value, "heads", split_axis=0, concat_axis=0, tiled=True)


def swap(value, axis, mask):
    count = lax.axis_size(axis)
    return lax.ppermute(value, axis, [(i, i ^ mask) for i in range(count)])


def piece(value, index, count):
    rows = value.shape[-2] // count
    return lax.dynamic_slice_in_dim(value, index * rows, rows, axis=value.ndim - 2)


def sum_low(*terms):
    total = terms[0].astype(f32)
    for term in terms[1:]:
        total = total + term.astype(f32)
    return total.astype(bf16)


def far_bits():
    bits = [2]
    while bits[-1] * 2 < lax.axis_size("fsdp"):
        bits.append(bits[-1] * 2)
    return bits


def sum_far(value):
    bits = far_bits()
    for bit, twice in zip(bits[0::2], bits[1::2]):
        value = sum_low(value, *[swap(value, "fsdp", m) for m in (bit, twice, bit | twice)])
    if len(bits) % 2:
        value = sum_low(value, swap(value, "fsdp", bits[-1]))
    return value


def scatter_near(value):
    core = lax.axis_index("fsdp") & 1
    return sum_low(piece(value, core, 2), swap(piece(value, 1 - core, 2), "fsdp", 1))


def scatter_heads(value):
    part = lax.axis_index("heads")
    terms = [swap(piece(value, part ^ m, PARTS), "heads", m) for m in (1, 2, 3)]
    return sum_low(piece(value, part, PARTS), *terms)


def body(
    inputs,
    cotangent,
    lengths,
    adapter_ids,
    query_weight,
    key_weight,
    value_weight,
    out_weight,
    up_weight,
    down_weight,
    attn_gain,
    mlp_gain,
    query_scale,
    adapter_in,
    adapter_out,
):
    part = lax.axis_index("heads")
    rows = inputs[0]
    low, high = rows[:HALF], rows[HALF:]
    near_high = swap(high, "heads", 1)
    far_low = swap(low, "heads", 2)
    offset = part * ROWS
    ends = PROMPT + jnp.cumsum(lengths[0])
    bounds = ends[:2].astype(jnp.int32)
    ids = adapter_ids[0]
    core = lax.axis_index("fsdp") & 1
    meta = jnp.concatenate([bounds, ids, jnp.stack([part, core]).astype(jnp.int32)])
    places = offset + lax.broadcasted_iota(jnp.int32, (ROWS, AR), 0)
    lanes = lax.broadcasted_iota(jnp.int32, (ROWS, AR), 1)
    chosen = (lanes // RANK == token_adapter(places, meta)).astype(f32)
    flat_down = jnp.transpose(adapter_in, (0, 2, 1, 3)).reshape(4, D, AR)
    flat_up = adapter_out.reshape(4, AR, D)
    gain_attn = attn_gain.astype(f32)
    gain_mlp = mlp_gain.astype(f32)

    def mine(weight):
        return lax.dynamic_slice_in_dim(weight, part * WIDTH, WIDTH, axis=1)

    weights_mine = jnp.concatenate([mine(query_weight), mine(key_weight), mine(value_weight)], axis=1)
    weights_mine = lax.all_gather(weights_mine, "fsdp", axis=0, tiled=True)
    w_out = lax.all_gather(out_weight, "fsdp", axis=0, tiled=True)
    w_up = lax.all_gather(up_weight, "fsdp", axis=0, tiled=True)
    w_down = lax.all_gather(down_weight, "fsdp", axis=0, tiled=True)
    weights_all = lax.all_gather(jnp.concatenate([query_weight, key_weight, value_weight], axis=1), "fsdp", axis=0, tiled=True)

    down_pair = jnp.concatenate([flat_down[0], flat_down[1]], axis=1)
    up_mine = lax.dynamic_slice_in_dim(flat_up[:2], part * WIDTH, WIDTH, axis=2)
    low_late, high_late, down_pair = lax.optimization_barrier((low, high, down_pair))
    near_low = swap(low_late, "heads", 1)
    far_high = swap(high_late, "heads", 2)
    both_low = swap(far_low, "heads", 1)
    both_high = swap(near_high, "heads", 2)
    scale_row = query_scale * HD ** (-0.5)
    scale_mine = jnp.tile(scale_row, LH)[:, None]

    wt, ut = weights_mine.T, jnp.transpose(up_mine, (0, 2, 1))
    done = ()
    for m, low, high in ((0, rows, None), (1, near_low, near_high), (2, far_low, far_high), (3, both_low, both_high)):
        done = qkv_project(meta, part ^ m, low, high, gain_attn[None, :], wt, down_pair, ut, scale_mine, done)
    qkvt, normed_all, inner_all = done
    out_pairs = w_out.reshape(PARTS, 2, PW, D)
    pair_weight = [out_pairs[:, p].reshape(PARTS * PW, D) for p in range(2)]
    head_mix, head_log = attn_fwd(bounds, qkvt, 2)
    mixed_head = exchange(head_mix)
    later, head_log = lax.optimization_barrier((bounds, head_log))
    tail_mix, tail_log = attn_fwd(later, qkvt, 1)
    tail_sent, mixed_head = lax.optimization_barrier((tail_mix, mixed_head))
    mixed_tail = exchange(tail_sent)
    mixture = jnp.concatenate([head_mix, tail_mix], axis=2)
    logsum = jnp.concatenate([head_log, tail_log], axis=3)

    rows_in = inputs[0].astype(f32)

    branch = [tn(m.reshape(D, m.shape[2]), w_out) for m in (mixed_head, mixed_tail)]
    middle = rows_in + jnp.concatenate(branch)
    normed_mlp, scaling_mlp = normalize(middle, gain_mlp)
    normed_mlp_low = normed_mlp.astype(bf16)
    inner_up = (nn(normed_mlp_low, flat_down[2]) * chosen).astype(bf16)
    before = nn(normed_mlp_low, w_up) + nn(inner_up, flat_up[2])
    gate = jax.nn.sigmoid(before)
    hidden_low = (before * gate).astype(bf16)
    inner_down = (nn(hidden_low, flat_down[3]) * chosen).astype(bf16)

    upstream = cotangent[0].astype(f32)
    grad_after = cotangent[0]
    spread_down = (nt(grad_after, flat_up[3]) * chosen).astype(bf16)
    grad_hidden = nt(grad_after, w_down) + nt(spread_down, flat_down[3])
    grad_before = (grad_hidden * gate * (1.0 + before * (1.0 - gate))).astype(bf16)
    spread_up = (nt(grad_before, flat_up[2]) * chosen).astype(bf16)
    grad_normed_mlp = nt(grad_before, w_up) + nt(spread_up, flat_down[2])
    grad_middle = upstream + normalize_back(middle, scaling_mlp, gain_mlp, grad_normed_mlp)
    grad_branch = grad_middle.astype(bf16)
    grad_heads = [exchange(nt(w, grad_branch).astype(bf16).reshape(PARTS, PW, ROWS)) for w in pair_weight]

    terms = [tn(spread_up, normed_mlp_low), tn(spread_down, hidden_low), tn(inner_up, grad_before), tn(inner_down, grad_after)]
    mlp_total = scatter_near(jnp.concatenate(terms).astype(bf16))
    mlp_total, grad_heads[0] = lax.optimization_barrier((mlp_total, grad_heads[0]))
    mlp_total = scatter_heads(mlp_total)
    grad_first_pair = attn_bwd(meta, scale_row[:, None], qkvt, grad_heads[0], mixture, logsum, 0)
    mlp_total, grad_first_pair = lax.optimization_barrier((mlp_total, grad_first_pair))
    arrived = [exchange(grad_first_pair.reshape(PARTS, 3 * PW, ROWS))]
    mlp_total = sum_far(mlp_total)
    meta, _ = lax.optimization_barrier((meta, grad_first_pair))
    grad_second_pair = attn_bwd(meta, scale_row[:, None], qkvt, grad_heads[1], mixture, logsum, 1)
    mlp_total, grad_second_pair = lax.optimization_barrier((mlp_total, grad_second_pair))
    arrived.append(exchange(grad_second_pair.reshape(PARTS, 3 * PW, ROWS)))

    meta, arrived[0] = lax.optimization_barrier((meta, arrived[0]))
    keep, send = adapter_grads(meta, [grad_first_pair, grad_second_pair], normed_all, inner_all, up_mine)
    hidden_late, inner_late, keep = lax.optimization_barrier((hidden_low, inner_down, keep))
    outputs = (middle + (nn(hidden_late, w_down) + nn(inner_late, flat_up[3]))).astype(bf16)
    total = sum_low(keep, swap(send, "fsdp", 1))
    total = jnp.concatenate([scatter_heads(total[:AR]), total[AR:]])
    total, arrived, outputs = lax.optimization_barrier((total, arrived, outputs))
    total = sum_far(total)
    meta, total = lax.optimization_barrier((meta, total))
    own = jnp.concatenate([total, mlp_total])
    pieces = [own] + [swap(own, "heads", m) for m in (1, 2, 3)]
    arrived = [a.reshape(PARTS, 3, PW, ROWS) for a in arrived]
    grad_inputs = back_inputs(meta, arrived, weights_all, flat_up[:2], down_pair, rows, gain_attn[None, :], grad_middle)
    pieces, grad_inputs = lax.optimization_barrier((pieces, grad_inputs))
    own = jnp.stack(pieces)
    grad_first, grad_second = assemble(meta, own, swap(own, "fsdp", 1))
    grad_first = jnp.transpose(grad_first.reshape(4, ADAPTERS, RANK, D), (0, 1, 3, 2))
    grad_second = grad_second.reshape(4, ADAPTERS, RANK, D)
    return (outputs[None], grad_inputs[None], grad_first, grad_second)


def solution(mesh):
    placed = (
        P("fsdp", "heads", None),
        P("fsdp", "heads", None),
        P("fsdp", None),
        P("fsdp", None),
        P("fsdp", None),
        P("fsdp", None),
        P("fsdp", None),
        P("fsdp", None),
        P("fsdp", None),
        P("fsdp", None),
        P(),
        P(),
        P(),
        P(),
        P(),
    )
    return jax.shard_map(
        body,
        mesh=mesh,
        in_specs=placed,
        out_specs=(P("fsdp", "heads", None), P("fsdp", "heads", None), P(), P()),
        check_vma=False,
    )
```

```python
import jax
import jax.numpy as jnp
from jax import lax
from jax.experimental import pallas as pl
from jax.experimental.pallas import tpu as pltpu
from jax.sharding import PartitionSpec as P

D = 1280
HEADS = 16
HD = 80
RANK = 16
ADAPTERS = 8
AR = ADAPTERS * RANK
TOK = 3072
PROMPT = 1536
ROWS = 768
QB = 256
PARTS = TOK // ROWS
LH = HEADS // PARTS
HALF = ROWS // 2
PH = LH // 2
PW = PH * HD
WIDTH = LH * HD
SR = WIDTH * 128 // D
EPSILON = 1e-06
B = 256
f32, bf16 = jnp.float32, jnp.bfloat16


def nt(a, b):
    return lax.dot_general(a, b, (((1,), (1,)), ((), ())), preferred_element_type=f32)


def tn(a, b):
    return lax.dot_general(a, b, (((0,), (0,)), ((), ())), preferred_element_type=f32)


def nn(a, b):
    return lax.dot_general(a, b, (((1,), (0,)), ((), ())), preferred_element_type=f32)

def start_row(qpos, b1, b2):
    return jnp.where(qpos < PROMPT, 0, jnp.where(qpos < b1, PROMPT, jnp.where(qpos < b2, b1, b2)))

def first_block(i, b1, b2):
    q0 = i * B
    return jnp.where(q0 < b1, PROMPT, jnp.where(q0 < b2, b1, b2)) // B


def token_adapter(pos, meta):
    return jnp.where(
        pos < PROMPT, meta[2], jnp.where(pos < meta[0], meta[3], jnp.where(pos < meta[1], meta[4], meta[5]))
    )


def qkv_kernel(meta, first, low_ref, high_ref, gain_ref, wt_ref, down_ref, up_ref, scale_ref, *refs):
    out_ref, normed_ref, inner_ref, rows = refs[-4:]
    step = pl.program_id(0)

    @pl.when(step == 0)
    def _():
        rows[0:HALF, :] = low_ref[...]
        rows[HALF:ROWS, :] = high_ref[...]

    x = rows[pl.ds(pl.multiple_of(step * QB, QB), QB), :].astype(f32)
    q = lax.rsqrt(jnp.mean(x * x, axis=1, keepdims=True) + EPSILON)
    normed = (x * q * gain_ref[...]).astype(bf16)
    normed_ref[...] = normed
    pos = (first[0] + step) * QB + lax.broadcasted_iota(jnp.int32, (QB, 1), 0)
    lane = lax.broadcasted_iota(jnp.int32, (QB, 2 * AR), 1)
    chosen = (lane % AR) // RANK == token_adapter(pos, meta)
    inner = jnp.where(chosen, nn(normed, down_ref[...]), 0.0).astype(bf16)
    inner_ref[...] = inner
    out = nt(wt_ref[...], normed)
    query = out[:WIDTH] + nt(up_ref[0], inner[:, :AR])
    out_ref[0:WIDTH, :] = (query * scale_ref[...]).astype(bf16)
    out_ref[WIDTH : 2 * WIDTH, :] = out[WIDTH : 2 * WIDTH].astype(bf16)
    out_ref[2 * WIDTH :, :] = (out[2 * WIDTH :] + nt(up_ref[1], inner[:, AR:])).astype(bf16)


def qkv_project(meta, chunk, low, high, gain, wt, down, up, scale, done):
    whole = lambda shape: pl.BlockSpec(shape, lambda i, *_: (0, 0))
    second = 1 if high is None else 0
    first = (chunk * (ROWS // QB))[None].astype(jnp.int32)
    return pl.pallas_call(
        qkv_kernel,
        out_shape=(
            jax.ShapeDtypeStruct((3 * WIDTH, TOK), bf16),
            jax.ShapeDtypeStruct((TOK, D), bf16),
            jax.ShapeDtypeStruct((TOK, 2 * AR), bf16),
        ),
        grid_spec=pltpu.PrefetchScalarGridSpec(
            num_scalar_prefetch=2,
            grid=(ROWS // QB,),
            in_specs=[
                whole((HALF, D)),
                pl.BlockSpec((HALF, D), lambda i, *_: (second, 0)),
                whole((1, D)),
                whole((3 * WIDTH, D)),
                whole((D, 2 * AR)),
                pl.BlockSpec((2, WIDTH, AR), lambda i, *_: (0, 0, 0)),
                whole((WIDTH, 1)),
            ]
            + [pl.BlockSpec(memory_space=pl.ANY)] * len(done),
            out_specs=[
                pl.BlockSpec((3 * WIDTH, QB), lambda i, m, first: (0, first[0] + i)),
                pl.BlockSpec((QB, D), lambda i, m, first: (first[0] + i, 0)),
                pl.BlockSpec((QB, 2 * AR), lambda i, m, first: (first[0] + i, 0)),
            ],
            scratch_shapes=[pltpu.VMEM((ROWS, D), bf16)],
        ),
        input_output_aliases={9 + i: i for i in range(len(done))},
        compiler_params=pltpu.CompilerParams(dimension_semantics=("arbitrary",), vmem_limit_bytes=60 << 20),
        cost_estimate=pl.CostEstimate(flops=2 * ROWS * D * (3 * WIDTH + 2 * AR), bytes_accessed=8 << 20, transcendentals=0),
        name="qkv_project",
    )(meta, first, low, low if high is None else high, gain, wt, down, up, scale, *done)


def adapter_kernel(meta, g0_ref, g1_ref, normed_ref, inner_ref, up_ref, keep_ref, send_ref, facc, sacc):
    step = pl.program_id(0)

    @pl.when(step == 0)
    def _():
        facc[...] = jnp.zeros_like(facc)
        sacc[...] = jnp.zeros_like(sacc)

    query = jnp.concatenate([g0_ref[0, 0], g1_ref[0, 0]], axis=0)
    value = jnp.concatenate([g0_ref[0, 2], g1_ref[0, 2]], axis=0)
    pos = step * ROWS + lax.broadcasted_iota(jnp.int32, (1, ROWS), 1)
    rank = lax.broadcasted_iota(jnp.int32, (AR, ROWS), 0)
    chosen = rank // RANK == token_adapter(pos, meta)
    for a, grad in enumerate((query, value)):
        spread = jnp.where(chosen, nn(up_ref[a], grad), 0.0).astype(bf16)
        facc[a] += nn(spread, normed_ref[...])
        sacc[a] += nn(grad, inner_ref[:, a * AR : (a + 1) * AR])

    @pl.when(step == PARTS - 1)
    def _():
        for ref, a in ((keep_ref, meta[7]), (send_ref, 1 - meta[7])):
            ref[0:AR, :] = facc[a].astype(bf16)
            for c in range(D // 128):
                ref[AR : AR + SR, c * 128 : (c + 1) * 128] = sacc[a, c * SR : (c + 1) * SR, :].astype(bf16)


def adapter_grads(meta, grads, normed, inner, up):
    return pl.pallas_call(
        adapter_kernel,
        out_shape=[jax.ShapeDtypeStruct((AR + SR, D), bf16)] * 2,
        grid_spec=pltpu.PrefetchScalarGridSpec(
            num_scalar_prefetch=1,
            grid=(PARTS,),
            in_specs=[pl.BlockSpec((1, 3, PW, ROWS), lambda i, m: (i, 0, 0, 0))] * 2
            + [
                pl.BlockSpec((ROWS, D), lambda i, m: (i, 0)),
                pl.BlockSpec((ROWS, 2 * AR), lambda i, m: (i, 0)),
                pl.BlockSpec((2, AR, WIDTH), lambda i, m: (0, 0, 0)),
            ],
            out_specs=[pl.BlockSpec((AR + SR, D), lambda i, m: (0, 0))] * 2,
            scratch_shapes=[pltpu.VMEM((2, AR, D), f32), pltpu.VMEM((2, WIDTH, AR), f32)],
        ),
        compiler_params=pltpu.CompilerParams(dimension_semantics=("arbitrary",), vmem_limit_bytes=60 << 20),
        cost_estimate=pl.CostEstimate(flops=4 * TOK * D * 2 * AR, bytes_accessed=20 << 20, transcendentals=0),
        name="adapter_grads",
    )(meta, *grads, normed, inner, up)


def back_kernel(meta, b0_ref, b1_ref, w_ref, up_ref, down_ref, rows_ref, gain_ref, middle_ref, out_ref, cols, total, spread):
    step = pl.program_id(0)
    for s in range(PARTS):
        for p, ref in enumerate((b0_ref, b1_ref)):
            r = (2 * s + p) * PW
            cols[r : r + PW, :] = ref[s, 0]

    part_sum = nn(w_ref[...], cols[...])

    @pl.when(step == 0)
    def _():
        total[...] = part_sum
        spread[0] = nn(up_ref[0], cols[...])

    @pl.when(step > 0)
    def _():
        total[...] += part_sum

    @pl.when(step == 2)
    def _():
        spread[1] = nn(up_ref[1], cols[...])
        pos = meta[6] * ROWS + lax.broadcasted_iota(jnp.int32, (1, ROWS), 1)
        rank = lax.broadcasted_iota(jnp.int32, (AR, ROWS), 0)
        chosen = rank // RANK == token_adapter(pos, meta)
        both = jnp.concatenate([jnp.where(chosen, spread[a], 0.0).astype(bf16) for a in range(2)], axis=0)
        total[...] += nn(down_ref[...], both)
        gain = gain_ref[...]
        for t in range(ROWS // 128):
            own = slice(t * 128, (t + 1) * 128)
            x = rows_ref[own, :].astype(f32)
            q = lax.rsqrt(jnp.mean(x * x, axis=1, keepdims=True) + EPSILON)
            weighted = gain * total[:, own].T
            inside = jnp.mean(x * weighted, axis=1, keepdims=True)
            out_ref[own, :] = middle_ref[own, :] + (q * weighted - x * (q * q * q * inside))


def back_inputs(meta, arrived, weights, up, down, rows, gain, grad_middle):
    whole = lambda shape: pl.BlockSpec(shape, lambda i, m: (0,) * len(shape))
    return pl.pallas_call(
        back_kernel,
        out_shape=jax.ShapeDtypeStruct((ROWS, D), f32),
        grid_spec=pltpu.PrefetchScalarGridSpec(
            num_scalar_prefetch=1,
            grid=(3,),
            in_specs=[pl.BlockSpec((PARTS, 1, PW, ROWS), lambda i, m: (0, i, 0, 0))] * 2
            + [
                pl.BlockSpec((D, D), lambda i, m: (0, i)),
                whole((2, AR, D)),
                whole((D, 2 * AR)),
                whole((ROWS, D)),
                whole((1, D)),
                whole((ROWS, D)),
            ],
            out_specs=whole((ROWS, D)),
            scratch_shapes=[pltpu.VMEM((D, ROWS), bf16), pltpu.VMEM((D, ROWS), f32), pltpu.VMEM((2, AR, ROWS), f32)],
        ),
        compiler_params=pltpu.CompilerParams(dimension_semantics=("arbitrary",), vmem_limit_bytes=60 << 20),
        cost_estimate=pl.CostEstimate(flops=6 * ROWS * D * D, bytes_accessed=24 << 20, transcendentals=0),
        name="back_inputs",
    )(meta, *arrived, weights, up, down, rows, gain, grad_middle)


def assemble_kernel(meta, own_ref, other_ref, first_ref, second_ref, turned):
    part, core = meta[6], meta[7]
    for ref, a in ((own_ref, core), (other_ref, 1 - core)):
        for m in range(PARTS):
            where = part ^ m
            piece_rows = lambda n: pl.ds(pl.multiple_of(where * n, n), n)
            first_ref[a, piece_rows(SR), :] = ref[m, 0:SR, :].astype(f32)
            for c in range(D // 128):
                turned[pl.ds(pl.multiple_of(where * WIDTH + c * SR, SR), SR), :] = ref[m, SR : 2 * SR, c * 128 : (c + 1) * 128]
            rows = pl.ds(pl.multiple_of((where % 2) * 2 * SR, 2 * SR), 2 * SR)
            mlp = ref[m, 2 * SR :, :].astype(f32)

            @pl.when(a == 0)
            def _(mlp=mlp, rows=rows, where=where):
                first_ref[2 + where // 2, rows, :] = mlp

            @pl.when(a == 1)
            def _(mlp=mlp, rows=rows, where=where):
                second_ref[2 + where // 2, rows, :] = mlp

        for c in range(D // 128):
            second_ref[a, :, c * 128 : (c + 1) * 128] = turned[c * 128 : (c + 1) * 128, :].T.astype(f32)


def assemble(meta, own, other):
    whole = lambda shape: pl.BlockSpec(shape, lambda i, m: (0,) * len(shape))
    return pl.pallas_call(
        assemble_kernel,
        out_shape=[jax.ShapeDtypeStruct((4, AR, D), f32)] * 2,
        grid_spec=pltpu.PrefetchScalarGridSpec(
            num_scalar_prefetch=1,
            grid=(1,),
            in_specs=[whole((PARTS, 4 * SR, D))] * 2,
            out_specs=[whole((4, AR, D))] * 2,
            scratch_shapes=[pltpu.VMEM((D, AR), bf16)],
        ),
        compiler_params=pltpu.CompilerParams(dimension_semantics=("arbitrary",), vmem_limit_bytes=60 << 20),
        cost_estimate=pl.CostEstimate(flops=1 << 20, bytes_accessed=8 << 20, transcendentals=0),
        name="assemble",
    )(meta, own, other)


HPB = LH
BLOCKS = ROWS // B
NEG = -1e30
FW = 512
NH = 2


def fwd_kernel(bounds, q_ref, k_ref, v_ref, o_ref, lse_ref, kp, qt, vt):
    b1, b2 = bounds[0], bounds[1]
    zpad = jnp.zeros((128 - HD, 128), bf16)
    for h in range(HPB):
        own = slice(h * HD, (h + 1) * HD)
        qt[h, 0:HD, :] = q_ref[own, :]
        qt[h, HD:128, :] = jnp.zeros((128 - HD, TOK), bf16)
        vt[h, 0:HD, :] = v_ref[own, :]
        vt[h, HD:96, :] = (lax.broadcasted_iota(jnp.int32, (16, TOK), 0) == 0).astype(bf16)
        for t in range(TOK // 128):
            kt = k_ref[own, t * 128:(t + 1) * 128]
            kp[h, t * 128:(t + 1) * 128, :] = jnp.concatenate([kt, zpad], axis=0).T

    subs = o_ref.shape[2] // B
    base = 0 if subs > 1 else BLOCKS - 1

    def qblock(n, _):
        chunk, sub = n // subs, n % subs
        i = chunk * BLOCKS + base + sub
        q0 = pl.multiple_of(i * B, B)
        here = pl.ds(pl.multiple_of(sub * B, B), B)
        qpos = q0 + lax.broadcasted_iota(jnp.int32, (1, B), 1)
        srow = start_row(qpos, b1, b2)

        def step(k0, width, masked, carry):
            ks = pl.ds(k0, width)
            ss = [nn(kp[h, ks, :], qt[h, :, pl.ds(q0, B)]) for h in range(HPB)]
            if masked:
                kpos = k0 + lax.broadcasted_iota(jnp.int32, (width, B), 0)
                ok = (kpos >= srow) & (kpos <= qpos)
                ss = [jnp.where(ok, s, NEG) for s in ss]
            out = []
            for h in range(HPB):
                m, acc = carry[h]
                m_new = jnp.maximum(m, jnp.max(ss[h], axis=0, keepdims=True))
                p = jnp.exp(ss[h] - m_new).astype(bf16)
                a = jnp.exp(m - m_new)
                out.append((m_new, acc * a + nn(vt[h, :, ks], p)))
            return tuple(out)

        full = jnp.minimum(i * B // FW, PROMPT // FW)
        lo = jnp.where(i < PROMPT // B, (FW // B) * (i * B // FW), first_block(i, b1, b2))
        carry = tuple((jnp.full((1, B), NEG, f32), jnp.zeros((96, B), f32)) for _ in range(HPB))
        carry = lax.fori_loop(0, full, lambda j, c: step(pl.multiple_of(j * FW, FW), FW, False, c), carry)
        carry = lax.fori_loop(lo, i + 1, lambda j, c: step(pl.multiple_of(j * B, B), B, True, c), carry)
        for h in range(HPB):
            m, acc = carry[h]
            l = acc[HD:HD + 1, :]
            o_ref[chunk, h * HD:(h + 1) * HD, here] = (acc[0:HD, :] / l).astype(bf16)
            lse_ref[h, chunk, :, here] = m + jnp.log(l)
        return 0
    lax.fori_loop(0, PARTS * subs, qblock, 0)

def attn_fwd(bounds, qkvt, subs):
    rows = lambda a: pl.BlockSpec((WIDTH, TOK), lambda i, b: (a, 0))
    width = subs * B
    return pl.pallas_call(
        fwd_kernel,
        out_shape=(jax.ShapeDtypeStruct((PARTS, WIDTH, width), bf16), jax.ShapeDtypeStruct((LH, PARTS, 1, width), f32)),
        grid_spec=pltpu.PrefetchScalarGridSpec(
            num_scalar_prefetch=1,
            grid=(1,),
            in_specs=[rows(0), rows(1), rows(2)],
            out_specs=[
                pl.BlockSpec((PARTS, WIDTH, width), lambda i, b: (0, 0, 0)),
                pl.BlockSpec((LH, PARTS, 1, width), lambda i, b: (0, 0, 0, 0)),
            ],
            scratch_shapes=[pltpu.VMEM((HPB, TOK, 128), bf16), pltpu.VMEM((HPB, 128, TOK), bf16), pltpu.VMEM((HPB, 96, TOK), bf16)],
        ),
        compiler_params=pltpu.CompilerParams(dimension_semantics=("arbitrary",), vmem_limit_bytes=60 << 20),
        cost_estimate=pl.CostEstimate(flops=subs * 13 * 10**9, bytes_accessed=5 << 20, transcendentals=0),
        name="attn_fwd",
    )(bounds, qkvt, qkvt, qkvt)


def parts3(x):
    hi = x.astype(bf16)
    r = x - hi.astype(f32)
    mid = r.astype(bf16)
    lo = (r - mid.astype(f32)).astype(bf16)
    return hi, mid, lo

def bwd_kernel(meta, scale_ref, q_ref, k_ref, v_ref, do_ref, o_ref, lse_ref, out_ref, kp, vp, qt, dot, dkt, dvt, dqt):
    b1, b2 = meta[0], meta[1]
    row16 = lax.broadcasted_iota(jnp.int32, (16, 128), 0)
    ones3 = (row16 < 3).astype(bf16)
    pad = jnp.zeros((32, 128), bf16)
    scale = scale_ref[...]

    def tail(x):
        hi, mid, lo = parts3(-x)
        rest = jnp.where(row16 == 1, mid.astype(f32), jnp.where(row16 == 2, lo.astype(f32), 0.0))
        return jnp.where(row16 == 0, hi.astype(f32), rest).astype(bf16)

    @pl.loop(0, 2 * PARTS)
    def _(step):
        chunk = step // 2
        for t in range(3):
            off = pl.multiple_of((step % 2) * HALF + t * 128, 128)
            sl, here = pl.ds(pl.multiple_of(chunk * ROWS + off, 128), 128), pl.ds(off, 128)
            for h in range(NH):
                own = slice(h * HD, (h + 1) * HD)
                do, o = do_ref[chunk, own, here], o_ref[chunk, own, here]
                delta = jnp.sum(do.astype(f32) * o.astype(f32), axis=0, keepdims=True)
                qt[h, :, sl] = jnp.concatenate([q_ref[own, sl], tail(lse_ref[h, chunk, :, here]), pad], axis=0)
                dot[h, :, sl] = jnp.concatenate([do, tail(delta), pad], axis=0)
                kp[h, sl, :] = jnp.concatenate([k_ref[own, sl], ones3, pad], axis=0).T
                vp[h, sl, :] = jnp.concatenate([v_ref[own, sl], ones3, pad], axis=0).T

    dkt[...] = jnp.zeros_like(dkt)
    dvt[...] = jnp.zeros_like(dvt)
    dqt[...] = jnp.zeros_like(dqt)

    def block(k0, q0, kw, qw, masked):
        k0, q0 = pl.multiple_of(k0, B), pl.multiple_of(q0, B)
        ks, qs = pl.ds(k0, kw), pl.ds(q0, qw)
        if masked:
            qpos = q0 + lax.broadcasted_iota(jnp.int32, (1, qw), 1)
            kpos = k0 + lax.broadcasted_iota(jnp.int32, (kw, qw), 0)
            ok = (kpos >= start_row(qpos, b1, b2)) & (kpos <= qpos)
        for h in range(NH):
            p = jnp.exp(nn(kp[h, ks, :], qt[h, :, qs]))
            if masked:
                p = jnp.where(ok, p, 0.0)
            ds = (p * nn(vp[h, ks, :], dot[h, :, qs])).astype(bf16)
            dvt[h, :, ks] += nt(dot[h, 0:HD, qs], p.astype(bf16))
            dkt[h, :, ks] += nt(qt[h, 0:HD, qs], ds)
            dqt[h, :, qs] += nn(k_ref[h * HD : (h + 1) * HD, ks], ds)

    @pl.loop(0, 12)
    def _(n):
        qb = jnp.where(n < 9, 3 + n // 3, jnp.where(n == 9, 1, 2))
        kb = jnp.where(n < 9, n % 3, jnp.where(n == 11, 1, 0))
        block(kb * FW, qb * FW, FW, FW, False)

    @pl.loop(0, TOK // FW)
    def _(i):
        lo = jnp.where(i < PROMPT // FW, i, first_block(i * (FW // B), b1, b2) * B // FW)

        @pl.loop(lo, i + 1)
        def _(j):
            block(j * FW, i * FW, FW, FW, True)

    @pl.loop(0, 2 * PARTS)
    def _(step):
        chunk = step // 2
        off = pl.multiple_of((step % 2) * HALF, 128)
        sl, here = pl.ds(pl.multiple_of(chunk * ROWS + off, 128), HALF), pl.ds(off, HALF)
        for h in range(NH):
            own = slice(h * HD, (h + 1) * HD)
            dq = dqt[h, :, sl].astype(bf16).astype(f32) * scale
            out_ref[chunk, 0, own, here] = dq.astype(bf16)
            out_ref[chunk, 1, own, here] = dkt[h, :, sl].astype(bf16)
            out_ref[chunk, 2, own, here] = dvt[h, :, sl].astype(bf16)


def attn_bwd(meta, scale, qkvt, grad, mixture, logsum, pair):
    steps = PH // NH
    rows = lambda a: pl.BlockSpec((NH * HD, TOK), lambda i, b: (steps * (2 * a + pair) + i, 0))
    return pl.pallas_call(
        bwd_kernel,
        out_shape=jax.ShapeDtypeStruct((PARTS, 3, PW, ROWS), bf16),
        grid_spec=pltpu.PrefetchScalarGridSpec(
            num_scalar_prefetch=1,
            grid=(steps,),
            in_specs=[
                pl.BlockSpec((HD, 1), lambda i, b: (0, 0)),
                rows(0),
                rows(1),
                rows(2),
                pl.BlockSpec((PARTS, NH * HD, ROWS), lambda i, b: (0, i, 0)),
                pl.BlockSpec((PARTS, NH * HD, ROWS), lambda i, b: (0, steps * pair + i, 0)),
                pl.BlockSpec((NH, PARTS, 1, ROWS), lambda i, b: (steps * pair + i, 0, 0, 0)),
            ],
            out_specs=pl.BlockSpec((PARTS, 3, NH * HD, ROWS), lambda i, b: (0, 0, i, 0)),
            scratch_shapes=[pltpu.VMEM((NH, TOK, 128), bf16)] * 2
            + [pltpu.VMEM((NH, 128, TOK), bf16)] * 2
            + [pltpu.VMEM((NH, HD, TOK), f32)] * 3,
        ),
        compiler_params=pltpu.CompilerParams(dimension_semantics=("arbitrary",), vmem_limit_bytes=60 << 20),
        cost_estimate=pl.CostEstimate(flops=36 * 10**9, bytes_accessed=16 << 20, transcendentals=0),
        name="attn_bwd",
    )(meta, scale, qkvt, qkvt, qkvt, grad, mixture, logsum)


def mlp_kernel(meta, head_ref, tail_ref, rows_ref, cot_ref, gain_ref, out_ref, up_ref, down_ref, fd_ref, fu_ref,
               hidden_ref, inner_ref, middle_ref, grad_ref, g0_ref, g1_ref, terms_ref, mixed, sums):
    step = pl.program_id(0)

    @pl.when(step == 0)
    def _():
        sums[...] = jnp.zeros_like(sums)

    @pl.when(step < 2)
    def _():
        mixed[...] = head_ref[...]

    @pl.when(step == 2)
    def _():
        mixed[...] = tail_ref[...]

    pos = meta[6] * ROWS + step * B + lax.broadcasted_iota(jnp.int32, (B, AR), 0)
    chosen = lax.broadcasted_iota(jnp.int32, (B, AR), 1) // RANK == token_adapter(pos, meta)
    choose = lambda x: jnp.where(chosen, x, 0.0).astype(bf16)
    gain = gain_ref[...]

    middle = rows_ref[...].astype(f32) + nn(mixed[...].T, out_ref[...])
    middle_ref[...] = middle
    q = lax.rsqrt(jnp.mean(middle * middle, axis=1, keepdims=True) + EPSILON)
    normed = (middle * q * gain).astype(bf16)
    inner_up = choose(nn(normed, fd_ref[0]))
    before = nn(normed, up_ref[...]) + nn(inner_up, fu_ref[0])
    gate = jax.nn.sigmoid(before)
    hidden = (before * gate).astype(bf16)
    hidden_ref[...] = hidden
    inner_down = choose(nn(hidden, fd_ref[1]))
    inner_ref[...] = inner_down

    after = cot_ref[...]
    spread_down = choose(nt(after, fu_ref[1]))
    grad_hidden = nt(after, down_ref[...]) + nt(spread_down, fd_ref[1])
    grad_before = (grad_hidden * gate * (1.0 + before * (1.0 - gate))).astype(bf16)
    spread_up = choose(nt(grad_before, fu_ref[0]))
    weighted = gain * (nt(grad_before, up_ref[...]) + nt(spread_up, fd_ref[0]))
    middle = middle_ref[...]
    inside = jnp.mean(middle * weighted, axis=1, keepdims=True)
    grad_middle = after.astype(f32) + (q * weighted - middle * (q * q * q * inside))
    grad_ref[...] = grad_middle
    grad_mixed = nt(out_ref[...], grad_middle.astype(bf16)).astype(bf16)
    for s in range(PARTS):
        g0_ref[s] = grad_mixed[2 * s * PW : (2 * s + 1) * PW]
        g1_ref[s] = grad_mixed[(2 * s + 1) * PW : (2 * s + 2) * PW]

    for n, (a, b) in enumerate(((spread_up, normed), (spread_down, hidden), (inner_up, grad_before), (inner_down, after))):
        sums[n] += nn(a.T, b)

    @pl.when(step == 2)
    def _():
        for n in range(4):
            terms_ref[n * AR : (n + 1) * AR, :] = sums[n].astype(bf16)


def mlp(meta, mixed_head, mixed_tail, rows, cotangent, gain, w_out, w_up, w_down, flat_down, flat_up):
    whole = lambda shape: pl.BlockSpec(shape, lambda i, m: (0,) * len(shape))
    block = pl.BlockSpec((B, D), lambda i, m: (i, 0))
    pair = pl.BlockSpec((PARTS, PW, B), lambda i, m: (0, 0, i))
    return pl.pallas_call(
        mlp_kernel,
        out_shape=[
            jax.ShapeDtypeStruct((ROWS, D), bf16),
            jax.ShapeDtypeStruct((ROWS, AR), bf16),
            jax.ShapeDtypeStruct((ROWS, D), f32),
            jax.ShapeDtypeStruct((ROWS, D), f32),
            jax.ShapeDtypeStruct((PARTS, PW, ROWS), bf16),
            jax.ShapeDtypeStruct((PARTS, PW, ROWS), bf16),
            jax.ShapeDtypeStruct((4 * AR, D), bf16),
        ],
        grid_spec=pltpu.PrefetchScalarGridSpec(
            num_scalar_prefetch=1,
            grid=(ROWS // B,),
            in_specs=[
                pl.BlockSpec((D, B), lambda i, m: (0, jnp.minimum(i, 1))),
                whole((D, B)),
                block,
                block,
                whole((1, D)),
                whole((D, D)),
                whole((D, D)),
                whole((D, D)),
                whole((2, D, AR)),
                whole((2, AR, D)),
            ],
            out_specs=[block, pl.BlockSpec((B, AR), lambda i, m: (i, 0)), block, block, pair, pair, whole((4 * AR, D))],
            scratch_shapes=[pltpu.VMEM((D, B), bf16), pltpu.VMEM((4, AR, D), f32)],
        ),
        compiler_params=pltpu.CompilerParams(dimension_semantics=("arbitrary",), vmem_limit_bytes=60 << 20),
        cost_estimate=pl.CostEstimate(flops=17 * 10**9, bytes_accessed=32 << 20, transcendentals=0),
        name="mlp",
    )(meta, mixed_head, mixed_tail, rows, cotangent, gain, w_out, w_up, w_down, flat_down, flat_up)


def exchange(value):
    return lax.all_to_all(value, "heads", split_axis=0, concat_axis=0, tiled=True)


def swap(value, axis, mask):
    count = lax.axis_size(axis)
    return lax.ppermute(value, axis, [(i, i ^ mask) for i in range(count)])


def piece(value, index, count):
    rows = value.shape[-2] // count
    return lax.dynamic_slice_in_dim(value, index * rows, rows, axis=value.ndim - 2)


def sum_low(*terms):
    total = terms[0].astype(f32)
    for term in terms[1:]:
        total = total + term.astype(f32)
    return total.astype(bf16)


def far_bits():
    bits = [2]
    while bits[-1] * 2 < lax.axis_size("fsdp"):
        bits.append(bits[-1] * 2)
    return bits


def sum_far(value):
    bits = far_bits()
    for bit, twice in zip(bits[0::2], bits[1::2]):
        value = sum_low(value, *[swap(value, "fsdp", m) for m in (bit, twice, bit | twice)])
    if len(bits) % 2:
        value = sum_low(value, swap(value, "fsdp", bits[-1]))
    return value


def scatter_near(value):
    core = lax.axis_index("fsdp") & 1
    return sum_low(piece(value, core, 2), swap(piece(value, 1 - core, 2), "fsdp", 1))


def scatter_heads(value):
    part = lax.axis_index("heads")
    terms = [swap(piece(value, part ^ m, PARTS), "heads", m) for m in (1, 2, 3)]
    return sum_low(piece(value, part, PARTS), *terms)


def body(
    inputs,
    cotangent,
    lengths,
    adapter_ids,
    query_weight,
    key_weight,
    value_weight,
    out_weight,
    up_weight,
    down_weight,
    attn_gain,
    mlp_gain,
    query_scale,
    adapter_in,
    adapter_out,
):
    part = lax.axis_index("heads")
    rows = inputs[0]
    low, high = rows[:HALF], rows[HALF:]
    near_high = swap(high, "heads", 1)
    far_low = swap(low, "heads", 2)
    ends = PROMPT + jnp.cumsum(lengths[0])
    bounds = ends[:2].astype(jnp.int32)
    ids = adapter_ids[0]
    core = lax.axis_index("fsdp") & 1
    meta = jnp.concatenate([bounds, ids, jnp.stack([part, core]).astype(jnp.int32)])
    flat_down = jnp.transpose(adapter_in, (0, 2, 1, 3)).reshape(4, D, AR)
    flat_up = adapter_out.reshape(4, AR, D)
    gain_attn = attn_gain.astype(f32)
    gain_mlp = mlp_gain.astype(f32)

    def mine(weight):
        return lax.dynamic_slice_in_dim(weight, part * WIDTH, WIDTH, axis=1)

    weights_mine = jnp.concatenate([mine(query_weight), mine(key_weight), mine(value_weight)], axis=1)
    weights_mine = lax.all_gather(weights_mine, "fsdp", axis=0, tiled=True)
    w_out = lax.all_gather(out_weight, "fsdp", axis=0, tiled=True)
    w_up = lax.all_gather(up_weight, "fsdp", axis=0, tiled=True)
    w_down = lax.all_gather(down_weight, "fsdp", axis=0, tiled=True)
    weights_all = lax.all_gather(jnp.concatenate([query_weight, key_weight, value_weight], axis=1), "fsdp", axis=0, tiled=True)

    down_pair = jnp.concatenate([flat_down[0], flat_down[1]], axis=1)
    up_mine = lax.dynamic_slice_in_dim(flat_up[:2], part * WIDTH, WIDTH, axis=2)
    low_late, high_late, down_pair = lax.optimization_barrier((low, high, down_pair))
    near_low = swap(low_late, "heads", 1)
    far_high = swap(high_late, "heads", 2)
    both_low = swap(far_low, "heads", 1)
    both_high = swap(near_high, "heads", 2)
    scale_row = query_scale * HD ** (-0.5)
    scale_mine = jnp.tile(scale_row, LH)[:, None]

    wt, ut = weights_mine.T, jnp.transpose(up_mine, (0, 2, 1))
    done = ()
    for m, low, high in ((0, rows, None), (1, near_low, near_high), (2, far_low, far_high), (3, both_low, both_high)):
        done = qkv_project(meta, part ^ m, low, high, gain_attn[None, :], wt, down_pair, ut, scale_mine, done)
    qkvt, normed_all, inner_all = done
    head_mix, head_log = attn_fwd(bounds, qkvt, 2)
    mixed_head = exchange(head_mix)
    later, head_log = lax.optimization_barrier((bounds, head_log))
    tail_mix, tail_log = attn_fwd(later, qkvt, 1)
    tail_sent, mixed_head = lax.optimization_barrier((tail_mix, mixed_head))
    mixed_tail = exchange(tail_sent)
    mixture = jnp.concatenate([head_mix, tail_mix], axis=2)
    logsum = jnp.concatenate([head_log, tail_log], axis=3)

    hidden_low, inner_down, middle, grad_middle, grad_first_heads, grad_second_heads, terms = mlp(
        meta, mixed_head.reshape(D, -1), mixed_tail.reshape(D, -1), rows, cotangent[0], gain_mlp[None, :],
        w_out, w_up, w_down, flat_down[2:], flat_up[2:],
    )
    grad_heads = [exchange(grad_first_heads), exchange(grad_second_heads)]

    mlp_total = scatter_near(terms)
    mlp_total, grad_heads[0] = lax.optimization_barrier((mlp_total, grad_heads[0]))
    mlp_total = scatter_heads(mlp_total)
    grad_first_pair = attn_bwd(meta, scale_row[:, None], qkvt, grad_heads[0], mixture, logsum, 0)
    mlp_total, grad_first_pair = lax.optimization_barrier((mlp_total, grad_first_pair))
    arrived = [exchange(grad_first_pair.reshape(PARTS, 3 * PW, ROWS))]
    mlp_total = sum_far(mlp_total)
    meta, _ = lax.optimization_barrier((meta, grad_first_pair))
    grad_second_pair = attn_bwd(meta, scale_row[:, None], qkvt, grad_heads[1], mixture, logsum, 1)
    mlp_total, grad_second_pair = lax.optimization_barrier((mlp_total, grad_second_pair))
    arrived.append(exchange(grad_second_pair.reshape(PARTS, 3 * PW, ROWS)))

    meta, arrived[0] = lax.optimization_barrier((meta, arrived[0]))
    keep, send = adapter_grads(meta, [grad_first_pair, grad_second_pair], normed_all, inner_all, up_mine)
    hidden_late, inner_late, keep = lax.optimization_barrier((hidden_low, inner_down, keep))
    outputs = (middle + (nn(hidden_late, w_down) + nn(inner_late, flat_up[3]))).astype(bf16)
    total = sum_low(keep, swap(send, "fsdp", 1))
    total = jnp.concatenate([scatter_heads(total[:AR]), total[AR:]])
    total, arrived, outputs = lax.optimization_barrier((total, arrived, outputs))
    total = sum_far(total)
    meta, total = lax.optimization_barrier((meta, total))
    own = jnp.concatenate([total, mlp_total])
    pieces = [own] + [swap(own, "heads", m) for m in (1, 2, 3)]
    arrived = [a.reshape(PARTS, 3, PW, ROWS) for a in arrived]
    grad_inputs = back_inputs(meta, arrived, weights_all, flat_up[:2], down_pair, rows, gain_attn[None, :], grad_middle)
    pieces, grad_inputs = lax.optimization_barrier((pieces, grad_inputs))
    own = jnp.stack(pieces)
    grad_first, grad_second = assemble(meta, own, swap(own, "fsdp", 1))
    grad_first = jnp.transpose(grad_first.reshape(4, ADAPTERS, RANK, D), (0, 1, 3, 2))
    grad_second = grad_second.reshape(4, ADAPTERS, RANK, D)
    return (outputs[None], grad_inputs[None], grad_first, grad_second)


def solution(mesh):
    placed = (
        P("fsdp", "heads", None),
        P("fsdp", "heads", None),
        P("fsdp", None),
        P("fsdp", None),
        P("fsdp", None),
        P("fsdp", None),
        P("fsdp", None),
        P("fsdp", None),
        P("fsdp", None),
        P("fsdp", None),
        P(),
        P(),
        P(),
        P(),
        P(),
    )
    return jax.shard_map(
        body,
        mesh=mesh,
        in_specs=placed,
        out_specs=(P("fsdp", "heads", None), P("fsdp", "heads", None), P(), P()),
        check_vma=False,
    )
```

```python
import jax
import jax.numpy as jnp
from jax import lax
from jax.experimental import pallas as pl
from jax.experimental.pallas import tpu as pltpu
from jax.sharding import PartitionSpec as P

D = 1280
HEADS = 16
HD = 80
RANK = 16
ADAPTERS = 8
AR = ADAPTERS * RANK
TOK = 3072
PROMPT = 1536
ROWS = 768
QB = 256
PARTS = TOK // ROWS
LH = HEADS // PARTS
HALF = ROWS // 2
PH = LH // 2
PW = PH * HD
WIDTH = LH * HD
SR = WIDTH * 128 // D
EPSILON = 1e-06
B = 256
f32, bf16 = jnp.float32, jnp.bfloat16


def nt(a, b):
    return lax.dot_general(a, b, (((1,), (1,)), ((), ())), preferred_element_type=f32)


def tn(a, b):
    return lax.dot_general(a, b, (((0,), (0,)), ((), ())), preferred_element_type=f32)


def nn(a, b):
    return lax.dot_general(a, b, (((1,), (0,)), ((), ())), preferred_element_type=f32)

def start_row(qpos, b1, b2):
    return jnp.where(qpos < PROMPT, 0, jnp.where(qpos < b1, PROMPT, jnp.where(qpos < b2, b1, b2)))

def first_block(i, b1, b2):
    q0 = i * B
    return jnp.where(q0 < b1, PROMPT, jnp.where(q0 < b2, b1, b2)) // B


def token_adapter(pos, meta):
    return jnp.where(
        pos < PROMPT, meta[2], jnp.where(pos < meta[0], meta[3], jnp.where(pos < meta[1], meta[4], meta[5]))
    )


def qkv_kernel(meta, first, low_ref, high_ref, gain_ref, wt_ref, down_ref, up_ref, scale_ref, *refs):
    out_ref, normed_ref, inner_ref, rows = refs[-4:]
    step = pl.program_id(0)

    @pl.when(step == 0)
    def _():
        rows[0:HALF, :] = low_ref[...]
        rows[HALF:ROWS, :] = high_ref[...]

    x = rows[pl.ds(pl.multiple_of(step * QB, QB), QB), :].astype(f32)
    q = lax.rsqrt(jnp.mean(x * x, axis=1, keepdims=True) + EPSILON)
    normed = (x * q * gain_ref[...]).astype(bf16)
    normed_ref[...] = normed
    pos = (first[0] + step) * QB + lax.broadcasted_iota(jnp.int32, (QB, 1), 0)
    lane = lax.broadcasted_iota(jnp.int32, (QB, 2 * AR), 1)
    chosen = (lane % AR) // RANK == token_adapter(pos, meta)
    inner = jnp.where(chosen, nn(normed, down_ref[...]), 0.0).astype(bf16)
    inner_ref[...] = inner
    out = nt(wt_ref[...], normed)
    query = out[:WIDTH] + nt(up_ref[0], inner[:, :AR])
    out_ref[0:WIDTH, :] = (query * scale_ref[...]).astype(bf16)
    out_ref[WIDTH : 2 * WIDTH, :] = out[WIDTH : 2 * WIDTH].astype(bf16)
    out_ref[2 * WIDTH :, :] = (out[2 * WIDTH :] + nt(up_ref[1], inner[:, AR:])).astype(bf16)


def qkv_project(meta, chunk, low, high, gain, wt, down, up, scale, done):
    whole = lambda shape: pl.BlockSpec(shape, lambda i, *_: (0, 0))
    second = 1 if high is None else 0
    first = (chunk * (ROWS // QB))[None].astype(jnp.int32)
    return pl.pallas_call(
        qkv_kernel,
        out_shape=(
            jax.ShapeDtypeStruct((3 * WIDTH, TOK), bf16),
            jax.ShapeDtypeStruct((TOK, D), bf16),
            jax.ShapeDtypeStruct((TOK, 2 * AR), bf16),
        ),
        grid_spec=pltpu.PrefetchScalarGridSpec(
            num_scalar_prefetch=2,
            grid=(ROWS // QB,),
            in_specs=[
                whole((HALF, D)),
                pl.BlockSpec((HALF, D), lambda i, *_: (second, 0)),
                whole((1, D)),
                whole((3 * WIDTH, D)),
                whole((D, 2 * AR)),
                pl.BlockSpec((2, WIDTH, AR), lambda i, *_: (0, 0, 0)),
                whole((WIDTH, 1)),
            ]
            + [pl.BlockSpec(memory_space=pl.ANY)] * len(done),
            out_specs=[
                pl.BlockSpec((3 * WIDTH, QB), lambda i, m, first: (0, first[0] + i)),
                pl.BlockSpec((QB, D), lambda i, m, first: (first[0] + i, 0)),
                pl.BlockSpec((QB, 2 * AR), lambda i, m, first: (first[0] + i, 0)),
            ],
            scratch_shapes=[pltpu.VMEM((ROWS, D), bf16)],
        ),
        input_output_aliases={9 + i: i for i in range(len(done))},
        compiler_params=pltpu.CompilerParams(dimension_semantics=("arbitrary",), vmem_limit_bytes=60 << 20),
        cost_estimate=pl.CostEstimate(flops=2 * ROWS * D * (3 * WIDTH + 2 * AR), bytes_accessed=8 << 20, transcendentals=0),
        name="qkv_project",
    )(meta, first, low, low if high is None else high, gain, wt, down, up, scale, *done)


def adapter_kernel(meta, *refs):
    grad_refs, (normed_ref, inner_ref, up_ref, keep_ref, send_ref, facc, sacc) = refs[:-7], refs[-7:]
    step = pl.program_id(0)

    @pl.when(step == 0)
    def _():
        facc[...] = jnp.zeros_like(facc)
        sacc[...] = jnp.zeros_like(sacc)

    query = jnp.concatenate([ref[0, 0] for ref in grad_refs], axis=0)
    value = jnp.concatenate([ref[0, 2] for ref in grad_refs], axis=0)
    pos = step * ROWS + lax.broadcasted_iota(jnp.int32, (1, ROWS), 1)
    rank = lax.broadcasted_iota(jnp.int32, (AR, ROWS), 0)
    chosen = rank // RANK == token_adapter(pos, meta)
    for a, grad in enumerate((query, value)):
        spread = jnp.where(chosen, nn(up_ref[a], grad), 0.0).astype(bf16)
        facc[a] += nn(spread, normed_ref[...])
        sacc[a] += nn(grad, inner_ref[:, a * AR : (a + 1) * AR])

    @pl.when(step == PARTS - 1)
    def _():
        for ref, a in ((keep_ref, meta[7]), (send_ref, 1 - meta[7])):
            ref[0:AR, :] = facc[a].astype(bf16)
            for c in range(D // 128):
                ref[AR : AR + SR, c * 128 : (c + 1) * 128] = sacc[a, c * SR : (c + 1) * SR, :].astype(bf16)


def adapter_grads(meta, grads, normed, inner, up):
    return pl.pallas_call(
        adapter_kernel,
        out_shape=[jax.ShapeDtypeStruct((AR + SR, D), bf16)] * 2,
        grid_spec=pltpu.PrefetchScalarGridSpec(
            num_scalar_prefetch=1,
            grid=(PARTS,),
            in_specs=[pl.BlockSpec((1,) + g.shape[1:], lambda i, m: (i, 0, 0, 0)) for g in grads]
            + [
                pl.BlockSpec((ROWS, D), lambda i, m: (i, 0)),
                pl.BlockSpec((ROWS, 2 * AR), lambda i, m: (i, 0)),
                pl.BlockSpec((2, AR, WIDTH), lambda i, m: (0, 0, 0)),
            ],
            out_specs=[pl.BlockSpec((AR + SR, D), lambda i, m: (0, 0))] * 2,
            scratch_shapes=[pltpu.VMEM((2, AR, D), f32), pltpu.VMEM((2, WIDTH, AR), f32)],
        ),
        compiler_params=pltpu.CompilerParams(dimension_semantics=("arbitrary",), vmem_limit_bytes=60 << 20),
        cost_estimate=pl.CostEstimate(flops=4 * TOK * D * 2 * AR, bytes_accessed=20 << 20, transcendentals=0),
        name="adapter_grads",
    )(meta, *grads, normed, inner, up)


def back_kernel(meta, *refs):
    grad_refs, rest = refs[:-10], refs[-10:]
    w_ref, up_ref, down_ref, rows_ref, gain_ref, middle_ref, out_ref, cols, total, spread = rest
    step = pl.program_id(0)
    for s in range(PARTS):
        r = s * WIDTH
        for ref in grad_refs:
            cols[r : r + ref.shape[2], :] = ref[s, 0]
            r += ref.shape[2]

    part_sum = nn(w_ref[...], cols[...])

    @pl.when(step == 0)
    def _():
        total[...] = part_sum
        spread[0] = nn(up_ref[0], cols[...])

    @pl.when(step > 0)
    def _():
        total[...] += part_sum

    @pl.when(step == 2)
    def _():
        spread[1] = nn(up_ref[1], cols[...])
        pos = meta[6] * ROWS + lax.broadcasted_iota(jnp.int32, (1, ROWS), 1)
        rank = lax.broadcasted_iota(jnp.int32, (AR, ROWS), 0)
        chosen = rank // RANK == token_adapter(pos, meta)
        both = jnp.concatenate([jnp.where(chosen, spread[a], 0.0).astype(bf16) for a in range(2)], axis=0)
        total[...] += nn(down_ref[...], both)
        gain = gain_ref[...]
        for t in range(ROWS // 128):
            own = slice(t * 128, (t + 1) * 128)
            x = rows_ref[own, :].astype(f32)
            q = lax.rsqrt(jnp.mean(x * x, axis=1, keepdims=True) + EPSILON)
            weighted = gain * total[:, own].T
            inside = jnp.mean(x * weighted, axis=1, keepdims=True)
            out_ref[own, :] = middle_ref[own, :] + (q * weighted - x * (q * q * q * inside))


def back_inputs(meta, arrived, weights, up, down, rows, gain, grad_middle):
    whole = lambda shape: pl.BlockSpec(shape, lambda i, m: (0,) * len(shape))
    return pl.pallas_call(
        back_kernel,
        out_shape=jax.ShapeDtypeStruct((ROWS, D), f32),
        grid_spec=pltpu.PrefetchScalarGridSpec(
            num_scalar_prefetch=1,
            grid=(3,),
            in_specs=[pl.BlockSpec((PARTS, 1) + g.shape[2:], lambda i, m: (0, i, 0, 0)) for g in arrived]
            + [
                pl.BlockSpec((D, D), lambda i, m: (0, i)),
                whole((2, AR, D)),
                whole((D, 2 * AR)),
                whole((ROWS, D)),
                whole((1, D)),
                whole((ROWS, D)),
            ],
            out_specs=whole((ROWS, D)),
            scratch_shapes=[pltpu.VMEM((D, ROWS), bf16), pltpu.VMEM((D, ROWS), f32), pltpu.VMEM((2, AR, ROWS), f32)],
        ),
        compiler_params=pltpu.CompilerParams(dimension_semantics=("arbitrary",), vmem_limit_bytes=60 << 20),
        cost_estimate=pl.CostEstimate(flops=6 * ROWS * D * D, bytes_accessed=24 << 20, transcendentals=0),
        name="back_inputs",
    )(meta, *arrived, weights, up, down, rows, gain, grad_middle)


def assemble_kernel(meta, own_ref, other_ref, first_ref, second_ref, turned):
    part, core = meta[6], meta[7]
    for ref, a in ((own_ref, core), (other_ref, 1 - core)):
        for m in range(PARTS):
            where = part ^ m
            piece_rows = lambda n: pl.ds(pl.multiple_of(where * n, n), n)
            first_ref[a, piece_rows(SR), :] = ref[m, 0:SR, :].astype(f32)
            for c in range(D // 128):
                turned[pl.ds(pl.multiple_of(where * WIDTH + c * SR, SR), SR), :] = ref[m, SR : 2 * SR, c * 128 : (c + 1) * 128]
            rows = pl.ds(pl.multiple_of((where % 2) * 2 * SR, 2 * SR), 2 * SR)
            mlp = ref[m, 2 * SR :, :].astype(f32)

            @pl.when(a == 0)
            def _(mlp=mlp, rows=rows, where=where):
                first_ref[2 + where // 2, rows, :] = mlp

            @pl.when(a == 1)
            def _(mlp=mlp, rows=rows, where=where):
                second_ref[2 + where // 2, rows, :] = mlp

        for c in range(D // 128):
            second_ref[a, :, c * 128 : (c + 1) * 128] = turned[c * 128 : (c + 1) * 128, :].T.astype(f32)


def assemble(meta, own, other):
    whole = lambda shape: pl.BlockSpec(shape, lambda i, m: (0,) * len(shape))
    return pl.pallas_call(
        assemble_kernel,
        out_shape=[jax.ShapeDtypeStruct((4, AR, D), f32)] * 2,
        grid_spec=pltpu.PrefetchScalarGridSpec(
            num_scalar_prefetch=1,
            grid=(1,),
            in_specs=[whole((PARTS, 4 * SR, D))] * 2,
            out_specs=[whole((4, AR, D))] * 2,
            scratch_shapes=[pltpu.VMEM((D, AR), bf16)],
        ),
        compiler_params=pltpu.CompilerParams(dimension_semantics=("arbitrary",), vmem_limit_bytes=60 << 20),
        cost_estimate=pl.CostEstimate(flops=1 << 20, bytes_accessed=8 << 20, transcendentals=0),
        name="assemble",
    )(meta, own, other)


HPB = LH
BLOCKS = ROWS // B
NEG = -1e30
FW = 512


def fwd_kernel(bounds, q_ref, k_ref, v_ref, o_ref, lse_ref, kp, qt, vt):
    b1, b2 = bounds[0], bounds[1]
    zpad = jnp.zeros((128 - HD, 128), bf16)
    for h in range(HPB):
        own = slice(h * HD, (h + 1) * HD)
        qt[h, 0:HD, :] = q_ref[own, :]
        qt[h, HD:128, :] = jnp.zeros((128 - HD, TOK), bf16)
        vt[h, 0:HD, :] = v_ref[own, :]
        vt[h, HD:96, :] = (lax.broadcasted_iota(jnp.int32, (16, TOK), 0) == 0).astype(bf16)
        for t in range(TOK // 128):
            kt = k_ref[own, t * 128:(t + 1) * 128]
            kp[h, t * 128:(t + 1) * 128, :] = jnp.concatenate([kt, zpad], axis=0).T

    subs = o_ref.shape[2] // B
    base = 0 if subs > 1 else BLOCKS - 1

    def qblock(n, _):
        chunk, sub = n // subs, n % subs
        i = chunk * BLOCKS + base + sub
        q0 = pl.multiple_of(i * B, B)
        here = pl.ds(pl.multiple_of(sub * B, B), B)
        qpos = q0 + lax.broadcasted_iota(jnp.int32, (1, B), 1)
        srow = start_row(qpos, b1, b2)

        def step(k0, width, masked, carry):
            ks = pl.ds(k0, width)
            ss = [nn(kp[h, ks, :], qt[h, :, pl.ds(q0, B)]) for h in range(HPB)]
            if masked:
                kpos = k0 + lax.broadcasted_iota(jnp.int32, (width, B), 0)
                ok = (kpos >= srow) & (kpos <= qpos)
                ss = [jnp.where(ok, s, NEG) for s in ss]
            out = []
            for h in range(HPB):
                m, acc = carry[h]
                m_new = jnp.maximum(m, jnp.max(ss[h], axis=0, keepdims=True))
                p = jnp.exp(ss[h] - m_new).astype(bf16)
                a = jnp.exp(m - m_new)
                out.append((m_new, acc * a + nn(vt[h, :, ks], p)))
            return tuple(out)

        full = jnp.minimum(i * B // FW, PROMPT // FW)
        lo = jnp.where(i < PROMPT // B, (FW // B) * (i * B // FW), first_block(i, b1, b2))
        carry = tuple((jnp.full((1, B), NEG, f32), jnp.zeros((96, B), f32)) for _ in range(HPB))
        carry = lax.fori_loop(0, full, lambda j, c: step(pl.multiple_of(j * FW, FW), FW, False, c), carry)
        carry = lax.fori_loop(lo, i + 1, lambda j, c: step(pl.multiple_of(j * B, B), B, True, c), carry)
        for h in range(HPB):
            m, acc = carry[h]
            l = acc[HD:HD + 1, :]
            o_ref[chunk, h * HD:(h + 1) * HD, here] = (acc[0:HD, :] / l).astype(bf16)
            lse_ref[h, chunk, :, here] = m + jnp.log(l)
        return 0
    lax.fori_loop(0, PARTS * subs, qblock, 0)

def attn_fwd(bounds, qkvt, subs):
    rows = lambda a: pl.BlockSpec((WIDTH, TOK), lambda i, b: (a, 0))
    width = subs * B
    return pl.pallas_call(
        fwd_kernel,
        out_shape=(jax.ShapeDtypeStruct((PARTS, WIDTH, width), bf16), jax.ShapeDtypeStruct((LH, PARTS, 1, width), f32)),
        grid_spec=pltpu.PrefetchScalarGridSpec(
            num_scalar_prefetch=1,
            grid=(1,),
            in_specs=[rows(0), rows(1), rows(2)],
            out_specs=[
                pl.BlockSpec((PARTS, WIDTH, width), lambda i, b: (0, 0, 0)),
                pl.BlockSpec((LH, PARTS, 1, width), lambda i, b: (0, 0, 0, 0)),
            ],
            scratch_shapes=[pltpu.VMEM((HPB, TOK, 128), bf16), pltpu.VMEM((HPB, 128, TOK), bf16), pltpu.VMEM((HPB, 96, TOK), bf16)],
        ),
        compiler_params=pltpu.CompilerParams(dimension_semantics=("arbitrary",), vmem_limit_bytes=60 << 20),
        cost_estimate=pl.CostEstimate(flops=subs * 13 * 10**9, bytes_accessed=5 << 20, transcendentals=0),
        name="attn_fwd",
    )(bounds, qkvt, qkvt, qkvt)


def parts3(x):
    hi = x.astype(bf16)
    r = x - hi.astype(f32)
    mid = r.astype(bf16)
    lo = (r - mid.astype(f32)).astype(bf16)
    return hi, mid, lo

def bwd_kernel(meta, scale_ref, q_ref, k_ref, v_ref, do_ref, o_ref, lse_ref, out_ref, kp, vp, qt, dot, dkt, dvt, dqt):
    NH = kp.shape[0]
    b1, b2 = meta[0], meta[1]
    row16 = lax.broadcasted_iota(jnp.int32, (16, 128), 0)
    ones3 = (row16 < 3).astype(bf16)
    pad = jnp.zeros((32, 128), bf16)
    scale = scale_ref[...]

    def tail(x):
        hi, mid, lo = parts3(-x)
        rest = jnp.where(row16 == 1, mid.astype(f32), jnp.where(row16 == 2, lo.astype(f32), 0.0))
        return jnp.where(row16 == 0, hi.astype(f32), rest).astype(bf16)

    @pl.loop(0, 2 * PARTS)
    def _(step):
        chunk = step // 2
        for t in range(3):
            off = pl.multiple_of((step % 2) * HALF + t * 128, 128)
            sl, here = pl.ds(pl.multiple_of(chunk * ROWS + off, 128), 128), pl.ds(off, 128)
            for h in range(NH):
                own = slice(h * HD, (h + 1) * HD)
                do, o = do_ref[chunk, own, here], o_ref[chunk, own, here]
                delta = jnp.sum(do.astype(f32) * o.astype(f32), axis=0, keepdims=True)
                qt[h, :, sl] = jnp.concatenate([q_ref[own, sl], tail(lse_ref[h, chunk, :, here]), pad], axis=0)
                dot[h, :, sl] = jnp.concatenate([do, tail(delta), pad], axis=0)
                kp[h, sl, :] = jnp.concatenate([k_ref[own, sl], ones3, pad], axis=0).T
                vp[h, sl, :] = jnp.concatenate([v_ref[own, sl], ones3, pad], axis=0).T

    dkt[...] = jnp.zeros_like(dkt)
    dvt[...] = jnp.zeros_like(dvt)
    dqt[...] = jnp.zeros_like(dqt)

    def block(k0, q0, kw, qw, masked):
        k0, q0 = pl.multiple_of(k0, B), pl.multiple_of(q0, B)
        ks, qs = pl.ds(k0, kw), pl.ds(q0, qw)
        if masked:
            qpos = q0 + lax.broadcasted_iota(jnp.int32, (1, qw), 1)
            kpos = k0 + lax.broadcasted_iota(jnp.int32, (kw, qw), 0)
            ok = (kpos >= start_row(qpos, b1, b2)) & (kpos <= qpos)
        for h in range(NH):
            p = jnp.exp(nn(kp[h, ks, :], qt[h, :, qs]))
            if masked:
                p = jnp.where(ok, p, 0.0)
            ds = (p * nn(vp[h, ks, :], dot[h, :, qs])).astype(bf16)
            dvt[h, :, ks] += nt(dot[h, 0:HD, qs], p.astype(bf16))
            dkt[h, :, ks] += nt(qt[h, 0:HD, qs], ds)
            dqt[h, :, qs] += nn(k_ref[h * HD : (h + 1) * HD, ks], ds)

    @pl.loop(0, 12)
    def _(n):
        qb = jnp.where(n < 9, 3 + n // 3, jnp.where(n == 9, 1, 2))
        kb = jnp.where(n < 9, n % 3, jnp.where(n == 11, 1, 0))
        block(kb * FW, qb * FW, FW, FW, False)

    @pl.loop(0, TOK // FW)
    def _(i):
        lo = jnp.where(i < PROMPT // FW, i, first_block(i * (FW // B), b1, b2) * B // FW)

        @pl.loop(lo, i + 1)
        def _(j):
            block(j * FW, i * FW, FW, FW, True)

    @pl.loop(0, 2 * PARTS)
    def _(step):
        chunk = step // 2
        off = pl.multiple_of((step % 2) * HALF, 128)
        sl, here = pl.ds(pl.multiple_of(chunk * ROWS + off, 128), HALF), pl.ds(off, HALF)
        for h in range(NH):
            own = slice(h * HD, (h + 1) * HD)
            dq = dqt[h, :, sl].astype(bf16).astype(f32) * scale
            out_ref[chunk, 0, own, here] = dq.astype(bf16)
            out_ref[chunk, 1, own, here] = dkt[h, :, sl].astype(bf16)
            out_ref[chunk, 2, own, here] = dvt[h, :, sl].astype(bf16)


def attn_bwd(meta, scale, qkvt, grad, mixture, logsum, first, count, slot):
    rows = lambda a: pl.BlockSpec((count * HD, TOK), lambda i, b: ((LH * a + first) // count, 0))
    return pl.pallas_call(
        bwd_kernel,
        out_shape=jax.ShapeDtypeStruct((PARTS, 3, count * HD, ROWS), bf16),
        grid_spec=pltpu.PrefetchScalarGridSpec(
            num_scalar_prefetch=1,
            grid=(1,),
            in_specs=[
                pl.BlockSpec((HD, 1), lambda i, b: (0, 0)),
                rows(0),
                rows(1),
                rows(2),
                pl.BlockSpec((PARTS, count * HD, ROWS), lambda i, b: (0, slot // count, 0)),
                pl.BlockSpec((PARTS, count * HD, ROWS), lambda i, b: (0, first // count, 0)),
                pl.BlockSpec((count, PARTS, 1, ROWS), lambda i, b: (first // count, 0, 0, 0)),
            ],
            out_specs=pl.BlockSpec((PARTS, 3, count * HD, ROWS), lambda i, b: (0, 0, 0, 0)),
            scratch_shapes=[pltpu.VMEM((count, TOK, 128), bf16)] * 2
            + [pltpu.VMEM((count, 128, TOK), bf16)] * 2
            + [pltpu.VMEM((count, HD, TOK), f32)] * 3,
        ),
        compiler_params=pltpu.CompilerParams(dimension_semantics=("arbitrary",), vmem_limit_bytes=60 << 20),
        cost_estimate=pl.CostEstimate(flops=count * 18 * 10**9, bytes_accessed=count * 8 << 20, transcendentals=0),
        name="attn_bwd",
    )(meta, scale, qkvt, qkvt, qkvt, grad, mixture, logsum)


def mlp_kernel(meta, head_ref, tail_ref, rows_ref, cot_ref, gain_ref, out_ref, up_ref, down_ref, fd_ref, fu_ref,
               hidden_ref, inner_ref, middle_ref, grad_ref, g0_ref, g1_ref, keep_ref, send_ref, mixed, sums):
    step = pl.program_id(0)

    @pl.when(step == 0)
    def _():
        sums[...] = jnp.zeros_like(sums)

    @pl.when(step < 2)
    def _():
        mixed[...] = head_ref[...]

    @pl.when(step == 2)
    def _():
        mixed[...] = tail_ref[...]

    pos = meta[6] * ROWS + step * B + lax.broadcasted_iota(jnp.int32, (B, AR), 0)
    chosen = lax.broadcasted_iota(jnp.int32, (B, AR), 1) // RANK == token_adapter(pos, meta)
    choose = lambda x: jnp.where(chosen, x, 0.0).astype(bf16)
    gain = gain_ref[...]

    middle = rows_ref[...].astype(f32) + nn(mixed[...].T, out_ref[...])
    middle_ref[...] = middle
    q = lax.rsqrt(jnp.mean(middle * middle, axis=1, keepdims=True) + EPSILON)
    normed = (middle * q * gain).astype(bf16)
    inner_up = choose(nn(normed, fd_ref[0]))
    before = nn(normed, up_ref[...]) + nn(inner_up, fu_ref[0])
    gate = jax.nn.sigmoid(before)
    hidden = (before * gate).astype(bf16)
    hidden_ref[...] = hidden
    inner_down = choose(nn(hidden, fd_ref[1]))
    inner_ref[...] = inner_down

    after = cot_ref[...]
    spread_down = choose(nt(after, fu_ref[1]))
    grad_hidden = nt(after, down_ref[...]) + nt(spread_down, fd_ref[1])
    grad_before = (grad_hidden * gate * (1.0 + before * (1.0 - gate))).astype(bf16)
    spread_up = choose(nt(grad_before, fu_ref[0]))
    weighted = gain * (nt(grad_before, up_ref[...]) + nt(spread_up, fd_ref[0]))
    middle = middle_ref[...]
    inside = jnp.mean(middle * weighted, axis=1, keepdims=True)
    grad_middle = after.astype(f32) + (q * weighted - middle * (q * q * q * inside))
    grad_ref[...] = grad_middle
    grad_mixed = nt(out_ref[...], grad_middle.astype(bf16)).astype(bf16)
    for s in range(PARTS):
        g0_ref[s] = grad_mixed[2 * s * PW : (2 * s + 1) * PW]
        g1_ref[s] = grad_mixed[(2 * s + 1) * PW : (2 * s + 2) * PW]

    for n, (a, b) in enumerate(((spread_up, normed), (spread_down, hidden), (inner_up, grad_before), (inner_down, after))):
        sums[n] += nn(a.T, b)

    @pl.when(step == 2)
    def _():
        for ref, half in ((keep_ref, meta[7]), (send_ref, 1 - meta[7])):
            for n in range(2):
                ref[n * AR : (n + 1) * AR, :] = sums[2 * half + n].astype(bf16)


def mlp(meta, mixed_head, mixed_tail, rows, cotangent, gain, weights, flat_down, flat_up):
    whole = lambda shape: pl.BlockSpec(shape, lambda i, m: (0,) * len(shape))
    block = pl.BlockSpec((B, D), lambda i, m: (i, 0))
    pair = pl.BlockSpec((PARTS, PW, B), lambda i, m: (0, 0, i))
    return pl.pallas_call(
        mlp_kernel,
        out_shape=[
            jax.ShapeDtypeStruct((ROWS, D), bf16),
            jax.ShapeDtypeStruct((ROWS, AR), bf16),
            jax.ShapeDtypeStruct((ROWS, D), f32),
            jax.ShapeDtypeStruct((ROWS, D), f32),
            jax.ShapeDtypeStruct((PARTS, PW, ROWS), bf16),
            jax.ShapeDtypeStruct((PARTS, PW, ROWS), bf16),
            jax.ShapeDtypeStruct((2 * AR, D), bf16),
            jax.ShapeDtypeStruct((2 * AR, D), bf16),
        ],
        grid_spec=pltpu.PrefetchScalarGridSpec(
            num_scalar_prefetch=1,
            grid=(ROWS // B,),
            in_specs=[
                pl.BlockSpec((D, B), lambda i, m: (0, jnp.minimum(i, 1))),
                whole((D, B)),
                block,
                block,
                whole((1, D)),
                *[pl.BlockSpec((D, D), lambda i, m, a=a: (0, a)) for a in range(3)],
                whole((2, D, AR)),
                whole((2, AR, D)),
            ],
            out_specs=[block, pl.BlockSpec((B, AR), lambda i, m: (i, 0)), block, block, pair, pair] + [whole((2 * AR, D))] * 2,
            scratch_shapes=[pltpu.VMEM((D, B), bf16), pltpu.VMEM((4, AR, D), f32)],
        ),
        compiler_params=pltpu.CompilerParams(dimension_semantics=("arbitrary",), vmem_limit_bytes=60 << 20),
        cost_estimate=pl.CostEstimate(flops=17 * 10**9, bytes_accessed=32 << 20, transcendentals=0),
        name="mlp",
    )(meta, mixed_head, mixed_tail, rows, cotangent, gain, weights, weights, weights, flat_down, flat_up)


def exchange(value):
    return lax.all_to_all(value, "heads", split_axis=0, concat_axis=0, tiled=True)


def swap(value, axis, mask):
    count = lax.axis_size(axis)
    return lax.ppermute(value, axis, [(i, i ^ mask) for i in range(count)])


def piece(value, index, count):
    rows = value.shape[-2] // count
    return lax.dynamic_slice_in_dim(value, index * rows, rows, axis=value.ndim - 2)


def sum_low(*terms):
    total = terms[0].astype(f32)
    for term in terms[1:]:
        total = total + term.astype(f32)
    return total.astype(bf16)


def far_bits():
    bits = [2]
    while bits[-1] * 2 < lax.axis_size("fsdp"):
        bits.append(bits[-1] * 2)
    return bits


def sum_far(value):
    bits = far_bits()
    for bit, twice in zip(bits[0::2], bits[1::2]):
        value = sum_low(value, *[swap(value, "fsdp", m) for m in (bit, twice, bit | twice)])
    if len(bits) % 2:
        value = sum_low(value, swap(value, "fsdp", bits[-1]))
    return value


def scatter_near(value):
    core = lax.axis_index("fsdp") & 1
    return sum_low(piece(value, core, 2), swap(piece(value, 1 - core, 2), "fsdp", 1))


def scatter_heads(value):
    part = lax.axis_index("heads")
    terms = [swap(piece(value, part ^ m, PARTS), "heads", m) for m in (1, 2, 3)]
    return sum_low(piece(value, part, PARTS), *terms)


def body(
    inputs,
    cotangent,
    lengths,
    adapter_ids,
    query_weight,
    key_weight,
    value_weight,
    out_weight,
    up_weight,
    down_weight,
    attn_gain,
    mlp_gain,
    query_scale,
    adapter_in,
    adapter_out,
):
    part = lax.axis_index("heads")
    rows = inputs[0]
    low, high = rows[:HALF], rows[HALF:]
    near_high = swap(high, "heads", 1)
    far_low = swap(low, "heads", 2)
    ends = PROMPT + jnp.cumsum(lengths[0])
    bounds = ends[:2].astype(jnp.int32)
    ids = adapter_ids[0]
    core = lax.axis_index("fsdp") & 1
    meta = jnp.concatenate([bounds, ids, jnp.stack([part, core]).astype(jnp.int32)])
    flat_down = jnp.transpose(adapter_in, (0, 2, 1, 3)).reshape(4, D, AR)
    flat_up = adapter_out.reshape(4, AR, D)
    gain_attn = attn_gain.astype(f32)
    gain_mlp = mlp_gain.astype(f32)

    def mine(weight):
        return lax.dynamic_slice_in_dim(weight, part * WIDTH, WIDTH, axis=1)

    weights_mine = jnp.concatenate([mine(query_weight), mine(key_weight), mine(value_weight)], axis=1)
    weights_mine = lax.all_gather(weights_mine, "fsdp", axis=0, tiled=True)
    weights_mlp = lax.all_gather(jnp.concatenate([out_weight, up_weight, down_weight], axis=1), "fsdp", axis=0, tiled=True)
    weights_all = lax.all_gather(jnp.concatenate([query_weight, key_weight, value_weight], axis=1), "fsdp", axis=0, tiled=True)

    down_pair = jnp.concatenate([flat_down[0], flat_down[1]], axis=1)
    up_mine = lax.dynamic_slice_in_dim(flat_up[:2], part * WIDTH, WIDTH, axis=2)
    low_late, high_late, down_pair = lax.optimization_barrier((low, high, down_pair))
    near_low = swap(low_late, "heads", 1)
    far_high = swap(high_late, "heads", 2)
    both_low = swap(far_low, "heads", 1)
    both_high = swap(near_high, "heads", 2)
    scale_row = query_scale * HD ** (-0.5)
    scale_mine = jnp.tile(scale_row, LH)[:, None]

    wt, ut = weights_mine.T, jnp.transpose(up_mine, (0, 2, 1))
    done = ()
    for m, low, high in ((0, rows, None), (1, near_low, near_high), (2, far_low, far_high), (3, both_low, both_high)):
        done = qkv_project(meta, part ^ m, low, high, gain_attn[None, :], wt, down_pair, ut, scale_mine, done)
    qkvt, normed_all, inner_all = done
    head_mix, head_log = attn_fwd(bounds, qkvt, 2)
    mixed_head = exchange(head_mix)
    later, head_log = lax.optimization_barrier((bounds, head_log))
    tail_mix, tail_log = attn_fwd(later, qkvt, 1)
    tail_sent, mixed_head = lax.optimization_barrier((tail_mix, mixed_head))
    mixed_tail = exchange(tail_sent)
    mixture = jnp.concatenate([head_mix, tail_mix], axis=2)
    logsum = jnp.concatenate([head_log, tail_log], axis=3)
    mixture, logsum, up_mine, mixed_head = lax.optimization_barrier((mixture, logsum, up_mine, mixed_head))

    hidden_low, inner_down, middle, grad_middle, grad_first_heads, grad_second_heads, mlp_keep, mlp_send = mlp(
        meta, mixed_head.reshape(D, -1), mixed_tail.reshape(D, -1), rows, cotangent[0], gain_mlp[None, :],
        weights_mlp, flat_down[2:], flat_up[2:],
    )
    grad_heads = [exchange(grad_first_heads), exchange(grad_second_heads)]

    mlp_total = sum_low(mlp_keep, swap(mlp_send, "fsdp", 1))
    mlp_total, grad_heads[0] = lax.optimization_barrier((mlp_total, grad_heads[0]))
    mlp_total = scatter_heads(mlp_total)
    scale_column = scale_row[:, None]
    send_back = lambda g: exchange(g.reshape(PARTS, -1, ROWS)).reshape(g.shape)
    grads, arrived = [], []
    grads.append(attn_bwd(meta, scale_column, qkvt, grad_heads[0], mixture, logsum, 0, 2, 0))
    mlp_total, grads[0] = lax.optimization_barrier((mlp_total, grads[0]))
    arrived.append(send_back(grads[0]))
    mlp_total = sum_far(mlp_total)
    meta, grads[0] = lax.optimization_barrier((meta, grads[0]))
    grads.append(attn_bwd(meta, scale_column, qkvt, grad_heads[1], mixture, logsum, 2, 2, 0))
    mlp_total, grads[1] = lax.optimization_barrier((mlp_total, grads[1]))
    arrived.append(send_back(grads[1]))

    meta, arrived[0] = lax.optimization_barrier((meta, arrived[0]))
    keep, send = adapter_grads(meta, grads, normed_all, inner_all, up_mine)
    hidden_late, inner_late, keep = lax.optimization_barrier((hidden_low, inner_down, keep))
    outputs = (middle + (nn(hidden_late, weights_mlp[:, 2 * D :]) + nn(inner_late, flat_up[3]))).astype(bf16)
    total = sum_low(keep, swap(send, "fsdp", 1))
    total = jnp.concatenate([scatter_heads(total[:AR]), total[AR:]])
    total, arrived, outputs = lax.optimization_barrier((total, arrived, outputs))
    total = sum_far(total)
    meta, total = lax.optimization_barrier((meta, total))
    own = jnp.concatenate([total, mlp_total])
    pieces = [own] + [swap(own, "heads", m) for m in (1, 2, 3)]
    grad_inputs = back_inputs(meta, arrived, weights_all, flat_up[:2], down_pair, rows, gain_attn[None, :], grad_middle)
    pieces, grad_inputs = lax.optimization_barrier((pieces, grad_inputs))
    own = jnp.stack(pieces)
    grad_first, grad_second = assemble(meta, own, swap(own, "fsdp", 1))
    grad_first = jnp.transpose(grad_first.reshape(4, ADAPTERS, RANK, D), (0, 1, 3, 2))
    grad_second = grad_second.reshape(4, ADAPTERS, RANK, D)
    return (outputs[None], grad_inputs[None], grad_first, grad_second)


def solution(mesh):
    placed = (
        P("fsdp", "heads", None),
        P("fsdp", "heads", None),
        P("fsdp", None),
        P("fsdp", None),
        P("fsdp", None),
        P("fsdp", None),
        P("fsdp", None),
        P("fsdp", None),
        P("fsdp", None),
        P("fsdp", None),
        P(),
        P(),
        P(),
        P(),
        P(),
    )
    return jax.shard_map(
        body,
        mesh=mesh,
        in_specs=placed,
        out_specs=(P("fsdp", "heads", None), P("fsdp", "heads", None), P(), P()),
        check_vma=False,
    )
```

```python
import functools

import jax
import jax.numpy as jnp
from jax import lax
from jax.experimental import pallas as pl
from jax.experimental.pallas import tpu as pltpu
from jax.sharding import PartitionSpec as P

D = 1280
HEADS = 16
HD = 80
RANK = 16
ADAPTERS = 8
AR = ADAPTERS * RANK
TOK = 3072
PROMPT = 1536
ROWS = 768
QB = 256
PARTS = TOK // ROWS
LH = HEADS // PARTS
HALF = ROWS // 2
PH = LH // 2
PW = PH * HD
WIDTH = LH * HD
SR = WIDTH * 128 // D
EPSILON = 1e-06
B = 256
f32, bf16 = jnp.float32, jnp.bfloat16


def nt(a, b):
    return lax.dot_general(a, b, (((1,), (1,)), ((), ())), preferred_element_type=f32)


def tn(a, b):
    return lax.dot_general(a, b, (((0,), (0,)), ((), ())), preferred_element_type=f32)


def nn(a, b):
    return lax.dot_general(a, b, (((1,), (0,)), ((), ())), preferred_element_type=f32)

def start_row(qpos, b1, b2):
    return jnp.where(qpos < PROMPT, 0, jnp.where(qpos < b1, PROMPT, jnp.where(qpos < b2, b1, b2)))

def first_block(i, b1, b2):
    q0 = i * B
    return jnp.where(q0 < b1, PROMPT, jnp.where(q0 < b2, b1, b2)) // B


def token_adapter(pos, meta):
    return jnp.where(
        pos < PROMPT, meta[2], jnp.where(pos < meta[0], meta[3], jnp.where(pos < meta[1], meta[4], meta[5]))
    )


def qkv_kernel(meta, first, low_ref, high_ref, gain_ref, wt_ref, down_ref, up_ref, scale_ref, *refs):
    out_ref, normed_ref, inner_ref, rows = refs[-4:]
    step = pl.program_id(0)

    @pl.when(step == 0)
    def _():
        rows[0:HALF, :] = low_ref[...]
        rows[HALF:ROWS, :] = high_ref[...]

    x = rows[pl.ds(pl.multiple_of(step * QB, QB), QB), :].astype(f32)
    q = lax.rsqrt(jnp.mean(x * x, axis=1, keepdims=True) + EPSILON)
    normed = (x * q * gain_ref[...]).astype(bf16)
    normed_ref[...] = normed
    pos = (first[0] + step) * QB + lax.broadcasted_iota(jnp.int32, (QB, 1), 0)
    lane = lax.broadcasted_iota(jnp.int32, (QB, 2 * AR), 1)
    chosen = (lane % AR) // RANK == token_adapter(pos, meta)
    inner = jnp.where(chosen, nn(normed, down_ref[...]), 0.0).astype(bf16)
    inner_ref[...] = inner
    out = nt(wt_ref[...], normed)
    query = out[:WIDTH] + nt(up_ref[0], inner[:, :AR])
    out_ref[0:WIDTH, :] = (query * scale_ref[...]).astype(bf16)
    out_ref[WIDTH : 2 * WIDTH, :] = out[WIDTH : 2 * WIDTH].astype(bf16)
    out_ref[2 * WIDTH :, :] = (out[2 * WIDTH :] + nt(up_ref[1], inner[:, AR:])).astype(bf16)


def qkv_project(meta, chunk, low, high, gain, wt, down, up, scale, done):
    whole = lambda shape: pl.BlockSpec(shape, lambda i, *_: (0, 0))
    second = 1 if high is None else 0
    first = (chunk * (ROWS // QB))[None].astype(jnp.int32)
    return pl.pallas_call(
        qkv_kernel,
        out_shape=(
            jax.ShapeDtypeStruct((3 * WIDTH, TOK), bf16),
            jax.ShapeDtypeStruct((TOK, D), bf16),
            jax.ShapeDtypeStruct((TOK, 2 * AR), bf16),
        ),
        grid_spec=pltpu.PrefetchScalarGridSpec(
            num_scalar_prefetch=2,
            grid=(ROWS // QB,),
            in_specs=[
                whole((HALF, D)),
                pl.BlockSpec((HALF, D), lambda i, *_: (second, 0)),
                whole((1, D)),
                whole((3 * WIDTH, D)),
                whole((D, 2 * AR)),
                pl.BlockSpec((2, WIDTH, AR), lambda i, *_: (0, 0, 0)),
                whole((WIDTH, 1)),
            ]
            + [pl.BlockSpec(memory_space=pl.ANY)] * len(done),
            out_specs=[
                pl.BlockSpec((3 * WIDTH, QB), lambda i, m, first: (0, first[0] + i)),
                pl.BlockSpec((QB, D), lambda i, m, first: (first[0] + i, 0)),
                pl.BlockSpec((QB, 2 * AR), lambda i, m, first: (first[0] + i, 0)),
            ],
            scratch_shapes=[pltpu.VMEM((ROWS, D), bf16)],
        ),
        input_output_aliases={9 + i: i for i in range(len(done))},
        compiler_params=pltpu.CompilerParams(dimension_semantics=("arbitrary",), vmem_limit_bytes=60 << 20),
        cost_estimate=pl.CostEstimate(flops=2 * ROWS * D * (3 * WIDTH + 2 * AR), bytes_accessed=8 << 20, transcendentals=0),
        name="qkv_project",
    )(meta, first, low, low if high is None else high, gain, wt, down, up, scale, *done)


def adapter_kernel(meta, *refs):
    grad_refs, (normed_ref, inner_ref, up_ref, keep_ref, send_ref, facc, sacc) = refs[:-7], refs[-7:]
    step = pl.program_id(0)

    @pl.when(step == 0)
    def _():
        facc[...] = jnp.zeros_like(facc)
        sacc[...] = jnp.zeros_like(sacc)

    query = jnp.concatenate([ref[0, 0] for ref in grad_refs], axis=0)
    value = jnp.concatenate([ref[0, 2] for ref in grad_refs], axis=0)
    pos = step * ROWS + lax.broadcasted_iota(jnp.int32, (1, ROWS), 1)
    rank = lax.broadcasted_iota(jnp.int32, (AR, ROWS), 0)
    chosen = rank // RANK == token_adapter(pos, meta)
    for a, grad in enumerate((query, value)):
        spread = jnp.where(chosen, nn(up_ref[a], grad), 0.0).astype(bf16)
        facc[a] += nn(spread, normed_ref[...])
        sacc[a] += nn(grad, inner_ref[:, a * AR : (a + 1) * AR])

    @pl.when(step == PARTS - 1)
    def _():
        for ref, a in ((keep_ref, meta[7]), (send_ref, 1 - meta[7])):
            ref[0:AR, :] = facc[a].astype(bf16)
            for c in range(D // 128):
                ref[AR : AR + SR, c * 128 : (c + 1) * 128] = sacc[a, c * SR : (c + 1) * SR, :].astype(bf16)


def adapter_grads(meta, grads, normed, inner, up):
    return pl.pallas_call(
        adapter_kernel,
        out_shape=[jax.ShapeDtypeStruct((AR + SR, D), bf16)] * 2,
        grid_spec=pltpu.PrefetchScalarGridSpec(
            num_scalar_prefetch=1,
            grid=(PARTS,),
            in_specs=[pl.BlockSpec((1,) + g.shape[1:], lambda i, m: (i, 0, 0, 0)) for g in grads]
            + [
                pl.BlockSpec((ROWS, D), lambda i, m: (i, 0)),
                pl.BlockSpec((ROWS, 2 * AR), lambda i, m: (i, 0)),
                pl.BlockSpec((2, AR, WIDTH), lambda i, m: (0, 0, 0)),
            ],
            out_specs=[pl.BlockSpec((AR + SR, D), lambda i, m: (0, 0))] * 2,
            scratch_shapes=[pltpu.VMEM((2, AR, D), f32), pltpu.VMEM((2, WIDTH, AR), f32)],
        ),
        compiler_params=pltpu.CompilerParams(dimension_semantics=("arbitrary",), vmem_limit_bytes=60 << 20),
        cost_estimate=pl.CostEstimate(flops=4 * TOK * D * 2 * AR, bytes_accessed=20 << 20, transcendentals=0),
        name="adapter_grads",
    )(meta, *grads, normed, inner, up)


def back_kernel(meta, *refs):
    grad_refs, rest = refs[:-10], refs[-10:]
    w_ref, up_ref, down_ref, rows_ref, gain_ref, middle_ref, out_ref, cols, total, spread = rest
    step = pl.program_id(0)
    for s in range(PARTS):
        r = s * WIDTH
        for ref in grad_refs:
            cols[r : r + ref.shape[2], :] = ref[s, 0]
            r += ref.shape[2]

    part_sum = nn(w_ref[...], cols[...])

    @pl.when(step == 0)
    def _():
        total[...] = part_sum
        spread[0] = nn(up_ref[0], cols[...])

    @pl.when(step > 0)
    def _():
        total[...] += part_sum

    @pl.when(step == 2)
    def _():
        spread[1] = nn(up_ref[1], cols[...])
        pos = meta[6] * ROWS + lax.broadcasted_iota(jnp.int32, (1, ROWS), 1)
        rank = lax.broadcasted_iota(jnp.int32, (AR, ROWS), 0)
        chosen = rank // RANK == token_adapter(pos, meta)
        both = jnp.concatenate([jnp.where(chosen, spread[a], 0.0).astype(bf16) for a in range(2)], axis=0)
        total[...] += nn(down_ref[...], both)
        gain = gain_ref[...]
        for t in range(ROWS // 128):
            own = slice(t * 128, (t + 1) * 128)
            x = rows_ref[own, :].astype(f32)
            q = lax.rsqrt(jnp.mean(x * x, axis=1, keepdims=True) + EPSILON)
            weighted = gain * total[:, own].T
            inside = jnp.mean(x * weighted, axis=1, keepdims=True)
            out_ref[own, :] = middle_ref[own, :] + (q * weighted - x * (q * q * q * inside))


def back_inputs(meta, arrived, weights, up, down, rows, gain, grad_middle):
    whole = lambda shape: pl.BlockSpec(shape, lambda i, m: (0,) * len(shape))
    return pl.pallas_call(
        back_kernel,
        out_shape=jax.ShapeDtypeStruct((ROWS, D), f32),
        grid_spec=pltpu.PrefetchScalarGridSpec(
            num_scalar_prefetch=1,
            grid=(3,),
            in_specs=[pl.BlockSpec((PARTS, 1) + g.shape[2:], lambda i, m: (0, i, 0, 0)) for g in arrived]
            + [
                pl.BlockSpec((D, D), lambda i, m: (0, i)),
                whole((2, AR, D)),
                whole((D, 2 * AR)),
                whole((ROWS, D)),
                whole((1, D)),
                whole((ROWS, D)),
            ],
            out_specs=whole((ROWS, D)),
            scratch_shapes=[pltpu.VMEM((D, ROWS), bf16), pltpu.VMEM((D, ROWS), f32), pltpu.VMEM((2, AR, ROWS), f32)],
        ),
        compiler_params=pltpu.CompilerParams(dimension_semantics=("arbitrary",), vmem_limit_bytes=60 << 20),
        cost_estimate=pl.CostEstimate(flops=6 * ROWS * D * D, bytes_accessed=24 << 20, transcendentals=0),
        name="back_inputs",
    )(meta, *arrived, weights, up, down, rows, gain, grad_middle)


def assemble_kernel(meta, own_ref, other_ref, first_ref, second_ref, turned):
    part, core = meta[6], meta[7]
    for ref, a in ((own_ref, core), (other_ref, 1 - core)):
        for m in range(PARTS):
            where = part ^ m
            piece_rows = lambda n: pl.ds(pl.multiple_of(where * n, n), n)
            first_ref[a, piece_rows(SR), :] = ref[m, 0:SR, :].astype(f32)
            for c in range(D // 128):
                turned[pl.ds(pl.multiple_of(where * WIDTH + c * SR, SR), SR), :] = ref[m, SR : 2 * SR, c * 128 : (c + 1) * 128]
            rows = pl.ds(pl.multiple_of((where % 2) * 2 * SR, 2 * SR), 2 * SR)
            mlp = ref[m, 2 * SR :, :].astype(f32)

            @pl.when(a == 0)
            def _(mlp=mlp, rows=rows, where=where):
                first_ref[2 + where // 2, rows, :] = mlp

            @pl.when(a == 1)
            def _(mlp=mlp, rows=rows, where=where):
                second_ref[2 + where // 2, rows, :] = mlp

        for c in range(D // 128):
            second_ref[a, :, c * 128 : (c + 1) * 128] = turned[c * 128 : (c + 1) * 128, :].T.astype(f32)


def assemble(meta, own, other):
    whole = lambda shape: pl.BlockSpec(shape, lambda i, m: (0,) * len(shape))
    return pl.pallas_call(
        assemble_kernel,
        out_shape=[jax.ShapeDtypeStruct((4, AR, D), f32)] * 2,
        grid_spec=pltpu.PrefetchScalarGridSpec(
            num_scalar_prefetch=1,
            grid=(1,),
            in_specs=[whole((PARTS, 4 * SR, D))] * 2,
            out_specs=[whole((4, AR, D))] * 2,
            scratch_shapes=[pltpu.VMEM((D, AR), bf16)],
        ),
        compiler_params=pltpu.CompilerParams(dimension_semantics=("arbitrary",), vmem_limit_bytes=60 << 20),
        cost_estimate=pl.CostEstimate(flops=1 << 20, bytes_accessed=8 << 20, transcendentals=0),
        name="assemble",
    )(meta, own, other)


HPB = LH
BLOCKS = ROWS // B
NEG = -1e30
FW = 512


def fwd_kernel(bounds, q_ref, k_ref, v_ref, o_ref, lse_ref, kp, qt, vt):
    b1, b2 = bounds[0], bounds[1]
    zpad = jnp.zeros((128 - HD, 128), bf16)
    for h in range(HPB):
        own = slice(h * HD, (h + 1) * HD)
        qt[h, 0:HD, :] = q_ref[own, :]
        qt[h, HD:128, :] = jnp.zeros((128 - HD, TOK), bf16)
        vt[h, 0:HD, :] = v_ref[own, :]
        vt[h, HD:96, :] = (lax.broadcasted_iota(jnp.int32, (16, TOK), 0) == 0).astype(bf16)
        for t in range(TOK // 128):
            kt = k_ref[own, t * 128:(t + 1) * 128]
            kp[h, t * 128:(t + 1) * 128, :] = jnp.concatenate([kt, zpad], axis=0).T

    subs = o_ref.shape[2] // B
    base = 0 if subs > 1 else BLOCKS - 1

    def qblock(n, _):
        chunk, sub = n // subs, n % subs
        i = chunk * BLOCKS + base + sub
        q0 = pl.multiple_of(i * B, B)
        here = pl.ds(pl.multiple_of(sub * B, B), B)
        qpos = q0 + lax.broadcasted_iota(jnp.int32, (1, B), 1)
        srow = start_row(qpos, b1, b2)

        def step(k0, width, masked, carry):
            ks = pl.ds(k0, width)
            ss = [nn(kp[h, ks, :], qt[h, :, pl.ds(q0, B)]) for h in range(HPB)]
            if masked:
                kpos = k0 + lax.broadcasted_iota(jnp.int32, (width, B), 0)
                ok = (kpos >= srow) & (kpos <= qpos)
                ss = [jnp.where(ok, s, NEG) for s in ss]
            out = []
            for h in range(HPB):
                m, acc = carry[h]
                m_new = jnp.maximum(m, jnp.max(ss[h], axis=0, keepdims=True))
                p = jnp.exp(ss[h] - m_new).astype(bf16)
                a = jnp.exp(m - m_new)
                out.append((m_new, acc * a + nn(vt[h, :, ks], p)))
            return tuple(out)

        full = jnp.minimum(i * B // FW, PROMPT // FW)
        lo = jnp.where(i < PROMPT // B, (FW // B) * (i * B // FW), first_block(i, b1, b2))
        carry = tuple((jnp.full((1, B), NEG, f32), jnp.zeros((96, B), f32)) for _ in range(HPB))
        carry = lax.fori_loop(0, full, lambda j, c: step(pl.multiple_of(j * FW, FW), FW, False, c), carry)
        carry = lax.fori_loop(lo, i + 1, lambda j, c: step(pl.multiple_of(j * B, B), B, True, c), carry)
        for h in range(HPB):
            m, acc = carry[h]
            l = acc[HD:HD + 1, :]
            o_ref[chunk, h * HD:(h + 1) * HD, here] = (acc[0:HD, :] / l).astype(bf16)
            lse_ref[h, chunk, :, here] = m + jnp.log(l)
        return 0
    lax.fori_loop(0, PARTS * subs, qblock, 0)

def attn_fwd(bounds, qkvt, subs):
    rows = lambda a: pl.BlockSpec((WIDTH, TOK), lambda i, b: (a, 0))
    width = subs * B
    return pl.pallas_call(
        fwd_kernel,
        out_shape=(jax.ShapeDtypeStruct((PARTS, WIDTH, width), bf16), jax.ShapeDtypeStruct((LH, PARTS, 1, width), f32)),
        grid_spec=pltpu.PrefetchScalarGridSpec(
            num_scalar_prefetch=1,
            grid=(1,),
            in_specs=[rows(0), rows(1), rows(2)],
            out_specs=[
                pl.BlockSpec((PARTS, WIDTH, width), lambda i, b: (0, 0, 0)),
                pl.BlockSpec((LH, PARTS, 1, width), lambda i, b: (0, 0, 0, 0)),
            ],
            scratch_shapes=[pltpu.VMEM((HPB, TOK, 128), bf16), pltpu.VMEM((HPB, 128, TOK), bf16), pltpu.VMEM((HPB, 96, TOK), bf16)],
        ),
        compiler_params=pltpu.CompilerParams(dimension_semantics=("arbitrary",), vmem_limit_bytes=60 << 20),
        cost_estimate=pl.CostEstimate(flops=subs * 13 * 10**9, bytes_accessed=5 << 20, transcendentals=0),
        name="attn_fwd",
    )(bounds, qkvt, qkvt, qkvt)


def parts3(x):
    hi = x.astype(bf16)
    r = x - hi.astype(f32)
    mid = r.astype(bf16)
    lo = (r - mid.astype(f32)).astype(bf16)
    return hi, mid, lo

def bwd_kernel(meta, scale_ref, q_ref, k_ref, v_ref, head_ref, tail_ref, o_ref, lse_ref, out_ref, kp, vp, qt, dot, dkt, dvt, dqt):
    NH = kp.shape[0]
    b1, b2 = meta[0], meta[1]
    row16 = lax.broadcasted_iota(jnp.int32, (16, 128), 0)
    ones3 = (row16 < 3).astype(bf16)
    pad = jnp.zeros((32, 128), bf16)
    scale = scale_ref[...]

    def tail(x):
        hi, mid, lo = parts3(-x)
        rest = jnp.where(row16 == 1, mid.astype(f32), jnp.where(row16 == 2, lo.astype(f32), 0.0))
        return jnp.where(row16 == 0, hi.astype(f32), rest).astype(bf16)

    @pl.loop(0, PARTS)
    def _(chunk):
        for off in range(0, ROWS, 128):
            sl, here = pl.ds(pl.multiple_of(chunk * ROWS + off, 128), 128), slice(off, off + 128)
            grad_ref, start = (head_ref, off) if off < 2 * B else (tail_ref, off - 2 * B)
            for h in range(NH):
                own = slice(h * HD, (h + 1) * HD)
                do, o = grad_ref[chunk, own, start : start + 128], o_ref[chunk, own, here]
                delta = jnp.sum(do.astype(f32) * o.astype(f32), axis=0, keepdims=True)
                qt[h, :, sl] = jnp.concatenate([q_ref[own, sl], tail(lse_ref[h, chunk, :, here]), pad], axis=0)
                dot[h, :, sl] = jnp.concatenate([do, tail(delta), pad], axis=0)
                kp[h, sl, :] = jnp.concatenate([k_ref[own, sl], ones3, pad], axis=0).T
                vp[h, sl, :] = jnp.concatenate([v_ref[own, sl], ones3, pad], axis=0).T

    dkt[...] = jnp.zeros_like(dkt)
    dvt[...] = jnp.zeros_like(dvt)
    dqt[...] = jnp.zeros_like(dqt)

    def block(k0, q0, kw, qw, masked):
        k0, q0 = pl.multiple_of(k0, B), pl.multiple_of(q0, B)
        ks, qs = pl.ds(k0, kw), pl.ds(q0, qw)
        if masked:
            qpos = q0 + lax.broadcasted_iota(jnp.int32, (1, qw), 1)
            kpos = k0 + lax.broadcasted_iota(jnp.int32, (kw, qw), 0)
            ok = (kpos >= start_row(qpos, b1, b2)) & (kpos <= qpos)
        for h in range(NH):
            p = jnp.exp(nn(kp[h, ks, :], qt[h, :, qs]))
            if masked:
                p = jnp.where(ok, p, 0.0)
            ds = (p * nn(vp[h, ks, :], dot[h, :, qs])).astype(bf16)
            dvt[h, :, ks] += nt(dot[h, 0:HD, qs], p.astype(bf16))
            dkt[h, :, ks] += nt(qt[h, 0:HD, qs], ds)
            dqt[h, :, qs] += nn(k_ref[h * HD : (h + 1) * HD, ks], ds)

    @pl.loop(0, 12)
    def _(n):
        qb = jnp.where(n < 9, 3 + n // 3, jnp.where(n == 9, 1, 2))
        kb = jnp.where(n < 9, n % 3, jnp.where(n == 11, 1, 0))
        block(kb * FW, qb * FW, FW, FW, False)

    @pl.loop(0, TOK // FW)
    def _(i):
        lo = jnp.where(i < PROMPT // FW, i, first_block(i * (FW // B), b1, b2) * B // FW)

        @pl.loop(lo, i + 1)
        def _(j):
            block(j * FW, i * FW, FW, FW, True)

    @pl.loop(0, 2 * PARTS)
    def _(step):
        chunk = step // 2
        off = pl.multiple_of((step % 2) * HALF, 128)
        sl, here = pl.ds(pl.multiple_of(chunk * ROWS + off, 128), HALF), pl.ds(off, HALF)
        for h in range(NH):
            own = slice(h * HD, (h + 1) * HD)
            dq = dqt[h, :, sl].astype(bf16).astype(f32) * scale
            out_ref[chunk, 0, own, here] = dq.astype(bf16)
            out_ref[chunk, 1, own, here] = dkt[h, :, sl].astype(bf16)
            out_ref[chunk, 2, own, here] = dvt[h, :, sl].astype(bf16)


def attn_bwd(meta, scale, qkvt, grad, mixture, logsum, first, count):
    rows = lambda a: pl.BlockSpec((count * HD, TOK), lambda i, b: ((LH * a + first) // count, 0))
    return pl.pallas_call(
        bwd_kernel,
        out_shape=jax.ShapeDtypeStruct((PARTS, 3, count * HD, ROWS), bf16),
        grid_spec=pltpu.PrefetchScalarGridSpec(
            num_scalar_prefetch=1,
            grid=(1,),
            in_specs=[
                pl.BlockSpec((HD, 1), lambda i, b: (0, 0)),
                rows(0),
                rows(1),
                rows(2),
                *[pl.BlockSpec((PARTS, count * HD, g.shape[2]), lambda i, b: (0, first // count, 0)) for g in grad],
                pl.BlockSpec((PARTS, count * HD, ROWS), lambda i, b: (0, first // count, 0)),
                pl.BlockSpec((count, PARTS, 1, ROWS), lambda i, b: (first // count, 0, 0, 0)),
            ],
            out_specs=pl.BlockSpec((PARTS, 3, count * HD, ROWS), lambda i, b: (0, 0, 0, 0)),
            scratch_shapes=[pltpu.VMEM((count, TOK, 128), bf16)] * 2
            + [pltpu.VMEM((count, 128, TOK), bf16)] * 2
            + [pltpu.VMEM((count, HD, TOK), f32)] * 3,
        ),
        compiler_params=pltpu.CompilerParams(dimension_semantics=("arbitrary",), vmem_limit_bytes=60 << 20),
        cost_estimate=pl.CostEstimate(flops=count * 18 * 10**9, bytes_accessed=count * 8 << 20, transcendentals=0),
        name="attn_bwd",
    )(meta, scale, qkvt, qkvt, qkvt, *grad, mixture, logsum)


def mlp_kernel(meta, mixed_ref, rows_ref, cot_ref, gain_ref, out_ref, up_ref, down_ref, fd_ref, fu_ref, *refs, first):
    step = pl.program_id(0)
    if first:
        hidden_ref, inner_ref, middle_ref, grad_ref, g_ref, keep_ref, send_ref, sums = refs[-8:]
        sums[...] = refs[0][...]
    else:
        hidden_ref, inner_ref, middle_ref, grad_ref, g_ref, sums = refs

        @pl.when(step == 0)
        def _():
            sums[...] = jnp.zeros_like(sums)

    pos = meta[6] * ROWS + (first + step) * B + lax.broadcasted_iota(jnp.int32, (B, AR), 0)
    chosen = lax.broadcasted_iota(jnp.int32, (B, AR), 1) // RANK == token_adapter(pos, meta)
    choose = lambda x: jnp.where(chosen, x, 0.0).astype(bf16)
    gain = gain_ref[...]

    middle = rows_ref[...].astype(f32) + nn(mixed_ref[...].T, out_ref[...])
    middle_ref[...] = middle
    q = lax.rsqrt(jnp.mean(middle * middle, axis=1, keepdims=True) + EPSILON)
    normed = (middle * q * gain).astype(bf16)
    inner_up = choose(nn(normed, fd_ref[0]))
    before = nn(normed, up_ref[...]) + nn(inner_up, fu_ref[0])
    gate = jax.nn.sigmoid(before)
    hidden = (before * gate).astype(bf16)
    hidden_ref[...] = hidden
    inner_down = choose(nn(hidden, fd_ref[1]))
    inner_ref[...] = inner_down

    after = cot_ref[...]
    spread_down = choose(nt(after, fu_ref[1]))
    grad_hidden = nt(after, down_ref[...]) + nt(spread_down, fd_ref[1])
    grad_before = (grad_hidden * gate * (1.0 + before * (1.0 - gate))).astype(bf16)
    spread_up = choose(nt(grad_before, fu_ref[0]))
    weighted = gain * (nt(grad_before, up_ref[...]) + nt(spread_up, fd_ref[0]))
    middle = middle_ref[...]
    inside = jnp.mean(middle * weighted, axis=1, keepdims=True)
    grad_middle = after.astype(f32) + (q * weighted - middle * (q * q * q * inside))
    grad_ref[...] = grad_middle
    grad_mixed = nt(out_ref[...], grad_middle.astype(bf16)).astype(bf16)
    for s in range(PARTS):
        g_ref[s] = grad_mixed[s * WIDTH : (s + 1) * WIDTH]

    for n, (a, b) in enumerate(((spread_up, normed), (spread_down, hidden), (inner_up, grad_before), (inner_down, after))):
        sums[n] += nn(a.T, b)

    if first:
        for ref, half in ((keep_ref, meta[7]), (send_ref, 1 - meta[7])):
            for n in range(2):
                ref[n * AR : (n + 1) * AR, :] = sums[2 * half + n].astype(bf16)


def mlp(meta, mixed, rows, cotangent, gain, weights, flat_down, flat_up, first, sums=None, done=()):
    whole = lambda shape: pl.BlockSpec(shape, lambda i, m: (0,) * len(shape))
    block = lambda width: pl.BlockSpec((B, width), lambda i, m: (first + i, 0))
    tokens = mixed.shape[1]
    out_shape = [
        jax.ShapeDtypeStruct((ROWS, D), bf16),
        jax.ShapeDtypeStruct((ROWS, AR), bf16),
        jax.ShapeDtypeStruct((ROWS, D), f32),
        jax.ShapeDtypeStruct((ROWS, D), f32),
        jax.ShapeDtypeStruct((PARTS, WIDTH, tokens), bf16),
    ]
    out_specs = [block(D), block(AR), block(D), block(D), pl.BlockSpec((PARTS, WIDTH, B), lambda i, m: (0, 0, i))]
    if first:
        out_shape += [jax.ShapeDtypeStruct((2 * AR, D), bf16)] * 2
        out_specs += [whole((2 * AR, D))] * 2
        extra, extra_specs = [sums, *done], [whole((4, AR, D))] + [pl.BlockSpec(memory_space=pl.ANY)] * 4
        aliases, scratch = {11 + n: n for n in range(4)}, [pltpu.VMEM((4, AR, D), f32)]
    else:
        out_shape += [jax.ShapeDtypeStruct((4, AR, D), f32)]
        out_specs += [whole((4, AR, D))]
        extra, extra_specs, aliases, scratch = [], [], {}, []
    return pl.pallas_call(
        functools.partial(mlp_kernel, first=first),
        out_shape=out_shape,
        grid_spec=pltpu.PrefetchScalarGridSpec(
            num_scalar_prefetch=1,
            grid=(tokens // B,),
            in_specs=[
                pl.BlockSpec((D, B), lambda i, m: (0, i)),
                block(D),
                block(D),
                whole((1, D)),
                *[pl.BlockSpec((D, D), lambda i, m, a=a: (0, a)) for a in range(3)],
                whole((2, D, AR)),
                whole((2, AR, D)),
            ]
            + extra_specs,
            out_specs=out_specs,
            scratch_shapes=scratch,
        ),
        input_output_aliases=aliases,
        compiler_params=pltpu.CompilerParams(dimension_semantics=("arbitrary",), vmem_limit_bytes=60 << 20),
        cost_estimate=pl.CostEstimate(flops=tokens * 22 * 10**6, bytes_accessed=20 << 20, transcendentals=0),
        name="mlp",
    )(meta, mixed, rows, cotangent, gain, weights, weights, weights, flat_down, flat_up, *extra)


def exchange(value):
    return lax.all_to_all(value, "heads", split_axis=0, concat_axis=0, tiled=True)


def swap(value, axis, mask):
    count = lax.axis_size(axis)
    return lax.ppermute(value, axis, [(i, i ^ mask) for i in range(count)])


def piece(value, index, count):
    rows = value.shape[-2] // count
    return lax.dynamic_slice_in_dim(value, index * rows, rows, axis=value.ndim - 2)


def sum_low(*terms):
    total = terms[0].astype(f32)
    for term in terms[1:]:
        total = total + term.astype(f32)
    return total.astype(bf16)


def far_bits():
    bits = [2]
    while bits[-1] * 2 < lax.axis_size("fsdp"):
        bits.append(bits[-1] * 2)
    return bits


def sum_far(value):
    bits = far_bits()
    for bit, twice in zip(bits[0::2], bits[1::2]):
        value = sum_low(value, *[swap(value, "fsdp", m) for m in (bit, twice, bit | twice)])
    if len(bits) % 2:
        value = sum_low(value, swap(value, "fsdp", bits[-1]))
    return value


def scatter_near(value):
    core = lax.axis_index("fsdp") & 1
    return sum_low(piece(value, core, 2), swap(piece(value, 1 - core, 2), "fsdp", 1))


def scatter_heads(value):
    part = lax.axis_index("heads")
    terms = [swap(piece(value, part ^ m, PARTS), "heads", m) for m in (1, 2, 3)]
    return sum_low(piece(value, part, PARTS), *terms)


def body(
    inputs,
    cotangent,
    lengths,
    adapter_ids,
    query_weight,
    key_weight,
    value_weight,
    out_weight,
    up_weight,
    down_weight,
    attn_gain,
    mlp_gain,
    query_scale,
    adapter_in,
    adapter_out,
):
    part = lax.axis_index("heads")
    rows = inputs[0]
    low, high = rows[:HALF], rows[HALF:]
    near_high = swap(high, "heads", 1)
    far_low = swap(low, "heads", 2)
    ends = PROMPT + jnp.cumsum(lengths[0])
    bounds = ends[:2].astype(jnp.int32)
    ids = adapter_ids[0]
    core = lax.axis_index("fsdp") & 1
    meta = jnp.concatenate([bounds, ids, jnp.stack([part, core]).astype(jnp.int32)])
    flat_down = jnp.transpose(adapter_in, (0, 2, 1, 3)).reshape(4, D, AR)
    flat_up = adapter_out.reshape(4, AR, D)
    gain_attn = attn_gain.astype(f32)
    gain_mlp = mlp_gain.astype(f32)

    def mine(weight):
        return lax.dynamic_slice_in_dim(weight, part * WIDTH, WIDTH, axis=1)

    weights_mine = jnp.concatenate([mine(query_weight), mine(key_weight), mine(value_weight)], axis=1)
    weights_mine = lax.all_gather(weights_mine, "fsdp", axis=0, tiled=True)
    weights_mlp = lax.all_gather(jnp.concatenate([out_weight, up_weight, down_weight], axis=1), "fsdp", axis=0, tiled=True)
    weights_all = lax.all_gather(jnp.concatenate([query_weight, key_weight, value_weight], axis=1), "fsdp", axis=0, tiled=True)

    down_pair = jnp.concatenate([flat_down[0], flat_down[1]], axis=1)
    up_mine = lax.dynamic_slice_in_dim(flat_up[:2], part * WIDTH, WIDTH, axis=2)
    low_late, high_late, down_pair = lax.optimization_barrier((low, high, down_pair))
    near_low = swap(low_late, "heads", 1)
    far_high = swap(high_late, "heads", 2)
    both_low = swap(far_low, "heads", 1)
    both_high = swap(near_high, "heads", 2)
    scale_row = query_scale * HD ** (-0.5)
    scale_mine = jnp.tile(scale_row, LH)[:, None]

    wt, ut = weights_mine.T, jnp.transpose(up_mine, (0, 2, 1))
    done = ()
    for m, low, high in ((0, rows, None), (1, near_low, near_high), (2, far_low, far_high), (3, both_low, both_high)):
        done = qkv_project(meta, part ^ m, low, high, gain_attn[None, :], wt, down_pair, ut, scale_mine, done)
    qkvt, normed_all, inner_all = done
    head_mix, head_log = attn_fwd(bounds, qkvt, 2)
    mixed_head = exchange(head_mix)
    later, head_log = lax.optimization_barrier((bounds, head_log))
    tail_mix, tail_log = attn_fwd(later, qkvt, 1)
    tail_sent, mixed_head = lax.optimization_barrier((tail_mix, mixed_head))
    mixed_tail = exchange(tail_sent)
    up_mine, mixed_head = lax.optimization_barrier((up_mine, mixed_head))

    shared = (rows, cotangent[0], gain_mlp[None, :], weights_mlp, flat_down[2:], flat_up[2:])
    *done, grad_part, sums = mlp(meta, mixed_head.reshape(D, -1), *shared, 0)
    grad_head = exchange(grad_part)
    hidden_low, inner_down, middle, grad_middle, grad_part, mlp_keep, mlp_send = mlp(
        meta, mixed_tail.reshape(D, -1), *shared, 2, sums, done
    )
    grad_part, grad_head = lax.optimization_barrier((grad_part, grad_head))
    forward, grad_part = lax.optimization_barrier(((head_mix, tail_mix, head_log, tail_log), grad_part))
    grad_heads = (grad_head, exchange(grad_part))
    mixture = jnp.concatenate(forward[:2], axis=2)
    logsum = jnp.concatenate(forward[2:], axis=3)

    mlp_total = sum_low(mlp_keep, swap(mlp_send, "fsdp", 1))
    mlp_total, grad_heads = lax.optimization_barrier((mlp_total, grad_heads))
    mlp_total = scatter_heads(mlp_total)
    scale_column = scale_row[:, None]
    send_back = lambda g: exchange(g.reshape(PARTS, -1, ROWS)).reshape(g.shape)
    grads, arrived = [], []
    grads.append(attn_bwd(meta, scale_column, qkvt, grad_heads, mixture, logsum, 0, 2))
    mlp_total, grads[0] = lax.optimization_barrier((mlp_total, grads[0]))
    arrived.append(send_back(grads[0]))
    mlp_total = sum_far(mlp_total)
    meta, grads[0] = lax.optimization_barrier((meta, grads[0]))
    grads.append(attn_bwd(meta, scale_column, qkvt, grad_heads, mixture, logsum, 2, 2))
    mlp_total, grads[1] = lax.optimization_barrier((mlp_total, grads[1]))
    arrived.append(send_back(grads[1]))

    meta, arrived[0] = lax.optimization_barrier((meta, arrived[0]))
    keep, send = adapter_grads(meta, grads, normed_all, inner_all, up_mine)
    hidden_late, inner_late, keep = lax.optimization_barrier((hidden_low, inner_down, keep))
    outputs = (middle + (nn(hidden_late, weights_mlp[:, 2 * D :]) + nn(inner_late, flat_up[3]))).astype(bf16)
    total = sum_low(keep, swap(send, "fsdp", 1))
    total = jnp.concatenate([scatter_heads(total[:AR]), total[AR:]])
    total, arrived, outputs = lax.optimization_barrier((total, arrived, outputs))
    total = sum_far(total)
    meta, total = lax.optimization_barrier((meta, total))
    own = jnp.concatenate([total, mlp_total])
    pieces = [own] + [swap(own, "heads", m) for m in (1, 2, 3)]
    grad_inputs = back_inputs(meta, arrived, weights_all, flat_up[:2], down_pair, rows, gain_attn[None, :], grad_middle)
    pieces, grad_inputs = lax.optimization_barrier((pieces, grad_inputs))
    own = jnp.stack(pieces)
    grad_first, grad_second = assemble(meta, own, swap(own, "fsdp", 1))
    grad_first = jnp.transpose(grad_first.reshape(4, ADAPTERS, RANK, D), (0, 1, 3, 2))
    grad_second = grad_second.reshape(4, ADAPTERS, RANK, D)
    return (outputs[None], grad_inputs[None], grad_first, grad_second)


def solution(mesh):
    placed = (
        P("fsdp", "heads", None),
        P("fsdp", "heads", None),
        P("fsdp", None),
        P("fsdp", None),
        P("fsdp", None),
        P("fsdp", None),
        P("fsdp", None),
        P("fsdp", None),
        P("fsdp", None),
        P("fsdp", None),
        P(),
        P(),
        P(),
        P(),
        P(),
    )
    return jax.shard_map(
        body,
        mesh=mesh,
        in_specs=placed,
        out_specs=(P("fsdp", "heads", None), P("fsdp", "heads", None), P(), P()),
        check_vma=False,
    )
```

```python
import functools

import jax
import jax.numpy as jnp
from jax import lax
from jax.experimental import pallas as pl
from jax.experimental.pallas import tpu as pltpu
from jax.sharding import PartitionSpec as P

D = 1280
HEADS = 16
HD = 80
RANK = 16
ADAPTERS = 8
AR = ADAPTERS * RANK
TOK = 3072
PROMPT = 1536
ROWS = 768
QB = 256
PARTS = TOK // ROWS
LH = HEADS // PARTS
HALF = ROWS // 2
PH = LH // 2
PW = PH * HD
WIDTH = LH * HD
SR = WIDTH * 128 // D
EPSILON = 1e-06
B = 256
f32, bf16 = jnp.float32, jnp.bfloat16


def nt(a, b):
    return lax.dot_general(a, b, (((1,), (1,)), ((), ())), preferred_element_type=f32)


def tn(a, b):
    return lax.dot_general(a, b, (((0,), (0,)), ((), ())), preferred_element_type=f32)


def nn(a, b):
    return lax.dot_general(a, b, (((1,), (0,)), ((), ())), preferred_element_type=f32)

def start_row(qpos, b1, b2):
    return jnp.where(qpos < PROMPT, 0, jnp.where(qpos < b1, PROMPT, jnp.where(qpos < b2, b1, b2)))

def first_block(i, b1, b2):
    q0 = i * B
    return jnp.where(q0 < b1, PROMPT, jnp.where(q0 < b2, b1, b2)) // B


def token_adapter(pos, meta):
    return jnp.where(
        pos < PROMPT, meta[2], jnp.where(pos < meta[0], meta[3], jnp.where(pos < meta[1], meta[4], meta[5]))
    )


def qkv_kernel(meta, first, low_ref, high_ref, gain_ref, wt_ref, down_ref, up_ref, scale_ref, *refs):
    out_ref, normed_ref, inner_ref, rows = refs[-4:]
    step = pl.program_id(0)

    @pl.when(step == 0)
    def _():
        rows[0:HALF, :] = low_ref[...]
        rows[HALF:ROWS, :] = high_ref[...]

    x = rows[pl.ds(pl.multiple_of(step * QB, QB), QB), :].astype(f32)
    q = lax.rsqrt(jnp.mean(x * x, axis=1, keepdims=True) + EPSILON)
    normed = (x * q * gain_ref[...]).astype(bf16)
    normed_ref[...] = normed
    pos = (first[0] + step) * QB + lax.broadcasted_iota(jnp.int32, (QB, 1), 0)
    lane = lax.broadcasted_iota(jnp.int32, (QB, 2 * AR), 1)
    chosen = (lane % AR) // RANK == token_adapter(pos, meta)
    inner = jnp.where(chosen, nn(normed, down_ref[...]), 0.0).astype(bf16)
    inner_ref[...] = inner
    out = nt(wt_ref[...], normed)
    query = out[:WIDTH] + nt(up_ref[0], inner[:, :AR])
    out_ref[0:WIDTH, :] = (query * scale_ref[...]).astype(bf16)
    out_ref[WIDTH : 2 * WIDTH, :] = out[WIDTH : 2 * WIDTH].astype(bf16)
    out_ref[2 * WIDTH :, :] = (out[2 * WIDTH :] + nt(up_ref[1], inner[:, AR:])).astype(bf16)


def qkv_project(meta, chunk, low, high, gain, wt, down, up, scale, done):
    whole = lambda shape: pl.BlockSpec(shape, lambda i, *_: (0, 0))
    second = 1 if high is None else 0
    first = (chunk * (ROWS // QB))[None].astype(jnp.int32)
    return pl.pallas_call(
        qkv_kernel,
        out_shape=(
            jax.ShapeDtypeStruct((3 * WIDTH, TOK), bf16),
            jax.ShapeDtypeStruct((TOK, D), bf16),
            jax.ShapeDtypeStruct((TOK, 2 * AR), bf16),
        ),
        grid_spec=pltpu.PrefetchScalarGridSpec(
            num_scalar_prefetch=2,
            grid=(ROWS // QB,),
            in_specs=[
                whole((HALF, D)),
                pl.BlockSpec((HALF, D), lambda i, *_: (second, 0)),
                whole((1, D)),
                whole((3 * WIDTH, D)),
                whole((D, 2 * AR)),
                pl.BlockSpec((2, WIDTH, AR), lambda i, *_: (0, 0, 0)),
                whole((WIDTH, 1)),
            ]
            + [pl.BlockSpec(memory_space=pl.ANY)] * len(done),
            out_specs=[
                pl.BlockSpec((3 * WIDTH, QB), lambda i, m, first: (0, first[0] + i)),
                pl.BlockSpec((QB, D), lambda i, m, first: (first[0] + i, 0)),
                pl.BlockSpec((QB, 2 * AR), lambda i, m, first: (first[0] + i, 0)),
            ],
            scratch_shapes=[pltpu.VMEM((ROWS, D), bf16)],
        ),
        input_output_aliases={9 + i: i for i in range(len(done))},
        compiler_params=pltpu.CompilerParams(dimension_semantics=("arbitrary",), vmem_limit_bytes=60 << 20),
        cost_estimate=pl.CostEstimate(flops=2 * ROWS * D * (3 * WIDTH + 2 * AR), bytes_accessed=8 << 20, transcendentals=0),
        name="qkv_project",
    )(meta, first, low, low if high is None else high, gain, wt, down, up, scale, *done)


def adapter_kernel(meta, *refs):
    grad_refs, (normed_ref, inner_ref, up_ref, keep_ref, send_ref, facc, sacc) = refs[:-7], refs[-7:]
    step = pl.program_id(0)

    @pl.when(step == 0)
    def _():
        facc[...] = jnp.zeros_like(facc)
        sacc[...] = jnp.zeros_like(sacc)

    query = jnp.concatenate([ref[0, 0] for ref in grad_refs], axis=0)
    value = jnp.concatenate([ref[0, 2] for ref in grad_refs], axis=0)
    pos = step * ROWS + lax.broadcasted_iota(jnp.int32, (1, ROWS), 1)
    rank = lax.broadcasted_iota(jnp.int32, (AR, ROWS), 0)
    chosen = rank // RANK == token_adapter(pos, meta)
    for a, grad in enumerate((query, value)):
        spread = jnp.where(chosen, nn(up_ref[a], grad), 0.0).astype(bf16)
        facc[a] += nn(spread, normed_ref[...])
        sacc[a] += nn(grad, inner_ref[:, a * AR : (a + 1) * AR])

    @pl.when(step == PARTS - 1)
    def _():
        for ref, a in ((keep_ref, meta[7]), (send_ref, 1 - meta[7])):
            ref[0:AR, :] = facc[a].astype(bf16)
            for c in range(D // 128):
                ref[AR : AR + SR, c * 128 : (c + 1) * 128] = sacc[a, c * SR : (c + 1) * SR, :].astype(bf16)


def adapter_grads(meta, grads, normed, inner, up):
    return pl.pallas_call(
        adapter_kernel,
        out_shape=[jax.ShapeDtypeStruct((AR + SR, D), bf16)] * 2,
        grid_spec=pltpu.PrefetchScalarGridSpec(
            num_scalar_prefetch=1,
            grid=(PARTS,),
            in_specs=[pl.BlockSpec((1,) + g.shape[1:], lambda i, m: (i, 0, 0, 0)) for g in grads]
            + [
                pl.BlockSpec((ROWS, D), lambda i, m: (i, 0)),
                pl.BlockSpec((ROWS, 2 * AR), lambda i, m: (i, 0)),
                pl.BlockSpec((2, AR, WIDTH), lambda i, m: (0, 0, 0)),
            ],
            out_specs=[pl.BlockSpec((AR + SR, D), lambda i, m: (0, 0))] * 2,
            scratch_shapes=[pltpu.VMEM((2, AR, D), f32), pltpu.VMEM((2, WIDTH, AR), f32)],
        ),
        compiler_params=pltpu.CompilerParams(dimension_semantics=("arbitrary",), vmem_limit_bytes=60 << 20),
        cost_estimate=pl.CostEstimate(flops=4 * TOK * D * 2 * AR, bytes_accessed=20 << 20, transcendentals=0),
        name="adapter_grads",
    )(meta, *grads, normed, inner, up)


def back_kernel(meta, *refs):
    grad_refs, rest = refs[:-10], refs[-10:]
    w_ref, up_ref, down_ref, rows_ref, gain_ref, middle_ref, out_ref, cols, total, spread = rest
    step = pl.program_id(0)
    for s in range(PARTS):
        r = s * WIDTH
        for ref in grad_refs:
            cols[r : r + ref.shape[2], :] = ref[s, 0]
            r += ref.shape[2]

    part_sum = nn(w_ref[...], cols[...])

    @pl.when(step == 0)
    def _():
        total[...] = part_sum
        spread[0] = nn(up_ref[0], cols[...])

    @pl.when(step > 0)
    def _():
        total[...] += part_sum

    @pl.when(step == 2)
    def _():
        spread[1] = nn(up_ref[1], cols[...])
        pos = meta[6] * ROWS + lax.broadcasted_iota(jnp.int32, (1, ROWS), 1)
        rank = lax.broadcasted_iota(jnp.int32, (AR, ROWS), 0)
        chosen = rank // RANK == token_adapter(pos, meta)
        both = jnp.concatenate([jnp.where(chosen, spread[a], 0.0).astype(bf16) for a in range(2)], axis=0)
        total[...] += nn(down_ref[...], both)
        gain = gain_ref[...]
        for t in range(ROWS // 128):
            own = slice(t * 128, (t + 1) * 128)
            x = rows_ref[own, :].astype(f32)
            q = lax.rsqrt(jnp.mean(x * x, axis=1, keepdims=True) + EPSILON)
            weighted = gain * total[:, own].T
            inside = jnp.mean(x * weighted, axis=1, keepdims=True)
            out_ref[own, :] = middle_ref[own, :] + (q * weighted - x * (q * q * q * inside))


def back_inputs(meta, arrived, weights, up, down, rows, gain, grad_middle):
    whole = lambda shape: pl.BlockSpec(shape, lambda i, m: (0,) * len(shape))
    return pl.pallas_call(
        back_kernel,
        out_shape=jax.ShapeDtypeStruct((ROWS, D), f32),
        grid_spec=pltpu.PrefetchScalarGridSpec(
            num_scalar_prefetch=1,
            grid=(3,),
            in_specs=[pl.BlockSpec((PARTS, 1) + g.shape[2:], lambda i, m: (0, i, 0, 0)) for g in arrived]
            + [
                pl.BlockSpec((D, D), lambda i, m: (0, i)),
                whole((2, AR, D)),
                whole((D, 2 * AR)),
                whole((ROWS, D)),
                whole((1, D)),
                whole((ROWS, D)),
            ],
            out_specs=whole((ROWS, D)),
            scratch_shapes=[pltpu.VMEM((D, ROWS), bf16), pltpu.VMEM((D, ROWS), f32), pltpu.VMEM((2, AR, ROWS), f32)],
        ),
        compiler_params=pltpu.CompilerParams(dimension_semantics=("arbitrary",), vmem_limit_bytes=60 << 20),
        cost_estimate=pl.CostEstimate(flops=6 * ROWS * D * D, bytes_accessed=24 << 20, transcendentals=0),
        name="back_inputs",
    )(meta, *arrived, weights, up, down, rows, gain, grad_middle)


def assemble_kernel(meta, own_ref, other_ref, first_ref, second_ref, turned):
    part, core = meta[6], meta[7]
    for ref, a in ((own_ref, core), (other_ref, 1 - core)):
        for m in range(PARTS):
            where = part ^ m
            piece_rows = lambda n: pl.ds(pl.multiple_of(where * n, n), n)
            first_ref[a, piece_rows(SR), :] = ref[m, 0:SR, :].astype(f32)
            for c in range(D // 128):
                turned[pl.ds(pl.multiple_of(where * WIDTH + c * SR, SR), SR), :] = ref[m, SR : 2 * SR, c * 128 : (c + 1) * 128]
            rows = pl.ds(pl.multiple_of((where % 2) * 2 * SR, 2 * SR), 2 * SR)
            mlp = ref[m, 2 * SR :, :].astype(f32)

            @pl.when(a == 0)
            def _(mlp=mlp, rows=rows, where=where):
                first_ref[2 + where // 2, rows, :] = mlp

            @pl.when(a == 1)
            def _(mlp=mlp, rows=rows, where=where):
                second_ref[2 + where // 2, rows, :] = mlp

        for c in range(D // 128):
            second_ref[a, :, c * 128 : (c + 1) * 128] = turned[c * 128 : (c + 1) * 128, :].T.astype(f32)


def assemble(meta, own, other):
    whole = lambda shape: pl.BlockSpec(shape, lambda i, m: (0,) * len(shape))
    return pl.pallas_call(
        assemble_kernel,
        out_shape=[jax.ShapeDtypeStruct((4, AR, D), f32)] * 2,
        grid_spec=pltpu.PrefetchScalarGridSpec(
            num_scalar_prefetch=1,
            grid=(1,),
            in_specs=[whole((PARTS, 4 * SR, D))] * 2,
            out_specs=[whole((4, AR, D))] * 2,
            scratch_shapes=[pltpu.VMEM((D, AR), bf16)],
        ),
        compiler_params=pltpu.CompilerParams(dimension_semantics=("arbitrary",), vmem_limit_bytes=60 << 20),
        cost_estimate=pl.CostEstimate(flops=1 << 20, bytes_accessed=8 << 20, transcendentals=0),
        name="assemble",
    )(meta, own, other)


HPB = LH
BLOCKS = ROWS // B
NEG = -1e30
FW = 512


def fwd_kernel(bounds, q_ref, k_ref, v_ref, o_ref, lse_ref, kp, qt, vt):
    b1, b2 = bounds[0], bounds[1]
    zpad = jnp.zeros((128 - HD, 128), bf16)
    for h in range(HPB):
        own = slice(h * HD, (h + 1) * HD)
        qt[h, 0:HD, :] = q_ref[own, :]
        qt[h, HD:128, :] = jnp.zeros((128 - HD, TOK), bf16)
        vt[h, 0:HD, :] = v_ref[own, :]
        vt[h, HD:96, :] = (lax.broadcasted_iota(jnp.int32, (16, TOK), 0) == 0).astype(bf16)
        for t in range(TOK // 128):
            kt = k_ref[own, t * 128:(t + 1) * 128]
            kp[h, t * 128:(t + 1) * 128, :] = jnp.concatenate([kt, zpad], axis=0).T

    subs = o_ref.shape[2] // B
    base = 0 if subs > 1 else BLOCKS - 1

    def qblock(n, _):
        chunk, sub = n // subs, n % subs
        i = chunk * BLOCKS + base + sub
        q0 = pl.multiple_of(i * B, B)
        here = pl.ds(pl.multiple_of(sub * B, B), B)
        qpos = q0 + lax.broadcasted_iota(jnp.int32, (1, B), 1)
        srow = start_row(qpos, b1, b2)

        def step(k0, width, masked, carry):
            ks = pl.ds(k0, width)
            ss = [nn(kp[h, ks, :], qt[h, :, pl.ds(q0, B)]) for h in range(HPB)]
            if masked:
                kpos = k0 + lax.broadcasted_iota(jnp.int32, (width, B), 0)
                ok = (kpos >= srow) & (kpos <= qpos)
                ss = [jnp.where(ok, s, NEG) for s in ss]
            out = []
            for h in range(HPB):
                m, acc = carry[h]
                m_new = jnp.maximum(m, jnp.max(ss[h], axis=0, keepdims=True))
                p = jnp.exp(ss[h] - m_new).astype(bf16)
                a = jnp.exp(m - m_new)
                out.append((m_new, acc * a + nn(vt[h, :, ks], p)))
            return tuple(out)

        full = jnp.minimum(i * B // FW, PROMPT // FW)
        lo = jnp.where(i < PROMPT // B, (FW // B) * (i * B // FW), first_block(i, b1, b2))
        carry = tuple((jnp.full((1, B), NEG, f32), jnp.zeros((96, B), f32)) for _ in range(HPB))
        carry = lax.fori_loop(0, full, lambda j, c: step(pl.multiple_of(j * FW, FW), FW, False, c), carry)
        carry = lax.fori_loop(lo, i + 1, lambda j, c: step(pl.multiple_of(j * B, B), B, True, c), carry)
        for h in range(HPB):
            m, acc = carry[h]
            l = acc[HD:HD + 1, :]
            o_ref[chunk, h * HD:(h + 1) * HD, here] = (acc[0:HD, :] / l).astype(bf16)
            lse_ref[h, chunk, :, here] = m + jnp.log(l)
        return 0
    lax.fori_loop(0, PARTS * subs, qblock, 0)

def attn_fwd(bounds, qkvt, subs):
    rows = lambda a: pl.BlockSpec((WIDTH, TOK), lambda i, b: (a, 0))
    width = subs * B
    return pl.pallas_call(
        fwd_kernel,
        out_shape=(jax.ShapeDtypeStruct((PARTS, WIDTH, width), bf16), jax.ShapeDtypeStruct((LH, PARTS, 1, width), f32)),
        grid_spec=pltpu.PrefetchScalarGridSpec(
            num_scalar_prefetch=1,
            grid=(1,),
            in_specs=[rows(0), rows(1), rows(2)],
            out_specs=[
                pl.BlockSpec((PARTS, WIDTH, width), lambda i, b: (0, 0, 0)),
                pl.BlockSpec((LH, PARTS, 1, width), lambda i, b: (0, 0, 0, 0)),
            ],
            scratch_shapes=[pltpu.VMEM((HPB, TOK, 128), bf16), pltpu.VMEM((HPB, 128, TOK), bf16), pltpu.VMEM((HPB, 96, TOK), bf16)],
        ),
        compiler_params=pltpu.CompilerParams(dimension_semantics=("arbitrary",), vmem_limit_bytes=60 << 20),
        cost_estimate=pl.CostEstimate(flops=subs * 13 * 10**9, bytes_accessed=5 << 20, transcendentals=0),
        name="attn_fwd",
    )(bounds, qkvt, qkvt, qkvt)


def parts3(x):
    hi = x.astype(bf16)
    r = x - hi.astype(f32)
    mid = r.astype(bf16)
    lo = (r - mid.astype(f32)).astype(bf16)
    return hi, mid, lo

def bwd_kernel(meta, scale_ref, q_ref, k_ref, v_ref, head_ref, tail_ref, o_ref, lse_ref, out_ref, kp, vp, qt, dot, dkt, dvt, dqt):
    NH = kp.shape[0]
    b1, b2 = meta[0], meta[1]
    row16 = lax.broadcasted_iota(jnp.int32, (16, 128), 0)
    ones3 = (row16 < 3).astype(bf16)
    pad = jnp.zeros((32, 128), bf16)
    scale = scale_ref[...]

    def tail(x):
        hi, mid, lo = parts3(-x)
        rest = jnp.where(row16 == 1, mid.astype(f32), jnp.where(row16 == 2, lo.astype(f32), 0.0))
        return jnp.where(row16 == 0, hi.astype(f32), rest).astype(bf16)

    @pl.loop(0, PARTS)
    def _(chunk):
        for off in range(0, ROWS, 128):
            sl, here = pl.ds(pl.multiple_of(chunk * ROWS + off, 128), 128), slice(off, off + 128)
            grad_ref, start = (head_ref, off) if off < 2 * B else (tail_ref, off - 2 * B)
            for h in range(NH):
                own = slice(h * HD, (h + 1) * HD)
                do, o = grad_ref[chunk, own, start : start + 128], o_ref[chunk, own, here]
                delta = jnp.sum(do.astype(f32) * o.astype(f32), axis=0, keepdims=True)
                qt[h, :, sl] = jnp.concatenate([q_ref[own, sl], tail(lse_ref[h, chunk, :, here]), pad], axis=0)
                dot[h, :, sl] = jnp.concatenate([do, tail(delta), pad], axis=0)
                kp[h, sl, :] = jnp.concatenate([k_ref[own, sl], ones3, pad], axis=0).T
                vp[h, sl, :] = jnp.concatenate([v_ref[own, sl], ones3, pad], axis=0).T

    dkt[...] = jnp.zeros_like(dkt)
    dvt[...] = jnp.zeros_like(dvt)
    dqt[...] = jnp.zeros_like(dqt)

    def block(k0, q0, kw, qw, masked):
        k0, q0 = pl.multiple_of(k0, B), pl.multiple_of(q0, B)
        ks, qs = pl.ds(k0, kw), pl.ds(q0, qw)
        if masked:
            qpos = q0 + lax.broadcasted_iota(jnp.int32, (1, qw), 1)
            kpos = k0 + lax.broadcasted_iota(jnp.int32, (kw, qw), 0)
            ok = (kpos >= start_row(qpos, b1, b2)) & (kpos <= qpos)
        for h in range(NH):
            p = jnp.exp(nn(kp[h, ks, :], qt[h, :, qs]))
            if masked:
                p = jnp.where(ok, p, 0.0)
            ds = (p * nn(vp[h, ks, :], dot[h, :, qs])).astype(bf16)
            dvt[h, :, ks] += nt(dot[h, 0:HD, qs], p.astype(bf16))
            dkt[h, :, ks] += nt(qt[h, 0:HD, qs], ds)
            dqt[h, :, qs] += nn(k_ref[h * HD : (h + 1) * HD, ks], ds)

    @pl.loop(0, 12)
    def _(n):
        qb = jnp.where(n < 9, 3 + n // 3, jnp.where(n == 9, 1, 2))
        kb = jnp.where(n < 9, n % 3, jnp.where(n == 11, 1, 0))
        block(kb * FW, qb * FW, FW, FW, False)

    @pl.loop(0, TOK // FW)
    def _(i):
        lo = jnp.where(i < PROMPT // FW, i, first_block(i * (FW // B), b1, b2) * B // FW)

        @pl.loop(lo, i + 1)
        def _(j):
            block(j * FW, i * FW, FW, FW, True)

    @pl.loop(0, 2 * PARTS)
    def _(step):
        chunk = step // 2
        off = pl.multiple_of((step % 2) * HALF, 128)
        sl, here = pl.ds(pl.multiple_of(chunk * ROWS + off, 128), HALF), pl.ds(off, HALF)
        for h in range(NH):
            own = slice(h * HD, (h + 1) * HD)
            dq = dqt[h, :, sl].astype(bf16).astype(f32) * scale
            out_ref[chunk, 0, own, here] = dq.astype(bf16)
            out_ref[chunk, 1, own, here] = dkt[h, :, sl].astype(bf16)
            out_ref[chunk, 2, own, here] = dvt[h, :, sl].astype(bf16)


def attn_bwd(meta, scale, qkvt, grad, mixture, logsum, first, count):
    rows = lambda a: pl.BlockSpec((count * HD, TOK), lambda i, b: ((LH * a + first) // count, 0))
    return pl.pallas_call(
        bwd_kernel,
        out_shape=jax.ShapeDtypeStruct((PARTS, 3, count * HD, ROWS), bf16),
        grid_spec=pltpu.PrefetchScalarGridSpec(
            num_scalar_prefetch=1,
            grid=(1,),
            in_specs=[
                pl.BlockSpec((HD, 1), lambda i, b: (0, 0)),
                rows(0),
                rows(1),
                rows(2),
                *[pl.BlockSpec((PARTS, count * HD, g.shape[2]), lambda i, b: (0, first // count, 0)) for g in grad],
                pl.BlockSpec((PARTS, count * HD, ROWS), lambda i, b: (0, first // count, 0)),
                pl.BlockSpec((count, PARTS, 1, ROWS), lambda i, b: (first // count, 0, 0, 0)),
            ],
            out_specs=pl.BlockSpec((PARTS, 3, count * HD, ROWS), lambda i, b: (0, 0, 0, 0)),
            scratch_shapes=[pltpu.VMEM((count, TOK, 128), bf16)] * 2
            + [pltpu.VMEM((count, 128, TOK), bf16)] * 2
            + [pltpu.VMEM((count, HD, TOK), f32)] * 3,
        ),
        compiler_params=pltpu.CompilerParams(dimension_semantics=("arbitrary",), vmem_limit_bytes=60 << 20),
        cost_estimate=pl.CostEstimate(flops=count * 18 * 10**9, bytes_accessed=count * 8 << 20, transcendentals=0),
        name="attn_bwd",
    )(meta, scale, qkvt, qkvt, qkvt, *grad, mixture, logsum)


def mlp_kernel(meta, mixed_ref, rows_ref, cot_ref, gain_ref, out_ref, up_ref, down_ref, fd_ref, fu_ref, *refs, first):
    step = pl.program_id(0)
    if first:
        hidden_ref, inner_ref, middle_ref, grad_ref, g_ref, keep_ref, send_ref, sums = refs[-8:]
        sums[...] = refs[0][...]
    else:
        hidden_ref, inner_ref, middle_ref, grad_ref, g_ref, sums = refs

        @pl.when(step == 0)
        def _():
            sums[...] = jnp.zeros_like(sums)

    pos = meta[6] * ROWS + (first + step) * B + lax.broadcasted_iota(jnp.int32, (B, AR), 0)
    chosen = lax.broadcasted_iota(jnp.int32, (B, AR), 1) // RANK == token_adapter(pos, meta)
    choose = lambda x: jnp.where(chosen, x, 0.0).astype(bf16)
    gain = gain_ref[...]

    middle = rows_ref[...].astype(f32) + nn(mixed_ref[...].T, out_ref[...])
    middle_ref[...] = middle
    q = lax.rsqrt(jnp.mean(middle * middle, axis=1, keepdims=True) + EPSILON)
    normed = (middle * q * gain).astype(bf16)
    inner_up = choose(nn(normed, fd_ref[0]))
    before = nn(normed, up_ref[...]) + nn(inner_up, fu_ref[0])
    gate = jax.nn.sigmoid(before)
    hidden = (before * gate).astype(bf16)
    hidden_ref[...] = hidden
    inner_down = choose(nn(hidden, fd_ref[1]))
    inner_ref[...] = inner_down

    after = cot_ref[...]
    spread_down = choose(nt(after, fu_ref[1]))
    grad_hidden = nt(after, down_ref[...]) + nt(spread_down, fd_ref[1])
    grad_before = (grad_hidden * gate * (1.0 + before * (1.0 - gate))).astype(bf16)
    spread_up = choose(nt(grad_before, fu_ref[0]))
    weighted = gain * (nt(grad_before, up_ref[...]) + nt(spread_up, fd_ref[0]))
    middle = middle_ref[...]
    inside = jnp.mean(middle * weighted, axis=1, keepdims=True)
    grad_middle = after.astype(f32) + (q * weighted - middle * (q * q * q * inside))
    grad_ref[...] = grad_middle
    grad_mixed = nt(out_ref[...], grad_middle.astype(bf16)).astype(bf16)
    for s in range(PARTS):
        g_ref[s] = grad_mixed[s * WIDTH : (s + 1) * WIDTH]

    for n, (a, b) in enumerate(((spread_up, normed), (spread_down, hidden), (inner_up, grad_before), (inner_down, after))):
        sums[n] += nn(a.T, b)

    if first:
        for ref, half in ((keep_ref, meta[7]), (send_ref, 1 - meta[7])):
            for n in range(2):
                ref[n * AR : (n + 1) * AR, :] = sums[2 * half + n].astype(bf16)


def mlp(meta, mixed, rows, cotangent, gain, weights, flat_down, flat_up, first, sums=None, done=()):
    whole = lambda shape: pl.BlockSpec(shape, lambda i, m: (0,) * len(shape))
    block = lambda width: pl.BlockSpec((B, width), lambda i, m: (first + i, 0))
    tokens = mixed.shape[1]
    out_shape = [
        jax.ShapeDtypeStruct((ROWS, D), bf16),
        jax.ShapeDtypeStruct((ROWS, AR), bf16),
        jax.ShapeDtypeStruct((ROWS, D), f32),
        jax.ShapeDtypeStruct((ROWS, D), f32),
        jax.ShapeDtypeStruct((PARTS, WIDTH, tokens), bf16),
    ]
    out_specs = [block(D), block(AR), block(D), block(D), pl.BlockSpec((PARTS, WIDTH, B), lambda i, m: (0, 0, i))]
    if first:
        out_shape += [jax.ShapeDtypeStruct((2 * AR, D), bf16)] * 2
        out_specs += [whole((2 * AR, D))] * 2
        extra, extra_specs = [sums, *done], [whole((4, AR, D))] + [pl.BlockSpec(memory_space=pl.ANY)] * 4
        aliases, scratch = {11 + n: n for n in range(4)}, [pltpu.VMEM((4, AR, D), f32)]
    else:
        out_shape += [jax.ShapeDtypeStruct((4, AR, D), f32)]
        out_specs += [whole((4, AR, D))]
        extra, extra_specs, aliases, scratch = [], [], {}, []
    return pl.pallas_call(
        functools.partial(mlp_kernel, first=first),
        out_shape=out_shape,
        grid_spec=pltpu.PrefetchScalarGridSpec(
            num_scalar_prefetch=1,
            grid=(tokens // B,),
            in_specs=[
                pl.BlockSpec((D, B), lambda i, m: (0, i)),
                block(D),
                block(D),
                whole((1, D)),
                *[pl.BlockSpec((D, D), lambda i, m, a=a: (0, a)) for a in range(3)],
                whole((2, D, AR)),
                whole((2, AR, D)),
            ]
            + extra_specs,
            out_specs=out_specs,
            scratch_shapes=scratch,
        ),
        input_output_aliases=aliases,
        compiler_params=pltpu.CompilerParams(dimension_semantics=("arbitrary",), vmem_limit_bytes=60 << 20),
        cost_estimate=pl.CostEstimate(flops=tokens * 22 * 10**6, bytes_accessed=20 << 20, transcendentals=0),
        name="mlp",
    )(meta, mixed, rows, cotangent, gain, weights, weights, weights, flat_down, flat_up, *extra)


def exchange(value):
    return lax.all_to_all(value, "heads", split_axis=0, concat_axis=0, tiled=True)


def swap(value, axis, mask):
    count = lax.axis_size(axis)
    return lax.ppermute(value, axis, [(i, i ^ mask) for i in range(count)])


def piece(value, index, count):
    rows = value.shape[-2] // count
    return lax.dynamic_slice_in_dim(value, index * rows, rows, axis=value.ndim - 2)


def sum_low(*terms):
    total = terms[0].astype(f32)
    for term in terms[1:]:
        total = total + term.astype(f32)
    return total.astype(bf16)


def far_bits():
    bits = [2]
    while bits[-1] * 2 < lax.axis_size("fsdp"):
        bits.append(bits[-1] * 2)
    return bits


def sum_far(value):
    bits = far_bits()
    for bit, twice in zip(bits[0::2], bits[1::2]):
        value = sum_low(value, *[swap(value, "fsdp", m) for m in (bit, twice, bit | twice)])
    if len(bits) % 2:
        value = sum_low(value, swap(value, "fsdp", bits[-1]))
    return value


def scatter_near(value):
    core = lax.axis_index("fsdp") & 1
    return sum_low(piece(value, core, 2), swap(piece(value, 1 - core, 2), "fsdp", 1))


def scatter_heads(value):
    part = lax.axis_index("heads")
    terms = [swap(piece(value, part ^ m, PARTS), "heads", m) for m in (1, 2, 3)]
    return sum_low(piece(value, part, PARTS), *terms)


def body(
    inputs,
    cotangent,
    lengths,
    adapter_ids,
    query_weight,
    key_weight,
    value_weight,
    out_weight,
    up_weight,
    down_weight,
    attn_gain,
    mlp_gain,
    query_scale,
    adapter_in,
    adapter_out,
):
    part = lax.axis_index("heads")
    rows = inputs[0]
    low, high = rows[:HALF], rows[HALF:]
    near_high = swap(high, "heads", 1)
    far_low = swap(low, "heads", 2)
    ends = PROMPT + jnp.cumsum(lengths[0])
    bounds = ends[:2].astype(jnp.int32)
    ids = adapter_ids[0]
    core = lax.axis_index("fsdp") & 1
    meta = jnp.concatenate([bounds, ids, jnp.stack([part, core]).astype(jnp.int32)])
    flat_down = jnp.transpose(adapter_in, (0, 2, 1, 3)).reshape(4, D, AR)
    flat_up = adapter_out.reshape(4, AR, D)
    gain_attn = attn_gain.astype(f32)
    gain_mlp = mlp_gain.astype(f32)

    def mine(weight):
        return lax.dynamic_slice_in_dim(weight, part * WIDTH, WIDTH, axis=1)

    weights_mine = jnp.concatenate([mine(query_weight), mine(key_weight), mine(value_weight)], axis=1)
    weights_mine = lax.all_gather(weights_mine, "fsdp", axis=0, tiled=True)
    weights_mlp = lax.all_gather(jnp.concatenate([out_weight, up_weight, down_weight], axis=1), "fsdp", axis=0, tiled=True)
    weights_all = lax.all_gather(jnp.concatenate([query_weight, key_weight, value_weight], axis=1), "fsdp", axis=0, tiled=True)

    down_pair = jnp.concatenate([flat_down[0], flat_down[1]], axis=1)
    up_mine = lax.dynamic_slice_in_dim(flat_up[:2], part * WIDTH, WIDTH, axis=2)
    low_late, high_late, down_pair = lax.optimization_barrier((low, high, down_pair))
    near_low = swap(low_late, "heads", 1)
    far_high = swap(high_late, "heads", 2)
    both_low = swap(far_low, "heads", 1)
    both_high = swap(near_high, "heads", 2)
    scale_row = query_scale * HD ** (-0.5)
    scale_mine = jnp.tile(scale_row, LH)[:, None]

    wt, ut = weights_mine.T, jnp.transpose(up_mine, (0, 2, 1))
    done = ()
    for m, low, high in ((0, rows, None), (1, near_low, near_high), (2, far_low, far_high), (3, both_low, both_high)):
        done = qkv_project(meta, part ^ m, low, high, gain_attn[None, :], wt, down_pair, ut, scale_mine, done)
    qkvt, normed_all, inner_all = done
    head_mix, head_log = attn_fwd(bounds, qkvt, 2)
    mixed_head = exchange(head_mix)
    later, head_log = lax.optimization_barrier((bounds, head_log))
    tail_mix, tail_log = attn_fwd(later, qkvt, 1)
    tail_sent, mixed_head = lax.optimization_barrier((tail_mix, mixed_head))
    mixed_tail = exchange(tail_sent)
    up_mine, mixed_head = lax.optimization_barrier((up_mine, mixed_head))

    shared = (rows, cotangent[0], gain_mlp[None, :], weights_mlp, flat_down[2:], flat_up[2:])
    *done, grad_part, sums = mlp(meta, mixed_head.reshape(D, -1), *shared, 0)
    grad_head = exchange(grad_part)
    hidden_low, inner_down, middle, grad_middle, grad_part, mlp_keep, mlp_send = mlp(
        meta, mixed_tail.reshape(D, -1), *shared, 2, sums, done
    )
    mlp_keep, mlp_send, grad_part, grad_head = lax.optimization_barrier((mlp_keep, mlp_send, grad_part, grad_head))
    forward, grad_part = lax.optimization_barrier(((head_mix, tail_mix, head_log, tail_log), grad_part))
    grad_heads = (grad_head, exchange(grad_part))
    mixture = jnp.concatenate(forward[:2], axis=2)
    logsum = jnp.concatenate(forward[2:], axis=3)

    mlp_total = sum_low(mlp_keep, swap(mlp_send, "fsdp", 1))
    mlp_total, grad_heads = lax.optimization_barrier((mlp_total, grad_heads))
    mlp_total = scatter_heads(mlp_total)
    scale_column = scale_row[:, None]
    send_back = lambda g: exchange(g.reshape(PARTS, -1, ROWS)).reshape(g.shape)
    grads, arrived = [], []
    grads.append(attn_bwd(meta, scale_column, qkvt, grad_heads, mixture, logsum, 0, 2))
    mlp_total, grads[0] = lax.optimization_barrier((mlp_total, grads[0]))
    arrived.append(send_back(grads[0]))
    mlp_total = sum_far(mlp_total)
    meta, grads[0] = lax.optimization_barrier((meta, grads[0]))
    grads.append(attn_bwd(meta, scale_column, qkvt, grad_heads, mixture, logsum, 2, 2))
    mlp_total, grads[1] = lax.optimization_barrier((mlp_total, grads[1]))
    arrived.append(send_back(grads[1]))

    meta, arrived[0] = lax.optimization_barrier((meta, arrived[0]))
    keep, send = adapter_grads(meta, grads, normed_all, inner_all, up_mine)
    hidden_late, inner_late, keep = lax.optimization_barrier((hidden_low, inner_down, keep))
    outputs = (middle + (nn(hidden_late, weights_mlp[:, 2 * D :]) + nn(inner_late, flat_up[3]))).astype(bf16)
    total = sum_low(keep, swap(send, "fsdp", 1))
    total = jnp.concatenate([scatter_heads(total[:AR]), total[AR:]])
    total, arrived, outputs = lax.optimization_barrier((total, arrived, outputs))
    total = sum_far(total)
    meta, total = lax.optimization_barrier((meta, total))
    own = jnp.concatenate([total, mlp_total])
    pieces = [own] + [swap(own, "heads", m) for m in (1, 2, 3)]
    grad_inputs = back_inputs(meta, arrived, weights_all, flat_up[:2], down_pair, rows, gain_attn[None, :], grad_middle)
    pieces, grad_inputs = lax.optimization_barrier((pieces, grad_inputs))
    own = jnp.stack(pieces)
    grad_first, grad_second = assemble(meta, own, swap(own, "fsdp", 1))
    grad_first = jnp.transpose(grad_first.reshape(4, ADAPTERS, RANK, D), (0, 1, 3, 2))
    grad_second = grad_second.reshape(4, ADAPTERS, RANK, D)
    return (outputs[None], grad_inputs[None], grad_first, grad_second)


def solution(mesh):
    placed = (
        P("fsdp", "heads", None),
        P("fsdp", "heads", None),
        P("fsdp", None),
        P("fsdp", None),
        P("fsdp", None),
        P("fsdp", None),
        P("fsdp", None),
        P("fsdp", None),
        P("fsdp", None),
        P("fsdp", None),
        P(),
        P(),
        P(),
        P(),
        P(),
    )
    return jax.shard_map(
        body,
        mesh=mesh,
        in_specs=placed,
        out_specs=(P("fsdp", "heads", None), P("fsdp", "heads", None), P(), P()),
        check_vma=False,
    )
```

```python
import functools

import jax
import jax.numpy as jnp
from jax import lax
from jax.experimental import pallas as pl
from jax.experimental.pallas import tpu as pltpu
from jax.sharding import PartitionSpec as P

D = 1280
HEADS = 16
HD = 80
RANK = 16
ADAPTERS = 8
AR = ADAPTERS * RANK
TOK = 3072
PROMPT = 1536
ROWS = 768
QB = 256
PARTS = TOK // ROWS
LH = HEADS // PARTS
HALF = ROWS // 2
PH = LH // 2
PW = PH * HD
WIDTH = LH * HD
SR = WIDTH * 128 // D
EPSILON = 1e-06
B = 256
f32, bf16 = jnp.float32, jnp.bfloat16


def nt(a, b):
    return lax.dot_general(a, b, (((1,), (1,)), ((), ())), preferred_element_type=f32)


def tn(a, b):
    return lax.dot_general(a, b, (((0,), (0,)), ((), ())), preferred_element_type=f32)


def nn(a, b):
    return lax.dot_general(a, b, (((1,), (0,)), ((), ())), preferred_element_type=f32)

def start_row(qpos, b1, b2):
    return jnp.where(qpos < PROMPT, 0, jnp.where(qpos < b1, PROMPT, jnp.where(qpos < b2, b1, b2)))

def first_block(i, b1, b2):
    q0 = i * B
    return jnp.where(q0 < b1, PROMPT, jnp.where(q0 < b2, b1, b2)) // B


def token_adapter(pos, meta):
    return jnp.where(
        pos < PROMPT, meta[2], jnp.where(pos < meta[0], meta[3], jnp.where(pos < meta[1], meta[4], meta[5]))
    )


def qkv_kernel(meta, first, low_ref, high_ref, gain_ref, wt_ref, down_ref, up_ref, scale_ref, *refs):
    out_ref, normed_ref, inner_ref, rows = refs[-4:]
    step = pl.program_id(0)

    @pl.when(step == 0)
    def _():
        rows[0:HALF, :] = low_ref[...]
        rows[HALF:ROWS, :] = high_ref[...]

    x = rows[pl.ds(pl.multiple_of(step * QB, QB), QB), :].astype(f32)
    q = lax.rsqrt(jnp.mean(x * x, axis=1, keepdims=True) + EPSILON)
    normed = (x * q * gain_ref[...]).astype(bf16)
    normed_ref[...] = normed
    pos = (first[0] + step) * QB + lax.broadcasted_iota(jnp.int32, (QB, 1), 0)
    lane = lax.broadcasted_iota(jnp.int32, (QB, 2 * AR), 1)
    chosen = (lane % AR) // RANK == token_adapter(pos, meta)
    inner = jnp.where(chosen, nn(normed, down_ref[...]), 0.0).astype(bf16)
    inner_ref[...] = inner
    out = nt(wt_ref[...], normed)
    query = out[:WIDTH] + nt(up_ref[0], inner[:, :AR])
    out_ref[0:WIDTH, :] = (query * scale_ref[...]).astype(bf16)
    out_ref[WIDTH : 2 * WIDTH, :] = out[WIDTH : 2 * WIDTH].astype(bf16)
    out_ref[2 * WIDTH :, :] = (out[2 * WIDTH :] + nt(up_ref[1], inner[:, AR:])).astype(bf16)


def qkv_project(meta, chunk, low, high, gain, wt, down, up, scale, done):
    whole = lambda shape: pl.BlockSpec(shape, lambda i, *_: (0, 0))
    second = 1 if high is None else 0
    first = (chunk * (ROWS // QB))[None].astype(jnp.int32)
    return pl.pallas_call(
        qkv_kernel,
        out_shape=(
            jax.ShapeDtypeStruct((3 * WIDTH, TOK), bf16),
            jax.ShapeDtypeStruct((TOK, D), bf16),
            jax.ShapeDtypeStruct((TOK, 2 * AR), bf16),
        ),
        grid_spec=pltpu.PrefetchScalarGridSpec(
            num_scalar_prefetch=2,
            grid=(ROWS // QB,),
            in_specs=[
                whole((HALF, D)),
                pl.BlockSpec((HALF, D), lambda i, *_: (second, 0)),
                whole((1, D)),
                whole((3 * WIDTH, D)),
                whole((D, 2 * AR)),
                pl.BlockSpec((2, WIDTH, AR), lambda i, *_: (0, 0, 0)),
                whole((WIDTH, 1)),
            ]
            + [pl.BlockSpec(memory_space=pl.ANY)] * len(done),
            out_specs=[
                pl.BlockSpec((3 * WIDTH, QB), lambda i, m, first: (0, first[0] + i)),
                pl.BlockSpec((QB, D), lambda i, m, first: (first[0] + i, 0)),
                pl.BlockSpec((QB, 2 * AR), lambda i, m, first: (first[0] + i, 0)),
            ],
            scratch_shapes=[pltpu.VMEM((ROWS, D), bf16)],
        ),
        input_output_aliases={9 + i: i for i in range(len(done))},
        compiler_params=pltpu.CompilerParams(dimension_semantics=("arbitrary",), vmem_limit_bytes=60 << 20),
        cost_estimate=pl.CostEstimate(flops=2 * ROWS * D * (3 * WIDTH + 2 * AR), bytes_accessed=8 << 20, transcendentals=0),
        name="qkv_project",
    )(meta, first, low, low if high is None else high, gain, wt, down, up, scale, *done)


def adapter_kernel(meta, *refs):
    grad_refs, (normed_ref, inner_ref, up_ref, keep_ref, send_ref, facc, sacc) = refs[:-7], refs[-7:]
    step = pl.program_id(0)

    @pl.when(step == 0)
    def _():
        facc[...] = jnp.zeros_like(facc)
        sacc[...] = jnp.zeros_like(sacc)

    query = jnp.concatenate([ref[0, 0] for ref in grad_refs], axis=0)
    value = jnp.concatenate([ref[0, 2] for ref in grad_refs], axis=0)
    pos = step * ROWS + lax.broadcasted_iota(jnp.int32, (1, ROWS), 1)
    rank = lax.broadcasted_iota(jnp.int32, (AR, ROWS), 0)
    chosen = rank // RANK == token_adapter(pos, meta)
    for a, grad in enumerate((query, value)):
        spread = jnp.where(chosen, nn(up_ref[a], grad), 0.0).astype(bf16)
        facc[a] += nn(spread, normed_ref[...])
        sacc[a] += nn(grad, inner_ref[:, a * AR : (a + 1) * AR])

    @pl.when(step == PARTS - 1)
    def _():
        for ref, a in ((keep_ref, meta[7]), (send_ref, 1 - meta[7])):
            ref[0:AR, :] = facc[a].astype(bf16)
            for c in range(D // 128):
                ref[AR : AR + SR, c * 128 : (c + 1) * 128] = sacc[a, c * SR : (c + 1) * SR, :].astype(bf16)


def adapter_grads(meta, grads, normed, inner, up):
    return pl.pallas_call(
        adapter_kernel,
        out_shape=[jax.ShapeDtypeStruct((AR + SR, D), bf16)] * 2,
        grid_spec=pltpu.PrefetchScalarGridSpec(
            num_scalar_prefetch=1,
            grid=(PARTS,),
            in_specs=[pl.BlockSpec((1,) + g.shape[1:], lambda i, m: (i, 0, 0, 0)) for g in grads]
            + [
                pl.BlockSpec((ROWS, D), lambda i, m: (i, 0)),
                pl.BlockSpec((ROWS, 2 * AR), lambda i, m: (i, 0)),
                pl.BlockSpec((2, AR, WIDTH), lambda i, m: (0, 0, 0)),
            ],
            out_specs=[pl.BlockSpec((AR + SR, D), lambda i, m: (0, 0))] * 2,
            scratch_shapes=[pltpu.VMEM((2, AR, D), f32), pltpu.VMEM((2, WIDTH, AR), f32)],
        ),
        compiler_params=pltpu.CompilerParams(dimension_semantics=("arbitrary",), vmem_limit_bytes=60 << 20),
        cost_estimate=pl.CostEstimate(flops=4 * TOK * D * 2 * AR, bytes_accessed=20 << 20, transcendentals=0),
        name="adapter_grads",
    )(meta, *grads, normed, inner, up)


def back_kernel(meta, *refs):
    grad_refs, rest = refs[:-10], refs[-10:]
    w_ref, up_ref, down_ref, rows_ref, gain_ref, middle_ref, out_ref, cols, total, spread = rest
    step = pl.program_id(0)
    for s in range(PARTS):
        r = s * WIDTH
        for ref in grad_refs:
            cols[r : r + ref.shape[2], :] = ref[s, 0]
            r += ref.shape[2]

    part_sum = nn(w_ref[...], cols[...])

    @pl.when(step == 0)
    def _():
        total[...] = part_sum
        spread[0] = nn(up_ref[0], cols[...])

    @pl.when(step > 0)
    def _():
        total[...] += part_sum

    @pl.when(step == 2)
    def _():
        spread[1] = nn(up_ref[1], cols[...])
        pos = meta[6] * ROWS + lax.broadcasted_iota(jnp.int32, (1, ROWS), 1)
        rank = lax.broadcasted_iota(jnp.int32, (AR, ROWS), 0)
        chosen = rank // RANK == token_adapter(pos, meta)
        both = jnp.concatenate([jnp.where(chosen, spread[a], 0.0).astype(bf16) for a in range(2)], axis=0)
        total[...] += nn(down_ref[...], both)
        gain = gain_ref[...]
        for t in range(ROWS // 128):
            own = slice(t * 128, (t + 1) * 128)
            x = rows_ref[own, :].astype(f32)
            q = lax.rsqrt(jnp.mean(x * x, axis=1, keepdims=True) + EPSILON)
            weighted = gain * total[:, own].T
            inside = jnp.mean(x * weighted, axis=1, keepdims=True)
            out_ref[own, :] = middle_ref[own, :] + (q * weighted - x * (q * q * q * inside))


def back_inputs(meta, arrived, weights, up, down, rows, gain, grad_middle):
    whole = lambda shape: pl.BlockSpec(shape, lambda i, m: (0,) * len(shape))
    return pl.pallas_call(
        back_kernel,
        out_shape=jax.ShapeDtypeStruct((ROWS, D), f32),
        grid_spec=pltpu.PrefetchScalarGridSpec(
            num_scalar_prefetch=1,
            grid=(3,),
            in_specs=[pl.BlockSpec((PARTS, 1) + g.shape[2:], lambda i, m: (0, i, 0, 0)) for g in arrived]
            + [
                pl.BlockSpec((D, D), lambda i, m: (0, i)),
                whole((2, AR, D)),
                whole((D, 2 * AR)),
                whole((ROWS, D)),
                whole((1, D)),
                whole((ROWS, D)),
            ],
            out_specs=whole((ROWS, D)),
            scratch_shapes=[pltpu.VMEM((D, ROWS), bf16), pltpu.VMEM((D, ROWS), f32), pltpu.VMEM((2, AR, ROWS), f32)],
        ),
        compiler_params=pltpu.CompilerParams(dimension_semantics=("arbitrary",), vmem_limit_bytes=60 << 20),
        cost_estimate=pl.CostEstimate(flops=6 * ROWS * D * D, bytes_accessed=24 << 20, transcendentals=0),
        name="back_inputs",
    )(meta, *arrived, weights, up, down, rows, gain, grad_middle)


def assemble_kernel(meta, own_ref, other_ref, first_ref, second_ref, turned):
    part, core = meta[6], meta[7]
    for ref, a in ((own_ref, core), (other_ref, 1 - core)):
        for m in range(PARTS):
            where = part ^ m
            piece_rows = lambda n: pl.ds(pl.multiple_of(where * n, n), n)
            first_ref[a, piece_rows(SR), :] = ref[m, 0:SR, :].astype(f32)
            for c in range(D // 128):
                turned[pl.ds(pl.multiple_of(where * WIDTH + c * SR, SR), SR), :] = ref[m, SR : 2 * SR, c * 128 : (c + 1) * 128]
            rows = pl.ds(pl.multiple_of((where % 2) * 2 * SR, 2 * SR), 2 * SR)
            mlp = ref[m, 2 * SR :, :].astype(f32)

            @pl.when(a == 0)
            def _(mlp=mlp, rows=rows, where=where):
                first_ref[2 + where // 2, rows, :] = mlp

            @pl.when(a == 1)
            def _(mlp=mlp, rows=rows, where=where):
                second_ref[2 + where // 2, rows, :] = mlp

        for c in range(D // 128):
            second_ref[a, :, c * 128 : (c + 1) * 128] = turned[c * 128 : (c + 1) * 128, :].T.astype(f32)


def assemble(meta, own, other):
    whole = lambda shape: pl.BlockSpec(shape, lambda i, m: (0,) * len(shape))
    return pl.pallas_call(
        assemble_kernel,
        out_shape=[jax.ShapeDtypeStruct((4, AR, D), f32)] * 2,
        grid_spec=pltpu.PrefetchScalarGridSpec(
            num_scalar_prefetch=1,
            grid=(1,),
            in_specs=[whole((PARTS, 4 * SR, D))] * 2,
            out_specs=[whole((4, AR, D))] * 2,
            scratch_shapes=[pltpu.VMEM((D, AR), bf16)],
        ),
        compiler_params=pltpu.CompilerParams(dimension_semantics=("arbitrary",), vmem_limit_bytes=60 << 20),
        cost_estimate=pl.CostEstimate(flops=1 << 20, bytes_accessed=8 << 20, transcendentals=0),
        name="assemble",
    )(meta, own, other)


HPB = LH
BLOCKS = ROWS // B
NEG = -1e30
FW = 512


def fwd_kernel(bounds, q_ref, k_ref, v_ref, o_ref, lse_ref, kp, qt, vt):
    b1, b2 = bounds[0], bounds[1]
    zpad = jnp.zeros((128 - HD, 128), bf16)
    for h in range(HPB):
        own = slice(h * HD, (h + 1) * HD)
        qt[h, 0:HD, :] = q_ref[own, :]
        qt[h, HD:128, :] = jnp.zeros((128 - HD, TOK), bf16)
        vt[h, 0:HD, :] = v_ref[own, :]
        vt[h, HD:96, :] = (lax.broadcasted_iota(jnp.int32, (16, TOK), 0) == 0).astype(bf16)
        for t in range(TOK // 128):
            kt = k_ref[own, t * 128:(t + 1) * 128]
            kp[h, t * 128:(t + 1) * 128, :] = jnp.concatenate([kt, zpad], axis=0).T

    subs = o_ref.shape[2] // B
    base = 0 if subs > 1 else BLOCKS - 1

    def qblock(n, _):
        chunk, sub = n // subs, n % subs
        i = chunk * BLOCKS + base + sub
        q0 = pl.multiple_of(i * B, B)
        here = pl.ds(pl.multiple_of(sub * B, B), B)
        qpos = q0 + lax.broadcasted_iota(jnp.int32, (1, B), 1)
        srow = start_row(qpos, b1, b2)

        def step(k0, width, masked, carry):
            ks = pl.ds(k0, width)
            ss = [nn(kp[h, ks, :], qt[h, :, pl.ds(q0, B)]) for h in range(HPB)]
            if masked:
                kpos = k0 + lax.broadcasted_iota(jnp.int32, (width, B), 0)
                ok = (kpos >= srow) & (kpos <= qpos)
                ss = [jnp.where(ok, s, NEG) for s in ss]
            out = []
            for h in range(HPB):
                m, acc = carry[h]
                m_new = jnp.maximum(m, jnp.max(ss[h], axis=0, keepdims=True))
                p = jnp.exp(ss[h] - m_new).astype(bf16)
                a = jnp.exp(m - m_new)
                out.append((m_new, acc * a + nn(vt[h, :, ks], p)))
            return tuple(out)

        full = jnp.minimum(i * B // FW, PROMPT // FW)
        lo = jnp.where(i < PROMPT // B, (FW // B) * (i * B // FW), first_block(i, b1, b2))
        carry = tuple((jnp.full((1, B), NEG, f32), jnp.zeros((96, B), f32)) for _ in range(HPB))
        carry = lax.fori_loop(0, full, lambda j, c: step(pl.multiple_of(j * FW, FW), FW, False, c), carry)
        carry = lax.fori_loop(lo, i + 1, lambda j, c: step(pl.multiple_of(j * B, B), B, True, c), carry)
        for h in range(HPB):
            m, acc = carry[h]
            l = acc[HD:HD + 1, :]
            o_ref[chunk, h * HD:(h + 1) * HD, here] = (acc[0:HD, :] / l).astype(bf16)
            lse_ref[h, chunk, :, here] = m + jnp.log(l)
        return 0
    lax.fori_loop(0, PARTS * subs, qblock, 0)

def attn_fwd(bounds, qkvt, subs):
    rows = lambda a: pl.BlockSpec((WIDTH, TOK), lambda i, b: (a, 0))
    width = subs * B
    return pl.pallas_call(
        fwd_kernel,
        out_shape=(jax.ShapeDtypeStruct((PARTS, WIDTH, width), bf16), jax.ShapeDtypeStruct((LH, PARTS, 1, width), f32)),
        grid_spec=pltpu.PrefetchScalarGridSpec(
            num_scalar_prefetch=1,
            grid=(1,),
            in_specs=[rows(0), rows(1), rows(2)],
            out_specs=[
                pl.BlockSpec((PARTS, WIDTH, width), lambda i, b: (0, 0, 0)),
                pl.BlockSpec((LH, PARTS, 1, width), lambda i, b: (0, 0, 0, 0)),
            ],
            scratch_shapes=[pltpu.VMEM((HPB, TOK, 128), bf16), pltpu.VMEM((HPB, 128, TOK), bf16), pltpu.VMEM((HPB, 96, TOK), bf16)],
        ),
        compiler_params=pltpu.CompilerParams(dimension_semantics=("arbitrary",), vmem_limit_bytes=60 << 20),
        cost_estimate=pl.CostEstimate(flops=subs * 13 * 10**9, bytes_accessed=5 << 20, transcendentals=0),
        name="attn_fwd",
    )(bounds, qkvt, qkvt, qkvt)


def parts3(x):
    hi = x.astype(bf16)
    r = x - hi.astype(f32)
    mid = r.astype(bf16)
    lo = (r - mid.astype(f32)).astype(bf16)
    return hi, mid, lo

def bwd_kernel(meta, scale_ref, q_ref, k_ref, v_ref, head_ref, tail_ref, o_ref, lse_ref, out_ref, kp, vp, qt, dot, dkt, dvt, dqt):
    NH = kp.shape[0]
    b1, b2 = meta[0], meta[1]
    row16 = lax.broadcasted_iota(jnp.int32, (16, 128), 0)
    ones3 = (row16 < 3).astype(bf16)
    pad = jnp.zeros((32, 128), bf16)
    scale = scale_ref[...]

    def tail(x):
        hi, mid, lo = parts3(-x)
        rest = jnp.where(row16 == 1, mid.astype(f32), jnp.where(row16 == 2, lo.astype(f32), 0.0))
        return jnp.where(row16 == 0, hi.astype(f32), rest).astype(bf16)

    @pl.loop(0, PARTS)
    def _(chunk):
        for off in range(0, ROWS, 128):
            sl, here = pl.ds(pl.multiple_of(chunk * ROWS + off, 128), 128), slice(off, off + 128)
            grad_ref, start = (head_ref, off) if off < 2 * B else (tail_ref, off - 2 * B)
            for h in range(NH):
                own = slice(h * HD, (h + 1) * HD)
                do, o = grad_ref[chunk, own, start : start + 128], o_ref[chunk, own, here]
                delta = jnp.sum(do.astype(f32) * o.astype(f32), axis=0, keepdims=True)
                qt[h, :, sl] = jnp.concatenate([q_ref[own, sl], tail(lse_ref[h, chunk, :, here]), pad], axis=0)
                dot[h, :, sl] = jnp.concatenate([do, tail(delta), pad], axis=0)
                kp[h, sl, :] = jnp.concatenate([k_ref[own, sl], ones3, pad], axis=0).T
                vp[h, sl, :] = jnp.concatenate([v_ref[own, sl], ones3, pad], axis=0).T

    dkt[...] = jnp.zeros_like(dkt)
    dvt[...] = jnp.zeros_like(dvt)
    dqt[...] = jnp.zeros_like(dqt)

    def block(k0, q0, kw, qw, masked):
        k0, q0 = pl.multiple_of(k0, B), pl.multiple_of(q0, B)
        ks, qs = pl.ds(k0, kw), pl.ds(q0, qw)
        if masked:
            qpos = q0 + lax.broadcasted_iota(jnp.int32, (1, qw), 1)
            kpos = k0 + lax.broadcasted_iota(jnp.int32, (kw, qw), 0)
            ok = (kpos >= start_row(qpos, b1, b2)) & (kpos <= qpos)
        for h in range(NH):
            p = jnp.exp(nn(kp[h, ks, :], qt[h, :, qs]))
            if masked:
                p = jnp.where(ok, p, 0.0)
            ds = (p * nn(vp[h, ks, :], dot[h, :, qs])).astype(bf16)
            dvt[h, :, ks] += nt(dot[h, 0:HD, qs], p.astype(bf16))
            dkt[h, :, ks] += nt(qt[h, 0:HD, qs], ds)
            dqt[h, :, qs] += nn(k_ref[h * HD : (h + 1) * HD, ks], ds)

    @pl.loop(0, 12)
    def _(n):
        qb = jnp.where(n < 9, 3 + n // 3, jnp.where(n == 9, 1, 2))
        kb = jnp.where(n < 9, n % 3, jnp.where(n == 11, 1, 0))
        block(kb * FW, qb * FW, FW, FW, False)

    @pl.loop(0, TOK // FW)
    def _(i):
        lo = jnp.where(i < PROMPT // FW, i, first_block(i * (FW // B), b1, b2) * B // FW)

        @pl.loop(lo, i + 1)
        def _(j):
            block(j * FW, i * FW, FW, FW, True)

    @pl.loop(0, 2 * PARTS)
    def _(step):
        chunk = step // 2
        off = pl.multiple_of((step % 2) * HALF, 128)
        sl, here = pl.ds(pl.multiple_of(chunk * ROWS + off, 128), HALF), pl.ds(off, HALF)
        for h in range(NH):
            own = slice(h * HD, (h + 1) * HD)
            dq = dqt[h, :, sl].astype(bf16).astype(f32) * scale
            out_ref[chunk, 0, own, here] = dq.astype(bf16)
            out_ref[chunk, 1, own, here] = dkt[h, :, sl].astype(bf16)
            out_ref[chunk, 2, own, here] = dvt[h, :, sl].astype(bf16)


def attn_bwd(meta, scale, qkvt, grad, mixture, logsum, first, count):
    rows = lambda a: pl.BlockSpec((count * HD, TOK), lambda i, b: ((LH * a + first) // count, 0))
    return pl.pallas_call(
        bwd_kernel,
        out_shape=jax.ShapeDtypeStruct((PARTS, 3, count * HD, ROWS), bf16),
        grid_spec=pltpu.PrefetchScalarGridSpec(
            num_scalar_prefetch=1,
            grid=(1,),
            in_specs=[
                pl.BlockSpec((HD, 1), lambda i, b: (0, 0)),
                rows(0),
                rows(1),
                rows(2),
                *[pl.BlockSpec((PARTS, count * HD, g.shape[2]), lambda i, b: (0, first // count, 0)) for g in grad],
                pl.BlockSpec((PARTS, count * HD, ROWS), lambda i, b: (0, first // count, 0)),
                pl.BlockSpec((count, PARTS, 1, ROWS), lambda i, b: (first // count, 0, 0, 0)),
            ],
            out_specs=pl.BlockSpec((PARTS, 3, count * HD, ROWS), lambda i, b: (0, 0, 0, 0)),
            scratch_shapes=[pltpu.VMEM((count, TOK, 128), bf16)] * 2
            + [pltpu.VMEM((count, 128, TOK), bf16)] * 2
            + [pltpu.VMEM((count, HD, TOK), f32)] * 3,
        ),
        compiler_params=pltpu.CompilerParams(dimension_semantics=("arbitrary",), vmem_limit_bytes=60 << 20),
        cost_estimate=pl.CostEstimate(flops=count * 18 * 10**9, bytes_accessed=count * 8 << 20, transcendentals=0),
        name="attn_bwd",
    )(meta, scale, qkvt, qkvt, qkvt, *grad, mixture, logsum)


def mlp_kernel(meta, mixed_ref, rows_ref, cot_ref, gain_ref, out_ref, up_ref, down_ref, fd_ref, fu_ref, *refs, first):
    step = pl.program_id(0)
    if first:
        hidden_ref, inner_ref, middle_ref, grad_ref, g_ref, keep_ref, send_ref, sums = refs[-8:]
        sums[...] = refs[0][...]
    else:
        hidden_ref, inner_ref, middle_ref, grad_ref, g_ref, sums = refs

        @pl.when(step == 0)
        def _():
            sums[...] = jnp.zeros_like(sums)

    pos = meta[6] * ROWS + (first + step) * B + lax.broadcasted_iota(jnp.int32, (B, AR), 0)
    chosen = lax.broadcasted_iota(jnp.int32, (B, AR), 1) // RANK == token_adapter(pos, meta)
    choose = lambda x: jnp.where(chosen, x, 0.0).astype(bf16)
    gain = gain_ref[...]

    middle = rows_ref[...].astype(f32) + nn(mixed_ref[...].T, out_ref[...])
    middle_ref[...] = middle
    q = lax.rsqrt(jnp.mean(middle * middle, axis=1, keepdims=True) + EPSILON)
    normed = (middle * q * gain).astype(bf16)
    inner_up = choose(nn(normed, fd_ref[0]))
    before = nn(normed, up_ref[...]) + nn(inner_up, fu_ref[0])
    gate = jax.nn.sigmoid(before)
    hidden = (before * gate).astype(bf16)
    hidden_ref[...] = hidden
    inner_down = choose(nn(hidden, fd_ref[1]))
    inner_ref[...] = inner_down

    after = cot_ref[...]
    spread_down = choose(nt(after, fu_ref[1]))
    grad_hidden = nt(after, down_ref[...]) + nt(spread_down, fd_ref[1])
    grad_before = (grad_hidden * gate * (1.0 + before * (1.0 - gate))).astype(bf16)
    spread_up = choose(nt(grad_before, fu_ref[0]))
    weighted = gain * (nt(grad_before, up_ref[...]) + nt(spread_up, fd_ref[0]))
    middle = middle_ref[...]
    inside = jnp.mean(middle * weighted, axis=1, keepdims=True)
    grad_middle = after.astype(f32) + (q * weighted - middle * (q * q * q * inside))
    grad_ref[...] = grad_middle
    grad_mixed = nt(out_ref[...], grad_middle.astype(bf16)).astype(bf16)
    for s in range(PARTS):
        g_ref[s] = grad_mixed[s * WIDTH : (s + 1) * WIDTH]

    for n, (a, b) in enumerate(((spread_up, normed), (spread_down, hidden), (inner_up, grad_before), (inner_down, after))):
        sums[n] += nn(a.T, b)

    if first:
        for ref, half in ((keep_ref, meta[7]), (send_ref, 1 - meta[7])):
            for n in range(2):
                ref[n * AR : (n + 1) * AR, :] = sums[2 * half + n].astype(bf16)


def mlp(meta, mixed, rows, cotangent, gain, weights, flat_down, flat_up, first, sums=None, done=()):
    whole = lambda shape: pl.BlockSpec(shape, lambda i, m: (0,) * len(shape))
    block = lambda width: pl.BlockSpec((B, width), lambda i, m: (first + i, 0))
    tokens = mixed.shape[1]
    out_shape = [
        jax.ShapeDtypeStruct((ROWS, D), bf16),
        jax.ShapeDtypeStruct((ROWS, AR), bf16),
        jax.ShapeDtypeStruct((ROWS, D), f32),
        jax.ShapeDtypeStruct((ROWS, D), f32),
        jax.ShapeDtypeStruct((PARTS, WIDTH, tokens), bf16),
    ]
    out_specs = [block(D), block(AR), block(D), block(D), pl.BlockSpec((PARTS, WIDTH, B), lambda i, m: (0, 0, i))]
    if first:
        out_shape += [jax.ShapeDtypeStruct((2 * AR, D), bf16)] * 2
        out_specs += [whole((2 * AR, D))] * 2
        extra, extra_specs = [sums, *done], [whole((4, AR, D))] + [pl.BlockSpec(memory_space=pl.ANY)] * 4
        aliases, scratch = {11 + n: n for n in range(4)}, [pltpu.VMEM((4, AR, D), f32)]
    else:
        out_shape += [jax.ShapeDtypeStruct((4, AR, D), f32)]
        out_specs += [whole((4, AR, D))]
        extra, extra_specs, aliases, scratch = [], [], {}, []
    return pl.pallas_call(
        functools.partial(mlp_kernel, first=first),
        out_shape=out_shape,
        grid_spec=pltpu.PrefetchScalarGridSpec(
            num_scalar_prefetch=1,
            grid=(tokens // B,),
            in_specs=[
                pl.BlockSpec((D, B), lambda i, m: (0, i)),
                block(D),
                block(D),
                whole((1, D)),
                *[pl.BlockSpec((D, D), lambda i, m, a=a: (0, a)) for a in range(3)],
                whole((2, D, AR)),
                whole((2, AR, D)),
            ]
            + extra_specs,
            out_specs=out_specs,
            scratch_shapes=scratch,
        ),
        input_output_aliases=aliases,
        compiler_params=pltpu.CompilerParams(dimension_semantics=("arbitrary",), vmem_limit_bytes=60 << 20),
        cost_estimate=pl.CostEstimate(flops=tokens * 22 * 10**6, bytes_accessed=20 << 20, transcendentals=0),
        name="mlp",
    )(meta, mixed, rows, cotangent, gain, weights, weights, weights, flat_down, flat_up, *extra)


def exchange(value):
    return lax.all_to_all(value, "heads", split_axis=0, concat_axis=0, tiled=True)


def swap(value, axis, mask):
    count = lax.axis_size(axis)
    return lax.ppermute(value, axis, [(i, i ^ mask) for i in range(count)])


def piece(value, index, count):
    rows = value.shape[-2] // count
    return lax.dynamic_slice_in_dim(value, index * rows, rows, axis=value.ndim - 2)


def sum_low(*terms):
    total = terms[0].astype(f32)
    for term in terms[1:]:
        total = total + term.astype(f32)
    return total.astype(bf16)


def far_bits():
    bits = [2]
    while bits[-1] * 2 < lax.axis_size("fsdp"):
        bits.append(bits[-1] * 2)
    return bits


def sum_far(value):
    bits = far_bits()
    for bit, twice in zip(bits[0::2], bits[1::2]):
        value = sum_low(value, *[swap(value, "fsdp", m) for m in (bit, twice, bit | twice)])
    if len(bits) % 2:
        value = sum_low(value, swap(value, "fsdp", bits[-1]))
    return value


def scatter_near(value):
    core = lax.axis_index("fsdp") & 1
    return sum_low(piece(value, core, 2), swap(piece(value, 1 - core, 2), "fsdp", 1))


def scatter_heads(value):
    part = lax.axis_index("heads")
    terms = [swap(piece(value, part ^ m, PARTS), "heads", m) for m in (1, 2, 3)]
    return sum_low(piece(value, part, PARTS), *terms)


def body(
    inputs,
    cotangent,
    lengths,
    adapter_ids,
    query_weight,
    key_weight,
    value_weight,
    out_weight,
    up_weight,
    down_weight,
    attn_gain,
    mlp_gain,
    query_scale,
    adapter_in,
    adapter_out,
):
    part = lax.axis_index("heads")
    rows = inputs[0]
    low, high = rows[:HALF], rows[HALF:]
    near_high = swap(high, "heads", 1)
    far_low = swap(low, "heads", 2)
    ends = PROMPT + jnp.cumsum(lengths[0])
    bounds = ends[:2].astype(jnp.int32)
    ids = adapter_ids[0]
    core = lax.axis_index("fsdp") & 1
    meta = jnp.concatenate([bounds, ids, jnp.stack([part, core]).astype(jnp.int32)])
    flat_down = jnp.transpose(adapter_in, (0, 2, 1, 3)).reshape(4, D, AR)
    flat_up = adapter_out.reshape(4, AR, D)
    gain_attn = attn_gain.astype(f32)
    gain_mlp = mlp_gain.astype(f32)

    def mine(weight):
        return lax.dynamic_slice_in_dim(weight, part * WIDTH, WIDTH, axis=1)

    weights_mine = jnp.concatenate([mine(query_weight), mine(key_weight), mine(value_weight)], axis=1)
    weights_mine = lax.all_gather(weights_mine, "fsdp", axis=0, tiled=True)
    weights_mlp = lax.all_gather(jnp.concatenate([out_weight, up_weight, down_weight], axis=1), "fsdp", axis=0, tiled=True)
    weights_all = lax.all_gather(jnp.concatenate([query_weight, key_weight, value_weight], axis=1), "fsdp", axis=0, tiled=True)

    down_pair = jnp.concatenate([flat_down[0], flat_down[1]], axis=1)
    up_mine = lax.dynamic_slice_in_dim(flat_up[:2], part * WIDTH, WIDTH, axis=2)
    low_late, high_late, down_pair = lax.optimization_barrier((low, high, down_pair))
    near_low = swap(low_late, "heads", 1)
    far_high = swap(high_late, "heads", 2)
    both_low = swap(far_low, "heads", 1)
    both_high = swap(near_high, "heads", 2)
    scale_row = query_scale * HD ** (-0.5)
    scale_mine = jnp.tile(scale_row, LH)[:, None]

    wt, ut = weights_mine.T, jnp.transpose(up_mine, (0, 2, 1))
    done = ()
    for m, low, high in ((0, rows, None), (1, near_low, near_high), (2, far_low, far_high), (3, both_low, both_high)):
        done = qkv_project(meta, part ^ m, low, high, gain_attn[None, :], wt, down_pair, ut, scale_mine, done)
    qkvt, normed_all, inner_all = done
    head_mix, head_log = attn_fwd(bounds, qkvt, 2)
    mixed_head = exchange(head_mix)
    later, head_log = lax.optimization_barrier((bounds, head_log))
    tail_mix, tail_log = attn_fwd(later, qkvt, 1)
    tail_sent, mixed_head = lax.optimization_barrier((tail_mix, mixed_head))
    mixed_tail = exchange(tail_sent)
    up_mine, mixed_head = lax.optimization_barrier((up_mine, mixed_head))

    shared = (rows, cotangent[0], gain_mlp[None, :], weights_mlp, flat_down[2:], flat_up[2:])
    *done, grad_part, sums = mlp(meta, mixed_head.reshape(D, -1), *shared, 0)
    grad_head = exchange(grad_part)
    hidden_low, inner_down, middle, grad_middle, grad_part, mlp_keep, mlp_send = mlp(
        meta, mixed_tail.reshape(D, -1), *shared, 2, sums, done
    )
    mlp_keep, mlp_send, grad_part, grad_head = lax.optimization_barrier((mlp_keep, mlp_send, grad_part, grad_head))
    forward, grad_part = lax.optimization_barrier(((head_mix, tail_mix, head_log, tail_log), grad_part))
    grad_heads = (grad_head, exchange(grad_part))
    mixture = jnp.concatenate(forward[:2], axis=2)
    logsum = jnp.concatenate(forward[2:], axis=3)

    mlp_total = sum_low(mlp_keep, swap(mlp_send, "fsdp", 1))
    mlp_total, grad_heads = lax.optimization_barrier((mlp_total, grad_heads))
    mlp_total = scatter_heads(mlp_total)
    scale_column = scale_row[:, None]
    send_back = lambda g: exchange(g.reshape(PARTS, -1, ROWS)).reshape(g.shape)
    grads, arrived = [], []
    grads.append(attn_bwd(meta, scale_column, qkvt, grad_heads, mixture, logsum, 0, 2))
    mlp_total, grads[0] = lax.optimization_barrier((mlp_total, grads[0]))
    arrived.append(send_back(grads[0]))
    mlp_total = sum_far(mlp_total)
    meta, grads[0] = lax.optimization_barrier((meta, grads[0]))
    grads.append(attn_bwd(meta, scale_column, qkvt, grad_heads, mixture, logsum, 2, 2))
    mlp_total, grads[1] = lax.optimization_barrier((mlp_total, grads[1]))

    meta, arrived[0] = lax.optimization_barrier((meta, arrived[0]))
    keep, send = adapter_grads(meta, grads, normed_all, inner_all, up_mine)
    hidden_late, inner_late, keep = lax.optimization_barrier((hidden_low, inner_down, keep))
    outputs = (middle + (nn(hidden_late, weights_mlp[:, 2 * D :]) + nn(inner_late, flat_up[3]))).astype(bf16)
    total = sum_low(keep, swap(send, "fsdp", 1))
    total = jnp.concatenate([scatter_heads(total[:AR]), total[AR:]])
    total, sent = lax.optimization_barrier((total, grads[1]))
    arrived.append(send_back(sent))
    total, outputs = lax.optimization_barrier((sum_far(total), outputs))
    own = jnp.concatenate([total, mlp_total])
    pieces = [own] + [swap(own, "heads", m) for m in (1, 2, 3)]
    grad_inputs = back_inputs(meta, arrived, weights_all, flat_up[:2], down_pair, rows, gain_attn[None, :], grad_middle)
    pieces, grad_inputs = lax.optimization_barrier((pieces, grad_inputs))
    own = jnp.stack(pieces)
    grad_first, grad_second = assemble(meta, own, swap(own, "fsdp", 1))
    grad_first = jnp.transpose(grad_first.reshape(4, ADAPTERS, RANK, D), (0, 1, 3, 2))
    grad_second = grad_second.reshape(4, ADAPTERS, RANK, D)
    return (outputs[None], grad_inputs[None], grad_first, grad_second)


def solution(mesh):
    placed = (
        P("fsdp", "heads", None),
        P("fsdp", "heads", None),
        P("fsdp", None),
        P("fsdp", None),
        P("fsdp", None),
        P("fsdp", None),
        P("fsdp", None),
        P("fsdp", None),
        P("fsdp", None),
        P("fsdp", None),
        P(),
        P(),
        P(),
        P(),
        P(),
    )
    return jax.shard_map(
        body,
        mesh=mesh,
        in_specs=placed,
        out_specs=(P("fsdp", "heads", None), P("fsdp", "heads", None), P(), P()),
        check_vma=False,
    )
```

```python
import jax
import jax.numpy as jnp
from jax import lax
from jax.experimental import pallas as pl
from jax.experimental.pallas import tpu as pltpu
from jax.sharding import PartitionSpec as P

D = 1280
HEADS = 16
HD = 80
RANK = 16
ADAPTERS = 8
AR = ADAPTERS * RANK
TOK = 3072
PROMPT = 1536
ROWS = 768
QB = 256
PARTS = TOK // ROWS
LH = HEADS // PARTS
HALF = ROWS // 2
PH = LH // 2
PW = PH * HD
WIDTH = LH * HD
SR = WIDTH * 128 // D
EPSILON = 1e-06
B = 256
f32, bf16 = jnp.float32, jnp.bfloat16


def nt(a, b):
    return lax.dot_general(a, b, (((1,), (1,)), ((), ())), preferred_element_type=f32)


def tn(a, b):
    return lax.dot_general(a, b, (((0,), (0,)), ((), ())), preferred_element_type=f32)


def nn(a, b):
    return lax.dot_general(a, b, (((1,), (0,)), ((), ())), preferred_element_type=f32)

def start_row(qpos, b1, b2):
    return jnp.where(qpos < PROMPT, 0, jnp.where(qpos < b1, PROMPT, jnp.where(qpos < b2, b1, b2)))

def first_block(i, b1, b2):
    q0 = i * B
    return jnp.where(q0 < b1, PROMPT, jnp.where(q0 < b2, b1, b2)) // B


def token_adapter(pos, meta):
    return jnp.where(
        pos < PROMPT, meta[2], jnp.where(pos < meta[0], meta[3], jnp.where(pos < meta[1], meta[4], meta[5]))
    )


def qkv_kernel(meta, first, low_ref, high_ref, gain_ref, wt_ref, down_ref, up_ref, scale_ref, *refs):
    out_ref, normed_ref, inner_ref, rows = refs[-4:]
    step = pl.program_id(0)

    @pl.when(step == 0)
    def _():
        rows[0:HALF, :] = low_ref[...]
        rows[HALF:ROWS, :] = high_ref[...]

    x = rows[pl.ds(pl.multiple_of(step * QB, QB), QB), :].astype(f32)
    q = lax.rsqrt(jnp.mean(x * x, axis=1, keepdims=True) + EPSILON)
    normed = (x * q * gain_ref[...]).astype(bf16)
    normed_ref[...] = normed
    pos = (first[0] + step) * QB + lax.broadcasted_iota(jnp.int32, (QB, 1), 0)
    lane = lax.broadcasted_iota(jnp.int32, (QB, 2 * AR), 1)
    chosen = (lane % AR) // RANK == token_adapter(pos, meta)
    inner = jnp.where(chosen, nn(normed, down_ref[...]), 0.0).astype(bf16)
    inner_ref[...] = inner
    out = nt(wt_ref[...], normed)
    query = out[:WIDTH] + nt(up_ref[0], inner[:, :AR])
    out_ref[0:WIDTH, :] = (query * scale_ref[...]).astype(bf16)
    out_ref[WIDTH : 2 * WIDTH, :] = out[WIDTH : 2 * WIDTH].astype(bf16)
    out_ref[2 * WIDTH :, :] = (out[2 * WIDTH :] + nt(up_ref[1], inner[:, AR:])).astype(bf16)


def qkv_project(meta, chunk, low, high, gain, wt, down, up, scale, done):
    whole = lambda shape: pl.BlockSpec(shape, lambda i, *_: (0, 0))
    second = 1 if high is None else 0
    first = (chunk * (ROWS // QB))[None].astype(jnp.int32)
    return pl.pallas_call(
        qkv_kernel,
        out_shape=(
            jax.ShapeDtypeStruct((3 * WIDTH, TOK), bf16),
            jax.ShapeDtypeStruct((TOK, D), bf16),
            jax.ShapeDtypeStruct((TOK, 2 * AR), bf16),
        ),
        grid_spec=pltpu.PrefetchScalarGridSpec(
            num_scalar_prefetch=2,
            grid=(ROWS // QB,),
            in_specs=[
                whole((HALF, D)),
                pl.BlockSpec((HALF, D), lambda i, *_: (second, 0)),
                whole((1, D)),
                whole((3 * WIDTH, D)),
                whole((D, 2 * AR)),
                pl.BlockSpec((2, WIDTH, AR), lambda i, *_: (0, 0, 0)),
                whole((WIDTH, 1)),
            ]
            + [pl.BlockSpec(memory_space=pl.ANY)] * len(done),
            out_specs=[
                pl.BlockSpec((3 * WIDTH, QB), lambda i, m, first: (0, first[0] + i)),
                pl.BlockSpec((QB, D), lambda i, m, first: (first[0] + i, 0)),
                pl.BlockSpec((QB, 2 * AR), lambda i, m, first: (first[0] + i, 0)),
            ],
            scratch_shapes=[pltpu.VMEM((ROWS, D), bf16)],
        ),
        input_output_aliases={9 + i: i for i in range(len(done))},
        compiler_params=pltpu.CompilerParams(dimension_semantics=("arbitrary",), vmem_limit_bytes=60 << 20),
        cost_estimate=pl.CostEstimate(flops=2 * ROWS * D * (3 * WIDTH + 2 * AR), bytes_accessed=8 << 20, transcendentals=0),
        name="qkv_project",
    )(meta, first, low, low if high is None else high, gain, wt, down, up, scale, *done)


def adapter_kernel(meta, *refs):
    grad_refs, (normed_ref, inner_ref, up_ref, keep_ref, send_ref, facc, sacc) = refs[:-7], refs[-7:]
    step = pl.program_id(0)

    @pl.when(step == 0)
    def _():
        facc[...] = jnp.zeros_like(facc)
        sacc[...] = jnp.zeros_like(sacc)

    query = jnp.concatenate([ref[0, 0] for ref in grad_refs], axis=0)
    value = jnp.concatenate([ref[0, 2] for ref in grad_refs], axis=0)
    pos = step * ROWS + lax.broadcasted_iota(jnp.int32, (1, ROWS), 1)
    rank = lax.broadcasted_iota(jnp.int32, (AR, ROWS), 0)
    chosen = rank // RANK == token_adapter(pos, meta)
    for a, grad in enumerate((query, value)):
        spread = jnp.where(chosen, nn(up_ref[a], grad), 0.0).astype(bf16)
        facc[a] += nn(spread, normed_ref[...])
        sacc[a] += nn(grad, inner_ref[:, a * AR : (a + 1) * AR])

    @pl.when(step == PARTS - 1)
    def _():
        for ref, a in ((keep_ref, meta[7]), (send_ref, 1 - meta[7])):
            ref[0:AR, :] = facc[a].astype(bf16)
            for c in range(D // 128):
                ref[AR : AR + SR, c * 128 : (c + 1) * 128] = sacc[a, c * SR : (c + 1) * SR, :].astype(bf16)


def adapter_grads(meta, grads, normed, inner, up):
    return pl.pallas_call(
        adapter_kernel,
        out_shape=[jax.ShapeDtypeStruct((AR + SR, D), bf16)] * 2,
        grid_spec=pltpu.PrefetchScalarGridSpec(
            num_scalar_prefetch=1,
            grid=(PARTS,),
            in_specs=[pl.BlockSpec((1,) + g.shape[1:], lambda i, m: (i, 0, 0, 0)) for g in grads]
            + [
                pl.BlockSpec((ROWS, D), lambda i, m: (i, 0)),
                pl.BlockSpec((ROWS, 2 * AR), lambda i, m: (i, 0)),
                pl.BlockSpec((2, AR, WIDTH), lambda i, m: (0, 0, 0)),
            ],
            out_specs=[pl.BlockSpec((AR + SR, D), lambda i, m: (0, 0))] * 2,
            scratch_shapes=[pltpu.VMEM((2, AR, D), f32), pltpu.VMEM((2, WIDTH, AR), f32)],
        ),
        compiler_params=pltpu.CompilerParams(dimension_semantics=("arbitrary",), vmem_limit_bytes=60 << 20),
        cost_estimate=pl.CostEstimate(flops=4 * TOK * D * 2 * AR, bytes_accessed=20 << 20, transcendentals=0),
        name="adapter_grads",
    )(meta, *grads, normed, inner, up)


def back_kernel(meta, *refs):
    grad_refs, rest = refs[:-10], refs[-10:]
    w_ref, up_ref, down_ref, rows_ref, gain_ref, middle_ref, out_ref, cols, total, spread = rest
    step = pl.program_id(0)
    for s in range(PARTS):
        r = s * WIDTH
        for ref in grad_refs:
            cols[r : r + ref.shape[2], :] = ref[s, 0]
            r += ref.shape[2]

    part_sum = nn(w_ref[...], cols[...])

    @pl.when(step == 0)
    def _():
        total[...] = part_sum
        spread[0] = nn(up_ref[0], cols[...])

    @pl.when(step > 0)
    def _():
        total[...] += part_sum

    @pl.when(step == 2)
    def _():
        spread[1] = nn(up_ref[1], cols[...])
        pos = meta[6] * ROWS + lax.broadcasted_iota(jnp.int32, (1, ROWS), 1)
        rank = lax.broadcasted_iota(jnp.int32, (AR, ROWS), 0)
        chosen = rank // RANK == token_adapter(pos, meta)
        both = jnp.concatenate([jnp.where(chosen, spread[a], 0.0).astype(bf16) for a in range(2)], axis=0)
        total[...] += nn(down_ref[...], both)
        gain = gain_ref[...]
        for t in range(ROWS // 128):
            own = slice(t * 128, (t + 1) * 128)
            x = rows_ref[own, :].astype(f32)
            q = lax.rsqrt(jnp.mean(x * x, axis=1, keepdims=True) + EPSILON)
            weighted = gain * total[:, own].T
            inside = jnp.mean(x * weighted, axis=1, keepdims=True)
            out_ref[own, :] = middle_ref[own, :] + (q * weighted - x * (q * q * q * inside))


def back_inputs(meta, arrived, weights, up, down, rows, gain, grad_middle):
    whole = lambda shape: pl.BlockSpec(shape, lambda i, m: (0,) * len(shape))
    return pl.pallas_call(
        back_kernel,
        out_shape=jax.ShapeDtypeStruct((ROWS, D), f32),
        grid_spec=pltpu.PrefetchScalarGridSpec(
            num_scalar_prefetch=1,
            grid=(3,),
            in_specs=[pl.BlockSpec((PARTS, 1) + g.shape[2:], lambda i, m: (0, i, 0, 0)) for g in arrived]
            + [
                pl.BlockSpec((D, D), lambda i, m: (0, i)),
                whole((2, AR, D)),
                whole((D, 2 * AR)),
                whole((ROWS, D)),
                whole((1, D)),
                whole((ROWS, D)),
            ],
            out_specs=whole((ROWS, D)),
            scratch_shapes=[pltpu.VMEM((D, ROWS), bf16), pltpu.VMEM((D, ROWS), f32), pltpu.VMEM((2, AR, ROWS), f32)],
        ),
        compiler_params=pltpu.CompilerParams(dimension_semantics=("arbitrary",), vmem_limit_bytes=60 << 20),
        cost_estimate=pl.CostEstimate(flops=6 * ROWS * D * D, bytes_accessed=24 << 20, transcendentals=0),
        name="back_inputs",
    )(meta, *arrived, weights, up, down, rows, gain, grad_middle)


def assemble_kernel(meta, own_ref, other_ref, first_ref, second_ref, turned):
    part, core = meta[6], meta[7]
    for ref, a in ((own_ref, core), (other_ref, 1 - core)):
        for m in range(PARTS):
            where = part ^ m
            piece_rows = lambda n: pl.ds(pl.multiple_of(where * n, n), n)
            first_ref[a, piece_rows(SR), :] = ref[m, 0:SR, :].astype(f32)
            for c in range(D // 128):
                turned[pl.ds(pl.multiple_of(where * WIDTH + c * SR, SR), SR), :] = ref[m, SR : 2 * SR, c * 128 : (c + 1) * 128]
            rows = pl.ds(pl.multiple_of((where % 2) * 2 * SR, 2 * SR), 2 * SR)
            mlp = ref[m, 2 * SR :, :].astype(f32)

            @pl.when(a == 0)
            def _(mlp=mlp, rows=rows, where=where):
                first_ref[2 + where // 2, rows, :] = mlp

            @pl.when(a == 1)
            def _(mlp=mlp, rows=rows, where=where):
                second_ref[2 + where // 2, rows, :] = mlp

        for c in range(D // 128):
            second_ref[a, :, c * 128 : (c + 1) * 128] = turned[c * 128 : (c + 1) * 128, :].T.astype(f32)


def assemble(meta, own, other):
    whole = lambda shape: pl.BlockSpec(shape, lambda i, m: (0,) * len(shape))
    return pl.pallas_call(
        assemble_kernel,
        out_shape=[jax.ShapeDtypeStruct((4, AR, D), f32)] * 2,
        grid_spec=pltpu.PrefetchScalarGridSpec(
            num_scalar_prefetch=1,
            grid=(1,),
            in_specs=[whole((PARTS, 4 * SR, D))] * 2,
            out_specs=[whole((4, AR, D))] * 2,
            scratch_shapes=[pltpu.VMEM((D, AR), bf16)],
        ),
        compiler_params=pltpu.CompilerParams(dimension_semantics=("arbitrary",), vmem_limit_bytes=60 << 20),
        cost_estimate=pl.CostEstimate(flops=1 << 20, bytes_accessed=8 << 20, transcendentals=0),
        name="assemble",
    )(meta, own, other)


HPB = LH
BLOCKS = ROWS // B
NEG = -1e30
FW = 512


def fwd_kernel(bounds, q_ref, k_ref, v_ref, o_ref, lse_ref, kp, qt, vt):
    b1, b2 = bounds[0], bounds[1]
    zpad = jnp.zeros((128 - HD, 128), bf16)
    for h in range(HPB):
        own = slice(h * HD, (h + 1) * HD)
        qt[h, 0:HD, :] = q_ref[own, :]
        qt[h, HD:128, :] = jnp.zeros((128 - HD, TOK), bf16)
        vt[h, 0:HD, :] = v_ref[own, :]
        vt[h, HD:96, :] = (lax.broadcasted_iota(jnp.int32, (16, TOK), 0) == 0).astype(bf16)
        for t in range(TOK // 128):
            kt = k_ref[own, t * 128:(t + 1) * 128]
            kp[h, t * 128:(t + 1) * 128, :] = jnp.concatenate([kt, zpad], axis=0).T

    subs = o_ref.shape[2] // B
    base = 0 if subs > 1 else BLOCKS - 1

    def qblock(n, _):
        chunk, sub = n // subs, n % subs
        i = chunk * BLOCKS + base + sub
        q0 = pl.multiple_of(i * B, B)
        here = pl.ds(pl.multiple_of(sub * B, B), B)
        qpos = q0 + lax.broadcasted_iota(jnp.int32, (1, B), 1)
        srow = start_row(qpos, b1, b2)

        def step(k0, width, masked, carry):
            ks = pl.ds(k0, width)
            ss = [nn(kp[h, ks, :], qt[h, :, pl.ds(q0, B)]) for h in range(HPB)]
            if masked:
                kpos = k0 + lax.broadcasted_iota(jnp.int32, (width, B), 0)
                ok = (kpos >= srow) & (kpos <= qpos)
                ss = [jnp.where(ok, s, NEG) for s in ss]
            out = []
            for h in range(HPB):
                m, acc = carry[h]
                m_new = jnp.maximum(m, jnp.max(ss[h], axis=0, keepdims=True))
                p = jnp.exp(ss[h] - m_new).astype(bf16)
                a = jnp.exp(m - m_new)
                out.append((m_new, acc * a + nn(vt[h, :, ks], p)))
            return tuple(out)

        full = jnp.minimum(i * B // FW, PROMPT // FW)
        lo = jnp.where(i < PROMPT // B, (FW // B) * (i * B // FW), first_block(i, b1, b2))
        carry = tuple((jnp.full((1, B), NEG, f32), jnp.zeros((96, B), f32)) for _ in range(HPB))
        carry = lax.fori_loop(0, full, lambda j, c: step(pl.multiple_of(j * FW, FW), FW, False, c), carry)
        carry = lax.fori_loop(lo, i + 1, lambda j, c: step(pl.multiple_of(j * B, B), B, True, c), carry)
        for h in range(HPB):
            m, acc = carry[h]
            l = acc[HD:HD + 1, :]
            o_ref[chunk, h * HD:(h + 1) * HD, here] = (acc[0:HD, :] / l).astype(bf16)
            lse_ref[h, chunk, :, here] = m + jnp.log(l)
        return 0
    lax.fori_loop(0, PARTS * subs, qblock, 0)

def attn_fwd(bounds, qkvt, subs):
    rows = lambda a: pl.BlockSpec((WIDTH, TOK), lambda i, b: (a, 0))
    width = subs * B
    return pl.pallas_call(
        fwd_kernel,
        out_shape=(jax.ShapeDtypeStruct((PARTS, WIDTH, width), bf16), jax.ShapeDtypeStruct((LH, PARTS, 1, width), f32)),
        grid_spec=pltpu.PrefetchScalarGridSpec(
            num_scalar_prefetch=1,
            grid=(1,),
            in_specs=[rows(0), rows(1), rows(2)],
            out_specs=[
                pl.BlockSpec((PARTS, WIDTH, width), lambda i, b: (0, 0, 0)),
                pl.BlockSpec((LH, PARTS, 1, width), lambda i, b: (0, 0, 0, 0)),
            ],
            scratch_shapes=[pltpu.VMEM((HPB, TOK, 128), bf16), pltpu.VMEM((HPB, 128, TOK), bf16), pltpu.VMEM((HPB, 96, TOK), bf16)],
        ),
        compiler_params=pltpu.CompilerParams(dimension_semantics=("arbitrary",), vmem_limit_bytes=60 << 20),
        cost_estimate=pl.CostEstimate(flops=subs * 13 * 10**9, bytes_accessed=5 << 20, transcendentals=0),
        name="attn_fwd",
    )(bounds, qkvt, qkvt, qkvt)


def parts3(x):
    hi = x.astype(bf16)
    r = x - hi.astype(f32)
    mid = r.astype(bf16)
    lo = (r - mid.astype(f32)).astype(bf16)
    return hi, mid, lo

def bwd_kernel(meta, scale_ref, q_ref, k_ref, v_ref, do_ref, o_ref, lse_ref, out_ref, kp, vp, qt, dot, dkt, dvt, dqt):
    NH = kp.shape[0]
    b1, b2 = meta[0], meta[1]
    row16 = lax.broadcasted_iota(jnp.int32, (16, 128), 0)
    ones3 = (row16 < 3).astype(bf16)
    pad = jnp.zeros((32, 128), bf16)
    scale = scale_ref[...]

    def tail(x):
        hi, mid, lo = parts3(-x)
        rest = jnp.where(row16 == 1, mid.astype(f32), jnp.where(row16 == 2, lo.astype(f32), 0.0))
        return jnp.where(row16 == 0, hi.astype(f32), rest).astype(bf16)

    @pl.loop(0, 2 * PARTS)
    def _(step):
        chunk = step // 2
        for t in range(3):
            off = pl.multiple_of((step % 2) * HALF + t * 128, 128)
            sl, here = pl.ds(pl.multiple_of(chunk * ROWS + off, 128), 128), pl.ds(off, 128)
            for h in range(NH):
                own = slice(h * HD, (h + 1) * HD)
                do, o = do_ref[chunk, own, here], o_ref[chunk, own, here]
                delta = jnp.sum(do.astype(f32) * o.astype(f32), axis=0, keepdims=True)
                qt[h, :, sl] = jnp.concatenate([q_ref[own, sl], tail(lse_ref[h, chunk, :, here]), pad], axis=0)
                dot[h, :, sl] = jnp.concatenate([do, tail(delta), pad], axis=0)
                kp[h, sl, :] = jnp.concatenate([k_ref[own, sl], ones3, pad], axis=0).T
                vp[h, sl, :] = jnp.concatenate([v_ref[own, sl], ones3, pad], axis=0).T

    dkt[...] = jnp.zeros_like(dkt)
    dvt[...] = jnp.zeros_like(dvt)
    dqt[...] = jnp.zeros_like(dqt)

    def block(k0, q0, kw, qw, masked):
        k0, q0 = pl.multiple_of(k0, B), pl.multiple_of(q0, B)
        ks, qs = pl.ds(k0, kw), pl.ds(q0, qw)
        if masked:
            qpos = q0 + lax.broadcasted_iota(jnp.int32, (1, qw), 1)
            kpos = k0 + lax.broadcasted_iota(jnp.int32, (kw, qw), 0)
            ok = (kpos >= start_row(qpos, b1, b2)) & (kpos <= qpos)
        for h in range(NH):
            p = jnp.exp(nn(kp[h, ks, :], qt[h, :, qs]))
            if masked:
                p = jnp.where(ok, p, 0.0)
            ds = (p * nn(vp[h, ks, :], dot[h, :, qs])).astype(bf16)
            dvt[h, :, ks] += nt(dot[h, 0:HD, qs], p.astype(bf16))
            dkt[h, :, ks] += nt(qt[h, 0:HD, qs], ds)
            dqt[h, :, qs] += nn(k_ref[h * HD : (h + 1) * HD, ks], ds)

    @pl.loop(0, 12)
    def _(n):
        qb = jnp.where(n < 9, 3 + n // 3, jnp.where(n == 9, 1, 2))
        kb = jnp.where(n < 9, n % 3, jnp.where(n == 11, 1, 0))
        block(kb * FW, qb * FW, FW, FW, False)

    @pl.loop(0, TOK // FW)
    def _(i):
        lo = jnp.where(i < PROMPT // FW, i, first_block(i * (FW // B), b1, b2) * B // FW)

        @pl.loop(lo, i + 1)
        def _(j):
            block(j * FW, i * FW, FW, FW, True)

    @pl.loop(0, 2 * PARTS)
    def _(step):
        chunk = step // 2
        off = pl.multiple_of((step % 2) * HALF, 128)
        sl, here = pl.ds(pl.multiple_of(chunk * ROWS + off, 128), HALF), pl.ds(off, HALF)
        for h in range(NH):
            own = slice(h * HD, (h + 1) * HD)
            dq = dqt[h, :, sl].astype(bf16).astype(f32) * scale
            out_ref[chunk, 0, own, here] = dq.astype(bf16)
            out_ref[chunk, 1, own, here] = dkt[h, :, sl].astype(bf16)
            out_ref[chunk, 2, own, here] = dvt[h, :, sl].astype(bf16)


def attn_bwd(meta, scale, qkvt, grad, mixture, logsum, first, count, slot):
    rows = lambda a: pl.BlockSpec((count * HD, TOK), lambda i, b: ((LH * a + first) // count, 0))
    return pl.pallas_call(
        bwd_kernel,
        out_shape=jax.ShapeDtypeStruct((PARTS, 3, count * HD, ROWS), bf16),
        grid_spec=pltpu.PrefetchScalarGridSpec(
            num_scalar_prefetch=1,
            grid=(1,),
            in_specs=[
                pl.BlockSpec((HD, 1), lambda i, b: (0, 0)),
                rows(0),
                rows(1),
                rows(2),
                pl.BlockSpec((PARTS, count * HD, ROWS), lambda i, b: (0, slot // count, 0)),
                pl.BlockSpec((PARTS, count * HD, ROWS), lambda i, b: (0, first // count, 0)),
                pl.BlockSpec((count, PARTS, 1, ROWS), lambda i, b: (first // count, 0, 0, 0)),
            ],
            out_specs=pl.BlockSpec((PARTS, 3, count * HD, ROWS), lambda i, b: (0, 0, 0, 0)),
            scratch_shapes=[pltpu.VMEM((count, TOK, 128), bf16)] * 2
            + [pltpu.VMEM((count, 128, TOK), bf16)] * 2
            + [pltpu.VMEM((count, HD, TOK), f32)] * 3,
        ),
        compiler_params=pltpu.CompilerParams(dimension_semantics=("arbitrary",), vmem_limit_bytes=60 << 20),
        cost_estimate=pl.CostEstimate(flops=count * 18 * 10**9, bytes_accessed=count * 8 << 20, transcendentals=0),
        name="attn_bwd",
    )(meta, scale, qkvt, qkvt, qkvt, grad, mixture, logsum)


def mlp_kernel(meta, head_ref, tail_ref, rows_ref, cot_ref, gain_ref, out_ref, up_ref, down_ref, fd_ref, fu_ref,
               hidden_ref, inner_ref, middle_ref, grad_ref, g0_ref, g1_ref, keep_ref, send_ref, mixed, sums):
    step = pl.program_id(0)

    @pl.when(step == 0)
    def _():
        sums[...] = jnp.zeros_like(sums)

    @pl.when(step < 2)
    def _():
        mixed[...] = head_ref[...]

    @pl.when(step == 2)
    def _():
        mixed[...] = tail_ref[...]

    pos = meta[6] * ROWS + step * B + lax.broadcasted_iota(jnp.int32, (B, AR), 0)
    chosen = lax.broadcasted_iota(jnp.int32, (B, AR), 1) // RANK == token_adapter(pos, meta)
    choose = lambda x: jnp.where(chosen, x, 0.0).astype(bf16)
    gain = gain_ref[...]

    middle = rows_ref[...].astype(f32) + nn(mixed[...].T, out_ref[...])
    middle_ref[...] = middle
    q = lax.rsqrt(jnp.mean(middle * middle, axis=1, keepdims=True) + EPSILON)
    normed = (middle * q * gain).astype(bf16)
    inner_up = choose(nn(normed, fd_ref[0]))
    before = nn(normed, up_ref[...]) + nn(inner_up, fu_ref[0])
    gate = jax.nn.sigmoid(before)
    hidden = (before * gate).astype(bf16)
    hidden_ref[...] = hidden
    inner_down = choose(nn(hidden, fd_ref[1]))
    inner_ref[...] = inner_down

    after = cot_ref[...]
    spread_down = choose(nt(after, fu_ref[1]))
    grad_hidden = nt(after, down_ref[...]) + nt(spread_down, fd_ref[1])
    grad_before = (grad_hidden * gate * (1.0 + before * (1.0 - gate))).astype(bf16)
    spread_up = choose(nt(grad_before, fu_ref[0]))
    weighted = gain * (nt(grad_before, up_ref[...]) + nt(spread_up, fd_ref[0]))
    middle = middle_ref[...]
    inside = jnp.mean(middle * weighted, axis=1, keepdims=True)
    grad_middle = after.astype(f32) + (q * weighted - middle * (q * q * q * inside))
    grad_ref[...] = grad_middle
    grad_mixed = nt(out_ref[...], grad_middle.astype(bf16)).astype(bf16)
    for s in range(PARTS):
        g0_ref[s] = grad_mixed[2 * s * PW : (2 * s + 1) * PW]
        g1_ref[s] = grad_mixed[(2 * s + 1) * PW : (2 * s + 2) * PW]

    for n, (a, b) in enumerate(((spread_up, normed), (spread_down, hidden), (inner_up, grad_before), (inner_down, after))):
        sums[n] += nn(a.T, b)

    @pl.when(step == 2)
    def _():
        for ref, half in ((keep_ref, meta[7]), (send_ref, 1 - meta[7])):
            for n in range(2):
                ref[n * AR : (n + 1) * AR, :] = sums[2 * half + n].astype(bf16)


def mlp(meta, mixed_head, mixed_tail, rows, cotangent, gain, weights, flat_down, flat_up):
    whole = lambda shape: pl.BlockSpec(shape, lambda i, m: (0,) * len(shape))
    block = pl.BlockSpec((B, D), lambda i, m: (i, 0))
    pair = pl.BlockSpec((PARTS, PW, B), lambda i, m: (0, 0, i))
    return pl.pallas_call(
        mlp_kernel,
        out_shape=[
            jax.ShapeDtypeStruct((ROWS, D), bf16),
            jax.ShapeDtypeStruct((ROWS, AR), bf16),
            jax.ShapeDtypeStruct((ROWS, D), f32),
            jax.ShapeDtypeStruct((ROWS, D), f32),
            jax.ShapeDtypeStruct((PARTS, PW, ROWS), bf16),
            jax.ShapeDtypeStruct((PARTS, PW, ROWS), bf16),
            jax.ShapeDtypeStruct((2 * AR, D), bf16),
            jax.ShapeDtypeStruct((2 * AR, D), bf16),
        ],
        grid_spec=pltpu.PrefetchScalarGridSpec(
            num_scalar_prefetch=1,
            grid=(ROWS // B,),
            in_specs=[
                pl.BlockSpec((D, B), lambda i, m: (0, jnp.minimum(i, 1))),
                whole((D, B)),
                block,
                block,
                whole((1, D)),
                *[pl.BlockSpec((D, D), lambda i, m, a=a: (0, a)) for a in range(3)],
                whole((2, D, AR)),
                whole((2, AR, D)),
            ],
            out_specs=[block, pl.BlockSpec((B, AR), lambda i, m: (i, 0)), block, block, pair, pair] + [whole((2 * AR, D))] * 2,
            scratch_shapes=[pltpu.VMEM((D, B), bf16), pltpu.VMEM((4, AR, D), f32)],
        ),
        compiler_params=pltpu.CompilerParams(dimension_semantics=("arbitrary",), vmem_limit_bytes=60 << 20),
        cost_estimate=pl.CostEstimate(flops=17 * 10**9, bytes_accessed=32 << 20, transcendentals=0),
        name="mlp",
    )(meta, mixed_head, mixed_tail, rows, cotangent, gain, weights, weights, weights, flat_down, flat_up)


def exchange(value):
    return lax.all_to_all(value, "heads", split_axis=0, concat_axis=0, tiled=True)


def swap(value, axis, mask):
    count = lax.axis_size(axis)
    return lax.ppermute(value, axis, [(i, i ^ mask) for i in range(count)])


def piece(value, index, count):
    rows = value.shape[-2] // count
    return lax.dynamic_slice_in_dim(value, index * rows, rows, axis=value.ndim - 2)


def sum_low(*terms):
    total = terms[0].astype(f32)
    for term in terms[1:]:
        total = total + term.astype(f32)
    return total.astype(bf16)


def far_bits():
    bits = [2]
    while bits[-1] * 2 < lax.axis_size("fsdp"):
        bits.append(bits[-1] * 2)
    return bits


def sum_far(value):
    bits = far_bits()
    for bit, twice in zip(bits[0::2], bits[1::2]):
        value = sum_low(value, *[swap(value, "fsdp", m) for m in (bit, twice, bit | twice)])
    if len(bits) % 2:
        value = sum_low(value, swap(value, "fsdp", bits[-1]))
    return value


def scatter_near(value):
    core = lax.axis_index("fsdp") & 1
    return sum_low(piece(value, core, 2), swap(piece(value, 1 - core, 2), "fsdp", 1))


def scatter_heads(value):
    part = lax.axis_index("heads")
    terms = [swap(piece(value, part ^ m, PARTS), "heads", m) for m in (1, 2, 3)]
    return sum_low(piece(value, part, PARTS), *terms)


def body(
    inputs,
    cotangent,
    lengths,
    adapter_ids,
    query_weight,
    key_weight,
    value_weight,
    out_weight,
    up_weight,
    down_weight,
    attn_gain,
    mlp_gain,
    query_scale,
    adapter_in,
    adapter_out,
):
    part = lax.axis_index("heads")
    rows = inputs[0]
    low, high = rows[:HALF], rows[HALF:]
    near_high = swap(high, "heads", 1)
    far_low = swap(low, "heads", 2)
    ends = PROMPT + jnp.cumsum(lengths[0])
    bounds = ends[:2].astype(jnp.int32)
    ids = adapter_ids[0]
    core = lax.axis_index("fsdp") & 1
    meta = jnp.concatenate([bounds, ids, jnp.stack([part, core]).astype(jnp.int32)])
    flat_down = jnp.transpose(adapter_in, (0, 2, 1, 3)).reshape(4, D, AR)
    flat_up = adapter_out.reshape(4, AR, D)
    gain_attn = attn_gain.astype(f32)
    gain_mlp = mlp_gain.astype(f32)

    def mine(weight):
        return lax.dynamic_slice_in_dim(weight, part * WIDTH, WIDTH, axis=1)

    weights_mine = jnp.concatenate([mine(query_weight), mine(key_weight), mine(value_weight)], axis=1)
    weights_mine = lax.all_gather(weights_mine, "fsdp", axis=0, tiled=True)
    weights_mlp = lax.all_gather(jnp.concatenate([out_weight, up_weight, down_weight], axis=1), "fsdp", axis=0, tiled=True)
    weights_all = lax.all_gather(jnp.concatenate([query_weight, key_weight, value_weight], axis=1), "fsdp", axis=0, tiled=True)

    down_pair = jnp.concatenate([flat_down[0], flat_down[1]], axis=1)
    up_mine = lax.dynamic_slice_in_dim(flat_up[:2], part * WIDTH, WIDTH, axis=2)
    low_late, high_late, down_pair = lax.optimization_barrier((low, high, down_pair))
    near_low = swap(low_late, "heads", 1)
    far_high = swap(high_late, "heads", 2)
    both_low = swap(far_low, "heads", 1)
    both_high = swap(near_high, "heads", 2)
    scale_row = query_scale * HD ** (-0.5)
    scale_mine = jnp.tile(scale_row, LH)[:, None]

    wt, ut = weights_mine.T, jnp.transpose(up_mine, (0, 2, 1))
    done = ()
    for m, low, high in ((0, rows, None), (1, near_low, near_high), (2, far_low, far_high), (3, both_low, both_high)):
        done = qkv_project(meta, part ^ m, low, high, gain_attn[None, :], wt, down_pair, ut, scale_mine, done)
    qkvt, normed_all, inner_all = done
    head_mix, head_log = attn_fwd(bounds, qkvt, 2)
    mixed_head = exchange(head_mix)
    later, head_log = lax.optimization_barrier((bounds, head_log))
    tail_mix, tail_log = attn_fwd(later, qkvt, 1)
    tail_sent, mixed_head = lax.optimization_barrier((tail_mix, mixed_head))
    mixed_tail = exchange(tail_sent)
    mixture = jnp.concatenate([head_mix, tail_mix], axis=2)
    logsum = jnp.concatenate([head_log, tail_log], axis=3)
    mixture, logsum, up_mine, mixed_head = lax.optimization_barrier((mixture, logsum, up_mine, mixed_head))

    hidden_low, inner_down, middle, grad_middle, grad_first_heads, grad_second_heads, mlp_keep, mlp_send = mlp(
        meta, mixed_head.reshape(D, -1), mixed_tail.reshape(D, -1), rows, cotangent[0], gain_mlp[None, :],
        weights_mlp, flat_down[2:], flat_up[2:],
    )
    grad_heads = [exchange(grad_first_heads), exchange(grad_second_heads)]

    mlp_total = sum_low(mlp_keep, swap(mlp_send, "fsdp", 1))
    mlp_total, grad_heads[0] = lax.optimization_barrier((mlp_total, grad_heads[0]))
    mlp_total = scatter_heads(mlp_total)
    scale_column = scale_row[:, None]
    send_back = lambda g: exchange(g.reshape(PARTS, -1, ROWS)).reshape(g.shape)
    grads, arrived = [], []
    grads.append(attn_bwd(meta, scale_column, qkvt, grad_heads[0], mixture, logsum, 0, 2, 0))
    mlp_total, grads[0] = lax.optimization_barrier((mlp_total, grads[0]))
    arrived.append(send_back(grads[0]))
    mlp_total = sum_far(mlp_total)
    meta, grads[0] = lax.optimization_barrier((meta, grads[0]))
    grads.append(attn_bwd(meta, scale_column, qkvt, grad_heads[1], mixture, logsum, 2, 2, 0))
    mlp_total, grads[1] = lax.optimization_barrier((mlp_total, grads[1]))

    meta, arrived[0] = lax.optimization_barrier((meta, arrived[0]))
    keep, send = adapter_grads(meta, grads, normed_all, inner_all, up_mine)
    hidden_late, inner_late, keep = lax.optimization_barrier((hidden_low, inner_down, keep))
    outputs = (middle + (nn(hidden_late, weights_mlp[:, 2 * D :]) + nn(inner_late, flat_up[3]))).astype(bf16)
    total = sum_low(keep, swap(send, "fsdp", 1))
    total = jnp.concatenate([scatter_heads(total[:AR]), total[AR:]])
    total, sent = lax.optimization_barrier((total, grads[1]))
    arrived.append(send_back(sent))
    total, outputs = lax.optimization_barrier((sum_far(total), outputs))
    own = jnp.concatenate([total, mlp_total])
    pieces = [own] + [swap(own, "heads", m) for m in (1, 2, 3)]
    grad_inputs = back_inputs(meta, arrived, weights_all, flat_up[:2], down_pair, rows, gain_attn[None, :], grad_middle)
    pieces, grad_inputs = lax.optimization_barrier((pieces, grad_inputs))
    own = jnp.stack(pieces)
    grad_first, grad_second = assemble(meta, own, swap(own, "fsdp", 1))
    grad_first = jnp.transpose(grad_first.reshape(4, ADAPTERS, RANK, D), (0, 1, 3, 2))
    grad_second = grad_second.reshape(4, ADAPTERS, RANK, D)
    return (outputs[None], grad_inputs[None], grad_first, grad_second)


def solution(mesh):
    placed = (
        P("fsdp", "heads", None),
        P("fsdp", "heads", None),
        P("fsdp", None),
        P("fsdp", None),
        P("fsdp", None),
        P("fsdp", None),
        P("fsdp", None),
        P("fsdp", None),
        P("fsdp", None),
        P("fsdp", None),
        P(),
        P(),
        P(),
        P(),
        P(),
    )
    return jax.shard_map(
        body,
        mesh=mesh,
        in_specs=placed,
        out_specs=(P("fsdp", "heads", None), P("fsdp", "heads", None), P(), P()),
        check_vma=False,
    )
```
